32 devices in a mesh: grp: 8 (over z, core), shard: 4 (over y, x).
Axes of the slice: x: 2, y: 2, z: 4, core: 2. Of those that a mesh axis runs over, the one named last changes fastest.
Arguments:
- prompt_rows: bfloat16 [8, 2048, 768], P('grp', 'shard'), may hold values from -6 to 6
- follow_rows: bfloat16 [8, 2048, 768], P('grp', 'shard'), may hold values from -6 to 6
- memory_rows: bfloat16 [8, 2, 10, 768], P('grp'), may hold values from -6 to 6
- follow_owner: int32 [8, 16], P('grp'), may hold values from 0 to 1, as said below
- follow_length: int32 [8, 16], P('grp'), may hold values from 32 to 118, as said below
- query_weight: bfloat16 [768, 768], P(('grp', 'shard')), may hold values from -0.21875 to 0.21875
- key_weight: bfloat16 [768, 768], P(('grp', 'shard')), may hold values from -0.21875 to 0.21875
- value_weight: bfloat16 [768, 768], P(('grp', 'shard')), may hold values from -0.21875 to 0.21875
- out_weight: bfloat16 [768, 768], P(('grp', 'shard')), may hold values from -0.875 to 0.875
- query_bias: bfloat16 [768], P(('grp', 'shard')), may hold values from -3 to 3
- value_bias: bfloat16 [768], P(('grp', 'shard')), may hold values from -3 to 3
- out_bias: bfloat16 [768], P(('grp', 'shard')), may hold values from -3 to 3
- first_gain: bfloat16 [768], P(('grp', 'shard')), may hold values from 0.5 to 1.5
- first_shift: bfloat16 [768], P(('grp', 'shard')), may hold values from -3 to 3
- up_weight: bfloat16 [768, 3072], P(('grp', 'shard')), may hold values from -0.21875 to 0.21875
- up_bias: bfloat16 [3072], P(('grp', 'shard')), may hold values from -3 to 3
- down_weight: bfloat16 [3072, 768], P(('grp', 'shard')), may hold values from -0.15625 to 0.15625
- down_bias: bfloat16 [768], P(('grp', 'shard')), may hold values from -3 to 3
- second_gain: bfloat16 [768], P(('grp', 'shard')), may hold values from 0.5 to 1.5
- second_shift: bfloat16 [768], P(('grp', 'shard')), may hold values from -3 to 3
- prompt_cotan: bfloat16 [8, 2048, 768], P('grp', 'shard'), may hold values from -6 to 6
- follow_cotan: bfloat16 [8, 2048, 768], P('grp', 'shard'), may hold values from -6 to 6
Outputs:
- prompt_out: bfloat16 [8, 2048, 768], P('grp', 'shard')
- follow_out: bfloat16 [8, 2048, 768], P('grp', 'shard')
- prompt_grad: bfloat16 [8, 2048, 768], P('grp', 'shard')
- follow_grad: bfloat16 [8, 2048, 768], P('grp', 'shard')
- memory_grad: bfloat16 [8, 2, 10, 768], P('grp')
- query_weight_grad: float32 [768, 768], P('shard')
- key_weight_grad: float32 [768, 768], P('shard')
- value_weight_grad: float32 [768, 768], P('shard')
- out_weight_grad: float32 [768, 768], P('shard')
- query_bias_grad: float32 [768], P('shard')
- value_bias_grad: float32 [768], P('shard')
- out_bias_grad: float32 [768], P('shard')
- first_gain_grad: float32 [768], P('shard')
- first_shift_grad: float32 [768], P('shard')
- up_weight_grad: float32 [768, 3072], P('shard')
- up_bias_grad: float32 [3072], P('shard')
- down_weight_grad: float32 [3072, 768], P('shard')
- down_bias_grad: float32 [768], P('shard')
- second_gain_grad: float32 [768], P('shard')
- second_shift_grad: float32 [768], P('shard')
The draws below stay inside these ranges and needn't reach their ends.
Inputs may be any that keep to these rules, and one draw needn't show every extreme that they name: `follow_owner`: each of the 2 prompts of a group owns exactly 8 of its 16 continuations; among the 4 continuations that one device of shard holds, those that share a prompt come in exactly twos. `follow_length`: every group has a continuation with 118 text tokens.
All inputs are finite; a program needn't handle non-finite values.
Results may differ from the reference program's by a relative error of at most 0.022.
Values may be sent and summed in bfloat16 or wider, within the bound.
A program may use at most 384 MiB of HBM per device.

```python
import jax
import jax.numpy as jnp
from jax import lax

D = 768
HEADS = 12
HEAD = 64
FF = 3072
READ = 10
WRITE = 10
PLEN = 1024
CLEN = 128
CONTS_PER = 8
FAM_UNIT = 1
FAMILIES = 2
CONTS = 16
GROUPS = 8


def draw_follow_owner(key, part):
    per_device = FAM_UNIT * CONTS_PER // 2
    devices = CONTS // per_device
    index = jnp.arange(CONTS)
    base = (FAM_UNIT * (index // per_device) + index % per_device // 2) % FAMILIES

    def one_group(group_key):
        key_one, key_two = jax.random.split(group_key)
        relabel = jax.random.permutation(key_one, FAMILIES)
        owners = relabel[base].reshape(devices, per_device)
        orders = jax.vmap(jax.random.permutation, in_axes=(0, None))(jax.random.split(key_two, devices), per_device)
        return jnp.take_along_axis(owners, orders, axis=1).reshape(CONTS)
    return jax.vmap(one_group)(jax.random.split(key, GROUPS)).astype(jnp.int32)


def draw_follow_length(key, part):
    key_one, key_two = jax.random.split(key)
    picked = jax.random.randint(key_one, (GROUPS, CONTS), CLEN // 4, CLEN - WRITE + 1)
    longest = jax.random.randint(key_two, (GROUPS, 1), 0, CONTS)
    chosen = jnp.arange(CONTS)[None, :] == longest
    return jnp.where(chosen, CLEN - WRITE, picked).astype(jnp.int32)


def block_levels(key, extent, pieces, least, top_value):
    level = 1.0
    for dim, shards_of in pieces:
        steps = jax.random.uniform(jax.random.fold_in(jax.random.fold_in(key, 6), dim), (shards_of,), jnp.float32, least / len(pieces), top_value / len(pieces))
        level = level * jnp.repeat(jnp.exp(steps), extent[dim] // shards_of).reshape((-1,) + (1,) * (len(extent) - 1 - dim))
    return level


def noise(rng, dims, scale, bound, cuts=(), held_as=jnp.bfloat16):
    drawn = jax.random.normal(rng, dims, jnp.float32) * scale
    if len(cuts) > 0:
        drawn = block_levels(rng, dims, cuts, -0.22, 0.18) * drawn
    return jnp.clip(drawn, min=-bound, max=bound).astype(held_as)


def setup_inputs(seed: int = 0) -> dict:
    splits = jax.random.split(jax.random.key(seed), 23)
    prompt_rows = noise(splits[0], (GROUPS, FAMILIES * PLEN, D), 1.0, 6.0, ((0, 8), (1, 4)))
    follow_rows = noise(splits[1], (GROUPS, CONTS * CLEN, D), 1.0, 6.0, ((0, 8), (1, 4)))
    memory_rows = noise(splits[2], (GROUPS, FAMILIES, READ, D), 1.0, 6.0, ((0, 8),))
    follow_owner = draw_follow_owner(jax.random.fold_in(splits[22], 71), 0)
    follow_length = draw_follow_length(jax.random.fold_in(splits[22], 71), 0)
    query_weight = noise(splits[5], (D, D), D ** -0.5, 0.21875, ((0, 32),))
    key_weight = noise(splits[6], (D, D), D ** -0.5, 0.21875, ((0, 32),))
    value_weight = noise(splits[7], (D, D), D ** -0.5, 0.21875, ((0, 32),))
    out_weight = noise(splits[8], (D, D), (D // 16) ** -0.5, 0.875, ((0, 32),))
    query_bias = noise(splits[9], (D,), 0.5, 3.0, ((0, 32),))
    value_bias = noise(splits[10], (D,), 0.5, 3.0, ((0, 32),))
    out_bias = noise(splits[11], (D,), 0.5, 3.0, ((0, 32),))
    first_gain = jnp.clip(1.0 + 0.1 * jax.random.normal(splits[12], (D,), jnp.float32), 0.5, 1.5).astype(jnp.bfloat16)
    first_shift = noise(splits[13], (D,), 0.5, 3.0, ((0, 32),))
    up_weight = noise(splits[14], (D, FF), D ** -0.5, 0.21875, ((0, 32),))
    up_bias = noise(splits[15], (FF,), 0.5, 3.0, ((0, 32),))
    down_weight = noise(splits[16], (FF, D), (FF // 2) ** -0.5, 0.15625, ((0, 32),))
    down_bias = noise(splits[17], (D,), 0.5, 3.0, ((0, 32),))
    second_gain = jnp.clip(1.0 + 0.1 * jax.random.normal(splits[18], (D,), jnp.float32), 0.5, 1.5).astype(jnp.bfloat16)
    second_shift = noise(splits[19], (D,), 0.5, 3.0, ((0, 32),))
    prompt_cotan = noise(splits[20], (GROUPS, FAMILIES * PLEN, D), 1.0, 6.0, ((0, 8), (1, 4)))
    follow_cotan = noise(splits[21], (GROUPS, CONTS * CLEN, D), 1.0, 6.0, ((0, 8), (1, 4)))
    return {"prompt_rows": prompt_rows, "follow_rows": follow_rows, "memory_rows": memory_rows, "follow_owner": follow_owner, "follow_length": follow_length, "query_weight": query_weight, "key_weight": key_weight, "value_weight": value_weight, "out_weight": out_weight, "query_bias": query_bias, "value_bias": value_bias, "out_bias": out_bias, "first_gain": first_gain, "first_shift": first_shift, "up_weight": up_weight, "up_bias": up_bias, "down_weight": down_weight, "down_bias": down_bias, "second_gain": second_gain, "second_shift": second_shift, "prompt_cotan": prompt_cotan, "follow_cotan": follow_cotan}


EPSILON = 1e-12
SCALE = 0.125
NEGATIVE = -1e+30
ROOT_HALF = 0.7071067811865476
HIGHEST = lax.Precision.HIGHEST

@jax.custom_vjp
def low(v):
    return lax.optimization_barrier(v.astype(jnp.bfloat16)).astype(jnp.float32)

@jax.custom_vjp
def low_back(v):
    return v

def low_keep(v):
    return (low(v), None)

def low_pass(kept, grad):
    return (grad,)

def back_keep(v):
    return (v, None)

def back_low(kept, grad):
    return (low(grad),)
low.defvjp(low_keep, low_pass)
low_back.defvjp(back_keep, back_low)

def product(left, right):
    return jnp.matmul(left, right, precision=HIGHEST)

def layer_norm(hidden, gain, shift):
    center = hidden - lax.optimization_barrier(jnp.mean(hidden, axis=-1, keepdims=True))
    inverse = lax.rsqrt(lax.optimization_barrier(jnp.mean(center * center, axis=-1, keepdims=True)) + EPSILON)
    return center * inverse * gain + shift

def gelu_exact(hidden):
    return 0.5 * hidden * (1.0 + lax.erf(hidden * ROOT_HALF))

def attend(queries, keys, values, valid):
    count, length, width = queries.shape
    span = keys.shape[1]
    query_heads = queries.reshape(count, length, HEADS, HEAD)
    key_heads = keys.reshape(count, span, HEADS, HEAD)
    value_heads = values.reshape(count, span, HEADS, HEAD)
    scores = low_back(jnp.einsum('nqhd,nkhd->nhqk', query_heads, key_heads, precision=HIGHEST) * SCALE)
    scores = jnp.where(valid[:, None, None, :], scores, NEGATIVE)
    powers = jnp.exp(scores - lax.optimization_barrier(jnp.max(scores, axis=-1, keepdims=True)))
    chances = low(powers / lax.optimization_barrier(jnp.sum(powers, axis=-1, keepdims=True)))
    result = jnp.einsum('nhqk,nkhd->nqhd', chances, value_heads, precision=HIGHEST)
    return result.reshape(count, length, width)

def forward(prompt, follow, memory, owner, length, query_weight, key_weight, value_weight, out_weight, query_bias, value_bias, out_bias, first_gain, first_shift, up_weight, up_bias, down_weight, down_bias, second_gain, second_shift):
    groups = prompt.shape[0]
    families = memory.shape[1]
    width = prompt.shape[2]
    items = groups * families

    def project(hidden):
        query = low(low_back(product(hidden, query_weight) + query_bias))
        key = low(low_back(product(hidden, key_weight)))
        value = low(low_back(product(hidden, value_weight) + value_bias))
        return (query, key, value)
    query_p, key_p, value_p = project(prompt)
    query_f, key_f, value_f = project(follow)
    key_m = low(low_back(product(memory, key_weight)))
    value_m = low(low_back(product(memory, value_weight) + value_bias))
    key_table = key_p.reshape(groups, families, PLEN, width)
    value_table = value_p.reshape(groups, families, PLEN, width)
    prompt_queries = query_p.reshape(items, 1, PLEN, width)
    prompt_keys = jnp.concatenate([key_m, key_table], axis=2).reshape(items, 1, READ + PLEN, width)
    prompt_values = jnp.concatenate([value_m, value_table], axis=2).reshape(items, 1, READ + PLEN, width)
    all_valid = jnp.ones((1, READ + PLEN), dtype=bool)

    def prompt_item(item):
        queries, keys, values = item
        return attend(queries, keys, values, all_valid)
    prompt_att = lax.map(jax.checkpoint(prompt_item), (prompt_queries, prompt_keys, prompt_values))
    prompt_att = prompt_att.reshape(groups, families * PLEN, width)
    follow_queries = query_f.reshape(items, CONTS_PER, CLEN, width)
    own_keys = key_f.reshape(items, CONTS_PER, CLEN, width)
    own_values = value_f.reshape(items, CONTS_PER, CLEN, width)
    owner_items = owner.reshape(items, CONTS_PER).astype(jnp.int32)
    length_items = length.reshape(items, CONTS_PER).astype(jnp.int32)
    group_items = (jnp.arange(items) // families).astype(jnp.int32)
    positions = jnp.arange(CLEN).astype(jnp.int32)
    open_span = jnp.ones((CONTS_PER, READ + PLEN), dtype=bool)

    def follow_item(item):
        queries, own_key, own_value, owners, lengths, group = item
        mem_keys = key_m[group][owners]
        mem_values = value_m[group][owners]
        pro_keys = key_table[group][owners]
        pro_values = value_table[group][owners]
        keys = jnp.concatenate([mem_keys, pro_keys, own_key], axis=1)
        values = jnp.concatenate([mem_values, pro_values, own_value], axis=1)
        own_valid = (positions[None, :] < lengths[:, None]) | (positions[None, :] >= CLEN - WRITE)
        valid = jnp.concatenate([open_span, own_valid], axis=1)
        return attend(queries, keys, values, valid)
    follow_att = lax.map(jax.checkpoint(follow_item), (follow_queries, own_keys, own_values, owner_items, length_items, group_items))
    follow_att = follow_att.reshape(groups, CONTS_PER * families * CLEN, width)

    def finish(hidden, attended):
        mixed = low(low_back(attended))
        branch = low_back(product(mixed, out_weight) + out_bias)
        normed = layer_norm(hidden + branch, first_gain, first_shift)
        inner = low_back(product(low(normed), up_weight) + up_bias)
        activated = low(gelu_exact(inner))
        second = low_back(product(activated, down_weight) + down_bias)
        return layer_norm(normed + second, second_gain, second_shift)
    return (finish(prompt, prompt_att), finish(follow, follow_att))

def reference(prompt_rows, follow_rows, memory_rows, follow_owner, follow_length, query_weight, key_weight, value_weight, out_weight, query_bias, value_bias, out_bias, first_gain, first_shift, up_weight, up_bias, down_weight, down_bias, second_gain, second_shift, prompt_cotan, follow_cotan):
    inputs = (prompt_rows, follow_rows, memory_rows, query_weight, key_weight, value_weight, out_weight, query_bias, value_bias, out_bias, first_gain, first_shift, up_weight, up_bias, down_weight, down_bias, second_gain, second_shift)
    floats = tuple((tensor.astype(jnp.float32) for tensor in inputs))

    def wrapped(*values):
        return forward(values[0], values[1], values[2], follow_owner, follow_length, *values[3:])
    outputs, pullback = jax.vjp(wrapped, *floats)
    grads = pullback((prompt_cotan.astype(jnp.float32), follow_cotan.astype(jnp.float32)))
    return (outputs[0].astype(jnp.bfloat16), outputs[1].astype(jnp.bfloat16), grads[0].astype(jnp.bfloat16), grads[1].astype(jnp.bfloat16), grads[2].astype(jnp.bfloat16), grads[3], grads[4], grads[5], grads[6], grads[7], grads[8], grads[9], grads[10], grads[11], grads[12], grads[13], grads[14], grads[15], grads[16], grads[17])
```

```python
import jax
import jax.numpy as jnp
from jax import lax
from jax.experimental import pallas as pl
from jax.experimental.pallas import tpu as pltpu
from jax.sharding import PartitionSpec as P

HEADS = 12
HEAD = 64
READ = 10
WRITE = 10
PLEN = 1024
CLEN = 128
CONTS_PER = 8


EPSILON = 1e-12
SCALE = 0.125
NEGATIVE = -1e30
ROOT_HALF = 0.7071067811865476
ROOT_GAUSS = 0.3989422804014327


def product(left, right):
    return jnp.dot(left, right, preferred_element_type=jnp.float32)


def times_back(left, right):
    return lax.dot_general(
        left, right, (((1,), (1,)), ((), ())), preferred_element_type=jnp.float32
    )


def outer_sum(left, right):
    return lax.dot_general(
        left, right, (((0,), (0,)), ((), ())), preferred_element_type=jnp.float32
    )


def column_sum(values):
    return jnp.sum(values.astype(jnp.float32), axis=0)


def layer_norm(hidden, gain, shift):
    center = hidden - jnp.mean(hidden, axis=-1, keepdims=True)
    inverse = lax.rsqrt(jnp.mean(center * center, axis=-1, keepdims=True) + EPSILON)
    normed = center * inverse
    return (normed * gain.astype(jnp.float32) + shift.astype(jnp.float32), normed, inverse)


def norm_back(grad_normed, normed, inverse):
    centered = grad_normed - jnp.mean(grad_normed, axis=-1, keepdims=True)
    return inverse * (centered - normed * jnp.mean(grad_normed * normed, axis=-1, keepdims=True))


def gelu_exact(hidden):
    return 0.5 * hidden * (1.0 + lax.erf(hidden * ROOT_HALF))


def gelu_slope(hidden):
    return (
        0.5 * (1.0 + lax.erf(hidden * ROOT_HALF))
        + hidden * jnp.exp(-0.5 * hidden * hidden) * ROOT_GAUSS
    )


def split_heads(values):
    return values.reshape(values.shape[0], values.shape[1], HEADS, HEAD)


def block_scores(queries, keys, valid):
    scores = (
        jnp.einsum(
            "nqhd,nkhd->nhqk",
            split_heads(queries),
            split_heads(keys),
            preferred_element_type=jnp.float32,
        )
        * SCALE
    )
    return jnp.where(valid[:, None, None, :], scores, NEGATIVE)


def attend_forward(queries, keys, values, valid):
    scores = block_scores(queries, keys, valid)
    maximum = jnp.max(scores, axis=-1, keepdims=True)
    powers = jnp.exp(scores - maximum)
    totals = jnp.sum(powers, axis=-1, keepdims=True)
    chances = (powers / totals).astype(jnp.bfloat16)
    result = jnp.einsum(
        "nhqk,nkhd->nqhd", chances, split_heads(values), preferred_element_type=jnp.float32
    )
    return (result.reshape(-1, queries.shape[2]), maximum + jnp.log(totals))


def attend_backward(queries, keys, values, valid, logsum, grad_out):
    width = queries.shape[2]
    scores = block_scores(queries, keys, valid)
    chances = jnp.exp(scores - logsum)
    grad_heads = split_heads(grad_out)
    grad_chance = jnp.einsum(
        "nqhd,nkhd->nhqk", grad_heads, split_heads(values), preferred_element_type=jnp.float32
    )
    inner = jnp.sum(chances * grad_chance, axis=-1, keepdims=True)
    grad_score = (chances * (grad_chance - inner)).astype(jnp.bfloat16)
    grad_query = (
        jnp.einsum(
            "nhqk,nkhd->nqhd", grad_score, split_heads(keys), preferred_element_type=jnp.float32
        )
        * SCALE
    )
    grad_key = (
        jnp.einsum(
            "nhqk,nqhd->nkhd", grad_score, split_heads(queries), preferred_element_type=jnp.float32
        )
        * SCALE
    )
    grad_value = jnp.einsum(
        "nhqk,nqhd->nkhd",
        chances.astype(jnp.bfloat16),
        grad_heads,
        preferred_element_type=jnp.float32,
    )
    span = keys.shape[1]
    return (
        grad_query.reshape(-1, width),
        grad_key.reshape(keys.shape[0], span, width),
        grad_value.reshape(keys.shape[0], span, width),
    )


def body_any(
    prompt_rows,
    follow_rows,
    memory_rows,
    follow_owner,
    follow_length,
    query_weight,
    key_weight,
    value_weight,
    out_weight,
    query_bias,
    value_bias,
    out_bias,
    first_gain,
    first_shift,
    up_weight,
    up_bias,
    down_weight,
    down_bias,
    second_gain,
    second_shift,
    prompt_cotan,
    follow_cotan,
):
    (
        query_mat,
        key_mat,
        value_mat,
        out_mat,
        query_add,
        value_add,
        out_add,
        gain_one,
        shift_one,
        up_mat,
        up_add,
        down_mat,
        down_add,
        gain_two,
        shift_two,
    ) = (
        lax.all_gather(query_weight, ("grp", "shard"), axis=0, tiled=True),
        lax.all_gather(key_weight, ("grp", "shard"), axis=0, tiled=True),
        lax.all_gather(value_weight, ("grp", "shard"), axis=0, tiled=True),
        lax.all_gather(out_weight, ("grp", "shard"), axis=0, tiled=True),
        lax.all_gather(query_bias, ("grp", "shard"), axis=0, tiled=True),
        lax.all_gather(value_bias, ("grp", "shard"), axis=0, tiled=True),
        lax.all_gather(out_bias, ("grp", "shard"), axis=0, tiled=True),
        lax.all_gather(first_gain, ("grp", "shard"), axis=0, tiled=True),
        lax.all_gather(first_shift, ("grp", "shard"), axis=0, tiled=True),
        lax.all_gather(up_weight, ("grp", "shard"), axis=0, tiled=True),
        lax.all_gather(up_bias, ("grp", "shard"), axis=0, tiled=True),
        lax.all_gather(down_weight, ("grp", "shard"), axis=0, tiled=True),
        lax.all_gather(down_bias, ("grp", "shard"), axis=0, tiled=True),
        lax.all_gather(second_gain, ("grp", "shard"), axis=0, tiled=True),
        lax.all_gather(second_shift, ("grp", "shard"), axis=0, tiled=True),
    )
    shard_index = lax.axis_index("shard")
    prompt = prompt_rows[0]
    follow = follow_rows[0]
    p_count = prompt.shape[0]
    f_count = follow.shape[0]
    width = prompt.shape[1]
    families = memory_rows.shape[1]
    all_rows = jnp.concatenate([prompt, follow], axis=0)
    memory_flat = memory_rows[0].reshape(families * READ, width)
    query_low = (product(all_rows, query_mat) + query_add.astype(jnp.float32)).astype(jnp.bfloat16)
    key_low = product(all_rows, key_mat).astype(jnp.bfloat16)
    value_low = (product(all_rows, value_mat) + value_add.astype(jnp.float32)).astype(jnp.bfloat16)
    mem_key = product(memory_flat, key_mat).astype(jnp.bfloat16).reshape(families, READ, width)
    mem_value = (
        (product(memory_flat, value_mat) + value_add.astype(jnp.float32))
        .astype(jnp.bfloat16)
        .reshape(families, READ, width)
    )
    half_prompt = PLEN // 2
    per_block = CONTS_PER // 2
    prompt_blocks = p_count // half_prompt
    conts_here = f_count // CLEN
    positions = jnp.arange(CLEN)
    open_span = jnp.ones((per_block, READ + PLEN), dtype=bool)
    owner_row = follow_owner[0]
    length_row = follow_length[0]
    prompt_keys, prompt_values = (
        lax.all_gather(key_low[:p_count], "shard", axis=0, tiled=True),
        lax.all_gather(value_low[:p_count], "shard", axis=0, tiled=True),
    )
    key_table = prompt_keys.reshape(families, PLEN, width)
    value_table = prompt_values.reshape(families, PLEN, width)

    def prompt_inputs(block):
        start = block * half_prompt
        family = (shard_index * p_count + start) // PLEN
        keys = jnp.concatenate([mem_key[family], key_table[family]], axis=0)[None]
        values = jnp.concatenate([mem_value[family], value_table[family]], axis=0)[None]
        valid = jnp.ones((1, READ + PLEN), dtype=bool)
        return (query_low[start : start + half_prompt][None], keys, values, valid, family)

    def follow_inputs(block):
        first_row = p_count + block * per_block * CLEN
        chosen = shard_index * conts_here + block * per_block + jnp.arange(per_block)
        owners = owner_row[chosen]
        lengths = length_row[chosen]
        own_keys = key_low[first_row : first_row + per_block * CLEN].reshape(per_block, CLEN, width)
        own_values = value_low[first_row : first_row + per_block * CLEN].reshape(
            per_block, CLEN, width
        )
        keys = jnp.concatenate([mem_key[owners], key_table[owners], own_keys], axis=1)
        values = jnp.concatenate([mem_value[owners], value_table[owners], own_values], axis=1)
        own_valid = (positions[None, :] < lengths[:, None]) | (positions[None, :] >= CLEN - WRITE)
        valid = jnp.concatenate([open_span, own_valid], axis=1)
        queries = query_low[first_row : first_row + per_block * CLEN].reshape(
            per_block, CLEN, width
        )
        return (queries, keys, values, valid, owners)

    attended = []
    saved = []
    block = 0
    queries, keys, values, valid, family = prompt_inputs(block)
    result, logsum = attend_forward(queries, keys, values, valid)
    attended.append(result)
    saved.append(logsum)
    block = 0
    queries, keys, values, valid, owners = follow_inputs(block)
    result, logsum = attend_forward(queries, keys, values, valid)
    attended.append(result)
    saved.append(logsum)
    mixed = jnp.concatenate(attended, axis=0).astype(jnp.bfloat16)
    branch = product(mixed, out_mat) + out_add.astype(jnp.float32)
    first, normed_one, inverse_one = layer_norm(
        all_rows.astype(jnp.float32) + branch, gain_one, shift_one
    )
    first_low = first.astype(jnp.bfloat16)
    inner = product(first_low, up_mat) + up_add.astype(jnp.float32)
    activated = gelu_exact(inner).astype(jnp.bfloat16)
    second = product(activated, down_mat) + down_add.astype(jnp.float32)
    output, normed_two, inverse_two = layer_norm(first + second, gain_two, shift_two)
    output = output.astype(jnp.bfloat16)
    (
        query_mat,
        key_mat,
        value_mat,
        out_mat,
        query_add,
        value_add,
        out_add,
        gain_one,
        shift_one,
        up_mat,
        up_add,
        down_mat,
        down_add,
        gain_two,
        shift_two,
    ) = (
        lax.all_gather(query_weight, ("grp", "shard"), axis=0, tiled=True),
        lax.all_gather(key_weight, ("grp", "shard"), axis=0, tiled=True),
        lax.all_gather(value_weight, ("grp", "shard"), axis=0, tiled=True),
        lax.all_gather(out_weight, ("grp", "shard"), axis=0, tiled=True),
        lax.all_gather(query_bias, ("grp", "shard"), axis=0, tiled=True),
        lax.all_gather(value_bias, ("grp", "shard"), axis=0, tiled=True),
        lax.all_gather(out_bias, ("grp", "shard"), axis=0, tiled=True),
        lax.all_gather(first_gain, ("grp", "shard"), axis=0, tiled=True),
        lax.all_gather(first_shift, ("grp", "shard"), axis=0, tiled=True),
        lax.all_gather(up_weight, ("grp", "shard"), axis=0, tiled=True),
        lax.all_gather(up_bias, ("grp", "shard"), axis=0, tiled=True),
        lax.all_gather(down_weight, ("grp", "shard"), axis=0, tiled=True),
        lax.all_gather(down_bias, ("grp", "shard"), axis=0, tiled=True),
        lax.all_gather(second_gain, ("grp", "shard"), axis=0, tiled=True),
        lax.all_gather(second_shift, ("grp", "shard"), axis=0, tiled=True),
    )
    cotangent = jnp.concatenate([prompt_cotan[0], follow_cotan[0]], axis=0).astype(jnp.float32)
    grad_gain_two = jnp.sum(cotangent * normed_two, axis=0)
    grad_shift_two = jnp.sum(cotangent, axis=0)
    grad_mid = norm_back(cotangent * gain_two.astype(jnp.float32), normed_two, inverse_two)
    grad_down = grad_mid.astype(jnp.bfloat16)
    grad_down_mat = outer_sum(activated, grad_down)
    grad_down_add = column_sum(grad_down)
    grad_inner = (times_back(grad_down, down_mat) * gelu_slope(inner)).astype(jnp.bfloat16)
    grad_up_mat = outer_sum(first_low, grad_inner)
    grad_up_add = column_sum(grad_inner)
    grad_first = grad_mid + times_back(grad_inner, up_mat)
    grad_gain_one = jnp.sum(grad_first * normed_one, axis=0)
    grad_shift_one = jnp.sum(grad_first, axis=0)
    grad_hidden = norm_back(grad_first * gain_one.astype(jnp.float32), normed_one, inverse_one)
    grad_branch = grad_hidden.astype(jnp.bfloat16)
    grad_out_mat = outer_sum(mixed, grad_branch)
    grad_out_add = column_sum(grad_branch)
    grad_mixed = times_back(grad_branch, out_mat).astype(jnp.bfloat16)
    mem_key_acc = jnp.zeros((families, READ, width), jnp.float32)
    mem_value_acc = jnp.zeros((families, READ, width), jnp.float32)
    prompt_key_acc = jnp.zeros((families, PLEN, width), jnp.float32)
    prompt_value_acc = jnp.zeros((families, PLEN, width), jnp.float32)
    block = 0
    queries, keys, values, valid, family = prompt_inputs(block)
    start = block * half_prompt
    grad_query, grad_key, grad_value = attend_backward(
        queries, keys, values, valid, saved[block], grad_mixed[start : start + half_prompt][None]
    )
    query_parts = grad_query
    mem_key_acc = mem_key_acc.at[family].add(grad_key[0, :READ])
    mem_value_acc = mem_value_acc.at[family].add(grad_value[0, :READ])
    prompt_key_acc = prompt_key_acc.at[family].add(grad_key[0, READ:])
    prompt_value_acc = prompt_value_acc.at[family].add(grad_value[0, READ:])
    prompt_query_low = query_parts.astype(jnp.bfloat16)
    block = 0
    queries, keys, values, valid, owners = follow_inputs(block)
    first_row = p_count + block * per_block * CLEN
    grad_slice = grad_mixed[first_row : first_row + per_block * CLEN].reshape(
        per_block, CLEN, width
    )
    grad_query, grad_key, grad_value = attend_backward(
        queries, keys, values, valid, saved[prompt_blocks + block], grad_slice
    )
    mem_key_acc = mem_key_acc.at[owners].add(grad_key[:, :READ])
    mem_value_acc = mem_value_acc.at[owners].add(grad_value[:, :READ])
    prompt_key_acc = prompt_key_acc.at[owners].add(grad_key[:, READ : READ + PLEN])
    prompt_value_acc = prompt_value_acc.at[owners].add(grad_value[:, READ : READ + PLEN])
    own_key_parts = grad_key[:, READ + PLEN :].reshape(-1, width)
    own_value_parts = grad_value[:, READ + PLEN :].reshape(-1, width)
    prompt_key_grad, prompt_value_grad = (
        lax.psum_scatter(
            prompt_key_acc.reshape(families * PLEN, width).astype(jnp.bfloat16),
            "shard",
            scatter_dimension=0,
            tiled=True,
        ).astype(jnp.float32),
        lax.psum_scatter(
            prompt_value_acc.reshape(families * PLEN, width).astype(jnp.bfloat16),
            "shard",
            scatter_dimension=0,
            tiled=True,
        ).astype(jnp.float32),
    )
    follow_query_low = grad_query.astype(jnp.bfloat16)
    follow_key_low = own_key_parts.astype(jnp.bfloat16)
    follow_value_low = own_value_parts.astype(jnp.bfloat16)
    mem_key_sum, mem_value_sum = (
        lax.psum(mem_key_acc.astype(jnp.bfloat16), "shard").astype(jnp.float32),
        lax.psum(mem_value_acc.astype(jnp.bfloat16), "shard").astype(jnp.float32),
    )
    grad_query_low = jnp.concatenate([prompt_query_low, follow_query_low], axis=0)
    grad_key_low = jnp.concatenate([prompt_key_grad.astype(jnp.bfloat16), follow_key_low], axis=0)
    grad_value_low = jnp.concatenate(
        [prompt_value_grad.astype(jnp.bfloat16), follow_value_low], axis=0
    )
    mem_key_low = mem_key_sum.astype(jnp.bfloat16).reshape(families * READ, width)
    mem_value_low = mem_value_sum.astype(jnp.bfloat16).reshape(families * READ, width)
    grad_rows_all = (
        grad_hidden
        + times_back(grad_query_low, query_mat)
        + times_back(grad_key_low, key_mat)
        + times_back(grad_value_low, value_mat)
    ).astype(jnp.bfloat16)
    grad_memory = (
        (times_back(mem_key_low, key_mat) + times_back(mem_value_low, value_mat))
        .astype(jnp.bfloat16)
        .reshape(1, families, READ, width)
    )
    leader = (shard_index == 0).astype(jnp.float32)
    grad_query_mat = outer_sum(all_rows, grad_query_low)
    grad_query_add = column_sum(grad_query_low)
    grad_key_mat = outer_sum(all_rows, grad_key_low) + leader * outer_sum(memory_flat, mem_key_low)
    grad_value_mat = outer_sum(all_rows, grad_value_low) + leader * outer_sum(
        memory_flat, mem_value_low
    )
    grad_value_add = column_sum(grad_value_low) + leader * column_sum(mem_value_low)
    pieces = (
        lax.psum_scatter(
            grad_query_mat.astype(jnp.bfloat16), "shard", scatter_dimension=0, tiled=True
        ).astype(jnp.float32),
        lax.psum_scatter(
            grad_key_mat.astype(jnp.bfloat16), "shard", scatter_dimension=0, tiled=True
        ).astype(jnp.float32),
        lax.psum_scatter(
            grad_value_mat.astype(jnp.bfloat16), "shard", scatter_dimension=0, tiled=True
        ).astype(jnp.float32),
        lax.psum_scatter(
            grad_out_mat.astype(jnp.bfloat16), "shard", scatter_dimension=0, tiled=True
        ).astype(jnp.float32),
        lax.psum_scatter(
            grad_query_add.astype(jnp.bfloat16), "shard", scatter_dimension=0, tiled=True
        ).astype(jnp.float32),
        lax.psum_scatter(
            grad_value_add.astype(jnp.bfloat16), "shard", scatter_dimension=0, tiled=True
        ).astype(jnp.float32),
        lax.psum_scatter(
            grad_out_add.astype(jnp.bfloat16), "shard", scatter_dimension=0, tiled=True
        ).astype(jnp.float32),
        lax.psum_scatter(
            grad_gain_one.astype(jnp.bfloat16), "shard", scatter_dimension=0, tiled=True
        ).astype(jnp.float32),
        lax.psum_scatter(
            grad_shift_one.astype(jnp.bfloat16), "shard", scatter_dimension=0, tiled=True
        ).astype(jnp.float32),
        lax.psum_scatter(
            grad_up_mat.astype(jnp.bfloat16), "shard", scatter_dimension=0, tiled=True
        ).astype(jnp.float32),
        lax.psum_scatter(
            grad_up_add.astype(jnp.bfloat16), "shard", scatter_dimension=0, tiled=True
        ).astype(jnp.float32),
        lax.psum_scatter(
            grad_down_mat.astype(jnp.bfloat16), "shard", scatter_dimension=0, tiled=True
        ).astype(jnp.float32),
        lax.psum_scatter(
            grad_down_add.astype(jnp.bfloat16), "shard", scatter_dimension=0, tiled=True
        ).astype(jnp.float32),
        lax.psum_scatter(
            grad_gain_two.astype(jnp.bfloat16), "shard", scatter_dimension=0, tiled=True
        ).astype(jnp.float32),
        lax.psum_scatter(
            grad_shift_two.astype(jnp.bfloat16), "shard", scatter_dimension=0, tiled=True
        ).astype(jnp.float32),
    )
    summed = (
        lax.psum(pieces[0].astype(jnp.bfloat16), "grp").astype(jnp.float32),
        lax.psum(pieces[1].astype(jnp.bfloat16), "grp").astype(jnp.float32),
        lax.psum(pieces[2].astype(jnp.bfloat16), "grp").astype(jnp.float32),
        lax.psum(pieces[3].astype(jnp.bfloat16), "grp").astype(jnp.float32),
        lax.psum(pieces[4].astype(jnp.bfloat16), "grp").astype(jnp.float32),
        lax.psum(pieces[5].astype(jnp.bfloat16), "grp").astype(jnp.float32),
        lax.psum(pieces[6].astype(jnp.bfloat16), "grp").astype(jnp.float32),
        lax.psum(pieces[7].astype(jnp.bfloat16), "grp").astype(jnp.float32),
        lax.psum(pieces[8].astype(jnp.bfloat16), "grp").astype(jnp.float32),
        lax.psum(pieces[9].astype(jnp.bfloat16), "grp").astype(jnp.float32),
        lax.psum(pieces[10].astype(jnp.bfloat16), "grp").astype(jnp.float32),
        lax.psum(pieces[11].astype(jnp.bfloat16), "grp").astype(jnp.float32),
        lax.psum(pieces[12].astype(jnp.bfloat16), "grp").astype(jnp.float32),
        lax.psum(pieces[13].astype(jnp.bfloat16), "grp").astype(jnp.float32),
        lax.psum(pieces[14].astype(jnp.bfloat16), "grp").astype(jnp.float32),
    )
    return (
        output[:p_count][None],
        output[p_count:][None],
        grad_rows_all[:p_count][None],
        grad_rows_all[p_count:][None],
        grad_memory,
        summed[0],
        summed[1],
        summed[2],
        summed[3],
        summed[4],
        summed[5],
        summed[6],
        summed[7],
        summed[8],
        summed[9],
        summed[10],
        summed[11],
        summed[12],
        summed[13],
        summed[14],
    )


MEM = 16
HALF = PLEN // 2
OWN = 512
CONT = HALF + HALF + MEM
KEYS = CONT + OWN
QROWS = HALF + OWN
PAIRS = HEADS // 2
NAMES = ("grp", "shard")


def pairs_fit(mesh):
    return mesh.shape["shard"] == 4 and mesh.shape["grp"] == 8


def head_mask(head):
    lane = lax.broadcasted_iota(jnp.int32, (1, 2 * HEAD), 1)
    return lane // HEAD == head


def pick(mask, values):
    return jnp.where(mask, values.astype(jnp.float32), 0.0).astype(jnp.bfloat16)


def flip(values):
    return values.astype(jnp.float32).T.astype(jnp.bfloat16)


def own_scores(keys, queries):
    parts = []
    for cont in range(OWN // CLEN):
        part = slice(cont * CLEN, (cont + 1) * CLEN)
        parts.append(times_back(keys[part], queries[part]))
    return jnp.concatenate(parts, axis=1)


def attend_kernel(query_ref, key_ref, value_ref, bias_ref, out_ref, log_ref):
    mem_valid = lax.broadcasted_iota(jnp.int32, (MEM, 1), 0) < READ
    value_flip = flip(value_ref[...])
    results = []
    for head in range(2):
        mask = head_mask(head)
        queries = pick(mask, query_ref[...])
        main = times_back(key_ref[: 2 * HALF], queries)
        memory = jnp.where(mem_valid, times_back(key_ref[2 * HALF : CONT], queries), NEGATIVE)
        own = own_scores(key_ref[CONT:], queries[HALF:]) + bias_ref[...]
        top = jnp.maximum(
            jnp.max(main, axis=0, keepdims=True), jnp.max(memory, axis=0, keepdims=True)
        )
        top_own = jnp.maximum(top[:, HALF:], jnp.max(own, axis=0, keepdims=True))
        top = jnp.concatenate([top[:, :HALF], top_own], axis=1)
        main = jnp.exp(main - top)
        memory = jnp.exp(memory - top)
        own = jnp.exp(own - top_own)
        total = jnp.sum(main, axis=0, keepdims=True) + jnp.sum(memory, axis=0, keepdims=True)
        total = jnp.concatenate(
            [total[:, :HALF], total[:, HALF:] + jnp.sum(own, axis=0, keepdims=True)], axis=1
        )
        flipped = value_flip[head * HEAD : (head + 1) * HEAD]
        result = product(flipped[:, : 2 * HALF], main.astype(jnp.bfloat16))
        result += product(flipped[:, 2 * HALF : CONT], memory.astype(jnp.bfloat16))
        own = own.astype(jnp.bfloat16)
        own_parts = []
        for cont in range(OWN // CLEN):
            own_parts.append(
                product(
                    flipped[:, CONT + cont * CLEN : CONT + (cont + 1) * CLEN],
                    own[:, cont * CLEN : (cont + 1) * CLEN],
                )
            )
        result = jnp.concatenate(
            [result[:, :HALF], result[:, HALF:] + jnp.concatenate(own_parts, axis=1)], axis=1
        )
        results.append(result / total)
        log_ref[head : head + 1] = top + jnp.log(total)
    out_ref[...] = jnp.concatenate(results, axis=0).T.astype(jnp.bfloat16)


def attend_back_kernel(
    query_ref, key_ref, value_ref, bias_ref, log_ref, mixed_ref, grad_ref,
    query_grad_ref, key_grad_ref, value_grad_ref, key_acc, value_acc,
):
    mem_valid = lax.broadcasted_iota(jnp.int32, (MEM, 1), 0) < READ
    key_flip = flip(key_ref[...])
    overlap = (mixed_ref[...].astype(jnp.float32) * grad_ref[...].astype(jnp.float32)).T
    key_acc[...] = jnp.zeros_like(key_acc)
    value_acc[...] = jnp.zeros_like(value_acc)

    def block_back(keys, values, bias, valid, queries, grads, log, delta, flipped, rows):
        scores = times_back(keys, queries)
        if bias is not None:
            scores = scores + bias
        chances = jnp.exp(scores - log)
        if valid is not None:
            chances = jnp.where(valid, chances, 0.0)
        slopes = (chances * (times_back(values, grads) - delta)).astype(jnp.bfloat16)
        value_acc[rows] += product(chances.astype(jnp.bfloat16), grads)
        key_acc[rows] += product(slopes, queries)
        return product(flipped, slopes)

    results = []
    for head in range(2):
        mask = head_mask(head)
        queries = pick(mask, query_ref[...])
        grads = pick(mask, grad_ref[...])
        span = slice(head * HEAD, (head + 1) * HEAD)
        delta = jnp.sum(overlap[span], axis=0, keepdims=True)
        log = log_ref[head : head + 1]
        flipped = key_flip[span]
        main_rows = slice(0, 2 * HALF)
        mem_rows = slice(2 * HALF, CONT)
        pieces = []
        for half in range(2):
            part = slice(half * HALF, (half + 1) * HALF)
            piece = block_back(
                key_ref[main_rows], value_ref[main_rows], None, None,
                queries[part], grads[part], log[:, part], delta[:, part],
                flipped[:, main_rows], main_rows,
            )
            piece += block_back(
                key_ref[mem_rows], value_ref[mem_rows], None, mem_valid,
                queries[part], grads[part], log[:, part], delta[:, part],
                flipped[:, mem_rows], mem_rows,
            )
            pieces.append(piece)
        own_parts = []
        for cont in range(OWN // CLEN):
            rows = slice(CONT + cont * CLEN, CONT + (cont + 1) * CLEN)
            part = slice(HALF + cont * CLEN, HALF + (cont + 1) * CLEN)
            own_parts.append(
                block_back(
                    key_ref[rows], value_ref[rows], bias_ref[:, cont * CLEN : (cont + 1) * CLEN],
                    None, queries[part], grads[part], log[:, part], delta[:, part],
                    flipped[:, rows], rows,
                )
            )
        pieces[1] += jnp.concatenate(own_parts, axis=1)
        results.append(jnp.concatenate(pieces, axis=1))
    query_grad_ref[...] = (jnp.concatenate(results, axis=0).T * SCALE).astype(jnp.bfloat16)
    key_grad_ref[...] = key_acc[...].astype(jnp.bfloat16)
    value_grad_ref[...] = value_acc[...].astype(jnp.bfloat16)


def pair_spec(rows):
    return pl.BlockSpec((rows, 2 * HEAD), lambda pair: (0, pair))


def attend(queries, keys, values, bias):
    width = queries.shape[1]
    return pl.pallas_call(
        attend_kernel,
        grid=(PAIRS,),
        in_specs=[
            pair_spec(QROWS), pair_spec(KEYS), pair_spec(KEYS),
            pl.BlockSpec((CLEN, OWN), lambda pair: (0, 0)),
        ],
        out_specs=[pair_spec(QROWS), pl.BlockSpec((None, 2, QROWS), lambda pair: (pair, 0, 0))],
        out_shape=[
            jax.ShapeDtypeStruct((QROWS, width), jnp.bfloat16),
            jax.ShapeDtypeStruct((PAIRS, 2, QROWS), jnp.float32),
        ],
        cost_estimate=pl.CostEstimate(
            flops=16 * 10**9, bytes_accessed=10**7, transcendentals=14 * 10**6
        ),
        compiler_params=pltpu.CompilerParams(vmem_limit_bytes=48 << 20),
        name="attend",
    )(queries, keys, values, bias)


def attend_back(queries, keys, values, bias, log, mixed, grads):
    width = queries.shape[1]
    return pl.pallas_call(
        attend_back_kernel,
        grid=(PAIRS,),
        in_specs=[
            pair_spec(QROWS), pair_spec(KEYS), pair_spec(KEYS),
            pl.BlockSpec((CLEN, OWN), lambda pair: (0, 0)),
            pl.BlockSpec((None, 2, QROWS), lambda pair: (pair, 0, 0)),
            pair_spec(QROWS), pair_spec(QROWS),
        ],
        out_specs=[pair_spec(QROWS), pair_spec(KEYS), pair_spec(KEYS)],
        out_shape=[
            jax.ShapeDtypeStruct((QROWS, width), jnp.bfloat16),
            jax.ShapeDtypeStruct((KEYS, width), jnp.bfloat16),
            jax.ShapeDtypeStruct((KEYS, width), jnp.bfloat16),
        ],
        scratch_shapes=[pltpu.VMEM((KEYS, 2 * HEAD), jnp.float32)] * 2,
        cost_estimate=pl.CostEstimate(
            flops=40 * 10**9, bytes_accessed=2 * 10**7, transcendentals=14 * 10**6
        ),
        compiler_params=pltpu.CompilerParams(vmem_limit_bytes=48 << 20),
        name="attend_back",
    )(queries, keys, values, bias, log, mixed, grads)


def trade(values, flip_bit):
    return lax.ppermute(values, "shard", [(i, i ^ flip_bit) for i in range(4)])


def body_pairs(
    prompt_rows, follow_rows, memory_rows, follow_owner, follow_length,
    query_weight, key_weight, value_weight, out_weight, query_bias, value_bias, out_bias,
    first_gain, first_shift, up_weight, up_bias, down_weight, down_bias,
    second_gain, second_shift, prompt_cotan, follow_cotan,
):
    shard_index = lax.axis_index("shard")
    family = shard_index // 2
    width = prompt_rows.shape[2]
    conts = OWN // CLEN
    low = jnp.bfloat16
    wide = jnp.float32

    def gather(values):
        return lax.all_gather(values, NAMES, axis=0, tiled=True)

    qkv_mat = gather(jnp.concatenate([query_weight, key_weight, value_weight], axis=1))
    query_mat, key_mat, value_mat = (
        qkv_mat[:, :width], qkv_mat[:, width : 2 * width], qkv_mat[:, 2 * width :]
    )
    vectors = (
        query_bias, value_bias, out_bias, first_gain, first_shift,
        down_bias, second_gain, second_shift,
    )
    share = query_bias.shape[0]
    packed = gather(jnp.concatenate(vectors + (up_bias,))[None])
    (
        query_add, value_add, out_add, gain_one, shift_one, down_add, gain_two, shift_two,
    ) = (
        packed[:, i * share : (i + 1) * share].reshape(1, width).astype(wide) for i in range(8)
    )
    up_add = packed[:, 8 * share :].reshape(1, -1).astype(wide)
    out_mat = gather(out_weight)
    up_mat = gather(up_weight)
    down_mat = gather(down_weight)

    owner_row = follow_owner[0]
    length_row = follow_length[0]

    def ranks(shard, prompt_of):
        owned = (lax.dynamic_slice(owner_row, (shard * conts,), (conts,)) == prompt_of).astype(
            jnp.int32
        )
        before = jnp.cumsum(owned) - owned
        return jnp.where(owned == 1, before, 2 + jnp.arange(conts) - before)

    place = ranks(shard_index, family)
    across = shard_index ^ 2
    place_across = ranks(across, across // 2)
    order = jnp.argmax(place[None, :] == jnp.arange(conts)[:, None], axis=1)
    order_across = jnp.argmax(place_across[None, :] == jnp.arange(conts)[:, None], axis=1)
    lengths = jnp.concatenate(
        [
            length_row[shard_index * conts + order[:2]],
            length_row[across * conts + order_across[2:]],
        ]
    )
    positions = jnp.arange(CLEN)
    own_valid = (positions[:, None] < lengths[None, :]) | (positions[:, None] >= CLEN - WRITE)
    bias = jnp.repeat(jnp.where(own_valid, 0.0, NEGATIVE).astype(wide), CLEN, axis=1)

    def sort_conts(values):
        blocks = values.reshape(conts, CLEN, width)[order].reshape(OWN, width)
        return (blocks[: OWN // 2], blocks[OWN // 2 :])

    def unsort(values, returned):
        blocks = jnp.concatenate([values, returned], axis=0).reshape(conts, CLEN, width)
        return blocks[place].reshape(OWN, width)

    prompt = prompt_rows[0]
    partner = trade(prompt, 1)
    kept, sent = sort_conts(follow_rows[0])
    conts_rows = jnp.concatenate([kept, trade(sent, 2)], axis=0)
    kept_cotan, sent_cotan = sort_conts(follow_cotan[0])
    cotangent = jnp.concatenate([prompt_cotan[0], kept_cotan, trade(sent_cotan, 2)], axis=0)
    memory = lax.dynamic_index_in_dim(memory_rows[0], family, 0, keepdims=False)
    memory = jnp.pad(memory, ((0, MEM - READ), (0, 0)))
    rows = jnp.concatenate([prompt, conts_rows], axis=0)
    key_rows = jnp.concatenate([prompt, partner, memory, conts_rows], axis=0)
    query_low = ((product(rows, query_mat) + query_add).astype(low) * SCALE).astype(low)
    key_low = product(key_rows, key_mat).astype(low)
    value_low = (product(key_rows, value_mat) + value_add).astype(low)
    mixed, log = attend(query_low, key_low, value_low, bias)

    branch = product(mixed, out_mat) + out_add
    first, normed_one, inverse_one = layer_norm(rows.astype(wide) + branch, gain_one, shift_one)
    first_low = first.astype(low)
    inner = product(first_low, up_mat) + up_add
    activated = gelu_exact(inner).astype(low)
    second = product(activated, down_mat) + down_add
    output, normed_two, inverse_two = layer_norm(first + second, gain_two, shift_two)
    output = output.astype(low)
    returned_out = trade(output[HALF + OWN // 2 :], 2)

    cotangent = cotangent.astype(wide)
    grad_gain_two = jnp.sum(cotangent * normed_two, axis=0)
    grad_shift_two = jnp.sum(cotangent, axis=0)
    grad_mid = norm_back(cotangent * gain_two, normed_two, inverse_two)
    grad_down = grad_mid.astype(low)
    grad_down_mat = outer_sum(activated, grad_down)
    grad_down_add = column_sum(grad_down)
    grad_inner = (times_back(grad_down, down_mat) * gelu_slope(inner)).astype(low)
    grad_up_mat = outer_sum(first_low, grad_inner)
    grad_up_add = column_sum(grad_inner)
    grad_first = grad_mid + times_back(grad_inner, up_mat)
    grad_gain_one = jnp.sum(grad_first * normed_one, axis=0)
    grad_shift_one = jnp.sum(grad_first, axis=0)
    grad_hidden = norm_back(grad_first * gain_one, normed_one, inverse_one)
    grad_branch = grad_hidden.astype(low)
    grad_out_mat = outer_sum(mixed, grad_branch)
    grad_out_add = column_sum(grad_branch)
    grad_mixed = times_back(grad_branch, out_mat).astype(low)

    def reduce(values):
        piece = lax.psum_scatter(values.astype(low), "shard", scatter_dimension=0, tiled=True)
        return lax.psum(piece, "grp").astype(wide)

    down_sum = reduce(grad_down_mat)
    up_sum = reduce(grad_up_mat)
    out_sum = reduce(grad_out_mat)

    query_grad, key_grad, value_grad = attend_back(
        query_low, key_low, value_low, bias, log, mixed, grad_mixed
    )
    key_side = times_back(key_grad, key_mat) + times_back(value_grad, value_mat)
    given = trade(key_side[HALF : 2 * HALF].astype(low), 1)
    memory_part = key_side[2 * HALF : 2 * HALF + READ]
    memory_all = jnp.where(
        (jnp.arange(2) == family)[:, None, None], memory_part[None], 0.0
    ).astype(low)
    grad_memory = lax.psum(memory_all, "shard")[None]
    row_side = grad_hidden + times_back(query_grad, query_mat)
    grad_prompt = (row_side[:HALF] + key_side[:HALF] + given.astype(wide)).astype(low)
    grad_conts = (row_side[HALF:] + key_side[CONT:]).astype(low)
    returned_grad = trade(grad_conts[OWN // 2 :], 2)
    qkv_sum = reduce(
        jnp.concatenate(
            [
                outer_sum(rows, query_grad),
                outer_sum(key_rows, key_grad),
                outer_sum(key_rows, value_grad),
            ],
            axis=1,
        )
    )
    sums = jnp.concatenate(
        [
            column_sum(query_grad), column_sum(value_grad), grad_out_add, grad_gain_one,
            grad_shift_one, grad_down_add, grad_gain_two, grad_shift_two, grad_up_add,
        ]
    )
    sums = lax.psum(sums.reshape(-1, width), NAMES)
    mine = width // 4

    def part(index):
        return lax.dynamic_slice(sums[index], (shard_index * mine,), (mine,))

    up_part = lax.dynamic_slice(sums[8:].reshape(-1), (shard_index * width,), (width,))
    follow_out = unsort(output[HALF : HALF + OWN // 2], returned_out)
    follow_grad = unsort(grad_conts[: OWN // 2], returned_grad)
    return (
        output[:HALF][None],
        follow_out[None],
        grad_prompt[None],
        follow_grad[None],
        grad_memory,
        qkv_sum[:, :width],
        qkv_sum[:, width : 2 * width],
        qkv_sum[:, 2 * width :],
        out_sum,
        part(0),
        part(1),
        part(2),
        part(3),
        part(4),
        up_sum,
        up_part,
        down_sum,
        part(5),
        part(6),
        part(7),
    )


def solution(mesh):
    return jax.shard_map(
        body_pairs if pairs_fit(mesh) else body_any,
        mesh=mesh,
        in_specs=(
            P("grp", "shard", None),
            P("grp", "shard", None),
            P("grp", None, None, None),
            P("grp", None),
            P("grp", None),
            P(("grp", "shard"), None),
            P(("grp", "shard"), None),
            P(("grp", "shard"), None),
            P(("grp", "shard"), None),
            P(("grp", "shard")),
            P(("grp", "shard")),
            P(("grp", "shard")),
            P(("grp", "shard")),
            P(("grp", "shard")),
            P(("grp", "shard"), None),
            P(("grp", "shard")),
            P(("grp", "shard"), None),
            P(("grp", "shard")),
            P(("grp", "shard")),
            P(("grp", "shard")),
            P("grp", "shard", None),
            P("grp", "shard", None),
        ),
        out_specs=(
            P("grp", "shard", None),
            P("grp", "shard", None),
            P("grp", "shard", None),
            P("grp", "shard", None),
            P("grp", None, None, None),
            P("shard", None),
            P("shard", None),
            P("shard", None),
            P("shard", None),
            P("shard"),
            P("shard"),
            P("shard"),
            P("shard"),
            P("shard"),
            P("shard", None),
            P("shard"),
            P("shard", None),
            P("shard"),
            P("shard"),
            P("shard"),
        ),
        check_vma=False,
    )
```

```python
import jax
import jax.numpy as jnp
from jax import lax
from jax.experimental import pallas as pl
from jax.experimental.pallas import tpu as pltpu
from jax.sharding import PartitionSpec as P

HEADS = 12
HEAD = 64
READ = 10
WRITE = 10
PLEN = 1024
CLEN = 128
CONTS_PER = 8


EPSILON = 1e-12
SCALE = 0.125
NEGATIVE = -1e30
ROOT_HALF = 0.7071067811865476
ROOT_GAUSS = 0.3989422804014327


def product(left, right):
    return jnp.dot(left, right, preferred_element_type=jnp.float32)


def times_back(left, right):
    return lax.dot_general(
        left, right, (((1,), (1,)), ((), ())), preferred_element_type=jnp.float32
    )


def outer_sum(left, right):
    return lax.dot_general(
        left, right, (((0,), (0,)), ((), ())), preferred_element_type=jnp.float32
    )


def column_sum(values):
    return jnp.sum(values.astype(jnp.float32), axis=0)


def layer_norm(hidden, gain, shift):
    center = hidden - jnp.mean(hidden, axis=-1, keepdims=True)
    inverse = lax.rsqrt(jnp.mean(center * center, axis=-1, keepdims=True) + EPSILON)
    normed = center * inverse
    return (normed * gain.astype(jnp.float32) + shift.astype(jnp.float32), normed, inverse)


def norm_back(grad_normed, normed, inverse):
    centered = grad_normed - jnp.mean(grad_normed, axis=-1, keepdims=True)
    return inverse * (centered - normed * jnp.mean(grad_normed * normed, axis=-1, keepdims=True))


def gelu_exact(hidden):
    return 0.5 * hidden * (1.0 + lax.erf(hidden * ROOT_HALF))


def gelu_slope(hidden):
    return (
        0.5 * (1.0 + lax.erf(hidden * ROOT_HALF))
        + hidden * jnp.exp(-0.5 * hidden * hidden) * ROOT_GAUSS
    )


def split_heads(values):
    return values.reshape(values.shape[0], values.shape[1], HEADS, HEAD)


def block_scores(queries, keys, valid):
    scores = (
        jnp.einsum(
            "nqhd,nkhd->nhqk",
            split_heads(queries),
            split_heads(keys),
            preferred_element_type=jnp.float32,
        )
        * SCALE
    )
    return jnp.where(valid[:, None, None, :], scores, NEGATIVE)


def attend_forward(queries, keys, values, valid):
    scores = block_scores(queries, keys, valid)
    maximum = jnp.max(scores, axis=-1, keepdims=True)
    powers = jnp.exp(scores - maximum)
    totals = jnp.sum(powers, axis=-1, keepdims=True)
    chances = (powers / totals).astype(jnp.bfloat16)
    result = jnp.einsum(
        "nhqk,nkhd->nqhd", chances, split_heads(values), preferred_element_type=jnp.float32
    )
    return (result.reshape(-1, queries.shape[2]), maximum + jnp.log(totals))


def attend_backward(queries, keys, values, valid, logsum, grad_out):
    width = queries.shape[2]
    scores = block_scores(queries, keys, valid)
    chances = jnp.exp(scores - logsum)
    grad_heads = split_heads(grad_out)
    grad_chance = jnp.einsum(
        "nqhd,nkhd->nhqk", grad_heads, split_heads(values), preferred_element_type=jnp.float32
    )
    inner = jnp.sum(chances * grad_chance, axis=-1, keepdims=True)
    grad_score = (chances * (grad_chance - inner)).astype(jnp.bfloat16)
    grad_query = (
        jnp.einsum(
            "nhqk,nkhd->nqhd", grad_score, split_heads(keys), preferred_element_type=jnp.float32
        )
        * SCALE
    )
    grad_key = (
        jnp.einsum(
            "nhqk,nqhd->nkhd", grad_score, split_heads(queries), preferred_element_type=jnp.float32
        )
        * SCALE
    )
    grad_value = jnp.einsum(
        "nhqk,nqhd->nkhd",
        chances.astype(jnp.bfloat16),
        grad_heads,
        preferred_element_type=jnp.float32,
    )
    span = keys.shape[1]
    return (
        grad_query.reshape(-1, width),
        grad_key.reshape(keys.shape[0], span, width),
        grad_value.reshape(keys.shape[0], span, width),
    )


def body_any(
    prompt_rows,
    follow_rows,
    memory_rows,
    follow_owner,
    follow_length,
    query_weight,
    key_weight,
    value_weight,
    out_weight,
    query_bias,
    value_bias,
    out_bias,
    first_gain,
    first_shift,
    up_weight,
    up_bias,
    down_weight,
    down_bias,
    second_gain,
    second_shift,
    prompt_cotan,
    follow_cotan,
):
    (
        query_mat,
        key_mat,
        value_mat,
        out_mat,
        query_add,
        value_add,
        out_add,
        gain_one,
        shift_one,
        up_mat,
        up_add,
        down_mat,
        down_add,
        gain_two,
        shift_two,
    ) = (
        lax.all_gather(query_weight, ("grp", "shard"), axis=0, tiled=True),
        lax.all_gather(key_weight, ("grp", "shard"), axis=0, tiled=True),
        lax.all_gather(value_weight, ("grp", "shard"), axis=0, tiled=True),
        lax.all_gather(out_weight, ("grp", "shard"), axis=0, tiled=True),
        lax.all_gather(query_bias, ("grp", "shard"), axis=0, tiled=True),
        lax.all_gather(value_bias, ("grp", "shard"), axis=0, tiled=True),
        lax.all_gather(out_bias, ("grp", "shard"), axis=0, tiled=True),
        lax.all_gather(first_gain, ("grp", "shard"), axis=0, tiled=True),
        lax.all_gather(first_shift, ("grp", "shard"), axis=0, tiled=True),
        lax.all_gather(up_weight, ("grp", "shard"), axis=0, tiled=True),
        lax.all_gather(up_bias, ("grp", "shard"), axis=0, tiled=True),
        lax.all_gather(down_weight, ("grp", "shard"), axis=0, tiled=True),
        lax.all_gather(down_bias, ("grp", "shard"), axis=0, tiled=True),
        lax.all_gather(second_gain, ("grp", "shard"), axis=0, tiled=True),
        lax.all_gather(second_shift, ("grp", "shard"), axis=0, tiled=True),
    )
    shard_index = lax.axis_index("shard")
    prompt = prompt_rows[0]
    follow = follow_rows[0]
    p_count = prompt.shape[0]
    f_count = follow.shape[0]
    width = prompt.shape[1]
    families = memory_rows.shape[1]
    all_rows = jnp.concatenate([prompt, follow], axis=0)
    memory_flat = memory_rows[0].reshape(families * READ, width)
    query_low = (product(all_rows, query_mat) + query_add.astype(jnp.float32)).astype(jnp.bfloat16)
    key_low = product(all_rows, key_mat).astype(jnp.bfloat16)
    value_low = (product(all_rows, value_mat) + value_add.astype(jnp.float32)).astype(jnp.bfloat16)
    mem_key = product(memory_flat, key_mat).astype(jnp.bfloat16).reshape(families, READ, width)
    mem_value = (
        (product(memory_flat, value_mat) + value_add.astype(jnp.float32))
        .astype(jnp.bfloat16)
        .reshape(families, READ, width)
    )
    half_prompt = PLEN // 2
    per_block = CONTS_PER // 2
    prompt_blocks = p_count // half_prompt
    conts_here = f_count // CLEN
    positions = jnp.arange(CLEN)
    open_span = jnp.ones((per_block, READ + PLEN), dtype=bool)
    owner_row = follow_owner[0]
    length_row = follow_length[0]
    prompt_keys, prompt_values = (
        lax.all_gather(key_low[:p_count], "shard", axis=0, tiled=True),
        lax.all_gather(value_low[:p_count], "shard", axis=0, tiled=True),
    )
    key_table = prompt_keys.reshape(families, PLEN, width)
    value_table = prompt_values.reshape(families, PLEN, width)

    def prompt_inputs(block):
        start = block * half_prompt
        family = (shard_index * p_count + start) // PLEN
        keys = jnp.concatenate([mem_key[family], key_table[family]], axis=0)[None]
        values = jnp.concatenate([mem_value[family], value_table[family]], axis=0)[None]
        valid = jnp.ones((1, READ + PLEN), dtype=bool)
        return (query_low[start : start + half_prompt][None], keys, values, valid, family)

    def follow_inputs(block):
        first_row = p_count + block * per_block * CLEN
        chosen = shard_index * conts_here + block * per_block + jnp.arange(per_block)
        owners = owner_row[chosen]
        lengths = length_row[chosen]
        own_keys = key_low[first_row : first_row + per_block * CLEN].reshape(per_block, CLEN, width)
        own_values = value_low[first_row : first_row + per_block * CLEN].reshape(
            per_block, CLEN, width
        )
        keys = jnp.concatenate([mem_key[owners], key_table[owners], own_keys], axis=1)
        values = jnp.concatenate([mem_value[owners], value_table[owners], own_values], axis=1)
        own_valid = (positions[None, :] < lengths[:, None]) | (positions[None, :] >= CLEN - WRITE)
        valid = jnp.concatenate([open_span, own_valid], axis=1)
        queries = query_low[first_row : first_row + per_block * CLEN].reshape(
            per_block, CLEN, width
        )
        return (queries, keys, values, valid, owners)

    attended = []
    saved = []
    block = 0
    queries, keys, values, valid, family = prompt_inputs(block)
    result, logsum = attend_forward(queries, keys, values, valid)
    attended.append(result)
    saved.append(logsum)
    block = 0
    queries, keys, values, valid, owners = follow_inputs(block)
    result, logsum = attend_forward(queries, keys, values, valid)
    attended.append(result)
    saved.append(logsum)
    mixed = jnp.concatenate(attended, axis=0).astype(jnp.bfloat16)
    branch = product(mixed, out_mat) + out_add.astype(jnp.float32)
    first, normed_one, inverse_one = layer_norm(
        all_rows.astype(jnp.float32) + branch, gain_one, shift_one
    )
    first_low = first.astype(jnp.bfloat16)
    inner = product(first_low, up_mat) + up_add.astype(jnp.float32)
    activated = gelu_exact(inner).astype(jnp.bfloat16)
    second = product(activated, down_mat) + down_add.astype(jnp.float32)
    output, normed_two, inverse_two = layer_norm(first + second, gain_two, shift_two)
    output = output.astype(jnp.bfloat16)
    (
        query_mat,
        key_mat,
        value_mat,
        out_mat,
        query_add,
        value_add,
        out_add,
        gain_one,
        shift_one,
        up_mat,
        up_add,
        down_mat,
        down_add,
        gain_two,
        shift_two,
    ) = (
        lax.all_gather(query_weight, ("grp", "shard"), axis=0, tiled=True),
        lax.all_gather(key_weight, ("grp", "shard"), axis=0, tiled=True),
        lax.all_gather(value_weight, ("grp", "shard"), axis=0, tiled=True),
        lax.all_gather(out_weight, ("grp", "shard"), axis=0, tiled=True),
        lax.all_gather(query_bias, ("grp", "shard"), axis=0, tiled=True),
        lax.all_gather(value_bias, ("grp", "shard"), axis=0, tiled=True),
        lax.all_gather(out_bias, ("grp", "shard"), axis=0, tiled=True),
        lax.all_gather(first_gain, ("grp", "shard"), axis=0, tiled=True),
        lax.all_gather(first_shift, ("grp", "shard"), axis=0, tiled=True),
        lax.all_gather(up_weight, ("grp", "shard"), axis=0, tiled=True),
        lax.all_gather(up_bias, ("grp", "shard"), axis=0, tiled=True),
        lax.all_gather(down_weight, ("grp", "shard"), axis=0, tiled=True),
        lax.all_gather(down_bias, ("grp", "shard"), axis=0, tiled=True),
        lax.all_gather(second_gain, ("grp", "shard"), axis=0, tiled=True),
        lax.all_gather(second_shift, ("grp", "shard"), axis=0, tiled=True),
    )
    cotangent = jnp.concatenate([prompt_cotan[0], follow_cotan[0]], axis=0).astype(jnp.float32)
    grad_gain_two = jnp.sum(cotangent * normed_two, axis=0)
    grad_shift_two = jnp.sum(cotangent, axis=0)
    grad_mid = norm_back(cotangent * gain_two.astype(jnp.float32), normed_two, inverse_two)
    grad_down = grad_mid.astype(jnp.bfloat16)
    grad_down_mat = outer_sum(activated, grad_down)
    grad_down_add = column_sum(grad_down)
    grad_inner = (times_back(grad_down, down_mat) * gelu_slope(inner)).astype(jnp.bfloat16)
    grad_up_mat = outer_sum(first_low, grad_inner)
    grad_up_add = column_sum(grad_inner)
    grad_first = grad_mid + times_back(grad_inner, up_mat)
    grad_gain_one = jnp.sum(grad_first * normed_one, axis=0)
    grad_shift_one = jnp.sum(grad_first, axis=0)
    grad_hidden = norm_back(grad_first * gain_one.astype(jnp.float32), normed_one, inverse_one)
    grad_branch = grad_hidden.astype(jnp.bfloat16)
    grad_out_mat = outer_sum(mixed, grad_branch)
    grad_out_add = column_sum(grad_branch)
    grad_mixed = times_back(grad_branch, out_mat).astype(jnp.bfloat16)
    mem_key_acc = jnp.zeros((families, READ, width), jnp.float32)
    mem_value_acc = jnp.zeros((families, READ, width), jnp.float32)
    prompt_key_acc = jnp.zeros((families, PLEN, width), jnp.float32)
    prompt_value_acc = jnp.zeros((families, PLEN, width), jnp.float32)
    block = 0
    queries, keys, values, valid, family = prompt_inputs(block)
    start = block * half_prompt
    grad_query, grad_key, grad_value = attend_backward(
        queries, keys, values, valid, saved[block], grad_mixed[start : start + half_prompt][None]
    )
    query_parts = grad_query
    mem_key_acc = mem_key_acc.at[family].add(grad_key[0, :READ])
    mem_value_acc = mem_value_acc.at[family].add(grad_value[0, :READ])
    prompt_key_acc = prompt_key_acc.at[family].add(grad_key[0, READ:])
    prompt_value_acc = prompt_value_acc.at[family].add(grad_value[0, READ:])
    prompt_query_low = query_parts.astype(jnp.bfloat16)
    block = 0
    queries, keys, values, valid, owners = follow_inputs(block)
    first_row = p_count + block * per_block * CLEN
    grad_slice = grad_mixed[first_row : first_row + per_block * CLEN].reshape(
        per_block, CLEN, width
    )
    grad_query, grad_key, grad_value = attend_backward(
        queries, keys, values, valid, saved[prompt_blocks + block], grad_slice
    )
    mem_key_acc = mem_key_acc.at[owners].add(grad_key[:, :READ])
    mem_value_acc = mem_value_acc.at[owners].add(grad_value[:, :READ])
    prompt_key_acc = prompt_key_acc.at[owners].add(grad_key[:, READ : READ + PLEN])
    prompt_value_acc = prompt_value_acc.at[owners].add(grad_value[:, READ : READ + PLEN])
    own_key_parts = grad_key[:, READ + PLEN :].reshape(-1, width)
    own_value_parts = grad_value[:, READ + PLEN :].reshape(-1, width)
    prompt_key_grad, prompt_value_grad = (
        lax.psum_scatter(
            prompt_key_acc.reshape(families * PLEN, width).astype(jnp.bfloat16),
            "shard",
            scatter_dimension=0,
            tiled=True,
        ).astype(jnp.float32),
        lax.psum_scatter(
            prompt_value_acc.reshape(families * PLEN, width).astype(jnp.bfloat16),
            "shard",
            scatter_dimension=0,
            tiled=True,
        ).astype(jnp.float32),
    )
    follow_query_low = grad_query.astype(jnp.bfloat16)
    follow_key_low = own_key_parts.astype(jnp.bfloat16)
    follow_value_low = own_value_parts.astype(jnp.bfloat16)
    mem_key_sum, mem_value_sum = (
        lax.psum(mem_key_acc.astype(jnp.bfloat16), "shard").astype(jnp.float32),
        lax.psum(mem_value_acc.astype(jnp.bfloat16), "shard").astype(jnp.float32),
    )
    grad_query_low = jnp.concatenate([prompt_query_low, follow_query_low], axis=0)
    grad_key_low = jnp.concatenate([prompt_key_grad.astype(jnp.bfloat16), follow_key_low], axis=0)
    grad_value_low = jnp.concatenate(
        [prompt_value_grad.astype(jnp.bfloat16), follow_value_low], axis=0
    )
    mem_key_low = mem_key_sum.astype(jnp.bfloat16).reshape(families * READ, width)
    mem_value_low = mem_value_sum.astype(jnp.bfloat16).reshape(families * READ, width)
    grad_rows_all = (
        grad_hidden
        + times_back(grad_query_low, query_mat)
        + times_back(grad_key_low, key_mat)
        + times_back(grad_value_low, value_mat)
    ).astype(jnp.bfloat16)
    grad_memory = (
        (times_back(mem_key_low, key_mat) + times_back(mem_value_low, value_mat))
        .astype(jnp.bfloat16)
        .reshape(1, families, READ, width)
    )
    leader = (shard_index == 0).astype(jnp.float32)
    grad_query_mat = outer_sum(all_rows, grad_query_low)
    grad_query_add = column_sum(grad_query_low)
    grad_key_mat = outer_sum(all_rows, grad_key_low) + leader * outer_sum(memory_flat, mem_key_low)
    grad_value_mat = outer_sum(all_rows, grad_value_low) + leader * outer_sum(
        memory_flat, mem_value_low
    )
    grad_value_add = column_sum(grad_value_low) + leader * column_sum(mem_value_low)
    pieces = (
        lax.psum_scatter(
            grad_query_mat.astype(jnp.bfloat16), "shard", scatter_dimension=0, tiled=True
        ).astype(jnp.float32),
        lax.psum_scatter(
            grad_key_mat.astype(jnp.bfloat16), "shard", scatter_dimension=0, tiled=True
        ).astype(jnp.float32),
        lax.psum_scatter(
            grad_value_mat.astype(jnp.bfloat16), "shard", scatter_dimension=0, tiled=True
        ).astype(jnp.float32),
        lax.psum_scatter(
            grad_out_mat.astype(jnp.bfloat16), "shard", scatter_dimension=0, tiled=True
        ).astype(jnp.float32),
        lax.psum_scatter(
            grad_query_add.astype(jnp.bfloat16), "shard", scatter_dimension=0, tiled=True
        ).astype(jnp.float32),
        lax.psum_scatter(
            grad_value_add.astype(jnp.bfloat16), "shard", scatter_dimension=0, tiled=True
        ).astype(jnp.float32),
        lax.psum_scatter(
            grad_out_add.astype(jnp.bfloat16), "shard", scatter_dimension=0, tiled=True
        ).astype(jnp.float32),
        lax.psum_scatter(
            grad_gain_one.astype(jnp.bfloat16), "shard", scatter_dimension=0, tiled=True
        ).astype(jnp.float32),
        lax.psum_scatter(
            grad_shift_one.astype(jnp.bfloat16), "shard", scatter_dimension=0, tiled=True
        ).astype(jnp.float32),
        lax.psum_scatter(
            grad_up_mat.astype(jnp.bfloat16), "shard", scatter_dimension=0, tiled=True
        ).astype(jnp.float32),
        lax.psum_scatter(
            grad_up_add.astype(jnp.bfloat16), "shard", scatter_dimension=0, tiled=True
        ).astype(jnp.float32),
        lax.psum_scatter(
            grad_down_mat.astype(jnp.bfloat16), "shard", scatter_dimension=0, tiled=True
        ).astype(jnp.float32),
        lax.psum_scatter(
            grad_down_add.astype(jnp.bfloat16), "shard", scatter_dimension=0, tiled=True
        ).astype(jnp.float32),
        lax.psum_scatter(
            grad_gain_two.astype(jnp.bfloat16), "shard", scatter_dimension=0, tiled=True
        ).astype(jnp.float32),
        lax.psum_scatter(
            grad_shift_two.astype(jnp.bfloat16), "shard", scatter_dimension=0, tiled=True
        ).astype(jnp.float32),
    )
    summed = (
        lax.psum(pieces[0].astype(jnp.bfloat16), "grp").astype(jnp.float32),
        lax.psum(pieces[1].astype(jnp.bfloat16), "grp").astype(jnp.float32),
        lax.psum(pieces[2].astype(jnp.bfloat16), "grp").astype(jnp.float32),
        lax.psum(pieces[3].astype(jnp.bfloat16), "grp").astype(jnp.float32),
        lax.psum(pieces[4].astype(jnp.bfloat16), "grp").astype(jnp.float32),
        lax.psum(pieces[5].astype(jnp.bfloat16), "grp").astype(jnp.float32),
        lax.psum(pieces[6].astype(jnp.bfloat16), "grp").astype(jnp.float32),
        lax.psum(pieces[7].astype(jnp.bfloat16), "grp").astype(jnp.float32),
        lax.psum(pieces[8].astype(jnp.bfloat16), "grp").astype(jnp.float32),
        lax.psum(pieces[9].astype(jnp.bfloat16), "grp").astype(jnp.float32),
        lax.psum(pieces[10].astype(jnp.bfloat16), "grp").astype(jnp.float32),
        lax.psum(pieces[11].astype(jnp.bfloat16), "grp").astype(jnp.float32),
        lax.psum(pieces[12].astype(jnp.bfloat16), "grp").astype(jnp.float32),
        lax.psum(pieces[13].astype(jnp.bfloat16), "grp").astype(jnp.float32),
        lax.psum(pieces[14].astype(jnp.bfloat16), "grp").astype(jnp.float32),
    )
    return (
        output[:p_count][None],
        output[p_count:][None],
        grad_rows_all[:p_count][None],
        grad_rows_all[p_count:][None],
        grad_memory,
        summed[0],
        summed[1],
        summed[2],
        summed[3],
        summed[4],
        summed[5],
        summed[6],
        summed[7],
        summed[8],
        summed[9],
        summed[10],
        summed[11],
        summed[12],
        summed[13],
        summed[14],
    )


MEM = 16
HALF = PLEN // 2
OWN = 512
CONT = HALF + HALF + MEM
KEYS = CONT + OWN
QROWS = HALF + OWN
PAIRS = HEADS // 2
NAMES = ("grp", "shard")


def pairs_fit(mesh):
    return mesh.shape["shard"] == 4 and mesh.shape["grp"] == 8


def head_mask(head):
    lane = lax.broadcasted_iota(jnp.int32, (1, 2 * HEAD), 1)
    return lane // HEAD == head


def pick(mask, values):
    return jnp.where(mask, values.astype(jnp.float32), 0.0).astype(jnp.bfloat16)


def flip(values):
    return values.astype(jnp.float32).T.astype(jnp.bfloat16)


def own_scores(keys, queries):
    parts = []
    for cont in range(OWN // CLEN):
        part = slice(cont * CLEN, (cont + 1) * CLEN)
        parts.append(times_back(keys[part], queries[part]))
    return jnp.concatenate(parts, axis=1)


def attend_pair(query_ref, key_ref, value_ref, bias_ref, out_ref, log_ref):
    mem_valid = lax.broadcasted_iota(jnp.int32, (MEM, 1), 0) < READ
    value_flip = flip(value_ref[...])
    results = []
    for head in range(2):
        mask = head_mask(head)
        queries = pick(mask, query_ref[...])
        main = times_back(key_ref[: 2 * HALF], queries)
        memory = jnp.where(mem_valid, times_back(key_ref[2 * HALF : CONT], queries), NEGATIVE)
        own = own_scores(key_ref[CONT:], queries[HALF:]) + bias_ref[...]
        top = jnp.maximum(
            jnp.max(main, axis=0, keepdims=True), jnp.max(memory, axis=0, keepdims=True)
        )
        top_own = jnp.maximum(top[:, HALF:], jnp.max(own, axis=0, keepdims=True))
        top = jnp.concatenate([top[:, :HALF], top_own], axis=1)
        main = jnp.exp(main - top)
        memory = jnp.exp(memory - top)
        own = jnp.exp(own - top_own)
        total = jnp.sum(main, axis=0, keepdims=True) + jnp.sum(memory, axis=0, keepdims=True)
        total = jnp.concatenate(
            [total[:, :HALF], total[:, HALF:] + jnp.sum(own, axis=0, keepdims=True)], axis=1
        )
        flipped = value_flip[head * HEAD : (head + 1) * HEAD]
        result = product(flipped[:, : 2 * HALF], main.astype(jnp.bfloat16))
        result += product(flipped[:, 2 * HALF : CONT], memory.astype(jnp.bfloat16))
        own = own.astype(jnp.bfloat16)
        own_parts = []
        for cont in range(OWN // CLEN):
            own_parts.append(
                product(
                    flipped[:, CONT + cont * CLEN : CONT + (cont + 1) * CLEN],
                    own[:, cont * CLEN : (cont + 1) * CLEN],
                )
            )
        result = jnp.concatenate(
            [result[:, :HALF], result[:, HALF:] + jnp.concatenate(own_parts, axis=1)], axis=1
        )
        results.append(result / total)
        log_ref[head : head + 1] = top + jnp.log(total)
    out_ref[...] = jnp.concatenate(results, axis=0).T.astype(jnp.bfloat16)


MESH = pl.DeviceIdType.MESH
WHERE = pl.BlockSpec(memory_space=pl.ANY)
INSIDE = pl.BlockSpec(memory_space=pltpu.VMEM)
VECTORS = 16


def seat():
    grp = lax.axis_index("grp")
    return (grp // 2, grp % 2, lax.axis_index("shard"))


def unit_of(z, core, shard):
    return (z * 2 + core) * 4 + shard


def device_of(z, core, shard):
    return (z * 2 + core, shard)


def greet():
    z, core, shard = seat()
    barrier = pltpu.get_barrier_semaphore()
    others = [device_of((z + step) % 4, core, shard) for step in (1, 2, 3)]
    others += [
        device_of(z, core, shard ^ 1),
        device_of(z, core, shard ^ 2),
        device_of(z, 1 - core, shard),
    ]
    for other in others:
        pl.semaphore_signal(barrier, inc=1, device_id=other, device_id_type=MESH)
    pl.semaphore_wait(barrier, len(others))


class Gather:
    def __init__(self, mine, full, send, recv, by_y=(0, 2)):
        self.mine, self.full, self.send, self.recv = mine, full, send, recv
        self.share = mine.shape[0]
        self.by_y = by_y
        self.z, self.core, self.shard = seat()
        self.sent = 0

    def rows(self, unit):
        return self.full.at[pl.ds(pl.multiple_of(unit * self.share, 8), self.share)]

    def link(self, index, unit, z, core, shard, source=None):
        return pltpu.make_async_remote_copy(
            src_ref=self.rows(unit) if source is None else source,
            dst_ref=self.rows(unit),
            send_sem=self.send.at[index],
            recv_sem=self.recv.at[unit],
            device_id=device_of(z, core, shard),
            device_id_type=MESH,
        )

    def push(self, unit, z, core, shard, source=None):
        self.link(self.sent, unit, z, core, shard, source).start()
        self.sent += 1

    def arrive(self, unit):
        self.link(0, unit, self.z, 1 - self.core, self.shard).wait_recv()

    def start_line(self):
        me = unit_of(self.z, self.core, self.shard)
        for step in (1, 2, 3):
            self.push(me, (self.z + step) % 4, self.core, self.shard, self.mine)

    def start_plane(self):
        z, core, shard = self.z, self.core, self.shard
        me = unit_of(z, core, shard)
        self.push(me, z, core, shard ^ 1, self.mine)
        self.push(me, z, core, shard ^ 2, self.mine)
        self.push(me, z, 1 - core, shard, self.mine)

    def own(self, semaphore):
        return pltpu.make_async_copy(
            self.mine, self.rows(unit_of(self.z, self.core, self.shard)), semaphore
        )

    def column(self, step):
        z, core, shard = self.z, self.core, self.shard
        unit = unit_of((z + step) % 4, core, shard)
        self.arrive(unit)
        self.push(unit, z, core, shard ^ 1)
        self.push(unit, z, core, shard ^ 2)
        self.push(unit, z, 1 - core, shard)

    def side(self, step):
        z, core, shard = self.z, self.core, self.shard
        for hop in (1, 2):
            unit = unit_of((z + step) % 4, core, shard ^ hop)
            self.arrive(unit)
            if (step in self.by_y) == (hop == 1):
                self.push(unit, z, core, shard ^ (3 - hop))
            self.push(unit, z, 1 - core, shard)

    def corner(self, step):
        z, core, shard = self.z, self.core, self.shard
        unit = unit_of((z + step) % 4, core, shard ^ 3)
        self.arrive(unit)
        self.push(unit, z, 1 - core, shard)

    def sibling(self):
        def wait(index, carry):
            unit = (index // 4) * 8 + (1 - self.core) * 4 + index % 4
            self.arrive(unit)
            return carry

        lax.fori_loop(0, 16, wait, 0)

    def finish(self):
        def wait(index, carry):
            pltpu.make_async_remote_copy(
                src_ref=self.mine,
                dst_ref=self.mine,
                send_sem=self.send.at[index],
                recv_sem=self.recv.at[0],
                device_id=device_of(self.z, 1 - self.core, self.shard),
                device_id_type=MESH,
            ).wait_send()
            return carry

        lax.fori_loop(0, self.sent, wait, 0)


class PlaneGather(Gather):
    def start_plane(self):
        z, core, shard = self.z, self.core, self.shard
        me = unit_of(z, core, shard)
        self.link(96, me, z, core, shard ^ 1, self.mine).start()
        self.link(97, me, z, core, shard ^ 2, self.mine).start()
        self.link(me, me, z, 1 - core, shard, self.mine).start()

    def along(self, unit, z_of, source=None):
        z, core, shard = self.z, self.core, self.shard

        @pl.when((z_of <= z) & (z < 3))
        def _():
            self.link(32 + unit, unit, z + 1, core, shard, source).start()

        @pl.when((z_of >= z) & (z > 0))
        def _():
            self.link(64 + unit, unit, z - 1, core, shard, source).start()

    def start_line(self):
        me = unit_of(self.z, self.core, self.shard)
        self.along(me, self.z, self.mine)

    def plane(self):
        z, core, shard = self.z, self.core, self.shard
        over_x = unit_of(z, core, shard ^ 1)
        over_y = unit_of(z, core, shard ^ 2)
        self.arrive(over_x)

        @pl.when(core == 0)
        def _():
            self.link(98, over_x, z, core, shard ^ 2).start()

        self.link(over_x, over_x, z, 1 - core, shard).start()
        self.along(over_x, z)
        self.arrive(over_y)

        @pl.when(core == 1)
        def _():
            self.link(98, over_y, z, core, shard ^ 1).start()

        self.link(over_y, over_y, z, 1 - core, shard).start()
        self.along(over_y, z)

    def corners(self):
        z, core, shard = self.z, self.core, self.shard
        unit = unit_of(z, core, shard ^ 3)
        self.arrive(unit)
        self.link(unit, unit, z, 1 - core, shard).start()
        self.along(unit, z)

    def far(self, distance, other):
        z, core, shard = self.z, self.core, self.shard
        for sign in (-1, 1):
            plane = z + sign * distance

            @pl.when((plane >= 0) & (plane < 4))
            def _():
                unit = unit_of(plane, core, shard ^ other)
                self.arrive(unit)
                self.link(unit, unit, z, 1 - core, shard).start()
                self.along(unit, plane)

    def finish(self):
        z, core, shard = self.z, self.core, self.shard

        def done(index, unit):
            self.link(index, unit, z, 1 - core, shard, self.mine).wait_send()

        for index in (96, 97, 98):
            done(index, 0)

        def wait(index, carry):
            plane = index // 4
            unit = plane * 8 + core * 4 + index % 4
            done(unit, unit)

            @pl.when((plane <= z) & (z < 3))
            def _():
                done(32 + unit, unit)

            @pl.when((plane >= z) & (z > 0))
            def _():
                done(64 + unit, unit)

            return carry

        lax.fori_loop(0, 16, wait, 0)


class Swap:
    def __init__(self, source, target, send, recv, z, core, shard):
        self.copy = pltpu.make_async_remote_copy(
            src_ref=source, dst_ref=target, send_sem=send, recv_sem=recv,
            device_id=device_of(z, core, shard), device_id_type=MESH,
        )

    def start(self):
        self.copy.start()

    def arrive(self):
        self.copy.wait_recv()

    def finish(self):
        self.copy.wait_send()


def spread_vector(vectors, index, width):
    narrow, broad = width // 32, 4 * width // 32
    row = lax.broadcasted_iota(jnp.int32, (32 * VECTORS, width), 0)
    lane = lax.broadcasted_iota(jnp.int32, (32 * VECTORS, width), 1)
    small = index < 8
    start = jnp.where(small, index, 8 + VECTORS * 8 * (index - 8))
    block = jnp.where(small, lane // narrow, lane // broad)
    select = jnp.where(row == VECTORS * block + start, 1.0, 0.0).astype(jnp.bfloat16)
    table = outer_sum(vectors, select)
    piece = lax.broadcasted_iota(jnp.int32, table.shape, 0)
    lane = lax.broadcasted_iota(jnp.int32, table.shape, 1)
    offset = jnp.where(small, lane % narrow, lane % broad)
    return jnp.sum(jnp.where(piece == offset, table, 0.0), axis=0, keepdims=True)


TILE = 512
PARTNERS = 4


def front_kernel(
    qkv_ref, wide_ref, down_ref, vec_ref, prompt_ref, kept_ref, sent_ref, mem_ref,
    prompt_cot, kept_cot, sent_cot, bias_ref,
    qkv_full, wide_full, down_full, vec_full, rows_out,
    out_ref, act_ref, first_ref, gdown_ref, ginner_ref, gbranch_ref, gmixed_ref, ghidden_ref,
    mixed_ref, log_ref, query_out, key_out, value_out, sums_ref,
    rows, weights, vectors, table, query, key, value, mixed, cotan, wide, down,
    act, slope, normed, first, total, hidden, small_low,
    send_a, recv_a, send_b, recv_b, send_c, recv_c, send_d, recv_d, swap_send, swap_recv, local,
    store,
):
    pair = pl.program_id(0)
    width = prompt_ref.shape[1]
    low = jnp.bfloat16
    one = Gather(qkv_ref, qkv_full, send_a, recv_a, (0, 1, 2))
    small = Gather(vec_ref, vec_full, send_d, recv_d)
    two = Gather(wide_ref, wide_full, send_b, recv_b)
    three = PlaneGather(down_ref, down_full, send_c, recv_c)
    z, core, shard = seat()
    step_rows = HALF // PARTNERS
    partner = [
        Swap(
            prompt_ref.at[pl.ds(index * step_rows, step_rows)],
            rows.at[pl.ds(HALF + index * step_rows, step_rows)],
            swap_send.at[index], swap_recv.at[index], z, core, shard ^ 1,
        )
        for index in range(PARTNERS)
    ]
    taken = Swap(
        sent_ref, rows.at[pl.ds(CONT + OWN // 2, OWN // 2)],
        swap_send.at[PARTNERS], swap_recv.at[PARTNERS], z, core, shard ^ 2,
    )
    taken_cot = Swap(
        sent_cot, cotan.at[pl.ds(HALF + OWN // 2, OWN // 2)],
        swap_send.at[PARTNERS + 1], swap_recv.at[PARTNERS + 1], z, core, shard ^ 2,
    )
    swaps = partner + [taken, taken_cot]
    own = [gather.own(local.at[index]) for index, gather in enumerate((one, small, two, three))]
    own += [
        pltpu.make_async_copy(prompt_ref, rows.at[pl.ds(0, HALF)], local.at[4]),
        pltpu.make_async_copy(mem_ref, rows.at[pl.ds(2 * HALF, MEM)], local.at[5]),
        pltpu.make_async_copy(kept_ref, rows.at[pl.ds(CONT, OWN // 2)], local.at[6]),
        pltpu.make_async_copy(prompt_cot, cotan.at[pl.ds(0, HALF)], local.at[7]),
        pltpu.make_async_copy(kept_cot, cotan.at[pl.ds(HALF, OWN // 2)], local.at[8]),
    ]
    load_weights = pltpu.make_async_copy(qkv_full, weights, local.at[9])
    load_vectors = pltpu.make_async_copy(vec_full, vectors, local.at[10])
    store_rows = pltpu.make_async_copy(rows, rows_out, local.at[11])
    load_wide = pltpu.make_async_copy(wide_full, wide, local.at[12])
    load_down = pltpu.make_async_copy(down_full, down, local.at[13])

    def project(start, query_start, count, queries):
        span = pl.ds(start, count)
        block = rows[span]
        if queries:
            result = (product(block, weights[:, :width]) + table[0:1]).astype(low)
            result = (result.astype(jnp.float32) * SCALE).astype(low)
            query[pl.ds(query_start, count)] = result
        key[span] = product(block, weights[:, width : 2 * width]).astype(low)
        value[span] = (product(block, weights[:, 2 * width :]) + table[1:2]).astype(low)

    @pl.when(pair == 0)
    def _():
        for copy in own[4:]:
            copy.start()
        greet()
        one.start_line()
        small.start_line()
        one.start_plane()
        small.start_plane()
        partner[0].start()
        two.start_line()
        three.start_line()
        for copy in own[:4]:
            copy.start()
        for step in (1, 2, 3):
            small.column(step)
            one.column(step)
        for index in range(1, PARTNERS):
            partner[index].start()
        taken.start()
        for step in range(4):
            small.side(step)
            one.side(step)
        three.start_plane()
        two.start_plane()
        for step in range(4):
            small.corner(step)
        small.sibling()
        own[1].wait()
        load_vectors.start()
        load_vectors.wait()

        def spread(index, carry):
            table[pl.ds(index, 1)] = spread_vector(vectors[...], index, width)
            return carry

        lax.fori_loop(0, 12, spread, 0)
        for step in range(4):
            one.corner(step)
        for step in (1, 2, 3):
            two.column(step)
        one.sibling()
        for index in (0, 2, 3, 4, 5, 6):
            own[index].wait()
        load_weights.start()
        load_weights.wait()
        project(0, 0, HALF, True)
        three.plane()
        taken.arrive()
        project(CONT, HALF, OWN, True)
        three.corners()
        taken_cot.start()
        for swap in partner:
            swap.arrive()
        project(HALF, 0, HALF + MEM, False)
        store_rows.start()

    def later(when, *actions):
        @pl.when(pair == when)
        def _():
            for action in actions:
                action[0](*action[1:])

    later(1, (two.side, 0), (three.far, 1, 0))
    later(2, (two.side, 1), (three.far, 1, 1), (three.far, 1, 2))
    later(3, (two.side, 2), (three.far, 1, 3), (three.far, 2, 0))
    later(4, (two.side, 3), (two.corner, 0), (three.far, 2, 1))
    later(5, (two.corner, 1), (two.corner, 2), (three.far, 2, 2))

    lanes = pl.ds(pl.multiple_of(pair * (2 * HEAD), 2 * HEAD), 2 * HEAD)
    query_out[...] = query[:, lanes]
    key_out[...] = key[:, lanes]
    value_out[...] = value[:, lanes]
    attend_pair(query_out, key_out, value_out, bias_ref, mixed_ref, log_ref)
    mixed[:, lanes] = mixed_ref[...]

    def fine(index):
        return table[index : index + 1]

    def save(tile, index):
        span = pl.ds(pl.multiple_of(tile * TILE, TILE), TILE)
        source, target = (
            (act, act_ref), (slope, ginner_ref), (hidden, ghidden_ref),
            (small_low.at[0], out_ref), (small_low.at[1], first_ref), (small_low.at[2], gdown_ref),
            (small_low.at[3], gbranch_ref), (small_low.at[4], gmixed_ref),
        )[index]
        return pltpu.make_async_copy(source, target.at[span], store.at[index])

    def up_chunk(step):
        return pl.ds(pl.multiple_of(step * width, 128), width)

    def up_columns(step):
        return pl.ds(pl.multiple_of((step + 1) * width, 128), width)

    def add_sum(index, values):
        sums_ref[pl.ds(index, 1)] += jnp.sum(values, axis=0, keepdims=True)

    def start_tile(tile):
        span = pl.ds(pl.multiple_of(tile * TILE, TILE), TILE)
        held = rows[pl.ds(pl.multiple_of(tile * CONT, MEM), TILE)].astype(jnp.float32)
        held = held + (product(mixed[span], wide[:, :width]) + fine(2))
        result, value_n, value_r = layer_norm(held, fine(3), fine(4))

        @pl.when(tile == 1)
        def _():
            for index in range(1, 8):
                save(0, index).wait()

        normed[...] = value_n
        first[...] = result
        small_low[1] = result.astype(low)
        return value_r

    def forward_chunk(step, carry):
        chunk = up_chunk(step)
        inner = product(small_low[1], wide[:, up_columns(step)]) + table[pl.ds(8 + step, 1)]
        half = 0.5 * (1.0 + lax.erf(inner * ROOT_HALF))
        active = (inner * half).astype(low)
        act[:, chunk] = active
        slope[:, chunk] = (half + inner * jnp.exp(-0.5 * inner * inner) * ROOT_GAUSS).astype(low)
        total[...] += product(active, down[chunk])
        return carry

    def backward_chunk(step, carry):
        chunk = up_chunk(step)
        grad = times_back(small_low[2], down[chunk]) * slope[:, chunk].astype(jnp.float32)
        grad = grad.astype(low)
        slope[:, chunk] = grad
        add_sum(8 + step, grad.astype(jnp.float32))
        total[...] += times_back(grad, wide[:, up_columns(step)])
        return carry

    def tile_body(tile, carry):
        span = pl.ds(pl.multiple_of(tile * TILE, TILE), TILE)
        inverse_one = start_tile(tile)
        total[...] = jnp.zeros_like(total)

        @pl.when(tile == 1)
        def _():
            save(0, 0).wait()

        lax.fori_loop(0, 4, forward_chunk, 0)
        save(tile, 0).start()
        result, value_n, inverse_two = layer_norm(
            first[...] + (total[...] + fine(5)), fine(6), fine(7)
        )
        small_low[0] = result.astype(low)
        save(tile, 3).start()
        save(tile, 4).start()
        cot = cotan[span].astype(jnp.float32)
        add_sum(6, cot * value_n)
        add_sum(7, cot)
        grad_mid = norm_back(cot * fine(6), value_n, inverse_two)
        grad_low = grad_mid.astype(low)
        small_low[2] = grad_low
        save(tile, 5).start()
        add_sum(5, grad_low.astype(jnp.float32))
        total[...] = grad_mid
        lax.fori_loop(0, 4, backward_chunk, 0)
        save(tile, 1).start()
        grad_first = total[...]
        add_sum(3, grad_first * normed[...])
        add_sum(4, grad_first)
        grad_hidden = norm_back(grad_first * fine(3), normed[...], inverse_one)
        hidden[...] = grad_hidden
        save(tile, 2).start()
        grad_low = grad_hidden.astype(low)
        small_low[3] = grad_low
        save(tile, 6).start()
        add_sum(2, grad_low.astype(jnp.float32))
        small_low[4] = times_back(grad_low, wide[:, :width]).astype(low)
        save(tile, 7).start()
        return carry

    @pl.when(pair == PAIRS - 1)
    def _():
        two.corner(3)
        two.sibling()
        load_wide.start()
        for step in (3,):
            three.far(2, step)
        for other in range(4):
            three.far(3, other)
        three.sibling()
        load_down.start()
        own[7].wait()
        own[8].wait()
        taken_cot.arrive()
        sums_ref[...] = jnp.zeros_like(sums_ref)
        load_wide.wait()
        load_down.wait()
        lax.fori_loop(0, 2, tile_body, 0)
        store_rows.wait()
        for index in range(8):
            save(1, index).wait()
        for sender in (one, small, two, three, *swaps):
            sender.finish()


def front(
    qkv, wide_share, down_share, vec, prompt, kept, sent, memory, prompt_cot, kept_cot, sent_cot,
    bias,
):
    width = prompt.shape[1]
    low = jnp.bfloat16
    wide = jnp.float32
    shape = jax.ShapeDtypeStruct

    def block(rows):
        return pl.BlockSpec((rows, 2 * HEAD), lambda pair: (0, pair))

    def full(share):
        return shape((32 * share.shape[0], share.shape[1]), low)

    dma = pltpu.SemaphoreType.DMA
    memory_space = pltpu.VMEM
    return pl.pallas_call(
        front_kernel,
        grid=(PAIRS,),
        in_specs=[INSIDE] * 4
        + [WHERE] * 7
        + [pl.BlockSpec((CLEN, OWN), lambda pair: (0, 0))],
        out_specs=[WHERE] * 13
        + [
            block(QROWS), pl.BlockSpec((None, 2, QROWS), lambda pair: (pair, 0, 0)),
            block(QROWS), block(KEYS), block(KEYS),
            pl.BlockSpec((VECTORS, width), lambda pair: (0, 0)),
        ],
        out_shape=[
            full(qkv), full(wide_share), full(down_share), full(vec),
            shape((KEYS, width), low),
            shape((QROWS, width), low),
            shape((QROWS, 4 * width), low),
            shape((QROWS, width), low),
            shape((QROWS, width), low),
            shape((QROWS, 4 * width), low),
            shape((QROWS, width), low),
            shape((QROWS, width), low),
            shape((QROWS, width), wide),
            shape((QROWS, width), low),
            shape((PAIRS, 2, QROWS), wide),
            shape((QROWS, width), low),
            shape((KEYS, width), low),
            shape((KEYS, width), low),
            shape((VECTORS, width), wide),
        ],
        scratch_shapes=[
            memory_space((KEYS, width), low),
            memory_space((width, 3 * width), low),
            memory_space((32 * VECTORS, 2 * HEAD), low),
            memory_space((VECTORS, width), wide),
            memory_space((QROWS, width), low),
            memory_space((KEYS, width), low),
            memory_space((KEYS, width), low),
            memory_space((QROWS, width), low),
            memory_space((QROWS, width), low),
            memory_space((width, 5 * width), low),
            memory_space((4 * width, width), low),
            memory_space((TILE, 4 * width), low),
            memory_space((TILE, 4 * width), low),
            memory_space((TILE, width), wide),
            memory_space((TILE, width), wide),
            memory_space((TILE, width), wide),
            memory_space((TILE, width), wide),
            memory_space((5, TILE, width), low),
        ]
        + [dma((32,))] * 4
        + [dma((100,)), dma((32,)), dma((32,)), dma((32,))]
        + [dma((PARTNERS + 2,)), dma((PARTNERS + 2,)), dma((14,)), dma((8,))],
        compiler_params=pltpu.CompilerParams(
            vmem_limit_bytes=67043328, collective_id=0, has_side_effects=True
        ),
        name="front",
    )(
        qkv, wide_share, down_share, vec, prompt, kept, sent, memory, prompt_cot, kept_cot,
        sent_cot, bias,
    )


SEND = 13
WIDE = 4
NARROW = 4


class Reduce:
    def __init__(self, mine, theirs, got, from_x, from_y, last_x, last_y, outer, total, send, recv):
        self.mine, self.theirs, self.got = mine, theirs, got
        self.from_x, self.from_y, self.last_x, self.last_y = from_x, from_y, last_x, last_y
        self.outer, self.total, self.send, self.recv = outer, total, send, recv
        self.half = mine.shape[1] // 2
        self.z, self.core, self.shard = seat()
        self.inner = (self.z == 1) | (self.z == 2)

    def copy(self, source, target, index, z, core, shard):
        return pltpu.make_async_remote_copy(
            src_ref=source, dst_ref=target, send_sem=self.send.at[index],
            recv_sem=self.recv.at[index], device_id=device_of(z, core, shard), device_id_type=MESH,
        )

    def upper(self, part):
        return self.mine.at[part, pl.ds(0, self.half)]

    def lower(self, part):
        return self.mine.at[part, pl.ds(self.half, self.half)]

    def link(self, index):
        z, core, shard = self.z, self.core, self.shard
        near = jnp.where(z < 2, 1 - z, 5 - z)
        if index < 4:
            ends = (self.theirs.at[index], self.got.at[index], z, 1 - core, shard)
        elif index < 6:
            source = self.upper(shard ^ (1 if index == 4 else 3))
            ends = (source, self.from_x.at[index - 4], z, core, shard ^ 1)
        elif index < 8:
            source = self.lower(shard ^ (2 if index == 6 else 3))
            ends = (source, self.from_y.at[index - 6], z, core, shard ^ 2)
        elif index == 8:
            ends = (self.upper(shard ^ 2), self.last_y, z, core, shard ^ 2)
        elif index == 9:
            ends = (self.lower(shard ^ 1), self.last_x, z, core, shard ^ 1)
        elif index == 10:
            ends = (self.mine.at[shard], self.outer, near, core, shard)
        elif index == 11:
            ends = (self.mine.at[shard], self.total, 3 - z, core, shard)
        else:
            ends = (self.total, self.total, near, core, shard)
        return self.copy(ends[0], ends[1], index, *ends[2:])

    def give(self, part):
        self.link(part).start()

    def given(self):
        for part in range(4):
            self.link(part).wait_send()

    def add(self, part, rows, other):
        total = self.mine[part, rows].astype(jnp.float32) + other.astype(jnp.float32)
        self.mine[part, rows] = total.astype(jnp.bfloat16)

    def chip(self):
        for part in range(4):
            self.link(part).wait_recv()

        def add_part(part, carry):
            self.add(part, slice(None), self.got[part])
            return carry

        lax.fori_loop(0, 4, add_part, 0)
        for index in (4, 5, 6, 7):
            self.link(index).start()

    def plane(self):
        upper, lower = slice(0, self.half), slice(self.half, 2 * self.half)
        shard = self.shard
        self.link(4).wait_recv()
        self.link(5).wait_recv()
        self.add(shard ^ 2, upper, self.from_x[1])
        self.link(8).start()
        self.link(6).wait_recv()
        self.link(7).wait_recv()
        self.add(shard ^ 1, lower, self.from_y[1])
        self.link(9).start()
        self.add(shard, upper, self.from_x[0])
        self.add(shard, lower, self.from_y[0])

    def line(self):
        upper, lower = slice(0, self.half), slice(self.half, 2 * self.half)
        self.link(8).wait_recv()
        self.add(self.shard, upper, self.last_y[...])
        self.link(9).wait_recv()
        self.add(self.shard, lower, self.last_x[...])

        @pl.when(jnp.logical_not(self.inner))
        def _():
            self.link(10).start()

    def middle(self):
        @pl.when(self.inner)
        def _():
            self.link(10).wait_recv()
            self.add(self.shard, slice(None), self.outer[...])
            self.link(11).start()

    def spread(self):
        @pl.when(self.inner)
        def _():
            self.link(11).wait_recv()
            total = self.total[...].astype(jnp.float32)
            total = total + self.mine[self.shard].astype(jnp.float32)
            self.total[...] = total.astype(jnp.bfloat16)
            self.link(12).start()

    def share(self, place, semaphore):
        @pl.when(jnp.logical_not(self.inner))
        def _():
            self.link(12).wait_recv()

        pltpu.make_async_copy(self.total, place, semaphore).start()
        pltpu.make_async_remote_copy(
            src_ref=self.total, dst_ref=place, send_sem=self.send.at[13],
            recv_sem=self.recv.at[13],
            device_id=device_of(self.z, 1 - self.core, self.shard), device_id_type=MESH,
        ).start()

    def finish(self, place, semaphore):
        pltpu.make_async_copy(self.total, place, semaphore).wait()
        last = pltpu.make_async_remote_copy(
            src_ref=self.total, dst_ref=place, send_sem=self.send.at[13],
            recv_sem=self.recv.at[13],
            device_id=device_of(self.z, 1 - self.core, self.shard), device_id_type=MESH,
        )
        last.wait_send()
        last.wait_recv()
        for index in range(4, 10):
            self.link(index).wait_send()

        @pl.when(jnp.logical_not(self.inner))
        def _():
            self.link(10).wait_send()

        @pl.when(self.inner)
        def _():
            self.link(11).wait_send()
            self.link(12).wait_send()


class Butterfly:
    def __init__(self, held, got, send, recv):
        self.held, self.got, self.send, self.recv = held, got, send, recv
        self.z, self.core, self.shard = seat()

    def copy(self, step):
        z, core, shard = self.z, self.core, self.shard
        where = ((z, core, shard ^ 1), (z, core, shard ^ 2), (z ^ 1, core, shard),
                 (z ^ 2, core, shard), (z, 1 - core, shard))[step]
        rows = pl.ds(0, 2 * VECTORS if step < 2 else VECTORS)
        return pltpu.make_async_remote_copy(
            src_ref=self.held.at[step, rows], dst_ref=self.got.at[step, rows],
            send_sem=self.send.at[step], recv_sem=self.recv.at[step],
            device_id=device_of(*where), device_id_type=MESH,
        )

    def start(self):
        self.copy(0).start()

    def step(self, step):
        self.copy(step).wait_recv()
        rows = slice(0, 2 * VECTORS if step < 2 else VECTORS)
        self.held[step + 1, rows] = self.held[step, rows] + self.got[step, rows]
        if step < 4:
            self.copy(step + 1).start()

    def finish(self):
        for step in range(5):
            self.copy(step).wait_send()


def back_head(
    head, query_ref, key_ref, value_ref, bias_ref, log_ref, grad_ref,
    overlap, key_flip, key_acc, value_acc,
):
    mem_valid = lax.broadcasted_iota(jnp.int32, (MEM, 1), 0) < READ

    def block_back(keys, values, bias, valid, queries, grads, log, delta, flipped, rows):
        scores = times_back(keys, queries)
        if bias is not None:
            scores = scores + bias
        chances = jnp.exp(scores - log)
        if valid is not None:
            chances = jnp.where(valid, chances, 0.0)
        slopes = (chances * (times_back(values, grads) - delta)).astype(jnp.bfloat16)
        value_acc[rows] += product(chances.astype(jnp.bfloat16), grads)
        key_acc[rows] += product(slopes, queries)
        return product(flipped, slopes)

    mask = head_mask(head)
    queries = pick(mask, query_ref[...])
    grads = pick(mask, grad_ref[...])
    span = slice(head * HEAD, (head + 1) * HEAD)
    delta = jnp.sum(overlap[span], axis=0, keepdims=True)
    log = log_ref[head : head + 1]
    flipped = key_flip[span]
    main_rows = slice(0, 2 * HALF)
    mem_rows = slice(2 * HALF, CONT)
    pieces = []
    for half in range(2):
        part = slice(half * HALF, (half + 1) * HALF)
        piece = block_back(
            key_ref[main_rows], value_ref[main_rows], None, None,
            queries[part], grads[part], log[:, part], delta[:, part],
            flipped[:, main_rows], main_rows,
        )
        piece += block_back(
            key_ref[mem_rows], value_ref[mem_rows], None, mem_valid,
            queries[part], grads[part], log[:, part], delta[:, part],
            flipped[:, mem_rows], mem_rows,
        )
        pieces.append(piece)
    own_parts = []
    for cont in range(OWN // CLEN):
        rows = slice(CONT + cont * CLEN, CONT + (cont + 1) * CLEN)
        part = slice(HALF + cont * CLEN, HALF + (cont + 1) * CLEN)
        own_parts.append(
            block_back(
                key_ref[rows], value_ref[rows], bias_ref[:, cont * CLEN : (cont + 1) * CLEN],
                None, queries[part], grads[part], log[:, part], delta[:, part],
                flipped[:, rows], rows,
            )
        )
    pieces[1] += jnp.concatenate(own_parts, axis=1)
    return jnp.concatenate(pieces, axis=1)


def back_kernel(
    act_ref, gdown_ref, first_ref, ginner_ref, mixed_all, gbranch_ref, ghidden_ref, rows_ref,
    qkv_ref, out_ref, sums_ref,
    query_ref, key_ref, value_ref, grad_ref, mixed_ref, log_ref, bias_ref,
    down_out, up_out, out_out, qkv_out, returned_out, grad_prompt, grad_kept, grad_back,
    memory_out, vec_out,
    wide_mine, wide_theirs, wide_got, wide_x, wide_y, wide_lx, wide_ly, wide_outer, wide_total,
    thin_mine, thin_theirs, thin_got, thin_x, thin_y, thin_lx, thin_ly, thin_outer, thin_total,
    pool, rows, dquery, dkey, dvalue, key_acc, value_acc, partner, ghidden, staged, held, got,
    send, recv, small_send, small_recv, swap_send, swap_recv, local, out_sem,
):
    pair = pl.program_id(0)
    z, core, shard = seat()
    other = 1 - core
    width = rows_ref.shape[1]
    part_rows = width // 4
    low = jnp.bfloat16

    items = []
    for index in range(WIDE):
        items.append(
            Reduce(
                wide_mine.at[index], wide_theirs.at[index % 2], wide_got.at[index],
                wide_x.at[index], wide_y.at[index], wide_lx.at[index], wide_ly.at[index],
                wide_outer.at[index], wide_total.at[index], send.at[index], recv.at[index],
            )
        )
    for index in range(NARROW):
        items.append(
            Reduce(
                thin_mine.at[index], thin_theirs.at[index % 2], thin_got.at[index],
                thin_x.at[index], thin_y.at[index], thin_lx.at[index], thin_ly.at[index],
                thin_outer.at[index], thin_total.at[index], send.at[WIDE + index],
                recv.at[WIDE + index],
            )
        )
    small = Butterfly(held, got, small_send, small_recv)
    half_hidden = width // 2

    def place(index):
        if index < 2:
            start = core * half_hidden + index * part_rows
            return down_out.at[pl.ds(pl.multiple_of(start, 64), part_rows)]
        if index < 4:
            start = core * (2 * width) + (index - 2) * width
            return up_out.at[:, pl.ds(pl.multiple_of(start, 128), width)]
        if index == 4:
            return out_out.at[:, pl.ds(pl.multiple_of(core * half_hidden, 128), half_hidden)]
        return qkv_out.at[index - 5, core]

    def chip(index):
        items[index].chip()

    def plane(index):
        items[index].plane()

    def line(index):
        items[index].line()

    def middle(index):
        items[index].middle()

    def spread(index):
        items[index].spread()

    def share(index):
        items[index].share(place(index), out_sem.at[index])

    returned = Swap(
        out_ref, returned_out, swap_send.at[0], swap_recv.at[0], z, core, shard ^ 2
    )
    to_partner = [
        Swap(
            pool.at[3, pl.ds(256 * index, 256)], partner.at[pl.ds(256 * index, 256)],
            swap_send.at[1 + index], swap_recv.at[1 + index], z, core, shard ^ 1,
        )
        for index in range(2)
    ]
    cont_back = Swap(
        pool.at[3, pl.ds(2 * 256, 256)], grad_back, swap_send.at[3], swap_recv.at[3],
        z, core, shard ^ 2,
    )

    def load(source, slot, semaphore):
        return pltpu.make_async_copy(source, pool.at[slot], local.at[semaphore])

    def act_chunk(part):
        return load(act_ref.at[:, pl.ds(part * width, width)], part % 2, part % 2)

    def inner_chunk(step):
        half = other if step < 2 else core
        start = pl.multiple_of(half * (2 * width) + (step % 2) * width, 128)
        return load(ginner_ref.at[:, pl.ds(start, width)], step % 2, step % 2)

    def parts_of(target, values):
        for part in range(4):
            target[part] = values[part * part_rows : (part + 1) * part_rows].astype(low)

    load_rows = pltpu.make_async_copy(rows_ref, rows, local.at[4])

    @pl.when(pair == 0)
    def _():
        act_chunk(0).start()
        load(gdown_ref, 2, 2).start()
        act_chunk(1).start()
        load(first_ref, 3, 3).start()
        load_rows.start()
        greet()
        returned.start()
        load(gdown_ref, 2, 2).wait()
        for part in range(4):
            act_chunk(part).wait()
            for half in (other, core):
                lanes = pl.ds(pl.multiple_of(half * half_hidden, 128), half_hidden)
                result = outer_sum(pool[part % 2, :, lanes], pool[2]).astype(low)
                for index in range(2):
                    piece = result[index * part_rows : (index + 1) * part_rows]
                    if half is other:
                        wide_theirs[index, part] = piece
                        items[index].give(part)
                    else:
                        wide_mine[index, part] = piece
            if part < 2:
                act_chunk(part + 2).start()
            else:
                inner_chunk(part - 2).start()
        load(mixed_all, 2, 2).start()
        load(first_ref, 3, 3).wait()
        for step in range(4):
            inner_chunk(step).wait()
            result = outer_sum(pool[3], pool[step % 2])
            if step < 2:
                items[step].given()
                parts_of(wide_theirs.at[step], result)
                for part in range(4):
                    items[2 + step].give(part)
                inner_chunk(step + 2).start()
            else:
                parts_of(wide_mine.at[step], result)
            if step == 1:
                chip(0)
            if step == 2:
                chip(1)
        load(gbranch_ref, 3, 3).start()
        load(mixed_all, 2, 2).wait()
        load(gbranch_ref, 3, 3).wait()
        for half in (other, core):
            lanes = pl.ds(pl.multiple_of(half * half_hidden, 128), half_hidden)
            result = outer_sum(pool[2], pool[3, :, lanes])
            if half is other:
                parts_of(thin_theirs.at[0], result)
                for part in range(4):
                    items[4].give(part)
            else:
                parts_of(thin_mine.at[0], result)
        for index in range(3):
            pltpu.make_async_copy(
                qkv_ref.at[:, pl.ds(index * width, width)],
                pool.at[index, pl.ds(0, width)], local.at[index],
            ).start()
        load_rows.wait()

    def qkv_part(index):
        for half in (other, core):
            lanes = pl.ds(pl.multiple_of((2 * index + half) * (2 * HEAD), 2 * HEAD), 2 * HEAD)
            query_side = outer_sum(rows[:HALF], dquery[:HALF, lanes])
            query_side += outer_sum(rows[CONT:], dquery[HALF:, lanes])
            both = jnp.concatenate([dkey[:, lanes], dvalue[:, lanes]], axis=1)
            result = jnp.concatenate([query_side, outer_sum(rows[...], both)], axis=1)
            if half is other:
                if index:
                    items[3 + index].given()
                parts_of(thin_theirs.at[(1 + index) % 2], result)
                for part in range(4):
                    items[5 + index].give(part)
            else:
                parts_of(thin_mine.at[1 + index], result)

    schedule = {
        0: [(plane, 0), (chip, 2)],
        2: [(line, 0), (plane, 1), (chip, 3)],
        3: [(qkv_part, 0)],
        4: [(plane, 2), (middle, 0)],
        5: [(line, 1), (chip, 4)],
        6: [(spread, 0), (plane, 3), (line, 2)],
        7: [(qkv_part, 1), (middle, 1), (chip, 5)],
        8: [(share, 0), (plane, 4), (line, 3)],
        9: [(spread, 1), (middle, 2), (plane, 5)],
        10: [(line, 4), (chip, 6), (middle, 3)],
        11: [(qkv_part, 2), (share, 1), (spread, 2), (line, 5)],
    }

    def slot(number):
        if number in schedule:
            @pl.when(pair == number // 2)
            def _():
                for action, index in schedule[number]:
                    action(index)

    def slots(head):
        for step in range(PAIRS):
            slot(2 * step + head)

    lanes = pl.ds(pl.multiple_of(pair * (2 * HEAD), 2 * HEAD), 2 * HEAD)
    key_flip = flip(key_ref[...])
    overlap = (mixed_ref[...].astype(jnp.float32) * grad_ref[...].astype(jnp.float32)).T
    key_acc[...] = jnp.zeros_like(key_acc)
    value_acc[...] = jnp.zeros_like(value_acc)
    results = []
    for head in range(2):
        results.append(
            back_head(
                head, query_ref, key_ref, value_ref, bias_ref, log_ref, grad_ref,
                overlap, key_flip, key_acc, value_acc,
            )
        )
        if head == 0:
            slots(0)
    dquery[:, lanes] = (jnp.concatenate(results, axis=0).T * SCALE).astype(low)
    dkey[:, lanes] = key_acc[...].astype(low)
    dvalue[:, lanes] = value_acc[...].astype(low)
    slots(1)

    def key_side(rows_of):
        return times_back(dkey[rows_of], pool[1, :width]) + times_back(
            dvalue[rows_of], pool[2, :width]
        )

    def hidden_chunk(index):
        return pltpu.make_async_copy(
            ghidden_ref.at[pl.ds(256 * index, 256)], ghidden.at[index % 2],
            local.at[5 + index % 2],
        )

    @pl.when(pair == PAIRS - 1)
    def _():
        hidden_chunk(3).start()
        hidden_chunk(2).start()
        sums = pltpu.make_async_copy(
            sums_ref, held.at[0, pl.ds(0, VECTORS)], local.at[7]
        )
        sums.start()
        for index in range(3):
            pltpu.make_async_copy(
                qkv_ref.at[:, pl.ds(index * width, width)],
                pool.at[index, pl.ds(0, width)], local.at[index],
            ).wait()
        for index in range(2):
            start = HALF + 256 * index
            pool[3, 256 * index : 256 * (index + 1)] = key_side(
                slice(start, start + 256)
            ).astype(low)
            if index == 0:
                chip(7)
            to_partner[index].start()
        sums.wait()
        held[0, 0:1] = jnp.sum(dquery[...].astype(jnp.float32), axis=0, keepdims=True)
        held[0, 1:2] = jnp.sum(dvalue[...].astype(jnp.float32), axis=0, keepdims=True)
        held[0, VECTORS:] = key_side(slice(2 * HALF, CONT))
        small.start()
        plane(6)
        hidden_chunk(3).wait()
        pool[3, 512:768] = (
            ghidden[1]
            + times_back(dquery[768:], pool[0, :width])
            + key_side(slice(CONT + 256, KEYS))
        ).astype(low)
        cont_back.start()
        hidden_chunk(1).start()
        middle(4)
        plane(7)
        small.step(0)
        hidden_chunk(2).wait()
        staged[2] = (
            ghidden[0]
            + times_back(dquery[512:768], pool[0, :width])
            + key_side(slice(CONT, CONT + 256))
        ).astype(low)
        hidden_chunk(0).start()
        store_kept = pltpu.make_async_copy(staged.at[2], grad_kept, local.at[8])
        store_kept.start()
        line(6)
        spread(3)
        share(2)
        small.step(1)
        spread(4)
        line(7)
        middle(5)
        middle(6)
        share(3)
        small.step(2)
        middle(7)
        share(4)
        spread(5)
        stores = []
        for index in (1, 0):
            hidden_chunk(index).wait()
            span = slice(256 * index, 256 * (index + 1))
            result = (
                ghidden[index]
                + times_back(dquery[span], pool[0, :width])
                + key_side(span)
            )
            to_partner[index].arrive()
            staged[index] = (result + partner[span].astype(jnp.float32)).astype(low)
            stores.append(
                pltpu.make_async_copy(
                    staged.at[index], grad_prompt.at[pl.ds(256 * index, 256)], local.at[9 + index]
                )
            )
            stores[-1].start()
            if index == 1:
                spread(6)
                small.step(3)
        spread(7)
        share(5)
        small.step(4)
        share(6)
        share(7)
        family = shard // 2
        memory_out[family] = held[1, VECTORS:]
        memory_out[1 - family] = got[1, VECTORS:]
        vec_out[...] = held[5, :VECTORS]
        returned.arrive()
        cont_back.arrive()
        store_kept.wait()
        for store in stores:
            store.wait()
        for index in (6, 7):
            items[index].given()
        for index in (2, 3):
            items[index].given()
        for index in range(WIDE + NARROW):
            items[index].finish(place(index), out_sem.at[index])
        small.finish()
        for swap in (returned, to_partner[0], to_partner[1], cont_back):
            swap.finish()


def back(
    act, gdown, first, ginner, mixed, gbranch, ghidden, rows, qkv, out_taken, sums,
    query, key, value, grads, log, bias,
):
    width = rows.shape[1]
    low = jnp.bfloat16
    wide = jnp.float32

    def block(count):
        return pl.BlockSpec((count, 2 * HEAD), lambda pair: (0, pair))

    dma = pltpu.SemaphoreType.DMA
    part = width // 4

    def buffers(count, columns):
        return [
            pltpu.VMEM((count, 4, part, columns), low),
            pltpu.VMEM((2, 4, part, columns), low),
            pltpu.VMEM((count, 4, part, columns), low),
            pltpu.VMEM((count, 2, part // 2, columns), low),
            pltpu.VMEM((count, 2, part // 2, columns), low),
            pltpu.VMEM((count, part // 2, columns), low),
            pltpu.VMEM((count, part // 2, columns), low),
            pltpu.VMEM((count, part, columns), low),
            pltpu.VMEM((count, part, columns), low),
        ]

    shape = jax.ShapeDtypeStruct
    return pl.pallas_call(
        back_kernel,
        grid=(PAIRS,),
        in_specs=[WHERE] * 11
        + [
            block(QROWS), block(KEYS), block(KEYS), block(QROWS), block(QROWS),
            pl.BlockSpec((None, 2, QROWS), lambda pair: (pair, 0, 0)),
            pl.BlockSpec((CLEN, OWN), lambda pair: (0, 0)),
        ],
        out_specs=[WHERE] * 8
        + [
            pl.BlockSpec((2, MEM, width), lambda pair: (0, 0, 0)),
            pl.BlockSpec((VECTORS, width), lambda pair: (0, 0)),
        ],
        out_shape=[
            shape((width, width), low),
            shape((part, 4 * width), low),
            shape((part, width), low),
            shape((3, 2, part, width // 2), low),
            shape((OWN // 2, width), low),
            shape((HALF, width), low),
            shape((OWN // 2, width), low),
            shape((OWN // 2, width), low),
            shape((2, MEM, width), wide),
            shape((VECTORS, width), wide),
        ],
        scratch_shapes=buffers(WIDE, width)
        + buffers(NARROW, width // 2)
        + [
            pltpu.VMEM((4, QROWS, width), low),
            pltpu.VMEM((KEYS, width), low),
            pltpu.VMEM((QROWS, width), low),
            pltpu.VMEM((KEYS, width), low),
            pltpu.VMEM((KEYS, width), low),
            pltpu.VMEM((KEYS, 2 * HEAD), wide),
            pltpu.VMEM((KEYS, 2 * HEAD), wide),
            pltpu.VMEM((HALF, width), low),
            pltpu.VMEM((2, 256, width), wide),
            pltpu.VMEM((3, 256, width), low),
            pltpu.VMEM((6, 2 * VECTORS, width), wide),
            pltpu.VMEM((5, 2 * VECTORS, width), wide),
            dma((WIDE + NARROW, SEND + 1)),
            dma((WIDE + NARROW, SEND + 1)),
            dma((5,)),
            dma((5,)),
            dma((4,)),
            dma((4,)),
            dma((11,)),
            dma((WIDE + NARROW,)),
        ],
        compiler_params=pltpu.CompilerParams(
            vmem_limit_bytes=67043328, collective_id=1, has_side_effects=True
        ),
        name="back",
    )(
        act, gdown, first, ginner, mixed, gbranch, ghidden, rows, qkv, out_taken, sums,
        query, key, value, grads, mixed, log, bias,
    )


def body_pairs(
    prompt_rows, follow_rows, memory_rows, follow_owner, follow_length,
    query_weight, key_weight, value_weight, out_weight, query_bias, value_bias, out_bias,
    first_gain, first_shift, up_weight, up_bias, down_weight, down_bias,
    second_gain, second_shift, prompt_cotan, follow_cotan,
):
    shard_index = lax.axis_index("shard")
    family = shard_index // 2
    width = prompt_rows.shape[2]
    conts = OWN // CLEN
    low = jnp.bfloat16
    wide = jnp.float32

    owner_row = follow_owner[0]
    length_row = follow_length[0]

    def ranks(shard, prompt_of):
        owned = (lax.dynamic_slice(owner_row, (shard * conts,), (conts,)) == prompt_of).astype(
            jnp.int32
        )
        before = jnp.cumsum(owned) - owned
        return jnp.where(owned == 1, before, 2 + jnp.arange(conts) - before)

    place = ranks(shard_index, family)
    across = shard_index ^ 2
    place_across = ranks(across, across // 2)
    order = jnp.argmax(place[None, :] == jnp.arange(conts)[:, None], axis=1)
    order_across = jnp.argmax(place_across[None, :] == jnp.arange(conts)[:, None], axis=1)
    lengths = jnp.concatenate(
        [
            length_row[shard_index * conts + order[:2]],
            length_row[across * conts + order_across[2:]],
        ]
    )
    positions = jnp.arange(CLEN)
    own_valid = (positions[:, None] < lengths[None, :]) | (positions[:, None] >= CLEN - WRITE)
    bias = jnp.repeat(jnp.where(own_valid, 0.0, NEGATIVE).astype(wide), CLEN, axis=1)

    def sort_conts(values):
        blocks = values.reshape(conts, CLEN, width)[order].reshape(OWN, width)
        return (blocks[: OWN // 2], blocks[OWN // 2 :])

    def unsort(values, returned):
        blocks = jnp.concatenate([values, returned], axis=0).reshape(conts, CLEN, width)
        return blocks[place].reshape(OWN, width)

    prompt = prompt_rows[0]
    kept, sent = sort_conts(follow_rows[0])
    kept_cotan, sent_cotan = sort_conts(follow_cotan[0])
    memory = lax.dynamic_index_in_dim(memory_rows[0], family, 0, keepdims=False)
    memory = jnp.pad(memory, ((0, MEM - READ), (0, 0)))
    share = query_bias.shape[0]
    vec = jnp.stack(
        [
            jnp.pad(vector, (0, 2 * HEAD - share))
            for vector in (
                query_bias, value_bias, out_bias, first_gain, first_shift,
                down_bias, second_gain, second_shift,
            )
        ]
        + [jnp.pad(up_bias, (0, 2 * HEAD - up_bias.shape[0]))]
    )
    vec = jnp.pad(vec, ((0, VECTORS - vec.shape[0]), (0, 0)))
    (
        qkv_mat, _, _, _, key_rows,
        output, activated, first_low, grad_down, grad_inner, grad_branch, grad_mixed, grad_hidden,
        mixed, log, query_low, key_low, value_low, sums,
    ) = front(
        jnp.concatenate([query_weight, key_weight, value_weight], axis=1),
        jnp.concatenate([out_weight, up_weight], axis=1),
        down_weight, vec, prompt, kept, sent, memory, prompt_cotan[0], kept_cotan, sent_cotan,
        bias,
    )
    (
        down_sum, up_sum, out_sum, qkv_sum, returned_out, grad_prompt, grad_kept, returned_grad,
        memory_sum, sums,
    ) = back(
        activated, grad_down, first_low, grad_inner, mixed, grad_branch, grad_hidden, key_rows,
        qkv_mat, output[HALF + OWN // 2 :], sums,
        query_low, key_low, value_low, grad_mixed, log, bias,
    )
    grad_memory = memory_sum[None, :, :READ].astype(low)
    qkv_sum = qkv_sum.reshape(3, 2, width // 4, 3, 2 * HEAD).transpose(3, 2, 0, 1, 4)
    qkv_sum = qkv_sum.reshape(3, width // 4, width).astype(wide)
    mine = width // 4

    def part(index):
        return lax.dynamic_slice(sums[index], (shard_index * mine,), (mine,))

    up_part = lax.dynamic_slice(sums[8:12].reshape(-1), (shard_index * width,), (width,))
    follow_out = unsort(output[HALF : HALF + OWN // 2], returned_out)
    follow_grad = unsort(grad_kept, returned_grad)
    return (
        output[:HALF][None],
        follow_out[None],
        grad_prompt[None],
        follow_grad[None],
        grad_memory,
        qkv_sum[0],
        qkv_sum[1],
        qkv_sum[2],
        out_sum.astype(wide),
        part(0),
        part(1),
        part(2),
        part(3),
        part(4),
        up_sum.astype(wide),
        up_part,
        down_sum.astype(wide),
        part(5),
        part(6),
        part(7),
    )


def solution(mesh):
    return jax.shard_map(
        body_pairs if pairs_fit(mesh) else body_any,
        mesh=mesh,
        in_specs=(
            P("grp", "shard", None),
            P("grp", "shard", None),
            P("grp", None, None, None),
            P("grp", None),
            P("grp", None),
            P(("grp", "shard"), None),
            P(("grp", "shard"), None),
            P(("grp", "shard"), None),
            P(("grp", "shard"), None),
            P(("grp", "shard")),
            P(("grp", "shard")),
            P(("grp", "shard")),
            P(("grp", "shard")),
            P(("grp", "shard")),
            P(("grp", "shard"), None),
            P(("grp", "shard")),
            P(("grp", "shard"), None),
            P(("grp", "shard")),
            P(("grp", "shard")),
            P(("grp", "shard")),
            P("grp", "shard", None),
            P("grp", "shard", None),
        ),
        out_specs=(
            P("grp", "shard", None),
            P("grp", "shard", None),
            P("grp", "shard", None),
            P("grp", "shard", None),
            P("grp", None, None, None),
            P("shard", None),
            P("shard", None),
            P("shard", None),
            P("shard", None),
            P("shard"),
            P("shard"),
            P("shard"),
            P("shard"),
            P("shard"),
            P("shard", None),
            P("shard"),
            P("shard", None),
            P("shard"),
            P("shard"),
            P("shard"),
        ),
        check_vma=False,
    )
```

```python
import jax
import jax.numpy as jnp
from jax import lax
from jax.experimental import pallas as pl
from jax.experimental.pallas import tpu as pltpu
from jax.sharding import PartitionSpec as P

HEADS = 12
HEAD = 64
READ = 10
WRITE = 10
PLEN = 1024
CLEN = 128
CONTS_PER = 8


EPSILON = 1e-12
SCALE = 0.125
NEGATIVE = -1e30
ROOT_HALF = 0.7071067811865476
ROOT_GAUSS = 0.3989422804014327


def product(left, right):
    return jnp.dot(left, right, preferred_element_type=jnp.float32)


def times_back(left, right):
    return lax.dot_general(
        left, right, (((1,), (1,)), ((), ())), preferred_element_type=jnp.float32
    )


def outer_sum(left, right):
    return lax.dot_general(
        left, right, (((0,), (0,)), ((), ())), preferred_element_type=jnp.float32
    )


def column_sum(values):
    return jnp.sum(values.astype(jnp.float32), axis=0)


def layer_norm(hidden, gain, shift):
    center = hidden - jnp.mean(hidden, axis=-1, keepdims=True)
    inverse = lax.rsqrt(jnp.mean(center * center, axis=-1, keepdims=True) + EPSILON)
    normed = center * inverse
    return (normed * gain.astype(jnp.float32) + shift.astype(jnp.float32), normed, inverse)


def norm_back(grad_normed, normed, inverse):
    centered = grad_normed - jnp.mean(grad_normed, axis=-1, keepdims=True)
    return inverse * (centered - normed * jnp.mean(grad_normed * normed, axis=-1, keepdims=True))


def gelu_exact(hidden):
    return 0.5 * hidden * (1.0 + lax.erf(hidden * ROOT_HALF))


def gelu_slope(hidden):
    return (
        0.5 * (1.0 + lax.erf(hidden * ROOT_HALF))
        + hidden * jnp.exp(-0.5 * hidden * hidden) * ROOT_GAUSS
    )


def split_heads(values):
    return values.reshape(values.shape[0], values.shape[1], HEADS, HEAD)


def block_scores(queries, keys, valid):
    scores = (
        jnp.einsum(
            "nqhd,nkhd->nhqk",
            split_heads(queries),
            split_heads(keys),
            preferred_element_type=jnp.float32,
        )
        * SCALE
    )
    return jnp.where(valid[:, None, None, :], scores, NEGATIVE)


def attend_forward(queries, keys, values, valid):
    scores = block_scores(queries, keys, valid)
    maximum = jnp.max(scores, axis=-1, keepdims=True)
    powers = jnp.exp(scores - maximum)
    totals = jnp.sum(powers, axis=-1, keepdims=True)
    chances = (powers / totals).astype(jnp.bfloat16)
    result = jnp.einsum(
        "nhqk,nkhd->nqhd", chances, split_heads(values), preferred_element_type=jnp.float32
    )
    return (result.reshape(-1, queries.shape[2]), maximum + jnp.log(totals))


def attend_backward(queries, keys, values, valid, logsum, grad_out):
    width = queries.shape[2]
    scores = block_scores(queries, keys, valid)
    chances = jnp.exp(scores - logsum)
    grad_heads = split_heads(grad_out)
    grad_chance = jnp.einsum(
        "nqhd,nkhd->nhqk", grad_heads, split_heads(values), preferred_element_type=jnp.float32
    )
    inner = jnp.sum(chances * grad_chance, axis=-1, keepdims=True)
    grad_score = (chances * (grad_chance - inner)).astype(jnp.bfloat16)
    grad_query = (
        jnp.einsum(
            "nhqk,nkhd->nqhd", grad_score, split_heads(keys), preferred_element_type=jnp.float32
        )
        * SCALE
    )
    grad_key = (
        jnp.einsum(
            "nhqk,nqhd->nkhd", grad_score, split_heads(queries), preferred_element_type=jnp.float32
        )
        * SCALE
    )
    grad_value = jnp.einsum(
        "nhqk,nqhd->nkhd",
        chances.astype(jnp.bfloat16),
        grad_heads,
        preferred_element_type=jnp.float32,
    )
    span = keys.shape[1]
    return (
        grad_query.reshape(-1, width),
        grad_key.reshape(keys.shape[0], span, width),
        grad_value.reshape(keys.shape[0], span, width),
    )


def body_any(
    prompt_rows,
    follow_rows,
    memory_rows,
    follow_owner,
    follow_length,
    query_weight,
    key_weight,
    value_weight,
    out_weight,
    query_bias,
    value_bias,
    out_bias,
    first_gain,
    first_shift,
    up_weight,
    up_bias,
    down_weight,
    down_bias,
    second_gain,
    second_shift,
    prompt_cotan,
    follow_cotan,
):
    (
        query_mat,
        key_mat,
        value_mat,
        out_mat,
        query_add,
        value_add,
        out_add,
        gain_one,
        shift_one,
        up_mat,
        up_add,
        down_mat,
        down_add,
        gain_two,
        shift_two,
    ) = (
        lax.all_gather(query_weight, ("grp", "shard"), axis=0, tiled=True),
        lax.all_gather(key_weight, ("grp", "shard"), axis=0, tiled=True),
        lax.all_gather(value_weight, ("grp", "shard"), axis=0, tiled=True),
        lax.all_gather(out_weight, ("grp", "shard"), axis=0, tiled=True),
        lax.all_gather(query_bias, ("grp", "shard"), axis=0, tiled=True),
        lax.all_gather(value_bias, ("grp", "shard"), axis=0, tiled=True),
        lax.all_gather(out_bias, ("grp", "shard"), axis=0, tiled=True),
        lax.all_gather(first_gain, ("grp", "shard"), axis=0, tiled=True),
        lax.all_gather(first_shift, ("grp", "shard"), axis=0, tiled=True),
        lax.all_gather(up_weight, ("grp", "shard"), axis=0, tiled=True),
        lax.all_gather(up_bias, ("grp", "shard"), axis=0, tiled=True),
        lax.all_gather(down_weight, ("grp", "shard"), axis=0, tiled=True),
        lax.all_gather(down_bias, ("grp", "shard"), axis=0, tiled=True),
        lax.all_gather(second_gain, ("grp", "shard"), axis=0, tiled=True),
        lax.all_gather(second_shift, ("grp", "shard"), axis=0, tiled=True),
    )
    shard_index = lax.axis_index("shard")
    prompt = prompt_rows[0]
    follow = follow_rows[0]
    p_count = prompt.shape[0]
    f_count = follow.shape[0]
    width = prompt.shape[1]
    families = memory_rows.shape[1]
    all_rows = jnp.concatenate([prompt, follow], axis=0)
    memory_flat = memory_rows[0].reshape(families * READ, width)
    query_low = (product(all_rows, query_mat) + query_add.astype(jnp.float32)).astype(jnp.bfloat16)
    key_low = product(all_rows, key_mat).astype(jnp.bfloat16)
    value_low = (product(all_rows, value_mat) + value_add.astype(jnp.float32)).astype(jnp.bfloat16)
    mem_key = product(memory_flat, key_mat).astype(jnp.bfloat16).reshape(families, READ, width)
    mem_value = (
        (product(memory_flat, value_mat) + value_add.astype(jnp.float32))
        .astype(jnp.bfloat16)
        .reshape(families, READ, width)
    )
    half_prompt = PLEN // 2
    per_block = CONTS_PER // 2
    prompt_blocks = p_count // half_prompt
    conts_here = f_count // CLEN
    positions = jnp.arange(CLEN)
    open_span = jnp.ones((per_block, READ + PLEN), dtype=bool)
    owner_row = follow_owner[0]
    length_row = follow_length[0]
    prompt_keys, prompt_values = (
        lax.all_gather(key_low[:p_count], "shard", axis=0, tiled=True),
        lax.all_gather(value_low[:p_count], "shard", axis=0, tiled=True),
    )
    key_table = prompt_keys.reshape(families, PLEN, width)
    value_table = prompt_values.reshape(families, PLEN, width)

    def prompt_inputs(block):
        start = block * half_prompt
        family = (shard_index * p_count + start) // PLEN
        keys = jnp.concatenate([mem_key[family], key_table[family]], axis=0)[None]
        values = jnp.concatenate([mem_value[family], value_table[family]], axis=0)[None]
        valid = jnp.ones((1, READ + PLEN), dtype=bool)
        return (query_low[start : start + half_prompt][None], keys, values, valid, family)

    def follow_inputs(block):
        first_row = p_count + block * per_block * CLEN
        chosen = shard_index * conts_here + block * per_block + jnp.arange(per_block)
        owners = owner_row[chosen]
        lengths = length_row[chosen]
        own_keys = key_low[first_row : first_row + per_block * CLEN].reshape(per_block, CLEN, width)
        own_values = value_low[first_row : first_row + per_block * CLEN].reshape(
            per_block, CLEN, width
        )
        keys = jnp.concatenate([mem_key[owners], key_table[owners], own_keys], axis=1)
        values = jnp.concatenate([mem_value[owners], value_table[owners], own_values], axis=1)
        own_valid = (positions[None, :] < lengths[:, None]) | (positions[None, :] >= CLEN - WRITE)
        valid = jnp.concatenate([open_span, own_valid], axis=1)
        queries = query_low[first_row : first_row + per_block * CLEN].reshape(
            per_block, CLEN, width
        )
        return (queries, keys, values, valid, owners)

    attended = []
    saved = []
    block = 0
    queries, keys, values, valid, family = prompt_inputs(block)
    result, logsum = attend_forward(queries, keys, values, valid)
    attended.append(result)
    saved.append(logsum)
    block = 0
    queries, keys, values, valid, owners = follow_inputs(block)
    result, logsum = attend_forward(queries, keys, values, valid)
    attended.append(result)
    saved.append(logsum)
    mixed = jnp.concatenate(attended, axis=0).astype(jnp.bfloat16)
    branch = product(mixed, out_mat) + out_add.astype(jnp.float32)
    first, normed_one, inverse_one = layer_norm(
        all_rows.astype(jnp.float32) + branch, gain_one, shift_one
    )
    first_low = first.astype(jnp.bfloat16)
    inner = product(first_low, up_mat) + up_add.astype(jnp.float32)
    activated = gelu_exact(inner).astype(jnp.bfloat16)
    second = product(activated, down_mat) + down_add.astype(jnp.float32)
    output, normed_two, inverse_two = layer_norm(first + second, gain_two, shift_two)
    output = output.astype(jnp.bfloat16)
    (
        query_mat,
        key_mat,
        value_mat,
        out_mat,
        query_add,
        value_add,
        out_add,
        gain_one,
        shift_one,
        up_mat,
        up_add,
        down_mat,
        down_add,
        gain_two,
        shift_two,
    ) = (
        lax.all_gather(query_weight, ("grp", "shard"), axis=0, tiled=True),
        lax.all_gather(key_weight, ("grp", "shard"), axis=0, tiled=True),
        lax.all_gather(value_weight, ("grp", "shard"), axis=0, tiled=True),
        lax.all_gather(out_weight, ("grp", "shard"), axis=0, tiled=True),
        lax.all_gather(query_bias, ("grp", "shard"), axis=0, tiled=True),
        lax.all_gather(value_bias, ("grp", "shard"), axis=0, tiled=True),
        lax.all_gather(out_bias, ("grp", "shard"), axis=0, tiled=True),
        lax.all_gather(first_gain, ("grp", "shard"), axis=0, tiled=True),
        lax.all_gather(first_shift, ("grp", "shard"), axis=0, tiled=True),
        lax.all_gather(up_weight, ("grp", "shard"), axis=0, tiled=True),
        lax.all_gather(up_bias, ("grp", "shard"), axis=0, tiled=True),
        lax.all_gather(down_weight, ("grp", "shard"), axis=0, tiled=True),
        lax.all_gather(down_bias, ("grp", "shard"), axis=0, tiled=True),
        lax.all_gather(second_gain, ("grp", "shard"), axis=0, tiled=True),
        lax.all_gather(second_shift, ("grp", "shard"), axis=0, tiled=True),
    )
    cotangent = jnp.concatenate([prompt_cotan[0], follow_cotan[0]], axis=0).astype(jnp.float32)
    grad_gain_two = jnp.sum(cotangent * normed_two, axis=0)
    grad_shift_two = jnp.sum(cotangent, axis=0)
    grad_mid = norm_back(cotangent * gain_two.astype(jnp.float32), normed_two, inverse_two)
    grad_down = grad_mid.astype(jnp.bfloat16)
    grad_down_mat = outer_sum(activated, grad_down)
    grad_down_add = column_sum(grad_down)
    grad_inner = (times_back(grad_down, down_mat) * gelu_slope(inner)).astype(jnp.bfloat16)
    grad_up_mat = outer_sum(first_low, grad_inner)
    grad_up_add = column_sum(grad_inner)
    grad_first = grad_mid + times_back(grad_inner, up_mat)
    grad_gain_one = jnp.sum(grad_first * normed_one, axis=0)
    grad_shift_one = jnp.sum(grad_first, axis=0)
    grad_hidden = norm_back(grad_first * gain_one.astype(jnp.float32), normed_one, inverse_one)
    grad_branch = grad_hidden.astype(jnp.bfloat16)
    grad_out_mat = outer_sum(mixed, grad_branch)
    grad_out_add = column_sum(grad_branch)
    grad_mixed = times_back(grad_branch, out_mat).astype(jnp.bfloat16)
    mem_key_acc = jnp.zeros((families, READ, width), jnp.float32)
    mem_value_acc = jnp.zeros((families, READ, width), jnp.float32)
    prompt_key_acc = jnp.zeros((families, PLEN, width), jnp.float32)
    prompt_value_acc = jnp.zeros((families, PLEN, width), jnp.float32)
    block = 0
    queries, keys, values, valid, family = prompt_inputs(block)
    start = block * half_prompt
    grad_query, grad_key, grad_value = attend_backward(
        queries, keys, values, valid, saved[block], grad_mixed[start : start + half_prompt][None]
    )
    query_parts = grad_query
    mem_key_acc = mem_key_acc.at[family].add(grad_key[0, :READ])
    mem_value_acc = mem_value_acc.at[family].add(grad_value[0, :READ])
    prompt_key_acc = prompt_key_acc.at[family].add(grad_key[0, READ:])
    prompt_value_acc = prompt_value_acc.at[family].add(grad_value[0, READ:])
    prompt_query_low = query_parts.astype(jnp.bfloat16)
    block = 0
    queries, keys, values, valid, owners = follow_inputs(block)
    first_row = p_count + block * per_block * CLEN
    grad_slice = grad_mixed[first_row : first_row + per_block * CLEN].reshape(
        per_block, CLEN, width
    )
    grad_query, grad_key, grad_value = attend_backward(
        queries, keys, values, valid, saved[prompt_blocks + block], grad_slice
    )
    mem_key_acc = mem_key_acc.at[owners].add(grad_key[:, :READ])
    mem_value_acc = mem_value_acc.at[owners].add(grad_value[:, :READ])
    prompt_key_acc = prompt_key_acc.at[owners].add(grad_key[:, READ : READ + PLEN])
    prompt_value_acc = prompt_value_acc.at[owners].add(grad_value[:, READ : READ + PLEN])
    own_key_parts = grad_key[:, READ + PLEN :].reshape(-1, width)
    own_value_parts = grad_value[:, READ + PLEN :].reshape(-1, width)
    prompt_key_grad, prompt_value_grad = (
        lax.psum_scatter(
            prompt_key_acc.reshape(families * PLEN, width).astype(jnp.bfloat16),
            "shard",
            scatter_dimension=0,
            tiled=True,
        ).astype(jnp.float32),
        lax.psum_scatter(
            prompt_value_acc.reshape(families * PLEN, width).astype(jnp.bfloat16),
            "shard",
            scatter_dimension=0,
            tiled=True,
        ).astype(jnp.float32),
    )
    follow_query_low = grad_query.astype(jnp.bfloat16)
    follow_key_low = own_key_parts.astype(jnp.bfloat16)
    follow_value_low = own_value_parts.astype(jnp.bfloat16)
    mem_key_sum, mem_value_sum = (
        lax.psum(mem_key_acc.astype(jnp.bfloat16), "shard").astype(jnp.float32),
        lax.psum(mem_value_acc.astype(jnp.bfloat16), "shard").astype(jnp.float32),
    )
    grad_query_low = jnp.concatenate([prompt_query_low, follow_query_low], axis=0)
    grad_key_low = jnp.concatenate([prompt_key_grad.astype(jnp.bfloat16), follow_key_low], axis=0)
    grad_value_low = jnp.concatenate(
        [prompt_value_grad.astype(jnp.bfloat16), follow_value_low], axis=0
    )
    mem_key_low = mem_key_sum.astype(jnp.bfloat16).reshape(families * READ, width)
    mem_value_low = mem_value_sum.astype(jnp.bfloat16).reshape(families * READ, width)
    grad_rows_all = (
        grad_hidden
        + times_back(grad_query_low, query_mat)
        + times_back(grad_key_low, key_mat)
        + times_back(grad_value_low, value_mat)
    ).astype(jnp.bfloat16)
    grad_memory = (
        (times_back(mem_key_low, key_mat) + times_back(mem_value_low, value_mat))
        .astype(jnp.bfloat16)
        .reshape(1, families, READ, width)
    )
    leader = (shard_index == 0).astype(jnp.float32)
    grad_query_mat = outer_sum(all_rows, grad_query_low)
    grad_query_add = column_sum(grad_query_low)
    grad_key_mat = outer_sum(all_rows, grad_key_low) + leader * outer_sum(memory_flat, mem_key_low)
    grad_value_mat = outer_sum(all_rows, grad_value_low) + leader * outer_sum(
        memory_flat, mem_value_low
    )
    grad_value_add = column_sum(grad_value_low) + leader * column_sum(mem_value_low)
    pieces = (
        lax.psum_scatter(
            grad_query_mat.astype(jnp.bfloat16), "shard", scatter_dimension=0, tiled=True
        ).astype(jnp.float32),
        lax.psum_scatter(
            grad_key_mat.astype(jnp.bfloat16), "shard", scatter_dimension=0, tiled=True
        ).astype(jnp.float32),
        lax.psum_scatter(
            grad_value_mat.astype(jnp.bfloat16), "shard", scatter_dimension=0, tiled=True
        ).astype(jnp.float32),
        lax.psum_scatter(
            grad_out_mat.astype(jnp.bfloat16), "shard", scatter_dimension=0, tiled=True
        ).astype(jnp.float32),
        lax.psum_scatter(
            grad_query_add.astype(jnp.bfloat16), "shard", scatter_dimension=0, tiled=True
        ).astype(jnp.float32),
        lax.psum_scatter(
            grad_value_add.astype(jnp.bfloat16), "shard", scatter_dimension=0, tiled=True
        ).astype(jnp.float32),
        lax.psum_scatter(
            grad_out_add.astype(jnp.bfloat16), "shard", scatter_dimension=0, tiled=True
        ).astype(jnp.float32),
        lax.psum_scatter(
            grad_gain_one.astype(jnp.bfloat16), "shard", scatter_dimension=0, tiled=True
        ).astype(jnp.float32),
        lax.psum_scatter(
            grad_shift_one.astype(jnp.bfloat16), "shard", scatter_dimension=0, tiled=True
        ).astype(jnp.float32),
        lax.psum_scatter(
            grad_up_mat.astype(jnp.bfloat16), "shard", scatter_dimension=0, tiled=True
        ).astype(jnp.float32),
        lax.psum_scatter(
            grad_up_add.astype(jnp.bfloat16), "shard", scatter_dimension=0, tiled=True
        ).astype(jnp.float32),
        lax.psum_scatter(
            grad_down_mat.astype(jnp.bfloat16), "shard", scatter_dimension=0, tiled=True
        ).astype(jnp.float32),
        lax.psum_scatter(
            grad_down_add.astype(jnp.bfloat16), "shard", scatter_dimension=0, tiled=True
        ).astype(jnp.float32),
        lax.psum_scatter(
            grad_gain_two.astype(jnp.bfloat16), "shard", scatter_dimension=0, tiled=True
        ).astype(jnp.float32),
        lax.psum_scatter(
            grad_shift_two.astype(jnp.bfloat16), "shard", scatter_dimension=0, tiled=True
        ).astype(jnp.float32),
    )
    summed = (
        lax.psum(pieces[0].astype(jnp.bfloat16), "grp").astype(jnp.float32),
        lax.psum(pieces[1].astype(jnp.bfloat16), "grp").astype(jnp.float32),
        lax.psum(pieces[2].astype(jnp.bfloat16), "grp").astype(jnp.float32),
        lax.psum(pieces[3].astype(jnp.bfloat16), "grp").astype(jnp.float32),
        lax.psum(pieces[4].astype(jnp.bfloat16), "grp").astype(jnp.float32),
        lax.psum(pieces[5].astype(jnp.bfloat16), "grp").astype(jnp.float32),
        lax.psum(pieces[6].astype(jnp.bfloat16), "grp").astype(jnp.float32),
        lax.psum(pieces[7].astype(jnp.bfloat16), "grp").astype(jnp.float32),
        lax.psum(pieces[8].astype(jnp.bfloat16), "grp").astype(jnp.float32),
        lax.psum(pieces[9].astype(jnp.bfloat16), "grp").astype(jnp.float32),
        lax.psum(pieces[10].astype(jnp.bfloat16), "grp").astype(jnp.float32),
        lax.psum(pieces[11].astype(jnp.bfloat16), "grp").astype(jnp.float32),
        lax.psum(pieces[12].astype(jnp.bfloat16), "grp").astype(jnp.float32),
        lax.psum(pieces[13].astype(jnp.bfloat16), "grp").astype(jnp.float32),
        lax.psum(pieces[14].astype(jnp.bfloat16), "grp").astype(jnp.float32),
    )
    return (
        output[:p_count][None],
        output[p_count:][None],
        grad_rows_all[:p_count][None],
        grad_rows_all[p_count:][None],
        grad_memory,
        summed[0],
        summed[1],
        summed[2],
        summed[3],
        summed[4],
        summed[5],
        summed[6],
        summed[7],
        summed[8],
        summed[9],
        summed[10],
        summed[11],
        summed[12],
        summed[13],
        summed[14],
    )


MEM = 16
HALF = PLEN // 2
OWN = 512
CONT = HALF + HALF + MEM
KEYS = CONT + OWN
QROWS = HALF + OWN
PAIRS = HEADS // 2
NAMES = ("grp", "shard")


def pairs_fit(mesh):
    return mesh.shape["shard"] == 4 and mesh.shape["grp"] == 8


def head_mask(head):
    lane = lax.broadcasted_iota(jnp.int32, (1, 2 * HEAD), 1)
    return lane // HEAD == head


def pick(mask, values):
    return jnp.where(mask, values.astype(jnp.float32), 0.0).astype(jnp.bfloat16)


def flip(values):
    return values.astype(jnp.float32).T.astype(jnp.bfloat16)


def own_scores(keys, queries):
    parts = []
    for cont in range(OWN // CLEN):
        part = slice(cont * CLEN, (cont + 1) * CLEN)
        parts.append(times_back(keys[part], queries[part]))
    return jnp.concatenate(parts, axis=1)


def attend_pair(query_ref, key_ref, value_ref, bias_ref, out_ref, log_ref):
    mem_valid = lax.broadcasted_iota(jnp.int32, (MEM, 1), 0) < READ
    value_flip = flip(value_ref[...])
    results = []
    for head in range(2):
        mask = head_mask(head)
        queries = pick(mask, query_ref[...])
        main = times_back(key_ref[: 2 * HALF], queries)
        memory = jnp.where(mem_valid, times_back(key_ref[2 * HALF : CONT], queries), NEGATIVE)
        own = own_scores(key_ref[CONT:], queries[HALF:]) + bias_ref[...]
        top = jnp.maximum(
            jnp.max(main, axis=0, keepdims=True), jnp.max(memory, axis=0, keepdims=True)
        )
        top_own = jnp.maximum(top[:, HALF:], jnp.max(own, axis=0, keepdims=True))
        top = jnp.concatenate([top[:, :HALF], top_own], axis=1)
        main = jnp.exp(main - top)
        memory = jnp.exp(memory - top)
        own = jnp.exp(own - top_own)
        total = jnp.sum(main, axis=0, keepdims=True) + jnp.sum(memory, axis=0, keepdims=True)
        total = jnp.concatenate(
            [total[:, :HALF], total[:, HALF:] + jnp.sum(own, axis=0, keepdims=True)], axis=1
        )
        flipped = value_flip[head * HEAD : (head + 1) * HEAD]
        result = product(flipped[:, : 2 * HALF], main.astype(jnp.bfloat16))
        result += product(flipped[:, 2 * HALF : CONT], memory.astype(jnp.bfloat16))
        own = own.astype(jnp.bfloat16)
        own_parts = []
        for cont in range(OWN // CLEN):
            own_parts.append(
                product(
                    flipped[:, CONT + cont * CLEN : CONT + (cont + 1) * CLEN],
                    own[:, cont * CLEN : (cont + 1) * CLEN],
                )
            )
        result = jnp.concatenate(
            [result[:, :HALF], result[:, HALF:] + jnp.concatenate(own_parts, axis=1)], axis=1
        )
        results.append(result / total)
        log_ref[head : head + 1] = top + jnp.log(total)
    out_ref[...] = jnp.concatenate(results, axis=0).T.astype(jnp.bfloat16)


MESH = pl.DeviceIdType.MESH
WHERE = pl.BlockSpec(memory_space=pl.ANY)
INSIDE = pl.BlockSpec(memory_space=pltpu.VMEM)
VECTORS = 16


def seat():
    grp = lax.axis_index("grp")
    return (grp // 2, grp % 2, lax.axis_index("shard"))


def unit_of(z, core, shard):
    return (z * 2 + core) * 4 + shard


def device_of(z, core, shard):
    return (z * 2 + core, shard)


def greet():
    z, core, shard = seat()
    barrier = pltpu.get_barrier_semaphore()
    others = [device_of((z + step) % 4, core, shard) for step in (1, 2, 3)]
    others += [
        device_of(z, core, shard ^ 1),
        device_of(z, core, shard ^ 2),
        device_of(z, 1 - core, shard),
    ]
    for other in others:
        pl.semaphore_signal(barrier, inc=1, device_id=other, device_id_type=MESH)
    pl.semaphore_wait(barrier, len(others))


class Gather:
    def __init__(self, mine, full, send, recv, by_y=(0, 2)):
        self.mine, self.full, self.send, self.recv = mine, full, send, recv
        self.share = mine.shape[0]
        self.by_y = by_y
        self.z, self.core, self.shard = seat()
        self.sent = 0

    def rows(self, unit):
        return self.full.at[pl.ds(pl.multiple_of(unit * self.share, 8), self.share)]

    def link(self, index, unit, z, core, shard, source=None):
        return pltpu.make_async_remote_copy(
            src_ref=self.rows(unit) if source is None else source,
            dst_ref=self.rows(unit),
            send_sem=self.send.at[index],
            recv_sem=self.recv.at[unit],
            device_id=device_of(z, core, shard),
            device_id_type=MESH,
        )

    def push(self, unit, z, core, shard, source=None):
        self.link(self.sent, unit, z, core, shard, source).start()
        self.sent += 1

    def arrive(self, unit):
        self.link(0, unit, self.z, 1 - self.core, self.shard).wait_recv()

    def start_line(self):
        me = unit_of(self.z, self.core, self.shard)
        for step in (1, 2, 3):
            self.push(me, (self.z + step) % 4, self.core, self.shard, self.mine)

    def start_plane(self):
        z, core, shard = self.z, self.core, self.shard
        me = unit_of(z, core, shard)
        self.push(me, z, core, shard ^ 1, self.mine)
        self.push(me, z, core, shard ^ 2, self.mine)
        self.push(me, z, 1 - core, shard, self.mine)

    def own(self, semaphore):
        return pltpu.make_async_copy(
            self.mine, self.rows(unit_of(self.z, self.core, self.shard)), semaphore
        )

    def column(self, step):
        z, core, shard = self.z, self.core, self.shard
        unit = unit_of((z + step) % 4, core, shard)
        self.arrive(unit)
        self.push(unit, z, core, shard ^ 1)
        self.push(unit, z, core, shard ^ 2)
        self.push(unit, z, 1 - core, shard)

    def side(self, step):
        z, core, shard = self.z, self.core, self.shard
        for hop in (1, 2):
            unit = unit_of((z + step) % 4, core, shard ^ hop)
            self.arrive(unit)
            if (step in self.by_y) == (hop == 1):
                self.push(unit, z, core, shard ^ (3 - hop))
            self.push(unit, z, 1 - core, shard)

    def corner(self, step):
        z, core, shard = self.z, self.core, self.shard
        unit = unit_of((z + step) % 4, core, shard ^ 3)
        self.arrive(unit)
        self.push(unit, z, 1 - core, shard)

    def sibling(self):
        def wait(index, carry):
            unit = (index // 4) * 8 + (1 - self.core) * 4 + index % 4
            self.arrive(unit)
            return carry

        lax.fori_loop(0, 16, wait, 0)

    def finish(self):
        def wait(index, carry):
            pltpu.make_async_remote_copy(
                src_ref=self.mine,
                dst_ref=self.mine,
                send_sem=self.send.at[index],
                recv_sem=self.recv.at[0],
                device_id=device_of(self.z, 1 - self.core, self.shard),
                device_id_type=MESH,
            ).wait_send()
            return carry

        lax.fori_loop(0, self.sent, wait, 0)


class PlaneGather(Gather):
    def start_plane(self):
        z, core, shard = self.z, self.core, self.shard
        me = unit_of(z, core, shard)
        self.link(96, me, z, core, shard ^ 1, self.mine).start()
        self.link(97, me, z, core, shard ^ 2, self.mine).start()
        self.link(me, me, z, 1 - core, shard, self.mine).start()

    def along(self, unit, z_of, source=None):
        z, core, shard = self.z, self.core, self.shard

        @pl.when((z_of <= z) & (z < 3))
        def _():
            self.link(32 + unit, unit, z + 1, core, shard, source).start()

        @pl.when((z_of >= z) & (z > 0))
        def _():
            self.link(64 + unit, unit, z - 1, core, shard, source).start()

    def start_line(self):
        me = unit_of(self.z, self.core, self.shard)
        self.along(me, self.z, self.mine)

    def plane(self):
        z, core, shard = self.z, self.core, self.shard
        over_x = unit_of(z, core, shard ^ 1)
        over_y = unit_of(z, core, shard ^ 2)
        self.arrive(over_x)

        @pl.when(core == 0)
        def _():
            self.link(98, over_x, z, core, shard ^ 2).start()

        self.link(over_x, over_x, z, 1 - core, shard).start()
        self.along(over_x, z)
        self.arrive(over_y)

        @pl.when(core == 1)
        def _():
            self.link(98, over_y, z, core, shard ^ 1).start()

        self.link(over_y, over_y, z, 1 - core, shard).start()
        self.along(over_y, z)

    def corners(self):
        z, core, shard = self.z, self.core, self.shard
        unit = unit_of(z, core, shard ^ 3)
        self.arrive(unit)
        self.link(unit, unit, z, 1 - core, shard).start()
        self.along(unit, z)

    def far(self, distance, other):
        z, core, shard = self.z, self.core, self.shard
        for sign in (-1, 1):
            plane = z + sign * distance

            @pl.when((plane >= 0) & (plane < 4))
            def _():
                unit = unit_of(plane, core, shard ^ other)
                self.arrive(unit)
                self.link(unit, unit, z, 1 - core, shard).start()
                self.along(unit, plane)

    def finish(self):
        z, core, shard = self.z, self.core, self.shard

        def done(index, unit):
            self.link(index, unit, z, 1 - core, shard, self.mine).wait_send()

        for index in (96, 97, 98):
            done(index, 0)

        def wait(index, carry):
            plane = index // 4
            unit = plane * 8 + core * 4 + index % 4
            done(unit, unit)

            @pl.when((plane <= z) & (z < 3))
            def _():
                done(32 + unit, unit)

            @pl.when((plane >= z) & (z > 0))
            def _():
                done(64 + unit, unit)

            return carry

        lax.fori_loop(0, 16, wait, 0)


class Swap:
    def __init__(self, source, target, send, recv, z, core, shard):
        self.copy = pltpu.make_async_remote_copy(
            src_ref=source, dst_ref=target, send_sem=send, recv_sem=recv,
            device_id=device_of(z, core, shard), device_id_type=MESH,
        )

    def start(self):
        self.copy.start()

    def arrive(self):
        self.copy.wait_recv()

    def finish(self):
        self.copy.wait_send()


def spread_vector(vectors, index, width):
    narrow, broad = width // 32, 4 * width // 32
    row = lax.broadcasted_iota(jnp.int32, (32 * VECTORS, width), 0)
    lane = lax.broadcasted_iota(jnp.int32, (32 * VECTORS, width), 1)
    small = index < 8
    start = jnp.where(small, index, 8 + VECTORS * 8 * (index - 8))
    block = jnp.where(small, lane // narrow, lane // broad)
    select = jnp.where(row == VECTORS * block + start, 1.0, 0.0).astype(jnp.bfloat16)
    table = outer_sum(vectors, select)
    piece = lax.broadcasted_iota(jnp.int32, table.shape, 0)
    lane = lax.broadcasted_iota(jnp.int32, table.shape, 1)
    offset = jnp.where(small, lane % narrow, lane % broad)
    return jnp.sum(jnp.where(piece == offset, table, 0.0), axis=0, keepdims=True)


TILE = 512
PARTNERS = 4


def front_kernel(
    qkv_ref, wide_ref, down_ref, vec_ref, prompt_ref, kept_ref, sent_ref, mem_ref,
    prompt_cot, kept_cot, sent_cot, bias_ref,
    qkv_full, wide_full, down_full, vec_full, rows_out,
    out_ref, act_ref, first_ref, gdown_ref, ginner_ref, gbranch_ref, gmixed_ref, ghidden_ref,
    mixed_ref, log_ref, query_out, key_out, value_out, sums_ref,
    rows, weights, vectors, table, query, key, value, mixed, cotan, wide, down,
    act, slope, normed, first, total, hidden, small_low,
    send_a, recv_a, send_b, recv_b, send_c, recv_c, send_d, recv_d, swap_send, swap_recv, local,
    store,
):
    pair = pl.program_id(0)
    width = prompt_ref.shape[1]
    low = jnp.bfloat16
    one = Gather(qkv_ref, qkv_full, send_a, recv_a, (0, 1, 2))
    small = Gather(vec_ref, vec_full, send_d, recv_d)
    two = Gather(wide_ref, wide_full, send_b, recv_b)
    three = PlaneGather(down_ref, down_full, send_c, recv_c)
    z, core, shard = seat()
    step_rows = HALF // PARTNERS
    partner = [
        Swap(
            prompt_ref.at[pl.ds(index * step_rows, step_rows)],
            rows.at[pl.ds(HALF + index * step_rows, step_rows)],
            swap_send.at[index], swap_recv.at[index], z, core, shard ^ 1,
        )
        for index in range(PARTNERS)
    ]
    taken = Swap(
        sent_ref, rows.at[pl.ds(CONT + OWN // 2, OWN // 2)],
        swap_send.at[PARTNERS], swap_recv.at[PARTNERS], z, core, shard ^ 2,
    )
    taken_cot = Swap(
        sent_cot, cotan.at[pl.ds(HALF + OWN // 2, OWN // 2)],
        swap_send.at[PARTNERS + 1], swap_recv.at[PARTNERS + 1], z, core, shard ^ 2,
    )
    swaps = partner + [taken, taken_cot]
    own = [gather.own(local.at[index]) for index, gather in enumerate((one, small, two, three))]
    own += [
        pltpu.make_async_copy(prompt_ref, rows.at[pl.ds(0, HALF)], local.at[4]),
        pltpu.make_async_copy(mem_ref, rows.at[pl.ds(2 * HALF, MEM)], local.at[5]),
        pltpu.make_async_copy(kept_ref, rows.at[pl.ds(CONT, OWN // 2)], local.at[6]),
        pltpu.make_async_copy(prompt_cot, cotan.at[pl.ds(0, HALF)], local.at[7]),
        pltpu.make_async_copy(kept_cot, cotan.at[pl.ds(HALF, OWN // 2)], local.at[8]),
    ]
    load_weights = pltpu.make_async_copy(qkv_full, weights, local.at[9])
    load_vectors = pltpu.make_async_copy(vec_full, vectors, local.at[10])
    store_rows = pltpu.make_async_copy(rows, rows_out, local.at[11])
    load_wide = pltpu.make_async_copy(wide_full, wide, local.at[12])
    load_down = pltpu.make_async_copy(down_full, down, local.at[13])

    def project(start, query_start, count, queries):
        span = pl.ds(start, count)
        block = rows[span]
        if queries:
            result = (product(block, weights[:, :width]) + table[0:1]).astype(low)
            result = (result.astype(jnp.float32) * SCALE).astype(low)
            query[pl.ds(query_start, count)] = result
        key[span] = product(block, weights[:, width : 2 * width]).astype(low)
        value[span] = (product(block, weights[:, 2 * width :]) + table[1:2]).astype(low)

    @pl.when(pair == 0)
    def _():
        for copy in own[4:]:
            copy.start()
        greet()
        one.start_line()
        small.start_line()
        one.start_plane()
        small.start_plane()
        partner[0].start()
        two.start_line()
        three.start_line()
        for copy in own[:4]:
            copy.start()
        for step in (1, 2, 3):
            small.column(step)
            one.column(step)
        for index in range(1, PARTNERS):
            partner[index].start()
        taken.start()
        for step in range(4):
            small.side(step)
            one.side(step)
        three.start_plane()
        two.start_plane()
        for step in range(4):
            small.corner(step)
        small.sibling()
        own[1].wait()
        load_vectors.start()
        load_vectors.wait()

        def spread(index, carry):
            table[pl.ds(index, 1)] = spread_vector(vectors[...], index, width)
            return carry

        lax.fori_loop(0, 12, spread, 0)
        for step in range(4):
            one.corner(step)
        for step in (1, 2, 3):
            two.column(step)
        one.sibling()
        for index in (0, 2, 3, 4, 5, 6):
            own[index].wait()
        load_weights.start()
        load_weights.wait()
        project(0, 0, HALF, True)
        three.plane()
        taken.arrive()
        project(CONT, HALF, OWN, True)
        three.corners()
        taken_cot.start()
        for swap in partner:
            swap.arrive()
        project(HALF, 0, HALF + MEM, False)
        store_rows.start()

    def later(when, *actions):
        @pl.when(pair == when)
        def _():
            for action in actions:
                action[0](*action[1:])

    later(1, (two.side, 0), (three.far, 1, 0))
    later(2, (two.side, 1), (three.far, 1, 1), (three.far, 1, 2))
    later(3, (two.side, 2), (three.far, 1, 3), (three.far, 2, 0))
    later(4, (two.side, 3), (two.corner, 0), (three.far, 2, 1))
    later(5, (two.corner, 1), (two.corner, 2), (three.far, 2, 2))

    lanes = pl.ds(pl.multiple_of(pair * (2 * HEAD), 2 * HEAD), 2 * HEAD)
    query_out[...] = query[:, lanes]
    key_out[...] = key[:, lanes]
    value_out[...] = value[:, lanes]
    attend_pair(query_out, key_out, value_out, bias_ref, mixed_ref, log_ref)
    mixed[:, lanes] = mixed_ref[...]

    def fine(index):
        return table[index : index + 1]

    def save(tile, index):
        span = pl.ds(pl.multiple_of(tile * TILE, TILE), TILE)
        source, target = (
            (act, act_ref), (slope, ginner_ref), (hidden, ghidden_ref),
            (small_low.at[0], out_ref), (small_low.at[1], first_ref), (small_low.at[2], gdown_ref),
            (small_low.at[3], gbranch_ref), (small_low.at[4], gmixed_ref),
        )[index]
        return pltpu.make_async_copy(source, target.at[span], store.at[index])

    def up_chunk(step):
        return pl.ds(pl.multiple_of(step * width, 128), width)

    def up_columns(step):
        return pl.ds(pl.multiple_of((step + 1) * width, 128), width)

    def add_sum(index, values):
        sums_ref[pl.ds(index, 1)] += jnp.sum(values, axis=0, keepdims=True)

    def start_tile(tile):
        span = pl.ds(pl.multiple_of(tile * TILE, TILE), TILE)
        held = rows[pl.ds(pl.multiple_of(tile * CONT, MEM), TILE)].astype(jnp.float32)
        held = held + (product(mixed[span], wide[:, :width]) + fine(2))
        result, value_n, value_r = layer_norm(held, fine(3), fine(4))

        @pl.when(tile == 1)
        def _():
            for index in range(1, 8):
                save(0, index).wait()

        normed[...] = value_n
        first[...] = result
        small_low[1] = result.astype(low)
        return value_r

    def forward_chunk(step, carry):
        chunk = up_chunk(step)
        inner = product(small_low[1], wide[:, up_columns(step)]) + table[pl.ds(8 + step, 1)]
        half = 0.5 * (1.0 + lax.erf(inner * ROOT_HALF))
        active = (inner * half).astype(low)
        act[:, chunk] = active
        slope[:, chunk] = (half + inner * jnp.exp(-0.5 * inner * inner) * ROOT_GAUSS).astype(low)
        total[...] += product(active, down[chunk])
        return carry

    def backward_chunk(step, carry):
        chunk = up_chunk(step)
        grad = times_back(small_low[2], down[chunk]) * slope[:, chunk].astype(jnp.float32)
        grad = grad.astype(low)
        slope[:, chunk] = grad
        add_sum(8 + step, grad.astype(jnp.float32))
        total[...] += times_back(grad, wide[:, up_columns(step)])
        return carry

    def tile_body(tile, carry):
        span = pl.ds(pl.multiple_of(tile * TILE, TILE), TILE)
        inverse_one = start_tile(tile)
        total[...] = jnp.zeros_like(total)

        @pl.when(tile == 1)
        def _():
            save(0, 0).wait()

        lax.fori_loop(0, 4, forward_chunk, 0)
        save(tile, 0).start()
        result, value_n, inverse_two = layer_norm(
            first[...] + (total[...] + fine(5)), fine(6), fine(7)
        )
        small_low[0] = result.astype(low)
        save(tile, 3).start()
        save(tile, 4).start()
        cot = cotan[span].astype(jnp.float32)
        add_sum(6, cot * value_n)
        add_sum(7, cot)
        grad_mid = norm_back(cot * fine(6), value_n, inverse_two)
        grad_low = grad_mid.astype(low)
        small_low[2] = grad_low
        save(tile, 5).start()
        add_sum(5, grad_low.astype(jnp.float32))
        total[...] = grad_mid
        lax.fori_loop(0, 4, backward_chunk, 0)
        save(tile, 1).start()
        grad_first = total[...]
        add_sum(3, grad_first * normed[...])
        add_sum(4, grad_first)
        grad_hidden = norm_back(grad_first * fine(3), normed[...], inverse_one)
        hidden[...] = grad_hidden
        save(tile, 2).start()
        grad_low = grad_hidden.astype(low)
        small_low[3] = grad_low
        save(tile, 6).start()
        add_sum(2, grad_low.astype(jnp.float32))
        small_low[4] = times_back(grad_low, wide[:, :width]).astype(low)
        save(tile, 7).start()
        return carry

    @pl.when(pair == PAIRS - 1)
    def _():
        two.corner(3)
        two.sibling()
        load_wide.start()
        for step in (3,):
            three.far(2, step)
        for other in range(4):
            three.far(3, other)
        three.sibling()
        load_down.start()
        own[7].wait()
        own[8].wait()
        taken_cot.arrive()
        sums_ref[...] = jnp.zeros_like(sums_ref)
        load_wide.wait()
        load_down.wait()
        lax.fori_loop(0, 2, tile_body, 0)
        store_rows.wait()
        for index in range(8):
            save(1, index).wait()
        for sender in (one, small, two, three, *swaps):
            sender.finish()


def front(
    qkv, wide_share, down_share, vec, prompt, kept, sent, memory, prompt_cot, kept_cot, sent_cot,
    bias,
):
    width = prompt.shape[1]
    low = jnp.bfloat16
    wide = jnp.float32
    shape = jax.ShapeDtypeStruct

    def block(rows):
        return pl.BlockSpec((rows, 2 * HEAD), lambda pair: (0, pair))

    def full(share):
        return shape((32 * share.shape[0], share.shape[1]), low)

    dma = pltpu.SemaphoreType.DMA
    memory_space = pltpu.VMEM
    return pl.pallas_call(
        front_kernel,
        grid=(PAIRS,),
        in_specs=[INSIDE] * 4
        + [WHERE] * 7
        + [pl.BlockSpec((CLEN, OWN), lambda pair: (0, 0))],
        out_specs=[WHERE] * 13
        + [
            block(QROWS), pl.BlockSpec((None, 2, QROWS), lambda pair: (pair, 0, 0)),
            block(QROWS), block(KEYS), block(KEYS),
            pl.BlockSpec((VECTORS, width), lambda pair: (0, 0)),
        ],
        out_shape=[
            full(qkv), full(wide_share), full(down_share), full(vec),
            shape((KEYS, width), low),
            shape((QROWS, width), low),
            shape((QROWS, 4 * width), low),
            shape((QROWS, width), low),
            shape((QROWS, width), low),
            shape((QROWS, 4 * width), low),
            shape((QROWS, width), low),
            shape((QROWS, width), low),
            shape((QROWS, width), wide),
            shape((QROWS, width), low),
            shape((PAIRS, 2, QROWS), wide),
            shape((QROWS, width), low),
            shape((KEYS, width), low),
            shape((KEYS, width), low),
            shape((VECTORS, width), wide),
        ],
        scratch_shapes=[
            memory_space((KEYS, width), low),
            memory_space((width, 3 * width), low),
            memory_space((32 * VECTORS, 2 * HEAD), low),
            memory_space((VECTORS, width), wide),
            memory_space((QROWS, width), low),
            memory_space((KEYS, width), low),
            memory_space((KEYS, width), low),
            memory_space((QROWS, width), low),
            memory_space((QROWS, width), low),
            memory_space((width, 5 * width), low),
            memory_space((4 * width, width), low),
            memory_space((TILE, 4 * width), low),
            memory_space((TILE, 4 * width), low),
            memory_space((TILE, width), wide),
            memory_space((TILE, width), wide),
            memory_space((TILE, width), wide),
            memory_space((TILE, width), wide),
            memory_space((5, TILE, width), low),
        ]
        + [dma((32,))] * 4
        + [dma((100,)), dma((32,)), dma((32,)), dma((32,))]
        + [dma((PARTNERS + 2,)), dma((PARTNERS + 2,)), dma((14,)), dma((8,))],
        compiler_params=pltpu.CompilerParams(
            vmem_limit_bytes=67043328, collective_id=0, has_side_effects=True
        ),
        name="front",
    )(
        qkv, wide_share, down_share, vec, prompt, kept, sent, memory, prompt_cot, kept_cot,
        sent_cot, bias,
    )


SEND = 13
SLOTS = {
    0: (("plane", 0), ("chip", 2),),
    1: (("chip", 3),),
    2: (("plane", 1), ("chip", 4),),
    3: (("line", 0),),
    6: (("plane", 2),),
    7: (("middle", 0),),
    8: (("plane", 3), ("chip", 5),),
    9: (("line", 1),),
    11: (("spread", 0), ("plane", 4),),
    12: (("line", 2),),
    13: (("middle", 1), ("line", 3),),
    15: (("share", 0), ("middle", 2), ("line", 4), ("plane", 5),),
    16: (("spread", 1), ("chip", 6),),
    17: (("line", 5),),
    18: (("middle", 3),),
    19: (("spread", 2), ("middle", 4), ("plane", 6),),
    20: (("share", 1), ("middle", 5),),
    21: (("line", 6),),
    22: (("spread", 3),),
    23: (("share", 2), ("spread", 4), ("middle", 6),),
}
TAIL = {
    0: (("spread", 5),),
    1: (("plane", 7), ("partner", 1), ("partner", 2), ("partner", 3), ("share", 3), ("share", 4), ("spread", 6), ("small", 0),),
    2: (("small", 1),),
    3: (("share", 5), ("small", 2), ("line", 7), ("share", 6), ("middle", 7),),
    4: (("small", 3),),
    5: (("spread", 7),),
}
LAST = (("small", 4), ("share", 7),)
WIDE = 4
NARROW = 4


class Reduce:
    def __init__(self, mine, theirs, got, from_x, from_y, last_x, last_y, outer, total, send, recv):
        self.mine, self.theirs, self.got = mine, theirs, got
        self.from_x, self.from_y, self.last_x, self.last_y = from_x, from_y, last_x, last_y
        self.outer, self.total, self.send, self.recv = outer, total, send, recv
        self.half = mine.shape[1] // 2
        self.z, self.core, self.shard = seat()
        self.inner = (self.z == 1) | (self.z == 2)

    def copy(self, source, target, index, z, core, shard):
        return pltpu.make_async_remote_copy(
            src_ref=source, dst_ref=target, send_sem=self.send.at[index],
            recv_sem=self.recv.at[index], device_id=device_of(z, core, shard), device_id_type=MESH,
        )

    def upper(self, part):
        return self.mine.at[part, pl.ds(0, self.half)]

    def lower(self, part):
        return self.mine.at[part, pl.ds(self.half, self.half)]

    def link(self, index):
        z, core, shard = self.z, self.core, self.shard
        near = jnp.where(z < 2, 1 - z, 5 - z)
        if index < 4:
            ends = (self.theirs.at[index], self.got.at[index], z, 1 - core, shard)
        elif index < 6:
            source = self.upper(shard ^ (1 if index == 4 else 3))
            ends = (source, self.from_x.at[index - 4], z, core, shard ^ 1)
        elif index < 8:
            source = self.lower(shard ^ (2 if index == 6 else 3))
            ends = (source, self.from_y.at[index - 6], z, core, shard ^ 2)
        elif index == 8:
            ends = (self.upper(shard ^ 2), self.last_y, z, core, shard ^ 2)
        elif index == 9:
            ends = (self.lower(shard ^ 1), self.last_x, z, core, shard ^ 1)
        elif index == 10:
            ends = (self.mine.at[shard], self.outer, near, core, shard)
        elif index == 11:
            ends = (self.mine.at[shard], self.total, 3 - z, core, shard)
        else:
            ends = (self.total, self.total, near, core, shard)
        return self.copy(ends[0], ends[1], index, *ends[2:])

    def give(self, part):
        self.copy(
            self.theirs.at[part], self.got.at[part], part, self.z, 1 - self.core, self.shard
        ).start()

    def given(self):
        for part in range(4):
            self.link(part).wait_send()

    def add(self, part, start, count, other):
        def step(index, carry):
            rows = pl.ds(pl.multiple_of(index * 48, 16), 48)
            span = pl.ds(pl.multiple_of(start + index * 48, 16), 48)
            total = self.mine[part, span].astype(jnp.float32) + other[rows].astype(jnp.float32)
            self.mine[part, span] = total.astype(jnp.bfloat16)
            return carry

        lax.fori_loop(0, count // 48, step, 0)

    def chip(self):
        for part in range(4):
            self.link(part).wait_recv()

        def add_part(part, carry):
            self.add(part, 0, 2 * self.half, self.got.at[part])
            return carry

        lax.fori_loop(0, 4, add_part, 0)
        for index in (4, 5, 6, 7):
            self.link(index).start()

    def plane(self):
        shard = self.shard
        self.link(4).wait_recv()
        self.link(5).wait_recv()
        self.add(shard ^ 2, 0, self.half, self.from_x.at[1])
        self.link(8).start()
        self.link(6).wait_recv()
        self.link(7).wait_recv()
        self.add(shard ^ 1, self.half, self.half, self.from_y.at[1])
        self.link(9).start()
        self.add(shard, 0, self.half, self.from_x.at[0])
        self.add(shard, self.half, self.half, self.from_y.at[0])

    def line(self):
        self.link(8).wait_recv()
        self.add(self.shard, 0, self.half, self.last_y)
        self.link(9).wait_recv()
        self.add(self.shard, self.half, self.half, self.last_x)

        @pl.when(jnp.logical_not(self.inner))
        def _():
            self.link(10).start()

    def middle(self):
        @pl.when(self.inner)
        def _():
            self.link(10).wait_recv()
            self.add(self.shard, 0, 2 * self.half, self.outer)
            self.link(11).start()

    def spread(self):
        @pl.when(self.inner)
        def _():
            self.link(11).wait_recv()

            def step(index, carry):
                rows = pl.ds(pl.multiple_of(index * 48, 16), 48)
                total = self.total[rows].astype(jnp.float32)
                total = total + self.mine[self.shard, rows].astype(jnp.float32)
                self.total[rows] = total.astype(jnp.bfloat16)
                return carry

            lax.fori_loop(0, 2 * self.half // 48, step, 0)
            self.link(12).start()

    def share(self, place, semaphore):
        @pl.when(jnp.logical_not(self.inner))
        def _():
            self.link(12).wait_recv()

        pltpu.make_async_copy(self.total, place, semaphore).start()
        pltpu.make_async_remote_copy(
            src_ref=self.total, dst_ref=place, send_sem=self.send.at[13],
            recv_sem=self.recv.at[13],
            device_id=device_of(self.z, 1 - self.core, self.shard), device_id_type=MESH,
        ).start()

    def finish(self, place, semaphore):
        pltpu.make_async_copy(self.total, place, semaphore).wait()
        last = pltpu.make_async_remote_copy(
            src_ref=self.total, dst_ref=place, send_sem=self.send.at[13],
            recv_sem=self.recv.at[13],
            device_id=device_of(self.z, 1 - self.core, self.shard), device_id_type=MESH,
        )
        last.wait_send()
        last.wait_recv()
        for index in range(4, 10):
            self.link(index).wait_send()

        @pl.when(jnp.logical_not(self.inner))
        def _():
            self.link(10).wait_send()

        @pl.when(self.inner)
        def _():
            self.link(11).wait_send()
            self.link(12).wait_send()


class Butterfly:
    def __init__(self, held, got, send, recv):
        self.held, self.got, self.send, self.recv = held, got, send, recv
        self.z, self.core, self.shard = seat()

    def copy(self, step):
        z, core, shard = self.z, self.core, self.shard
        where = ((z, core, shard ^ 1), (z, core, shard ^ 2), (z ^ 1, core, shard),
                 (z ^ 2, core, shard), (z, 1 - core, shard))[step]
        rows = pl.ds(0, 2 * VECTORS if step < 2 else VECTORS)
        return pltpu.make_async_remote_copy(
            src_ref=self.held.at[step, rows], dst_ref=self.got.at[step, rows],
            send_sem=self.send.at[step], recv_sem=self.recv.at[step],
            device_id=device_of(*where), device_id_type=MESH,
        )

    def start(self):
        self.copy(0).start()

    def step(self, step):
        self.copy(step).wait_recv()
        rows = slice(0, 2 * VECTORS if step < 2 else VECTORS)
        self.held[step + 1, rows] = self.held[step, rows] + self.got[step, rows]
        if step < 4:
            self.copy(step + 1).start()

    def finish(self):
        for step in range(5):
            self.copy(step).wait_send()


def back_piece(
    head, half, query_ref, key_ref, value_ref, bias_ref, log_ref, grad_ref,
    overlap, key_flip, key_acc, value_acc, query_flip,
):
    mem_valid = lax.broadcasted_iota(jnp.int32, (MEM, 1), 0) < READ
    mask = head_mask(head)
    span = pl.ds(pl.multiple_of(head * HEAD, HEAD), HEAD)

    def block_back(keys, values, bias, valid, queries, grads, log, delta, flipped, rows):
        scores = times_back(keys, queries)
        if bias is not None:
            scores = scores + bias
        chances = jnp.exp(scores - log)
        if valid is not None:
            chances = jnp.where(valid, chances, 0.0)
        slopes = (chances * (times_back(values, grads) - delta)).astype(jnp.bfloat16)
        value_acc[rows] += product(chances.astype(jnp.bfloat16), grads)
        key_acc[rows] += product(slopes, queries)
        return product(flipped, slopes)

    part = pl.ds(pl.multiple_of(half * HALF, HALF), HALF)
    queries = pick(mask, query_ref[part])
    grads = pick(mask, grad_ref[part])
    delta = jnp.sum(overlap[span, part], axis=0, keepdims=True)
    log = log_ref[pl.ds(head, 1), part]
    main_rows = slice(0, 2 * HALF)
    mem_rows = slice(2 * HALF, CONT)
    piece = block_back(
        key_ref[main_rows], value_ref[main_rows], None, None,
        queries, grads, log, delta, key_flip[span, main_rows], main_rows,
    )
    piece += block_back(
        key_ref[mem_rows], value_ref[mem_rows], None, mem_valid,
        queries, grads, log, delta, key_flip[span, mem_rows], mem_rows,
    )
    query_flip[span, part] = piece

    @pl.when(half == 1)
    def _():
        for cont in range(OWN // CLEN):
            rows = slice(CONT + cont * CLEN, CONT + (cont + 1) * CLEN)
            part = slice(cont * CLEN, (cont + 1) * CLEN)
            query_flip[span, HALF + cont * CLEN : HALF + (cont + 1) * CLEN] += block_back(
                key_ref[rows], value_ref[rows], bias_ref[:, part], None,
                queries[part], grads[part], log[:, part], delta[:, part],
                key_flip[span, rows], rows,
            )


def back_kernel(
    act_ref, gdown_ref, first_ref, ginner_ref, mixed_all, gbranch_ref, ghidden_ref, rows_ref,
    qkv_ref, out_ref, sums_ref,
    query_ref, key_ref, value_ref, grad_ref, mixed_ref, log_ref, bias_ref,
    down_out, up_out, out_out, qkv_out, returned_out, grad_prompt, grad_kept, grad_back,
    memory_out, vec_out,
    wide_mine, wide_theirs, wide_got, wide_x, wide_y, wide_lx, wide_ly, wide_outer, wide_total,
    thin_mine, thin_theirs, thin_got, thin_x, thin_y, thin_lx, thin_ly, thin_outer, thin_total,
    pool, rows, dquery, dkey, dvalue, key_acc, value_acc, overlap, key_flip, query_flip,
    partner, ghidden, staged, held, got,
    send, recv, small_send, small_recv, swap_send, swap_recv, local, out_sem,
):
    pair = pl.program_id(0)
    z, core, shard = seat()
    other = 1 - core
    width = rows_ref.shape[1]
    part_rows = width // 4
    low = jnp.bfloat16

    def item(index):
        if isinstance(index, int) and index >= WIDE:
            return thin(index - WIDE)
        return Reduce(
            wide_mine.at[index], wide_theirs.at[index % 2], wide_got.at[index],
            wide_x.at[index], wide_y.at[index], wide_lx.at[index], wide_ly.at[index],
            wide_outer.at[index], wide_total.at[index], send.at[index], recv.at[index],
        )

    def thin(index):
        return Reduce(
            thin_mine.at[index], thin_theirs.at[index % 2], thin_got.at[index],
            thin_x.at[index], thin_y.at[index], thin_lx.at[index], thin_ly.at[index],
            thin_outer.at[index], thin_total.at[index], send.at[WIDE + index],
            recv.at[WIDE + index],
        )

    small = Butterfly(held, got, small_send, small_recv)
    half_hidden = width // 2

    def place(index):
        if index < 2:
            start = core * half_hidden + index * part_rows
            return down_out.at[pl.ds(pl.multiple_of(start, 64), part_rows)]
        if index < 4:
            start = core * (2 * width) + (index - 2) * width
            return up_out.at[:, pl.ds(pl.multiple_of(start, 128), width)]
        if index == 4:
            return out_out.at[:, pl.ds(pl.multiple_of(core * half_hidden, 128), half_hidden)]
        return qkv_out.at[index - 5, core]

    def stage(name, index):
        if name == "share":
            item(index).share(place(index), out_sem.at[index])
        else:
            getattr(item(index), name)()

    returned = Swap(
        out_ref.at[pl.ds(HALF + OWN // 2, OWN // 2)], returned_out, swap_send.at[0], swap_recv.at[0], z, core, shard ^ 2
    )
    def to_partner(index):
        span = pl.ds(pl.multiple_of(128 * index, 128), 128)
        return Swap(
            pool.at[3, span], partner.at[span], swap_send.at[index + 1], swap_recv.at[index + 1],
            z, core, shard ^ 1,
        )

    cont_back = Swap(
        pool.at[3, pl.ds(2 * 256, 256)], grad_back, swap_send.at[5], swap_recv.at[5],
        z, core, shard ^ 2,
    )

    def load(source, slot, semaphore):
        return pltpu.make_async_copy(source, pool.at[slot], local.at[semaphore])

    def act_chunk(part):
        return load(act_ref.at[:, pl.ds(part * width, width)], part % 2, part % 2)

    def inner_chunk(step):
        half = other if step < 2 else core
        start = pl.multiple_of(half * (2 * width) + (step % 2) * width, 128)
        return load(ginner_ref.at[:, pl.ds(start, width)], step % 2, step % 2)

    def parts_of(target, values):
        for part in range(4):
            target[part] = values[part * part_rows : (part + 1) * part_rows].astype(low)

    load_rows = pltpu.make_async_copy(rows_ref, rows, local.at[4])

    def inner_load(step):
        half = jnp.where(step < 2, other, core)
        start = pl.multiple_of(half * (2 * width) + (step % 2) * width, 128)
        return load(ginner_ref.at[:, pl.ds(start, width)], step % 2, step % 2)

    def act_load(part):
        lanes = pl.ds(pl.multiple_of(part * width, 128), width)
        return load(act_ref.at[:, lanes], part % 2, part % 2)

    def weight_load(index):
        return pltpu.make_async_copy(
            qkv_ref.at[:, pl.ds(index * width, width)],
            pool.at[index, pl.ds(0, width)], local.at[index],
        )

    def down_part(part, carry):
        act_load(part).wait()

        def down_half(side, carry):
            half = jnp.where(side == 0, other, core)
            lanes = pl.ds(pl.multiple_of(half * half_hidden, 128), half_hidden)
            result = outer_sum(pool[part % 2, :, lanes], pool[2]).astype(low)
            for index in range(2):
                piece = result[index * part_rows : (index + 1) * part_rows]

                @pl.when(side == 0)
                def _():
                    wide_theirs[index, part] = piece
                    item(index).give(part)

                @pl.when(side == 1)
                def _():
                    wide_mine[index, part] = piece

            return carry

        lax.fori_loop(0, 2, down_half, 0)

        @pl.when(part < 2)
        def _():
            act_load(part + 2).start()

        @pl.when(part >= 2)
        def _():
            inner_load(part - 2).start()

        return carry

    def up_part(step, carry):
        inner_load(step).wait()
        result = outer_sum(pool[3], pool[step % 2])

        @pl.when(step < 2)
        def _():
            item(step).given()
            parts_of(wide_theirs.at[step], result)
            for part in range(4):
                item(step + 2).give(part)
            inner_load(step + 2).start()

        @pl.when(step >= 2)
        def _():
            parts_of(wide_mine.at[step], result)

        @pl.when((step == 1) | (step == 2))
        def _():
            item(step - 1).chip()

        return carry

    def out_half(side, carry):
        half = jnp.where(side == 0, other, core)
        lanes = pl.ds(pl.multiple_of(half * half_hidden, 128), half_hidden)
        result = outer_sum(pool[2], pool[3, :, lanes])

        @pl.when(side == 0)
        def _():
            parts_of(thin_theirs.at[0], result)
            for part in range(4):
                thin(0).give(part)

        @pl.when(side == 1)
        def _():
            parts_of(thin_mine.at[0], result)

        return carry

    def qkv_part(index):
        def one_half(side, carry):
            half = jnp.where(side == 0, other, core)
            lanes = pl.ds(pl.multiple_of((2 * index + half) * (2 * HEAD), 2 * HEAD), 2 * HEAD)
            query_side = outer_sum(rows[:HALF], dquery[:HALF, lanes])
            query_side += outer_sum(rows[CONT:], dquery[HALF:, lanes])
            both = jnp.concatenate([dkey[:, lanes], dvalue[:, lanes]], axis=1)
            result = jnp.concatenate([query_side, outer_sum(rows[...], both)], axis=1)

            @pl.when(side == 0)
            def _():
                @pl.when(index > 0)
                def _():
                    thin(index - 1).given()

                parts_of(thin_theirs.at[(1 + index) % 2], result)
                for part in range(4):
                    thin(1 + index).give(part)

            @pl.when(side == 1)
            def _():
                parts_of(thin_mine.at[1 + index], result)

            return carry

        lax.fori_loop(0, 2, one_half, 0)

    @pl.when(pair == 0)
    def _():
        act_load(0).start()
        load(gdown_ref, 2, 2).start()
        act_load(1).start()
        load(first_ref, 3, 3).start()
        load_rows.start()
        greet()
        returned.start()
        load(gdown_ref, 2, 2).wait()
        lax.fori_loop(0, 4, down_part, 0)
        load(mixed_all, 2, 2).start()
        load(first_ref, 3, 3).wait()
        lax.fori_loop(0, 4, up_part, 0)
        load(gbranch_ref, 3, 3).start()
        load(mixed_all, 2, 2).wait()
        load(gbranch_ref, 3, 3).wait()
        lax.fori_loop(0, 2, out_half, 0)
        for index in range(3):
            weight_load(index).start()
        load_rows.wait()

    lanes = pl.ds(pl.multiple_of(pair * (2 * HEAD), 2 * HEAD), 2 * HEAD)
    key_flip[...] = flip(key_ref[...])
    overlap[...] = (mixed_ref[...].astype(jnp.float32) * grad_ref[...].astype(jnp.float32)).T
    key_acc[...] = jnp.zeros_like(key_acc)
    value_acc[...] = jnp.zeros_like(value_acc)

    def piece_body(piece, carry):
        back_piece(
            piece // 2, piece % 2, query_ref, key_ref, value_ref, bias_ref, log_ref, grad_ref,
            overlap, key_flip, key_acc, value_acc, query_flip,
        )

        @pl.when(piece == 3)
        def _():
            dquery[:, lanes] = (query_flip[...].T * SCALE).astype(low)
            dkey[:, lanes] = key_acc[...].astype(low)
            dvalue[:, lanes] = value_acc[...].astype(low)

        @pl.when((piece == 3) & (pair % 2 == 1))
        def _():
            qkv_part(pair // 2)

        for number, stages in SLOTS.items():

            @pl.when(pair * 4 + piece == number)
            def _():
                for name, index in stages:
                    stage(name, index)

        return carry

    lax.fori_loop(0, 4, piece_body, 0)

    def hidden_load(step):
        start = pl.multiple_of((5 - step) * 256, 256)
        return pltpu.make_async_copy(
            ghidden_ref.at[pl.ds(start, 256)], ghidden.at[step % 2], local.at[5 + step % 2]
        )

    def staged_store(step):
        slot = step % 2
        return staged.at[slot], local.at[8 + slot]

    def chunk_body(step, carry):
        start = jnp.where(step < 2, HALF + 256 * step, jnp.where(step < 4, CONT, HALF))
        start = jnp.where(step >= 2, start + jnp.where(step % 2 == 0, 256, 0), start)
        start = jnp.where(step >= 4, start - HALF, start)
        span = pl.ds(pl.multiple_of(start, MEM), 256)
        result = times_back(dkey[span], pool[1, :width]) + times_back(dvalue[span], pool[2, :width])

        @pl.when(step < 2)
        def _():
            pool[3, pl.ds(pl.multiple_of(256 * step, 256), 256)] = result.astype(low)

        @pl.when(step == 0)
        def _():
            to_partner(0).start()

        @pl.when(step >= 2)
        def _():
            hidden_load(step).wait()
            mine = pl.ds(pl.multiple_of((5 - step) * 256, 256), 256)
            full = result + (
                ghidden[step % 2] + times_back(dquery[mine], pool[0, :width])
            )

            @pl.when(step == 2)
            def _():
                pool[3, 512:768] = full.astype(low)
                cont_back.start()

            @pl.when(step == 3)
            def _():
                staged[1] = full.astype(low)
                pltpu.make_async_copy(staged.at[1], grad_kept, local.at[9]).start()

            @pl.when(step >= 4)
            def _():
                to_partner(2 * (5 - step)).arrive()
                to_partner(2 * (5 - step) + 1).arrive()

                @pl.when(step == 5)
                def _():
                    pltpu.make_async_copy(staged.at[1], grad_kept, local.at[9]).wait()

                mine = pl.ds(pl.multiple_of((5 - step) * 256, 256), 256)
                staged[step % 2] = (full + partner[mine].astype(jnp.float32)).astype(low)
                pltpu.make_async_copy(
                    staged.at[step % 2], grad_prompt.at[mine], local.at[8 + step % 2]
                ).start()

            @pl.when(step < 4)
            def _():
                hidden_load(step + 2).start()

        for number, stages in TAIL.items():

            @pl.when(step == number)
            def _():
                for name, index in stages:
                    if name == "small":
                        small.step(index)
                    elif name == "partner":
                        to_partner(index).start()
                    else:
                        stage(name, index)

        return carry

    @pl.when(pair == PAIRS - 1)
    def _():
        hidden_load(2).start()
        hidden_load(3).start()
        sums = pltpu.make_async_copy(sums_ref, held.at[0, pl.ds(0, VECTORS)], local.at[7])
        sums.start()
        for index in range(3):
            weight_load(index).wait()
        sums.wait()
        held[0, 0:1] = jnp.sum(dquery[...].astype(jnp.float32), axis=0, keepdims=True)
        held[0, 1:2] = jnp.sum(dvalue[...].astype(jnp.float32), axis=0, keepdims=True)
        mem_span = slice(2 * HALF, CONT)
        held[0, VECTORS:] = times_back(dkey[mem_span], pool[1, :width]) + times_back(
            dvalue[mem_span], pool[2, :width]
        )
        stage("chip", 7)
        small.start()
        lax.fori_loop(0, 6, chunk_body, 0)
        for name, index in LAST:
            if name == "small":
                small.step(index)
            else:
                stage(name, index)
        family = shard // 2
        memory_out[family] = held[1, VECTORS:]
        memory_out[1 - family] = got[1, VECTORS:]
        vec_out[...] = held[5, :VECTORS]
        returned.arrive()
        cont_back.arrive()
        for step in (4, 5):
            mine = pl.ds((5 - step) * 256, 256)
            pltpu.make_async_copy(
                staged.at[step % 2], grad_prompt.at[mine], local.at[8 + step % 2]
            ).wait()
        for index in (2, 3, 6, 7):
            item(index).given()
        for index in range(WIDE + NARROW):
            item(index).finish(place(index), out_sem.at[index])
        small.finish()
        for swap in (returned, cont_back, *(to_partner(index) for index in range(4))):
            swap.finish()


def back(
    act, gdown, first, ginner, mixed, gbranch, ghidden, rows, qkv, out_taken, sums,
    query, key, value, grads, log, bias,
):
    width = rows.shape[1]
    low = jnp.bfloat16
    wide = jnp.float32

    def block(count):
        return pl.BlockSpec((count, 2 * HEAD), lambda pair: (0, pair))

    dma = pltpu.SemaphoreType.DMA
    part = width // 4

    def buffers(count, columns):
        return [
            pltpu.VMEM((count, 4, part, columns), low),
            pltpu.VMEM((2, 4, part, columns), low),
            pltpu.VMEM((count, 4, part, columns), low),
            pltpu.VMEM((count, 2, part // 2, columns), low),
            pltpu.VMEM((count, 2, part // 2, columns), low),
            pltpu.VMEM((count, part // 2, columns), low),
            pltpu.VMEM((count, part // 2, columns), low),
            pltpu.VMEM((count, part, columns), low),
            pltpu.VMEM((count, part, columns), low),
        ]

    shape = jax.ShapeDtypeStruct
    return pl.pallas_call(
        back_kernel,
        grid=(PAIRS,),
        in_specs=[WHERE] * 11
        + [
            block(QROWS), block(KEYS), block(KEYS), block(QROWS), block(QROWS),
            pl.BlockSpec((None, 2, QROWS), lambda pair: (pair, 0, 0)),
            pl.BlockSpec((CLEN, OWN), lambda pair: (0, 0)),
        ],
        out_specs=[WHERE] * 8
        + [
            pl.BlockSpec((2, MEM, width), lambda pair: (0, 0, 0)),
            pl.BlockSpec((VECTORS, width), lambda pair: (0, 0)),
        ],
        out_shape=[
            shape((width, width), low),
            shape((part, 4 * width), low),
            shape((part, width), low),
            shape((3, 2, part, width // 2), low),
            shape((OWN // 2, width), low),
            shape((HALF, width), low),
            shape((OWN // 2, width), low),
            shape((OWN // 2, width), low),
            shape((2, MEM, width), wide),
            shape((VECTORS, width), wide),
        ],
        scratch_shapes=buffers(WIDE, width)
        + buffers(NARROW, width // 2)
        + [
            pltpu.VMEM((4, QROWS, width), low),
            pltpu.VMEM((KEYS, width), low),
            pltpu.VMEM((QROWS, width), low),
            pltpu.VMEM((KEYS, width), low),
            pltpu.VMEM((KEYS, width), low),
            pltpu.VMEM((KEYS, 2 * HEAD), wide),
            pltpu.VMEM((KEYS, 2 * HEAD), wide),
            pltpu.VMEM((2 * HEAD, QROWS), wide),
            pltpu.VMEM((2 * HEAD, KEYS), low),
            pltpu.VMEM((2 * HEAD, QROWS), wide),
            pltpu.VMEM((HALF, width), low),
            pltpu.VMEM((2, 256, width), wide),
            pltpu.VMEM((2, 256, width), low),
            pltpu.VMEM((6, 2 * VECTORS, width), wide),
            pltpu.VMEM((5, 2 * VECTORS, width), wide),
            dma((WIDE + NARROW, SEND + 1)),
            dma((WIDE + NARROW, SEND + 1)),
            dma((5,)),
            dma((5,)),
            dma((6,)),
            dma((6,)),
            dma((10,)),
            dma((WIDE + NARROW,)),
        ],
        compiler_params=pltpu.CompilerParams(
            vmem_limit_bytes=67043328, collective_id=1, has_side_effects=True
        ),
        name="back",
    )(
        act, gdown, first, ginner, mixed, gbranch, ghidden, rows, qkv, out_taken, sums,
        query, key, value, grads, mixed, log, bias,
    )


def cont_ranks(owner_ref, shard):
    prompt_of = shard // 2
    conts = OWN // CLEN
    place = []
    before = jnp.int32(0)
    for cont in range(conts):
        owned = (owner_ref[0, shard * conts + cont] == prompt_of).astype(jnp.int32)
        place.append(jnp.where(owned == 1, before, 2 + cont - before))
        before = before + owned
    order = []
    for position in range(conts):
        found = jnp.int32(0)
        for cont in range(conts):
            found = found + jnp.where(place[cont] == position, cont, 0)
        order.append(found)
    return place, order


def block_of(index):
    return pl.ds(pl.multiple_of(index * CLEN, CLEN), CLEN)


def prepare_kernel(
    owner_ref, length_ref, follow_ref, cotan_ref, memory_ref, query_ref, key_ref, value_ref,
    out_ref, up_ref, *refs,
):
    vectors = refs[:9]
    (
        qkv, wide, vec, kept, sent, memory, kept_cot, sent_cot, bias,
    ) = refs[9:]
    shard = lax.axis_index("shard")
    across = shard ^ 2
    conts = OWN // CLEN
    width = query_ref.shape[1]
    _, order = cont_ranks(owner_ref, shard)
    _, order_across = cont_ranks(owner_ref, across)
    for index in range(2):
        span = slice(index * CLEN, (index + 1) * CLEN)
        kept[span] = follow_ref[0, block_of(order[index])]
        sent[span] = follow_ref[0, block_of(order[2 + index])]
        kept_cot[span] = cotan_ref[0, block_of(order[index])]
        sent_cot[span] = cotan_ref[0, block_of(order[2 + index])]
    position = lax.broadcasted_iota(jnp.int32, (CLEN, CLEN), 0)
    for index in range(conts):
        if index < 2:
            length = length_ref[0, shard * conts + order[index]]
        else:
            length = length_ref[0, across * conts + order_across[index]]
        valid = (position < length) | (position >= CLEN - WRITE)
        bias[:, index * CLEN : (index + 1) * CLEN] = jnp.where(valid, 0.0, NEGATIVE)
    memory[...] = jnp.zeros_like(memory)
    memory[:READ] = memory_ref[0, shard // 2]
    qkv[:, :width] = query_ref[...]
    qkv[:, width : 2 * width] = key_ref[...]
    qkv[:, 2 * width :] = value_ref[...]
    wide[:, :width] = out_ref[...]
    wide[:, width:] = up_ref[...]
    vec[...] = jnp.zeros_like(vec)
    for index, vector in enumerate(vectors):
        vec[index : index + 1, : vector.shape[1]] = vector[...]


def prepare(owner, length, follow, cotan, memory, query, key, value, out, up, vectors):
    low = jnp.bfloat16
    width = query.shape[1]
    share = query.shape[0]
    shape = jax.ShapeDtypeStruct
    half = shape((OWN // 2, width), low)
    inside = pl.BlockSpec(memory_space=pltpu.VMEM)
    scalars = pl.BlockSpec(memory_space=pltpu.SMEM)
    return pl.pallas_call(
        prepare_kernel,
        in_specs=[scalars] * 2 + [inside] * 17,
        out_specs=[inside] * 9,
        out_shape=[
            shape((share, 3 * width), low), shape((share, 5 * width), low),
            shape((VECTORS, 2 * HEAD), low), half, half, shape((MEM, width), low), half, half,
            shape((CLEN, OWN), jnp.float32),
        ],
        name="prepare",
    )(
        owner, length, follow, cotan, memory, query, key, value, out, up,
        *(vector[None] for vector in vectors),
    )


def finish_kernel(
    owner_ref, output_ref, returned_ref, kept_grad, back_grad, down_ref, up_ref, out_ref, qkv_ref,
    memory_ref, vec_ref,
    prompt_out, follow_out, follow_grad, memory_grad, query_sum, key_sum, value_sum, out_sum,
    up_sum, down_sum, *vectors,
):
    shard = lax.axis_index("shard")
    wide = jnp.float32
    width = down_ref.shape[1]
    part = width // 4
    place, _ = cont_ranks(owner_ref, shard)
    prompt_out[0] = output_ref[:HALF]
    for cont, position in enumerate(place):
        span = slice(cont * CLEN, (cont + 1) * CLEN)
        here = block_of(jnp.where(position < 2, position, 0))
        there = block_of(jnp.where(position < 2, 0, position - 2))
        kept = position < 2

        @pl.when(kept)
        def _():
            follow_out[0, span] = output_ref[pl.ds(HALF + here.start, CLEN)]
            follow_grad[0, span] = kept_grad[here]

        @pl.when(jnp.logical_not(kept))
        def _():
            follow_out[0, span] = returned_ref[there]
            follow_grad[0, span] = back_grad[there]

    memory_grad[0] = memory_ref[:, :READ].astype(jnp.bfloat16)
    down_sum[...] = down_ref[...].astype(wide)
    up_sum[...] = up_ref[...].astype(wide)
    out_sum[...] = out_ref[...].astype(wide)
    for index in range(3):
        for side in range(2):
            lanes = slice((2 * index + side) * 2 * HEAD, (2 * index + side + 1) * 2 * HEAD)
            for number, target in enumerate((query_sum, key_sum, value_sum)):
                source = slice(number * 2 * HEAD, (number + 1) * 2 * HEAD)
                target[:, lanes] = qkv_ref[index, side, :, source].astype(wide)
    for index in range(8):
        row = vec_ref[index : index + 1]
        total = jnp.zeros((1, part), wide)
        for quarter in range(4):
            total += jnp.where(shard == quarter, row[:, quarter * part : (quarter + 1) * part], 0.0)
        vectors[index][...] = total.reshape(part)
    total = jnp.zeros((1, width), wide)
    for quarter in range(4):
        total += jnp.where(shard == quarter, vec_ref[8 + quarter : 9 + quarter], 0.0)
    vectors[8][...] = total.reshape(width)


def finish(owner, output, returned, kept, back_grad, down, up, out, qkv, memory, vec):
    low = jnp.bfloat16
    wide = jnp.float32
    shape = jax.ShapeDtypeStruct
    width = down.shape[1]
    part = width // 4
    inside = pl.BlockSpec(memory_space=pltpu.VMEM)
    square = shape((part, width), wide)

    def whole(array):
        return pl.BlockSpec(array.shape, lambda step: (0,) * array.ndim)

    return pl.pallas_call(
        finish_kernel,
        grid=(1,),
        in_specs=[pl.BlockSpec(memory_space=pltpu.SMEM)]
        + [
            whole(array)
            for array in (output, returned, kept, back_grad, down, up, out, qkv, memory, vec)
        ],
        out_specs=[inside] * 19,
        out_shape=[
            shape((1, HALF, width), low), shape((1, OWN, width), low), shape((1, OWN, width), low),
            shape((1, 2, READ, width), low), square, square, square, square,
            shape((part, 4 * width), wide), shape((width, width), wide),
        ]
        + [shape((part,), wide)] * 8
        + [shape((width,), wide)],
        compiler_params=pltpu.CompilerParams(vmem_limit_bytes=67043328),
        name="finish",
    )(owner, output, returned, kept, back_grad, down, up, out, qkv, memory, vec)


def body_pairs(
    prompt_rows, follow_rows, memory_rows, follow_owner, follow_length,
    query_weight, key_weight, value_weight, out_weight, query_bias, value_bias, out_bias,
    first_gain, first_shift, up_weight, up_bias, down_weight, down_bias,
    second_gain, second_shift, prompt_cotan, follow_cotan,
):
    qkv, wide, vec, kept, sent, memory, kept_cot, sent_cot, bias = prepare(
        follow_owner, follow_length, follow_rows, follow_cotan, memory_rows,
        query_weight, key_weight, value_weight, out_weight, up_weight,
        (
            query_bias, value_bias, out_bias, first_gain, first_shift, down_bias,
            second_gain, second_shift, up_bias,
        ),
    )
    (
        qkv_mat, _, _, _, key_rows,
        output, activated, first_low, grad_down, grad_inner, grad_branch, grad_mixed, grad_hidden,
        mixed, log, query_low, key_low, value_low, sums,
    ) = front(
        qkv, wide, down_weight, vec, prompt_rows[0], kept, sent, memory, prompt_cotan[0],
        kept_cot, sent_cot, bias,
    )
    (
        down_sum, up_sum, out_sum, qkv_sum, returned_out, grad_prompt, grad_kept, returned_grad,
        memory_sum, sums,
    ) = back(
        activated, grad_down, first_low, grad_inner, mixed, grad_branch, grad_hidden, key_rows,
        qkv_mat, output, sums,
        query_low, key_low, value_low, grad_mixed, log, bias,
    )
    (
        prompt_out, follow_out, follow_grad, grad_memory, query_sum, key_sum, value_sum, out_sum,
        up_sum, down_sum, *vectors,
    ) = finish(
        follow_owner, output, returned_out, grad_kept, returned_grad, down_sum, up_sum, out_sum,
        qkv_sum, memory_sum, sums,
    )
    return (
        prompt_out, follow_out, grad_prompt[None], follow_grad, grad_memory,
        query_sum, key_sum, value_sum, out_sum, vectors[0], vectors[1], vectors[2], vectors[3],
        vectors[4], up_sum, vectors[8], down_sum, vectors[5], vectors[6], vectors[7],
    )


def solution(mesh):
    return jax.shard_map(
        body_pairs if pairs_fit(mesh) else body_any,
        mesh=mesh,
        in_specs=(
            P("grp", "shard", None),
            P("grp", "shard", None),
            P("grp", None, None, None),
            P("grp", None),
            P("grp", None),
            P(("grp", "shard"), None),
            P(("grp", "shard"), None),
            P(("grp", "shard"), None),
            P(("grp", "shard"), None),
            P(("grp", "shard")),
            P(("grp", "shard")),
            P(("grp", "shard")),
            P(("grp", "shard")),
            P(("grp", "shard")),
            P(("grp", "shard"), None),
            P(("grp", "shard")),
            P(("grp", "shard"), None),
            P(("grp", "shard")),
            P(("grp", "shard")),
            P(("grp", "shard")),
            P("grp", "shard", None),
            P("grp", "shard", None),
        ),
        out_specs=(
            P("grp", "shard", None),
            P("grp", "shard", None),
            P("grp", "shard", None),
            P("grp", "shard", None),
            P("grp", None, None, None),
            P("shard", None),
            P("shard", None),
            P("shard", None),
            P("shard", None),
            P("shard"),
            P("shard"),
            P("shard"),
            P("shard"),
            P("shard"),
            P("shard", None),
            P("shard"),
            P("shard", None),
            P("shard"),
            P("shard"),
            P("shard"),
        ),
        check_vma=False,
    )
```

```python
import jax
import jax.numpy as jnp
from jax import lax
from jax.experimental import pallas as pl
from jax.experimental.pallas import tpu as pltpu
from jax.sharding import PartitionSpec as P

HEADS = 12
HEAD = 64
READ = 10
WRITE = 10
PLEN = 1024
CLEN = 128
CONTS_PER = 8


EPSILON = 1e-12
SCALE = 0.125
NEGATIVE = -1e30
ROOT_HALF = 0.7071067811865476
ROOT_GAUSS = 0.3989422804014327


def product(left, right):
    return jnp.dot(left, right, preferred_element_type=jnp.float32)


def times_back(left, right):
    return lax.dot_general(
        left, right, (((1,), (1,)), ((), ())), preferred_element_type=jnp.float32
    )


def outer_sum(left, right):
    return lax.dot_general(
        left, right, (((0,), (0,)), ((), ())), preferred_element_type=jnp.float32
    )


def column_sum(values):
    return jnp.sum(values.astype(jnp.float32), axis=0)


def layer_norm(hidden, gain, shift):
    center = hidden - jnp.mean(hidden, axis=-1, keepdims=True)
    inverse = lax.rsqrt(jnp.mean(center * center, axis=-1, keepdims=True) + EPSILON)
    normed = center * inverse
    return (normed * gain.astype(jnp.float32) + shift.astype(jnp.float32), normed, inverse)


def norm_back(grad_normed, normed, inverse):
    centered = grad_normed - jnp.mean(grad_normed, axis=-1, keepdims=True)
    return inverse * (centered - normed * jnp.mean(grad_normed * normed, axis=-1, keepdims=True))


def gelu_exact(hidden):
    return 0.5 * hidden * (1.0 + lax.erf(hidden * ROOT_HALF))


def gelu_slope(hidden):
    return (
        0.5 * (1.0 + lax.erf(hidden * ROOT_HALF))
        + hidden * jnp.exp(-0.5 * hidden * hidden) * ROOT_GAUSS
    )


def split_heads(values):
    return values.reshape(values.shape[0], values.shape[1], HEADS, HEAD)


def block_scores(queries, keys, valid):
    scores = (
        jnp.einsum(
            "nqhd,nkhd->nhqk",
            split_heads(queries),
            split_heads(keys),
            preferred_element_type=jnp.float32,
        )
        * SCALE
    )
    return jnp.where(valid[:, None, None, :], scores, NEGATIVE)


def attend_forward(queries, keys, values, valid):
    scores = block_scores(queries, keys, valid)
    maximum = jnp.max(scores, axis=-1, keepdims=True)
    powers = jnp.exp(scores - maximum)
    totals = jnp.sum(powers, axis=-1, keepdims=True)
    chances = (powers / totals).astype(jnp.bfloat16)
    result = jnp.einsum(
        "nhqk,nkhd->nqhd", chances, split_heads(values), preferred_element_type=jnp.float32
    )
    return (result.reshape(-1, queries.shape[2]), maximum + jnp.log(totals))


def attend_backward(queries, keys, values, valid, logsum, grad_out):
    width = queries.shape[2]
    scores = block_scores(queries, keys, valid)
    chances = jnp.exp(scores - logsum)
    grad_heads = split_heads(grad_out)
    grad_chance = jnp.einsum(
        "nqhd,nkhd->nhqk", grad_heads, split_heads(values), preferred_element_type=jnp.float32
    )
    inner = jnp.sum(chances * grad_chance, axis=-1, keepdims=True)
    grad_score = (chances * (grad_chance - inner)).astype(jnp.bfloat16)
    grad_query = (
        jnp.einsum(
            "nhqk,nkhd->nqhd", grad_score, split_heads(keys), preferred_element_type=jnp.float32
        )
        * SCALE
    )
    grad_key = (
        jnp.einsum(
            "nhqk,nqhd->nkhd", grad_score, split_heads(queries), preferred_element_type=jnp.float32
        )
        * SCALE
    )
    grad_value = jnp.einsum(
        "nhqk,nqhd->nkhd",
        chances.astype(jnp.bfloat16),
        grad_heads,
        preferred_element_type=jnp.float32,
    )
    span = keys.shape[1]
    return (
        grad_query.reshape(-1, width),
        grad_key.reshape(keys.shape[0], span, width),
        grad_value.reshape(keys.shape[0], span, width),
    )


def body_any(
    prompt_rows,
    follow_rows,
    memory_rows,
    follow_owner,
    follow_length,
    query_weight,
    key_weight,
    value_weight,
    out_weight,
    query_bias,
    value_bias,
    out_bias,
    first_gain,
    first_shift,
    up_weight,
    up_bias,
    down_weight,
    down_bias,
    second_gain,
    second_shift,
    prompt_cotan,
    follow_cotan,
):
    (
        query_mat,
        key_mat,
        value_mat,
        out_mat,
        query_add,
        value_add,
        out_add,
        gain_one,
        shift_one,
        up_mat,
        up_add,
        down_mat,
        down_add,
        gain_two,
        shift_two,
    ) = (
        lax.all_gather(query_weight, ("grp", "shard"), axis=0, tiled=True),
        lax.all_gather(key_weight, ("grp", "shard"), axis=0, tiled=True),
        lax.all_gather(value_weight, ("grp", "shard"), axis=0, tiled=True),
        lax.all_gather(out_weight, ("grp", "shard"), axis=0, tiled=True),
        lax.all_gather(query_bias, ("grp", "shard"), axis=0, tiled=True),
        lax.all_gather(value_bias, ("grp", "shard"), axis=0, tiled=True),
        lax.all_gather(out_bias, ("grp", "shard"), axis=0, tiled=True),
        lax.all_gather(first_gain, ("grp", "shard"), axis=0, tiled=True),
        lax.all_gather(first_shift, ("grp", "shard"), axis=0, tiled=True),
        lax.all_gather(up_weight, ("grp", "shard"), axis=0, tiled=True),
        lax.all_gather(up_bias, ("grp", "shard"), axis=0, tiled=True),
        lax.all_gather(down_weight, ("grp", "shard"), axis=0, tiled=True),
        lax.all_gather(down_bias, ("grp", "shard"), axis=0, tiled=True),
        lax.all_gather(second_gain, ("grp", "shard"), axis=0, tiled=True),
        lax.all_gather(second_shift, ("grp", "shard"), axis=0, tiled=True),
    )
    shard_index = lax.axis_index("shard")
    prompt = prompt_rows[0]
    follow = follow_rows[0]
    p_count = prompt.shape[0]
    f_count = follow.shape[0]
    width = prompt.shape[1]
    families = memory_rows.shape[1]
    all_rows = jnp.concatenate([prompt, follow], axis=0)
    memory_flat = memory_rows[0].reshape(families * READ, width)
    query_low = (product(all_rows, query_mat) + query_add.astype(jnp.float32)).astype(jnp.bfloat16)
    key_low = product(all_rows, key_mat).astype(jnp.bfloat16)
    value_low = (product(all_rows, value_mat) + value_add.astype(jnp.float32)).astype(jnp.bfloat16)
    mem_key = product(memory_flat, key_mat).astype(jnp.bfloat16).reshape(families, READ, width)
    mem_value = (
        (product(memory_flat, value_mat) + value_add.astype(jnp.float32))
        .astype(jnp.bfloat16)
        .reshape(families, READ, width)
    )
    half_prompt = PLEN // 2
    per_block = CONTS_PER // 2
    prompt_blocks = p_count // half_prompt
    conts_here = f_count // CLEN
    positions = jnp.arange(CLEN)
    open_span = jnp.ones((per_block, READ + PLEN), dtype=bool)
    owner_row = follow_owner[0]
    length_row = follow_length[0]
    prompt_keys, prompt_values = (
        lax.all_gather(key_low[:p_count], "shard", axis=0, tiled=True),
        lax.all_gather(value_low[:p_count], "shard", axis=0, tiled=True),
    )
    key_table = prompt_keys.reshape(families, PLEN, width)
    value_table = prompt_values.reshape(families, PLEN, width)

    def prompt_inputs(block):
        start = block * half_prompt
        family = (shard_index * p_count + start) // PLEN
        keys = jnp.concatenate([mem_key[family], key_table[family]], axis=0)[None]
        values = jnp.concatenate([mem_value[family], value_table[family]], axis=0)[None]
        valid = jnp.ones((1, READ + PLEN), dtype=bool)
        return (query_low[start : start + half_prompt][None], keys, values, valid, family)

    def follow_inputs(block):
        first_row = p_count + block * per_block * CLEN
        chosen = shard_index * conts_here + block * per_block + jnp.arange(per_block)
        owners = owner_row[chosen]
        lengths = length_row[chosen]
        own_keys = key_low[first_row : first_row + per_block * CLEN].reshape(per_block, CLEN, width)
        own_values = value_low[first_row : first_row + per_block * CLEN].reshape(
            per_block, CLEN, width
        )
        keys = jnp.concatenate([mem_key[owners], key_table[owners], own_keys], axis=1)
        values = jnp.concatenate([mem_value[owners], value_table[owners], own_values], axis=1)
        own_valid = (positions[None, :] < lengths[:, None]) | (positions[None, :] >= CLEN - WRITE)
        valid = jnp.concatenate([open_span, own_valid], axis=1)
        queries = query_low[first_row : first_row + per_block * CLEN].reshape(
            per_block, CLEN, width
        )
        return (queries, keys, values, valid, owners)

    attended = []
    saved = []
    block = 0
    queries, keys, values, valid, family = prompt_inputs(block)
    result, logsum = attend_forward(queries, keys, values, valid)
    attended.append(result)
    saved.append(logsum)
    block = 0
    queries, keys, values, valid, owners = follow_inputs(block)
    result, logsum = attend_forward(queries, keys, values, valid)
    attended.append(result)
    saved.append(logsum)
    mixed = jnp.concatenate(attended, axis=0).astype(jnp.bfloat16)
    branch = product(mixed, out_mat) + out_add.astype(jnp.float32)
    first, normed_one, inverse_one = layer_norm(
        all_rows.astype(jnp.float32) + branch, gain_one, shift_one
    )
    first_low = first.astype(jnp.bfloat16)
    inner = product(first_low, up_mat) + up_add.astype(jnp.float32)
    activated = gelu_exact(inner).astype(jnp.bfloat16)
    second = product(activated, down_mat) + down_add.astype(jnp.float32)
    output, normed_two, inverse_two = layer_norm(first + second, gain_two, shift_two)
    output = output.astype(jnp.bfloat16)
    (
        query_mat,
        key_mat,
        value_mat,
        out_mat,
        query_add,
        value_add,
        out_add,
        gain_one,
        shift_one,
        up_mat,
        up_add,
        down_mat,
        down_add,
        gain_two,
        shift_two,
    ) = (
        lax.all_gather(query_weight, ("grp", "shard"), axis=0, tiled=True),
        lax.all_gather(key_weight, ("grp", "shard"), axis=0, tiled=True),
        lax.all_gather(value_weight, ("grp", "shard"), axis=0, tiled=True),
        lax.all_gather(out_weight, ("grp", "shard"), axis=0, tiled=True),
        lax.all_gather(query_bias, ("grp", "shard"), axis=0, tiled=True),
        lax.all_gather(value_bias, ("grp", "shard"), axis=0, tiled=True),
        lax.all_gather(out_bias, ("grp", "shard"), axis=0, tiled=True),
        lax.all_gather(first_gain, ("grp", "shard"), axis=0, tiled=True),
        lax.all_gather(first_shift, ("grp", "shard"), axis=0, tiled=True),
        lax.all_gather(up_weight, ("grp", "shard"), axis=0, tiled=True),
        lax.all_gather(up_bias, ("grp", "shard"), axis=0, tiled=True),
        lax.all_gather(down_weight, ("grp", "shard"), axis=0, tiled=True),
        lax.all_gather(down_bias, ("grp", "shard"), axis=0, tiled=True),
        lax.all_gather(second_gain, ("grp", "shard"), axis=0, tiled=True),
        lax.all_gather(second_shift, ("grp", "shard"), axis=0, tiled=True),
    )
    cotangent = jnp.concatenate([prompt_cotan[0], follow_cotan[0]], axis=0).astype(jnp.float32)
    grad_gain_two = jnp.sum(cotangent * normed_two, axis=0)
    grad_shift_two = jnp.sum(cotangent, axis=0)
    grad_mid = norm_back(cotangent * gain_two.astype(jnp.float32), normed_two, inverse_two)
    grad_down = grad_mid.astype(jnp.bfloat16)
    grad_down_mat = outer_sum(activated, grad_down)
    grad_down_add = column_sum(grad_down)
    grad_inner = (times_back(grad_down, down_mat) * gelu_slope(inner)).astype(jnp.bfloat16)
    grad_up_mat = outer_sum(first_low, grad_inner)
    grad_up_add = column_sum(grad_inner)
    grad_first = grad_mid + times_back(grad_inner, up_mat)
    grad_gain_one = jnp.sum(grad_first * normed_one, axis=0)
    grad_shift_one = jnp.sum(grad_first, axis=0)
    grad_hidden = norm_back(grad_first * gain_one.astype(jnp.float32), normed_one, inverse_one)
    grad_branch = grad_hidden.astype(jnp.bfloat16)
    grad_out_mat = outer_sum(mixed, grad_branch)
    grad_out_add = column_sum(grad_branch)
    grad_mixed = times_back(grad_branch, out_mat).astype(jnp.bfloat16)
    mem_key_acc = jnp.zeros((families, READ, width), jnp.float32)
    mem_value_acc = jnp.zeros((families, READ, width), jnp.float32)
    prompt_key_acc = jnp.zeros((families, PLEN, width), jnp.float32)
    prompt_value_acc = jnp.zeros((families, PLEN, width), jnp.float32)
    block = 0
    queries, keys, values, valid, family = prompt_inputs(block)
    start = block * half_prompt
    grad_query, grad_key, grad_value = attend_backward(
        queries, keys, values, valid, saved[block], grad_mixed[start : start + half_prompt][None]
    )
    query_parts = grad_query
    mem_key_acc = mem_key_acc.at[family].add(grad_key[0, :READ])
    mem_value_acc = mem_value_acc.at[family].add(grad_value[0, :READ])
    prompt_key_acc = prompt_key_acc.at[family].add(grad_key[0, READ:])
    prompt_value_acc = prompt_value_acc.at[family].add(grad_value[0, READ:])
    prompt_query_low = query_parts.astype(jnp.bfloat16)
    block = 0
    queries, keys, values, valid, owners = follow_inputs(block)
    first_row = p_count + block * per_block * CLEN
    grad_slice = grad_mixed[first_row : first_row + per_block * CLEN].reshape(
        per_block, CLEN, width
    )
    grad_query, grad_key, grad_value = attend_backward(
        queries, keys, values, valid, saved[prompt_blocks + block], grad_slice
    )
    mem_key_acc = mem_key_acc.at[owners].add(grad_key[:, :READ])
    mem_value_acc = mem_value_acc.at[owners].add(grad_value[:, :READ])
    prompt_key_acc = prompt_key_acc.at[owners].add(grad_key[:, READ : READ + PLEN])
    prompt_value_acc = prompt_value_acc.at[owners].add(grad_value[:, READ : READ + PLEN])
    own_key_parts = grad_key[:, READ + PLEN :].reshape(-1, width)
    own_value_parts = grad_value[:, READ + PLEN :].reshape(-1, width)
    prompt_key_grad, prompt_value_grad = (
        lax.psum_scatter(
            prompt_key_acc.reshape(families * PLEN, width).astype(jnp.bfloat16),
            "shard",
            scatter_dimension=0,
            tiled=True,
        ).astype(jnp.float32),
        lax.psum_scatter(
            prompt_value_acc.reshape(families * PLEN, width).astype(jnp.bfloat16),
            "shard",
            scatter_dimension=0,
            tiled=True,
        ).astype(jnp.float32),
    )
    follow_query_low = grad_query.astype(jnp.bfloat16)
    follow_key_low = own_key_parts.astype(jnp.bfloat16)
    follow_value_low = own_value_parts.astype(jnp.bfloat16)
    mem_key_sum, mem_value_sum = (
        lax.psum(mem_key_acc.astype(jnp.bfloat16), "shard").astype(jnp.float32),
        lax.psum(mem_value_acc.astype(jnp.bfloat16), "shard").astype(jnp.float32),
    )
    grad_query_low = jnp.concatenate([prompt_query_low, follow_query_low], axis=0)
    grad_key_low = jnp.concatenate([prompt_key_grad.astype(jnp.bfloat16), follow_key_low], axis=0)
    grad_value_low = jnp.concatenate(
        [prompt_value_grad.astype(jnp.bfloat16), follow_value_low], axis=0
    )
    mem_key_low = mem_key_sum.astype(jnp.bfloat16).reshape(families * READ, width)
    mem_value_low = mem_value_sum.astype(jnp.bfloat16).reshape(families * READ, width)
    grad_rows_all = (
        grad_hidden
        + times_back(grad_query_low, query_mat)
        + times_back(grad_key_low, key_mat)
        + times_back(grad_value_low, value_mat)
    ).astype(jnp.bfloat16)
    grad_memory = (
        (times_back(mem_key_low, key_mat) + times_back(mem_value_low, value_mat))
        .astype(jnp.bfloat16)
        .reshape(1, families, READ, width)
    )
    leader = (shard_index == 0).astype(jnp.float32)
    grad_query_mat = outer_sum(all_rows, grad_query_low)
    grad_query_add = column_sum(grad_query_low)
    grad_key_mat = outer_sum(all_rows, grad_key_low) + leader * outer_sum(memory_flat, mem_key_low)
    grad_value_mat = outer_sum(all_rows, grad_value_low) + leader * outer_sum(
        memory_flat, mem_value_low
    )
    grad_value_add = column_sum(grad_value_low) + leader * column_sum(mem_value_low)
    pieces = (
        lax.psum_scatter(
            grad_query_mat.astype(jnp.bfloat16), "shard", scatter_dimension=0, tiled=True
        ).astype(jnp.float32),
        lax.psum_scatter(
            grad_key_mat.astype(jnp.bfloat16), "shard", scatter_dimension=0, tiled=True
        ).astype(jnp.float32),
        lax.psum_scatter(
            grad_value_mat.astype(jnp.bfloat16), "shard", scatter_dimension=0, tiled=True
        ).astype(jnp.float32),
        lax.psum_scatter(
            grad_out_mat.astype(jnp.bfloat16), "shard", scatter_dimension=0, tiled=True
        ).astype(jnp.float32),
        lax.psum_scatter(
            grad_query_add.astype(jnp.bfloat16), "shard", scatter_dimension=0, tiled=True
        ).astype(jnp.float32),
        lax.psum_scatter(
            grad_value_add.astype(jnp.bfloat16), "shard", scatter_dimension=0, tiled=True
        ).astype(jnp.float32),
        lax.psum_scatter(
            grad_out_add.astype(jnp.bfloat16), "shard", scatter_dimension=0, tiled=True
        ).astype(jnp.float32),
        lax.psum_scatter(
            grad_gain_one.astype(jnp.bfloat16), "shard", scatter_dimension=0, tiled=True
        ).astype(jnp.float32),
        lax.psum_scatter(
            grad_shift_one.astype(jnp.bfloat16), "shard", scatter_dimension=0, tiled=True
        ).astype(jnp.float32),
        lax.psum_scatter(
            grad_up_mat.astype(jnp.bfloat16), "shard", scatter_dimension=0, tiled=True
        ).astype(jnp.float32),
        lax.psum_scatter(
            grad_up_add.astype(jnp.bfloat16), "shard", scatter_dimension=0, tiled=True
        ).astype(jnp.float32),
        lax.psum_scatter(
            grad_down_mat.astype(jnp.bfloat16), "shard", scatter_dimension=0, tiled=True
        ).astype(jnp.float32),
        lax.psum_scatter(
            grad_down_add.astype(jnp.bfloat16), "shard", scatter_dimension=0, tiled=True
        ).astype(jnp.float32),
        lax.psum_scatter(
            grad_gain_two.astype(jnp.bfloat16), "shard", scatter_dimension=0, tiled=True
        ).astype(jnp.float32),
        lax.psum_scatter(
            grad_shift_two.astype(jnp.bfloat16), "shard", scatter_dimension=0, tiled=True
        ).astype(jnp.float32),
    )
    summed = (
        lax.psum(pieces[0].astype(jnp.bfloat16), "grp").astype(jnp.float32),
        lax.psum(pieces[1].astype(jnp.bfloat16), "grp").astype(jnp.float32),
        lax.psum(pieces[2].astype(jnp.bfloat16), "grp").astype(jnp.float32),
        lax.psum(pieces[3].astype(jnp.bfloat16), "grp").astype(jnp.float32),
        lax.psum(pieces[4].astype(jnp.bfloat16), "grp").astype(jnp.float32),
        lax.psum(pieces[5].astype(jnp.bfloat16), "grp").astype(jnp.float32),
        lax.psum(pieces[6].astype(jnp.bfloat16), "grp").astype(jnp.float32),
        lax.psum(pieces[7].astype(jnp.bfloat16), "grp").astype(jnp.float32),
        lax.psum(pieces[8].astype(jnp.bfloat16), "grp").astype(jnp.float32),
        lax.psum(pieces[9].astype(jnp.bfloat16), "grp").astype(jnp.float32),
        lax.psum(pieces[10].astype(jnp.bfloat16), "grp").astype(jnp.float32),
        lax.psum(pieces[11].astype(jnp.bfloat16), "grp").astype(jnp.float32),
        lax.psum(pieces[12].astype(jnp.bfloat16), "grp").astype(jnp.float32),
        lax.psum(pieces[13].astype(jnp.bfloat16), "grp").astype(jnp.float32),
        lax.psum(pieces[14].astype(jnp.bfloat16), "grp").astype(jnp.float32),
    )
    return (
        output[:p_count][None],
        output[p_count:][None],
        grad_rows_all[:p_count][None],
        grad_rows_all[p_count:][None],
        grad_memory,
        summed[0],
        summed[1],
        summed[2],
        summed[3],
        summed[4],
        summed[5],
        summed[6],
        summed[7],
        summed[8],
        summed[9],
        summed[10],
        summed[11],
        summed[12],
        summed[13],
        summed[14],
    )


MEM = 16
HALF = PLEN // 2
OWN = 512
CONT = HALF + HALF + MEM
KEYS = CONT + OWN
QROWS = HALF + OWN
PAIRS = HEADS // 2
NAMES = ("grp", "shard")


def pairs_fit(mesh):
    return mesh.shape["shard"] == 4 and mesh.shape["grp"] == 8


def head_mask(head):
    lane = lax.broadcasted_iota(jnp.int32, (1, 2 * HEAD), 1)
    return lane // HEAD == head


def pick(mask, values):
    return jnp.where(mask, values.astype(jnp.float32), 0.0).astype(jnp.bfloat16)


def flip(values):
    return values.astype(jnp.float32).T.astype(jnp.bfloat16)


def own_scores(keys, queries):
    parts = []
    for cont in range(OWN // CLEN):
        part = slice(cont * CLEN, (cont + 1) * CLEN)
        parts.append(times_back(keys[part], queries[part]))
    return jnp.concatenate(parts, axis=1)


def attend_pair(query_ref, key_ref, value_ref, bias_ref, out_ref, log_ref):
    mem_valid = lax.broadcasted_iota(jnp.int32, (MEM, 1), 0) < READ
    value_flip = flip(value_ref[...])
    results = []
    for head in range(2):
        mask = head_mask(head)
        queries = pick(mask, query_ref[...])
        main = times_back(key_ref[: 2 * HALF], queries)
        memory = jnp.where(mem_valid, times_back(key_ref[2 * HALF : CONT], queries), NEGATIVE)
        own = own_scores(key_ref[CONT:], queries[HALF:]) + bias_ref[...]
        top = jnp.maximum(
            jnp.max(main, axis=0, keepdims=True), jnp.max(memory, axis=0, keepdims=True)
        )
        top_own = jnp.maximum(top[:, HALF:], jnp.max(own, axis=0, keepdims=True))
        top = jnp.concatenate([top[:, :HALF], top_own], axis=1)
        main = jnp.exp(main - top)
        memory = jnp.exp(memory - top)
        own = jnp.exp(own - top_own)
        total = jnp.sum(main, axis=0, keepdims=True) + jnp.sum(memory, axis=0, keepdims=True)
        total = jnp.concatenate(
            [total[:, :HALF], total[:, HALF:] + jnp.sum(own, axis=0, keepdims=True)], axis=1
        )
        flipped = value_flip[head * HEAD : (head + 1) * HEAD]
        result = product(flipped[:, : 2 * HALF], main.astype(jnp.bfloat16))
        result += product(flipped[:, 2 * HALF : CONT], memory.astype(jnp.bfloat16))
        own = own.astype(jnp.bfloat16)
        own_parts = []
        for cont in range(OWN // CLEN):
            own_parts.append(
                product(
                    flipped[:, CONT + cont * CLEN : CONT + (cont + 1) * CLEN],
                    own[:, cont * CLEN : (cont + 1) * CLEN],
                )
            )
        result = jnp.concatenate(
            [result[:, :HALF], result[:, HALF:] + jnp.concatenate(own_parts, axis=1)], axis=1
        )
        results.append(result / total)
        log_ref[head : head + 1] = top + jnp.log(total)
    out_ref[...] = jnp.concatenate(results, axis=0).T.astype(jnp.bfloat16)


MESH = pl.DeviceIdType.MESH
WHERE = pl.BlockSpec(memory_space=pl.ANY)
INSIDE = pl.BlockSpec(memory_space=pltpu.VMEM)
VECTORS = 16


def seat():
    grp = lax.axis_index("grp")
    return (grp // 2, grp % 2, lax.axis_index("shard"))


def unit_of(z, core, shard):
    return (z * 2 + core) * 4 + shard


def device_of(z, core, shard):
    return (z * 2 + core, shard)


def greet():
    z, core, shard = seat()
    barrier = pltpu.get_barrier_semaphore()
    others = [device_of((z + step) % 4, core, shard) for step in (1, 2, 3)]
    others += [
        device_of(z, core, shard ^ 1),
        device_of(z, core, shard ^ 2),
        device_of(z, 1 - core, shard),
    ]
    for other in others:
        pl.semaphore_signal(barrier, inc=1, device_id=other, device_id_type=MESH)
    pl.semaphore_wait(barrier, len(others))


class Gather:
    def __init__(self, mine, full, send, recv, by_y=(0, 2)):
        self.mine, self.full, self.send, self.recv = mine, full, send, recv
        self.share = mine.shape[0]
        self.by_y = by_y
        self.z, self.core, self.shard = seat()
        self.sent = 0

    def rows(self, unit):
        return self.full.at[pl.ds(pl.multiple_of(unit * self.share, 8), self.share)]

    def link(self, index, unit, z, core, shard, source=None):
        return pltpu.make_async_remote_copy(
            src_ref=self.rows(unit) if source is None else source,
            dst_ref=self.rows(unit),
            send_sem=self.send.at[index],
            recv_sem=self.recv.at[unit],
            device_id=device_of(z, core, shard),
            device_id_type=MESH,
        )

    def push(self, unit, z, core, shard, source=None):
        self.link(self.sent, unit, z, core, shard, source).start()
        self.sent += 1

    def arrive(self, unit):
        self.link(0, unit, self.z, 1 - self.core, self.shard).wait_recv()

    def start_line(self):
        me = unit_of(self.z, self.core, self.shard)
        for step in (1, 2, 3):
            self.push(me, (self.z + step) % 4, self.core, self.shard, self.mine)

    def start_plane(self):
        z, core, shard = self.z, self.core, self.shard
        me = unit_of(z, core, shard)
        self.push(me, z, core, shard ^ 1, self.mine)
        self.push(me, z, core, shard ^ 2, self.mine)
        self.push(me, z, 1 - core, shard, self.mine)

    def own(self, semaphore):
        return pltpu.make_async_copy(
            self.mine, self.rows(unit_of(self.z, self.core, self.shard)), semaphore
        )

    def column(self, step):
        z, core, shard = self.z, self.core, self.shard
        unit = unit_of((z + step) % 4, core, shard)
        self.arrive(unit)
        self.push(unit, z, core, shard ^ 1)
        self.push(unit, z, core, shard ^ 2)
        self.push(unit, z, 1 - core, shard)

    def side(self, step):
        z, core, shard = self.z, self.core, self.shard
        for hop in (1, 2):
            unit = unit_of((z + step) % 4, core, shard ^ hop)
            self.arrive(unit)
            if (step in self.by_y) == (hop == 1):
                self.push(unit, z, core, shard ^ (3 - hop))
            self.push(unit, z, 1 - core, shard)

    def corner(self, step):
        z, core, shard = self.z, self.core, self.shard
        unit = unit_of((z + step) % 4, core, shard ^ 3)
        self.arrive(unit)
        self.push(unit, z, 1 - core, shard)

    def sibling(self):
        def wait(index, carry):
            unit = (index // 4) * 8 + (1 - self.core) * 4 + index % 4
            self.arrive(unit)
            return carry

        lax.fori_loop(0, 16, wait, 0)

    def finish(self):
        def wait(index, carry):
            pltpu.make_async_remote_copy(
                src_ref=self.mine,
                dst_ref=self.mine,
                send_sem=self.send.at[index],
                recv_sem=self.recv.at[0],
                device_id=device_of(self.z, 1 - self.core, self.shard),
                device_id_type=MESH,
            ).wait_send()
            return carry

        lax.fori_loop(0, self.sent, wait, 0)


class PlaneGather(Gather):
    def start_plane(self):
        z, core, shard = self.z, self.core, self.shard
        me = unit_of(z, core, shard)
        self.link(96, me, z, core, shard ^ 1, self.mine).start()
        self.link(97, me, z, core, shard ^ 2, self.mine).start()
        self.link(me, me, z, 1 - core, shard, self.mine).start()

    def along(self, unit, z_of, source=None):
        z, core, shard = self.z, self.core, self.shard

        @pl.when((z_of <= z) & (z < 3))
        def _():
            self.link(32 + unit, unit, z + 1, core, shard, source).start()

        @pl.when((z_of >= z) & (z > 0))
        def _():
            self.link(64 + unit, unit, z - 1, core, shard, source).start()

    def start_line(self):
        me = unit_of(self.z, self.core, self.shard)
        self.along(me, self.z, self.mine)

    def plane(self):
        z, core, shard = self.z, self.core, self.shard
        over_x = unit_of(z, core, shard ^ 1)
        over_y = unit_of(z, core, shard ^ 2)
        self.arrive(over_x)

        @pl.when(core == 0)
        def _():
            self.link(98, over_x, z, core, shard ^ 2).start()

        self.link(over_x, over_x, z, 1 - core, shard).start()
        self.along(over_x, z)
        self.arrive(over_y)

        @pl.when(core == 1)
        def _():
            self.link(98, over_y, z, core, shard ^ 1).start()

        self.link(over_y, over_y, z, 1 - core, shard).start()
        self.along(over_y, z)

    def corners(self):
        z, core, shard = self.z, self.core, self.shard
        unit = unit_of(z, core, shard ^ 3)
        self.arrive(unit)
        self.link(unit, unit, z, 1 - core, shard).start()
        self.along(unit, z)

    def far(self, distance, other):
        z, core, shard = self.z, self.core, self.shard
        for sign in (-1, 1):
            plane = z + sign * distance

            @pl.when((plane >= 0) & (plane < 4))
            def _():
                unit = unit_of(plane, core, shard ^ other)
                self.arrive(unit)
                self.link(unit, unit, z, 1 - core, shard).start()
                self.along(unit, plane)

    def finish(self):
        z, core, shard = self.z, self.core, self.shard

        def done(index, unit):
            self.link(index, unit, z, 1 - core, shard, self.mine).wait_send()

        for index in (96, 97, 98):
            done(index, 0)

        def wait(index, carry):
            plane = index // 4
            unit = plane * 8 + core * 4 + index % 4
            done(unit, unit)

            @pl.when((plane <= z) & (z < 3))
            def _():
                done(32 + unit, unit)

            @pl.when((plane >= z) & (z > 0))
            def _():
                done(64 + unit, unit)

            return carry

        lax.fori_loop(0, 16, wait, 0)


class Swap:
    def __init__(self, source, target, send, recv, z, core, shard):
        self.copy = pltpu.make_async_remote_copy(
            src_ref=source, dst_ref=target, send_sem=send, recv_sem=recv,
            device_id=device_of(z, core, shard), device_id_type=MESH,
        )

    def start(self):
        self.copy.start()

    def arrive(self):
        self.copy.wait_recv()

    def finish(self):
        self.copy.wait_send()


def spread_vector(vectors, index, width):
    narrow, broad = width // 32, 4 * width // 32
    row = lax.broadcasted_iota(jnp.int32, (32 * VECTORS, width), 0)
    lane = lax.broadcasted_iota(jnp.int32, (32 * VECTORS, width), 1)
    small = index < 8
    start = jnp.where(small, index, 8 + VECTORS * 8 * (index - 8))
    block = jnp.where(small, lane // narrow, lane // broad)
    select = jnp.where(row == VECTORS * block + start, 1.0, 0.0).astype(jnp.bfloat16)
    table = outer_sum(vectors, select)
    piece = lax.broadcasted_iota(jnp.int32, table.shape, 0)
    lane = lax.broadcasted_iota(jnp.int32, table.shape, 1)
    offset = jnp.where(small, lane % narrow, lane % broad)
    return jnp.sum(jnp.where(piece == offset, table, 0.0), axis=0, keepdims=True)


TILE = 512
PARTNERS = 4


def front_kernel(
    qkv_ref, wide_ref, down_ref, vec_ref, prompt_ref, kept_ref, sent_ref, mem_ref,
    prompt_cot, kept_cot, sent_cot, bias_ref,
    qkv_full, wide_full, down_full, vec_full, rows_out,
    out_ref, act_ref, first_ref, gdown_ref, ginner_ref, gbranch_ref, gmixed_ref, ghidden_ref,
    mixed_ref, log_ref, query_out, key_out, value_out, sums_ref,
    rows, weights, vectors, table, query, key, value, mixed, cotan, wide, down,
    act, slope, normed, first, total, hidden, small_low,
    send_a, recv_a, send_b, recv_b, send_c, recv_c, send_d, recv_d, swap_send, swap_recv, local,
    store,
):
    pair = pl.program_id(0)
    width = prompt_ref.shape[1]
    low = jnp.bfloat16
    one = Gather(qkv_ref, qkv_full, send_a, recv_a, (0, 1))
    small = Gather(vec_ref, vec_full, send_d, recv_d)
    two = Gather(wide_ref, wide_full, send_b, recv_b, (0, 1))
    three = PlaneGather(down_ref, down_full, send_c, recv_c)
    z, core, shard = seat()
    step_rows = HALF // PARTNERS
    partner = [
        Swap(
            prompt_ref.at[pl.ds(index * step_rows, step_rows)],
            rows.at[pl.ds(HALF + index * step_rows, step_rows)],
            swap_send.at[index], swap_recv.at[index], z, core, shard ^ 1,
        )
        for index in range(PARTNERS)
    ]
    taken = [
        Swap(
            sent_ref.at[pl.ds(index * step_rows, step_rows)],
            rows.at[pl.ds(CONT + OWN // 2 + index * step_rows, step_rows)],
            swap_send.at[PARTNERS + index], swap_recv.at[PARTNERS + index], z, core, shard ^ 2,
        )
        for index in range(2)
    ]
    taken_cot = Swap(
        sent_cot, cotan.at[pl.ds(HALF + OWN // 2, OWN // 2)],
        swap_send.at[PARTNERS + 2], swap_recv.at[PARTNERS + 2], z, core, shard ^ 2,
    )
    swaps = partner + taken + [taken_cot]
    own = [gather.own(local.at[index]) for index, gather in enumerate((one, small, two, three))]
    own += [
        pltpu.make_async_copy(prompt_ref, rows.at[pl.ds(0, HALF)], local.at[4]),
        pltpu.make_async_copy(mem_ref, rows.at[pl.ds(2 * HALF, MEM)], local.at[5]),
        pltpu.make_async_copy(kept_ref, rows.at[pl.ds(CONT, OWN // 2)], local.at[6]),
        pltpu.make_async_copy(prompt_cot, cotan.at[pl.ds(0, HALF)], local.at[7]),
        pltpu.make_async_copy(kept_cot, cotan.at[pl.ds(HALF, OWN // 2)], local.at[8]),
    ]
    load_weights = pltpu.make_async_copy(qkv_full, weights, local.at[9])
    load_vectors = pltpu.make_async_copy(vec_full, vectors, local.at[10])
    store_rows = pltpu.make_async_copy(rows, rows_out, local.at[11])
    load_wide = pltpu.make_async_copy(wide_full, wide, local.at[12])
    load_down = pltpu.make_async_copy(down_full, down, local.at[13])

    def project(start, query_start, count, queries):
        span = pl.ds(start, count)
        block = rows[span]
        if queries:
            result = (product(block, weights[:, :width]) + table[0:1]).astype(low)
            result = (result.astype(jnp.float32) * SCALE).astype(low)
            query[pl.ds(query_start, count)] = result
        key[span] = product(block, weights[:, width : 2 * width]).astype(low)
        value[span] = (product(block, weights[:, 2 * width :]) + table[1:2]).astype(low)

    @pl.when(pair == 0)
    def _():
        for copy in own[4:]:
            copy.start()
        greet()
        small.start_line()
        one.start_line()
        small.start_plane()
        one.start_plane()
        partner[0].start()
        three.start_line()
        taken[0].start()
        three.start_plane()
        for copy in own[:4]:
            copy.start()
        for step in (1, 2, 3):
            small.column(step)
            one.column(step)
        two.start_line()
        for step in range(4):
            small.side(step)
            one.side(step)
        partner[1].start()
        taken[1].start()
        partner[2].start()
        partner[3].start()
        two.start_plane()
        for step in range(4):
            small.corner(step)
            one.corner(step)
        small.sibling()
        own[1].wait()
        load_vectors.start()
        one.sibling()
        own[0].wait()
        load_weights.start()
        three.plane()
        for step in (1, 2, 3):
            two.column(step)
        load_vectors.wait()

        def spread(index, carry):
            table[pl.ds(index, 1)] = spread_vector(vectors[...], index, width)
            return carry

        lax.fori_loop(0, 12, spread, 0)
        for index in (2, 3, 4, 5, 6):
            own[index].wait()
        load_weights.wait()
        project(0, 0, HALF, True)
        three.corners()
        three.far(1, 0)
        for swap in taken:
            swap.arrive()
        project(CONT, HALF, OWN, True)
        three.far(1, 1)
        for swap in partner:
            swap.arrive()
        project(HALF, 0, HALF + MEM, False)
        store_rows.start()

    def later(when, *actions):
        @pl.when(pair == when)
        def _():
            for action in actions:
                action[0](*action[1:])

    later(0, (two.side, 0), (three.far, 1, 2))
    later(1, (two.side, 1), (three.far, 1, 3))
    later(2, (two.side, 2), (three.far, 2, 0), (three.far, 2, 1))
    later(3, (two.side, 3), (three.far, 2, 2))
    later(4, (two.corner, 0), (two.corner, 1), (three.far, 2, 3), (three.far, 3, 0))
    later(5, (two.corner, 2), (three.far, 3, 1))

    lanes = pl.ds(pl.multiple_of(pair * (2 * HEAD), 2 * HEAD), 2 * HEAD)
    query_out[...] = query[:, lanes]
    key_out[...] = key[:, lanes]
    value_out[...] = value[:, lanes]
    attend_pair(query_out, key_out, value_out, bias_ref, mixed_ref, log_ref)
    mixed[:, lanes] = mixed_ref[...]

    def fine(index):
        return table[index : index + 1]

    def save(tile, index):
        span = pl.ds(pl.multiple_of(tile * TILE, TILE), TILE)
        source, target = (
            (act, act_ref), (slope, ginner_ref), (hidden, ghidden_ref),
            (small_low.at[0], out_ref), (small_low.at[1], first_ref), (small_low.at[2], gdown_ref),
            (small_low.at[3], gbranch_ref), (small_low.at[4], gmixed_ref),
        )[index]
        return pltpu.make_async_copy(source, target.at[span], store.at[index])

    def up_chunk(step):
        return pl.ds(pl.multiple_of(step * width, 128), width)

    def up_columns(step):
        return pl.ds(pl.multiple_of((step + 1) * width, 128), width)

    def add_sum(index, values):
        sums_ref[pl.ds(index, 1)] += jnp.sum(values, axis=0, keepdims=True)

    def start_tile(tile):
        span = pl.ds(pl.multiple_of(tile * TILE, TILE), TILE)
        held = rows[pl.ds(pl.multiple_of(tile * CONT, MEM), TILE)].astype(jnp.float32)
        held = held + (product(mixed[span], wide[:, :width]) + fine(2))
        result, value_n, value_r = layer_norm(held, fine(3), fine(4))

        @pl.when(tile == 1)
        def _():
            for index in range(1, 8):
                save(0, index).wait()

        normed[...] = value_n
        first[...] = result
        small_low[1] = result.astype(low)
        return value_r

    def forward_chunk(step, carry):
        chunk = up_chunk(step)
        inner = product(small_low[1], wide[:, up_columns(step)]) + table[pl.ds(8 + step, 1)]
        half = 0.5 * (1.0 + lax.erf(inner * ROOT_HALF))
        active = (inner * half).astype(low)
        act[:, chunk] = active
        slope[:, chunk] = (half + inner * jnp.exp(-0.5 * inner * inner) * ROOT_GAUSS).astype(low)
        total[...] += product(active, down[chunk])
        return carry

    def backward_chunk(step, carry):
        chunk = up_chunk(step)
        grad = times_back(small_low[2], down[chunk]) * slope[:, chunk].astype(jnp.float32)
        grad = grad.astype(low)
        slope[:, chunk] = grad
        add_sum(8 + step, grad.astype(jnp.float32))
        total[...] += times_back(grad, wide[:, up_columns(step)])
        return carry

    def tile_body(tile, carry):
        span = pl.ds(pl.multiple_of(tile * TILE, TILE), TILE)
        inverse_one = start_tile(tile)
        total[...] = jnp.zeros_like(total)

        @pl.when(tile == 0)
        def _():
            three.far(3, 2)
            three.far(3, 3)
            three.sibling()
            load_down.start()
            load_down.wait()

        @pl.when(tile == 1)
        def _():
            save(0, 0).wait()
            taken_cot.arrive()

        lax.fori_loop(0, 4, forward_chunk, 0)
        save(tile, 0).start()
        result, value_n, inverse_two = layer_norm(
            first[...] + (total[...] + fine(5)), fine(6), fine(7)
        )
        small_low[0] = result.astype(low)
        save(tile, 3).start()
        save(tile, 4).start()
        cot = cotan[span].astype(jnp.float32)
        add_sum(6, cot * value_n)
        add_sum(7, cot)
        grad_mid = norm_back(cot * fine(6), value_n, inverse_two)
        grad_low = grad_mid.astype(low)
        small_low[2] = grad_low
        save(tile, 5).start()
        add_sum(5, grad_low.astype(jnp.float32))
        total[...] = grad_mid
        lax.fori_loop(0, 4, backward_chunk, 0)
        save(tile, 1).start()
        grad_first = total[...]
        add_sum(3, grad_first * normed[...])
        add_sum(4, grad_first)
        grad_hidden = norm_back(grad_first * fine(3), normed[...], inverse_one)
        hidden[...] = grad_hidden
        save(tile, 2).start()
        grad_low = grad_hidden.astype(low)
        small_low[3] = grad_low
        save(tile, 6).start()
        add_sum(2, grad_low.astype(jnp.float32))
        small_low[4] = times_back(grad_low, wide[:, :width]).astype(low)
        save(tile, 7).start()
        return carry

    @pl.when(pair == PAIRS - 1)
    def _():
        taken_cot.start()
        two.corner(3)
        two.sibling()
        load_wide.start()
        own[7].wait()
        own[8].wait()
        sums_ref[...] = jnp.zeros_like(sums_ref)
        load_wide.wait()
        lax.fori_loop(0, 2, tile_body, 0)
        store_rows.wait()
        for index in range(8):
            save(1, index).wait()
        for sender in (one, small, two, three, *swaps):
            sender.finish()


def front(
    qkv, wide_share, down_share, vec, prompt, kept, sent, memory, prompt_cot, kept_cot, sent_cot,
    bias,
):
    width = prompt.shape[1]
    low = jnp.bfloat16
    wide = jnp.float32
    shape = jax.ShapeDtypeStruct

    def block(rows):
        return pl.BlockSpec((rows, 2 * HEAD), lambda pair: (0, pair))

    def full(share):
        return shape((32 * share.shape[0], share.shape[1]), low)

    dma = pltpu.SemaphoreType.DMA
    memory_space = pltpu.VMEM
    return pl.pallas_call(
        front_kernel,
        grid=(PAIRS,),
        in_specs=[INSIDE] * 4
        + [WHERE] * 7
        + [pl.BlockSpec((CLEN, OWN), lambda pair: (0, 0))],
        out_specs=[WHERE] * 13
        + [
            block(QROWS), pl.BlockSpec((None, 2, QROWS), lambda pair: (pair, 0, 0)),
            block(QROWS), block(KEYS), block(KEYS),
            pl.BlockSpec((VECTORS, width), lambda pair: (0, 0)),
        ],
        out_shape=[
            full(qkv), full(wide_share), full(down_share), full(vec),
            shape((KEYS, width), low),
            shape((QROWS, width), low),
            shape((QROWS, 4 * width), low),
            shape((QROWS, width), low),
            shape((QROWS, width), low),
            shape((QROWS, 4 * width), low),
            shape((QROWS, width), low),
            shape((QROWS, width), low),
            shape((QROWS, width), wide),
            shape((QROWS, width), low),
            shape((PAIRS, 2, QROWS), wide),
            shape((QROWS, width), low),
            shape((KEYS, width), low),
            shape((KEYS, width), low),
            shape((VECTORS, width), wide),
        ],
        scratch_shapes=[
            memory_space((KEYS, width), low),
            memory_space((width, 3 * width), low),
            memory_space((32 * VECTORS, 2 * HEAD), low),
            memory_space((VECTORS, width), wide),
            memory_space((QROWS, width), low),
            memory_space((KEYS, width), low),
            memory_space((KEYS, width), low),
            memory_space((QROWS, width), low),
            memory_space((QROWS, width), low),
            memory_space((width, 5 * width), low),
            memory_space((4 * width, width), low),
            memory_space((TILE, 4 * width), low),
            memory_space((TILE, 4 * width), low),
            memory_space((TILE, width), wide),
            memory_space((TILE, width), wide),
            memory_space((TILE, width), wide),
            memory_space((TILE, width), wide),
            memory_space((5, TILE, width), low),
        ]
        + [dma((32,))] * 4
        + [dma((100,)), dma((32,)), dma((32,)), dma((32,))]
        + [dma((PARTNERS + 3,)), dma((PARTNERS + 3,)), dma((14,)), dma((8,))],
        compiler_params=pltpu.CompilerParams(
            vmem_limit_bytes=67043328, collective_id=0, has_side_effects=True
        ),
        name="front",
    )(
        qkv, wide_share, down_share, vec, prompt, kept, sent, memory, prompt_cot, kept_cot,
        sent_cot, bias,
    )


SEND = 13
CHIP, PLANE, LINE, MIDDLE, SPREAD, SHARE, SMALL, PARTNER = range(8)
SLOTS = {
    0: ((PLANE, 0), (CHIP, 2),),
    1: ((CHIP, 3),),
    2: ((PLANE, 1), (CHIP, 4),),
    3: ((LINE, 0),),
    6: ((PLANE, 2),),
    7: ((MIDDLE, 0),),
    8: ((PLANE, 3), (CHIP, 5),),
    9: ((LINE, 1),),
    11: ((SPREAD, 0), (PLANE, 4),),
    12: ((LINE, 2),),
    13: ((MIDDLE, 1), (LINE, 3),),
    15: ((SHARE, 0), (MIDDLE, 2), (LINE, 4), (PLANE, 5),),
    16: ((SPREAD, 1), (CHIP, 6),),
    17: ((LINE, 5),),
    18: ((MIDDLE, 3),),
    19: ((SPREAD, 2), (MIDDLE, 4), (PLANE, 6),),
    20: ((SHARE, 1), (MIDDLE, 5),),
    21: ((LINE, 6),),
    22: ((SPREAD, 3),),
    23: ((SHARE, 2), (SPREAD, 4), (MIDDLE, 6),),
}
TAIL = {
    0: ((SPREAD, 5),),
    1: ((PLANE, 7), (PARTNER, 1), (PARTNER, 2), (PARTNER, 3), (SHARE, 3), (SHARE, 4), (SPREAD, 6), (SMALL, 0),),
    2: ((SMALL, 1),),
    3: ((SHARE, 5), (SMALL, 2), (LINE, 7), (SHARE, 6), (MIDDLE, 7),),
    4: ((SMALL, 3),),
    5: ((SPREAD, 7),),
}
LAST = ((SMALL, 4), (SHARE, 7),)
WIDE = 4
NARROW = 4


class Reduce:
    def __init__(self, mine, theirs, got, from_x, from_y, last_x, last_y, outer, total, send, recv):
        self.mine, self.theirs, self.got = mine, theirs, got
        self.from_x, self.from_y, self.last_x, self.last_y = from_x, from_y, last_x, last_y
        self.outer, self.total, self.send, self.recv = outer, total, send, recv
        self.half = mine.shape[1] // 2
        self.z, self.core, self.shard = seat()
        self.inner = (self.z == 1) | (self.z == 2)

    def copy(self, source, target, index, z, core, shard):
        return pltpu.make_async_remote_copy(
            src_ref=source, dst_ref=target, send_sem=self.send.at[index],
            recv_sem=self.recv.at[index], device_id=device_of(z, core, shard), device_id_type=MESH,
        )

    def upper(self, part):
        return self.mine.at[part, pl.ds(0, self.half)]

    def lower(self, part):
        return self.mine.at[part, pl.ds(self.half, self.half)]

    def link(self, index):
        z, core, shard = self.z, self.core, self.shard
        near = jnp.where(z < 2, 1 - z, 5 - z)
        if index < 4:
            ends = (self.theirs.at[index], self.got.at[index], z, 1 - core, shard)
        elif index < 6:
            source = self.upper(shard ^ (1 if index == 4 else 3))
            ends = (source, self.from_x.at[index - 4], z, core, shard ^ 1)
        elif index < 8:
            source = self.lower(shard ^ (2 if index == 6 else 3))
            ends = (source, self.from_y.at[index - 6], z, core, shard ^ 2)
        elif index == 8:
            ends = (self.upper(shard ^ 2), self.last_y, z, core, shard ^ 2)
        elif index == 9:
            ends = (self.lower(shard ^ 1), self.last_x, z, core, shard ^ 1)
        elif index == 10:
            ends = (self.mine.at[shard], self.outer, near, core, shard)
        elif index == 11:
            ends = (self.mine.at[shard], self.total, 3 - z, core, shard)
        else:
            ends = (self.total, self.total, near, core, shard)
        return self.copy(ends[0], ends[1], index, *ends[2:])

    def give(self, part):
        self.copy(
            self.theirs.at[part], self.got.at[part], part, self.z, 1 - self.core, self.shard
        ).start()

    def given(self):
        for part in range(4):
            self.link(part).wait_send()

    def add(self, part, start, count, other):
        def step(index, carry):
            rows = pl.ds(pl.multiple_of(index * 48, 16), 48)
            span = pl.ds(pl.multiple_of(start + index * 48, 16), 48)
            total = self.mine[part, span].astype(jnp.float32) + other[rows].astype(jnp.float32)
            self.mine[part, span] = total.astype(jnp.bfloat16)
            return carry

        lax.fori_loop(0, count // 48, step, 0)

    def chip(self):
        for part in range(4):
            self.link(part).wait_recv()

        def add_part(part, carry):
            self.add(part, 0, 2 * self.half, self.got.at[part])
            return carry

        lax.fori_loop(0, 4, add_part, 0)
        for index in (4, 5, 6, 7):
            self.link(index).start()

    def plane(self):
        shard = self.shard
        self.link(4).wait_recv()
        self.link(5).wait_recv()
        self.add(shard ^ 2, 0, self.half, self.from_x.at[1])
        self.link(8).start()
        self.link(6).wait_recv()
        self.link(7).wait_recv()
        self.add(shard ^ 1, self.half, self.half, self.from_y.at[1])
        self.link(9).start()
        self.add(shard, 0, self.half, self.from_x.at[0])
        self.add(shard, self.half, self.half, self.from_y.at[0])

    def line(self):
        self.link(8).wait_recv()
        self.add(self.shard, 0, self.half, self.last_y)
        self.link(9).wait_recv()
        self.add(self.shard, self.half, self.half, self.last_x)

        @pl.when(jnp.logical_not(self.inner))
        def _():
            self.link(10).start()

    def middle(self):
        @pl.when(self.inner)
        def _():
            self.link(10).wait_recv()
            self.add(self.shard, 0, 2 * self.half, self.outer)
            self.link(11).start()

    def spread(self):
        @pl.when(self.inner)
        def _():
            self.link(11).wait_recv()

            def step(index, carry):
                rows = pl.ds(pl.multiple_of(index * 48, 16), 48)
                total = self.total[rows].astype(jnp.float32)
                total = total + self.mine[self.shard, rows].astype(jnp.float32)
                self.total[rows] = total.astype(jnp.bfloat16)
                return carry

            lax.fori_loop(0, 2 * self.half // 48, step, 0)
            self.link(12).start()

    def share(self, place, semaphore):
        @pl.when(jnp.logical_not(self.inner))
        def _():
            self.link(12).wait_recv()

        pltpu.make_async_copy(self.total, place, semaphore).start()
        pltpu.make_async_remote_copy(
            src_ref=self.total, dst_ref=place, send_sem=self.send.at[13],
            recv_sem=self.recv.at[13],
            device_id=device_of(self.z, 1 - self.core, self.shard), device_id_type=MESH,
        ).start()

    def finish(self, place, semaphore):
        pltpu.make_async_copy(self.total, place, semaphore).wait()
        last = pltpu.make_async_remote_copy(
            src_ref=self.total, dst_ref=place, send_sem=self.send.at[13],
            recv_sem=self.recv.at[13],
            device_id=device_of(self.z, 1 - self.core, self.shard), device_id_type=MESH,
        )
        last.wait_send()
        last.wait_recv()
        for index in range(4, 10):
            self.link(index).wait_send()

        @pl.when(jnp.logical_not(self.inner))
        def _():
            self.link(10).wait_send()

        @pl.when(self.inner)
        def _():
            self.link(11).wait_send()
            self.link(12).wait_send()


class Butterfly:
    def __init__(self, held, got, send, recv):
        self.held, self.got, self.send, self.recv = held, got, send, recv
        self.z, self.core, self.shard = seat()

    def copy(self, step):
        z, core, shard = self.z, self.core, self.shard
        where = ((z, core, shard ^ 1), (z, core, shard ^ 2), (z ^ 1, core, shard),
                 (z ^ 2, core, shard), (z, 1 - core, shard))[step]
        rows = pl.ds(0, 2 * VECTORS if step < 2 else VECTORS)
        return pltpu.make_async_remote_copy(
            src_ref=self.held.at[step, rows], dst_ref=self.got.at[step, rows],
            send_sem=self.send.at[step], recv_sem=self.recv.at[step],
            device_id=device_of(*where), device_id_type=MESH,
        )

    def start(self):
        self.copy(0).start()

    def step(self, step):
        self.copy(step).wait_recv()
        rows = slice(0, 2 * VECTORS if step < 2 else VECTORS)
        self.held[step + 1, rows] = self.held[step, rows] + self.got[step, rows]
        if step < 4:
            self.copy(step + 1).start()

    def finish(self):
        for step in range(5):
            self.copy(step).wait_send()


def back_piece(
    head, half, query_ref, key_ref, value_ref, bias_ref, log_ref, grad_ref,
    overlap, key_flip, key_acc, value_acc, query_flip,
):
    mem_valid = lax.broadcasted_iota(jnp.int32, (MEM, 1), 0) < READ
    mask = head_mask(head)
    span = pl.ds(pl.multiple_of(head * HEAD, HEAD), HEAD)

    def block_back(keys, values, bias, valid, queries, grads, log, delta, flipped, rows):
        scores = times_back(keys, queries)
        if bias is not None:
            scores = scores + bias
        chances = jnp.exp(scores - log)
        if valid is not None:
            chances = jnp.where(valid, chances, 0.0)
        slopes = (chances * (times_back(values, grads) - delta)).astype(jnp.bfloat16)
        value_acc[rows] += product(chances.astype(jnp.bfloat16), grads)
        key_acc[rows] += product(slopes, queries)
        return product(flipped, slopes)

    part = pl.ds(pl.multiple_of(half * HALF, HALF), HALF)
    queries = pick(mask, query_ref[part])
    grads = pick(mask, grad_ref[part])
    delta = jnp.sum(overlap[span, part], axis=0, keepdims=True)
    log = log_ref[pl.ds(head, 1), part]
    main_rows = slice(0, 2 * HALF)
    mem_rows = slice(2 * HALF, CONT)
    piece = block_back(
        key_ref[main_rows], value_ref[main_rows], None, None,
        queries, grads, log, delta, key_flip[span, main_rows], main_rows,
    )
    piece += block_back(
        key_ref[mem_rows], value_ref[mem_rows], None, mem_valid,
        queries, grads, log, delta, key_flip[span, mem_rows], mem_rows,
    )
    query_flip[span, part] = piece

    @pl.when(half == 1)
    def _():
        for cont in range(OWN // CLEN):
            rows = slice(CONT + cont * CLEN, CONT + (cont + 1) * CLEN)
            part = slice(cont * CLEN, (cont + 1) * CLEN)
            query_flip[span, HALF + cont * CLEN : HALF + (cont + 1) * CLEN] += block_back(
                key_ref[rows], value_ref[rows], bias_ref[:, part], None,
                queries[part], grads[part], log[:, part], delta[:, part],
                key_flip[span, rows], rows,
            )


def back_kernel(
    act_ref, gdown_ref, first_ref, ginner_ref, mixed_all, gbranch_ref, ghidden_ref, rows_ref,
    qkv_ref, out_ref, sums_ref,
    query_ref, key_ref, value_ref, grad_ref, mixed_ref, log_ref, bias_ref,
    down_out, up_out, out_out, qkv_out, returned_out, grad_prompt, grad_kept, grad_back,
    memory_out, vec_out,
    wide_mine, wide_theirs, wide_got, wide_x, wide_y, wide_lx, wide_ly, wide_outer, wide_total,
    thin_mine, thin_theirs, thin_got, thin_x, thin_y, thin_lx, thin_ly, thin_outer, thin_total,
    pool, rows, dquery, dkey, dvalue, key_acc, value_acc, overlap, key_flip, query_flip,
    partner, ghidden, staged, held, got,
    send, recv, small_send, small_recv, swap_send, swap_recv, local, out_sem,
):
    pair = pl.program_id(0)
    z, core, shard = seat()
    other = 1 - core
    width = rows_ref.shape[1]
    part_rows = width // 4
    low = jnp.bfloat16

    def item(index):
        if isinstance(index, int) and index >= WIDE:
            return thin(index - WIDE)
        return Reduce(
            wide_mine.at[index], wide_theirs.at[index % 2], wide_got.at[index],
            wide_x.at[index], wide_y.at[index], wide_lx.at[index], wide_ly.at[index],
            wide_outer.at[index], wide_total.at[index], send.at[index], recv.at[index],
        )

    def thin(index):
        return Reduce(
            thin_mine.at[index], thin_theirs.at[index % 2], thin_got.at[index],
            thin_x.at[index], thin_y.at[index], thin_lx.at[index], thin_ly.at[index],
            thin_outer.at[index], thin_total.at[index], send.at[WIDE + index],
            recv.at[WIDE + index],
        )

    small = Butterfly(held, got, small_send, small_recv)
    half_hidden = width // 2

    def place(index):
        if index < 2:
            start = core * half_hidden + index * part_rows
            return down_out.at[pl.ds(pl.multiple_of(start, 64), part_rows)]
        if index < 4:
            start = core * (2 * width) + (index - 2) * width
            return up_out.at[:, pl.ds(pl.multiple_of(start, 128), width)]
        if index == 4:
            return out_out.at[:, pl.ds(pl.multiple_of(core * half_hidden, 128), half_hidden)]
        return qkv_out.at[index - 5, core]

    def stage(name, index):
        if name == SHARE:
            item(index).share(place(index), out_sem.at[index])
        else:
            held = item(index)
            (held.chip, held.plane, held.line, held.middle, held.spread)[name]()

    returned = Swap(
        out_ref.at[pl.ds(HALF + OWN // 2, OWN // 2)], returned_out, swap_send.at[0], swap_recv.at[0], z, core, shard ^ 2
    )
    def to_partner(index):
        span = pl.ds(pl.multiple_of(128 * index, 128), 128)
        return Swap(
            pool.at[3, span], partner.at[span], swap_send.at[index + 1], swap_recv.at[index + 1],
            z, core, shard ^ 1,
        )

    cont_back = Swap(
        pool.at[3, pl.ds(2 * 256, 256)], grad_back, swap_send.at[5], swap_recv.at[5],
        z, core, shard ^ 2,
    )

    def load(source, slot, semaphore):
        return pltpu.make_async_copy(source, pool.at[slot], local.at[semaphore])

    def act_chunk(part):
        return load(act_ref.at[:, pl.ds(part * width, width)], part % 2, part % 2)

    def inner_chunk(step):
        half = other if step < 2 else core
        start = pl.multiple_of(half * (2 * width) + (step % 2) * width, 128)
        return load(ginner_ref.at[:, pl.ds(start, width)], step % 2, step % 2)

    def parts_of(target, values):
        for part in range(4):
            target[part] = values[part * part_rows : (part + 1) * part_rows].astype(low)

    load_rows = pltpu.make_async_copy(rows_ref, rows, local.at[4])

    def inner_load(step):
        half = jnp.where(step < 2, other, core)
        start = pl.multiple_of(half * (2 * width) + (step % 2) * width, 128)
        return load(ginner_ref.at[:, pl.ds(start, width)], step % 2, step % 2)

    def act_load(part):
        lanes = pl.ds(pl.multiple_of(part * width, 128), width)
        return load(act_ref.at[:, lanes], part % 2, part % 2)

    def weight_load(index):
        return pltpu.make_async_copy(
            qkv_ref.at[:, pl.ds(index * width, width)],
            pool.at[index, pl.ds(0, width)], local.at[index],
        )

    def down_part(part, carry):
        act_load(part).wait()

        def down_half(side, carry):
            half = jnp.where(side == 0, other, core)
            lanes = pl.ds(pl.multiple_of(half * half_hidden, 128), half_hidden)
            result = outer_sum(pool[part % 2, :, lanes], pool[2]).astype(low)
            for index in range(2):
                piece = result[index * part_rows : (index + 1) * part_rows]

                @pl.when(side == 0)
                def _():
                    wide_theirs[index, part] = piece
                    item(index).give(part)

                @pl.when(side == 1)
                def _():
                    wide_mine[index, part] = piece

            return carry

        lax.fori_loop(0, 2, down_half, 0)

        @pl.when(part < 2)
        def _():
            act_load(part + 2).start()

        @pl.when(part >= 2)
        def _():
            inner_load(part - 2).start()

        return carry

    def up_part(step, carry):
        inner_load(step).wait()
        result = outer_sum(pool[3], pool[step % 2])

        @pl.when(step < 2)
        def _():
            item(step).given()
            parts_of(wide_theirs.at[step], result)
            for part in range(4):
                item(step + 2).give(part)
            inner_load(step + 2).start()

        @pl.when(step >= 2)
        def _():
            parts_of(wide_mine.at[step], result)

        @pl.when((step == 1) | (step == 2))
        def _():
            item(step - 1).chip()

        return carry

    def out_half(side, carry):
        half = jnp.where(side == 0, other, core)
        lanes = pl.ds(pl.multiple_of(half * half_hidden, 128), half_hidden)
        result = outer_sum(pool[2], pool[3, :, lanes])

        @pl.when(side == 0)
        def _():
            parts_of(thin_theirs.at[0], result)
            for part in range(4):
                thin(0).give(part)

        @pl.when(side == 1)
        def _():
            parts_of(thin_mine.at[0], result)

        return carry

    def qkv_part(index):
        def one_half(side, carry):
            half = jnp.where(side == 0, other, core)
            lanes = pl.ds(pl.multiple_of((2 * index + half) * (2 * HEAD), 2 * HEAD), 2 * HEAD)
            query_side = outer_sum(rows[:HALF], dquery[:HALF, lanes])
            query_side += outer_sum(rows[CONT:], dquery[HALF:, lanes])
            both = jnp.concatenate([dkey[:, lanes], dvalue[:, lanes]], axis=1)
            result = jnp.concatenate([query_side, outer_sum(rows[...], both)], axis=1)

            @pl.when(side == 0)
            def _():
                @pl.when(index > 0)
                def _():
                    thin(index - 1).given()

                parts_of(thin_theirs.at[(1 + index) % 2], result)
                for part in range(4):
                    thin(1 + index).give(part)

            @pl.when(side == 1)
            def _():
                parts_of(thin_mine.at[1 + index], result)

            return carry

        lax.fori_loop(0, 2, one_half, 0)

    @pl.when(pair == 0)
    def _():
        act_load(0).start()
        load(gdown_ref, 2, 2).start()
        act_load(1).start()
        load(first_ref, 3, 3).start()
        load_rows.start()
        greet()
        returned.start()
        load(gdown_ref, 2, 2).wait()
        lax.fori_loop(0, 4, down_part, 0)
        load(mixed_all, 2, 2).start()
        load(first_ref, 3, 3).wait()
        lax.fori_loop(0, 4, up_part, 0)
        load(gbranch_ref, 3, 3).start()
        load(mixed_all, 2, 2).wait()
        load(gbranch_ref, 3, 3).wait()
        lax.fori_loop(0, 2, out_half, 0)
        for index in range(3):
            weight_load(index).start()
        load_rows.wait()

    lanes = pl.ds(pl.multiple_of(pair * (2 * HEAD), 2 * HEAD), 2 * HEAD)
    key_flip[...] = flip(key_ref[...])
    overlap[...] = (mixed_ref[...].astype(jnp.float32) * grad_ref[...].astype(jnp.float32)).T
    key_acc[...] = jnp.zeros_like(key_acc)
    value_acc[...] = jnp.zeros_like(value_acc)

    def piece_body(piece, carry):
        back_piece(
            piece // 2, piece % 2, query_ref, key_ref, value_ref, bias_ref, log_ref, grad_ref,
            overlap, key_flip, key_acc, value_acc, query_flip,
        )

        @pl.when(piece == 3)
        def _():
            dquery[:, lanes] = (query_flip[...].T * SCALE).astype(low)
            dkey[:, lanes] = key_acc[...].astype(low)
            dvalue[:, lanes] = value_acc[...].astype(low)

        @pl.when((piece == 3) & (pair % 2 == 1))
        def _():
            qkv_part(pair // 2)

        for number, stages in SLOTS.items():

            @pl.when(pair * 4 + piece == number)
            def _():
                for name, index in stages:
                    stage(name, index)

        return carry

    lax.fori_loop(0, 4, piece_body, 0)

    def hidden_load(step):
        start = pl.multiple_of((5 - step) * 256, 256)
        return pltpu.make_async_copy(
            ghidden_ref.at[pl.ds(start, 256)], ghidden.at[step % 2], local.at[5 + step % 2]
        )

    def staged_store(step):
        slot = step % 2
        return staged.at[slot], local.at[8 + slot]

    def chunk_body(step, carry):
        start = jnp.where(step < 2, HALF + 256 * step, jnp.where(step < 4, CONT, HALF))
        start = jnp.where(step >= 2, start + jnp.where(step % 2 == 0, 256, 0), start)
        start = jnp.where(step >= 4, start - HALF, start)
        span = pl.ds(pl.multiple_of(start, MEM), 256)
        result = times_back(dkey[span], pool[1, :width]) + times_back(dvalue[span], pool[2, :width])

        @pl.when(step < 2)
        def _():
            pool[3, pl.ds(pl.multiple_of(256 * step, 256), 256)] = result.astype(low)

        @pl.when(step == 0)
        def _():
            to_partner(0).start()

        @pl.when(step >= 2)
        def _():
            hidden_load(step).wait()
            mine = pl.ds(pl.multiple_of((5 - step) * 256, 256), 256)
            full = result + (
                ghidden[step % 2] + times_back(dquery[mine], pool[0, :width])
            )

            @pl.when(step == 2)
            def _():
                pool[3, 512:768] = full.astype(low)
                cont_back.start()

            @pl.when(step == 3)
            def _():
                staged[1] = full.astype(low)
                pltpu.make_async_copy(staged.at[1], grad_kept, local.at[9]).start()

            @pl.when(step >= 4)
            def _():
                to_partner(2 * (5 - step)).arrive()
                to_partner(2 * (5 - step) + 1).arrive()

                @pl.when(step == 5)
                def _():
                    pltpu.make_async_copy(staged.at[1], grad_kept, local.at[9]).wait()

                mine = pl.ds(pl.multiple_of((5 - step) * 256, 256), 256)
                staged[step % 2] = (full + partner[mine].astype(jnp.float32)).astype(low)
                pltpu.make_async_copy(
                    staged.at[step % 2], grad_prompt.at[mine], local.at[8 + step % 2]
                ).start()

            @pl.when(step < 4)
            def _():
                hidden_load(step + 2).start()

        for number, stages in TAIL.items():

            @pl.when(step == number)
            def _():
                for name, index in stages:
                    if name == SMALL:
                        small.step(index)
                    elif name == PARTNER:
                        to_partner(index).start()
                    else:
                        stage(name, index)

        return carry

    @pl.when(pair == PAIRS - 1)
    def _():
        hidden_load(2).start()
        hidden_load(3).start()
        sums = pltpu.make_async_copy(sums_ref, held.at[0, pl.ds(0, VECTORS)], local.at[7])
        sums.start()
        for index in range(3):
            weight_load(index).wait()
        sums.wait()
        held[0, 0:1] = jnp.sum(dquery[...].astype(jnp.float32), axis=0, keepdims=True)
        held[0, 1:2] = jnp.sum(dvalue[...].astype(jnp.float32), axis=0, keepdims=True)
        mem_span = slice(2 * HALF, CONT)
        held[0, VECTORS:] = times_back(dkey[mem_span], pool[1, :width]) + times_back(
            dvalue[mem_span], pool[2, :width]
        )
        stage(CHIP, 7)
        small.start()
        lax.fori_loop(0, 6, chunk_body, 0)
        for name, index in LAST:
            if name == SMALL:
                small.step(index)
            else:
                stage(name, index)
        family = shard // 2
        memory_out[family] = held[1, VECTORS:]
        memory_out[1 - family] = got[1, VECTORS:]
        vec_out[...] = held[5, :VECTORS]
        returned.arrive()
        cont_back.arrive()
        for step in (4, 5):
            mine = pl.ds((5 - step) * 256, 256)
            pltpu.make_async_copy(
                staged.at[step % 2], grad_prompt.at[mine], local.at[8 + step % 2]
            ).wait()
        for index in (2, 3, 6, 7):
            item(index).given()
        for index in range(WIDE + NARROW):
            item(index).finish(place(index), out_sem.at[index])
        small.finish()
        for swap in (returned, cont_back, *(to_partner(index) for index in range(4))):
            swap.finish()


def back(
    act, gdown, first, ginner, mixed, gbranch, ghidden, rows, qkv, out_taken, sums,
    query, key, value, grads, log, bias,
):
    width = rows.shape[1]
    low = jnp.bfloat16
    wide = jnp.float32

    def block(count):
        return pl.BlockSpec((count, 2 * HEAD), lambda pair: (0, pair))

    dma = pltpu.SemaphoreType.DMA
    part = width // 4

    def buffers(count, columns):
        return [
            pltpu.VMEM((count, 4, part, columns), low),
            pltpu.VMEM((2, 4, part, columns), low),
            pltpu.VMEM((count, 4, part, columns), low),
            pltpu.VMEM((count, 2, part // 2, columns), low),
            pltpu.VMEM((count, 2, part // 2, columns), low),
            pltpu.VMEM((count, part // 2, columns), low),
            pltpu.VMEM((count, part // 2, columns), low),
            pltpu.VMEM((count, part, columns), low),
            pltpu.VMEM((count, part, columns), low),
        ]

    shape = jax.ShapeDtypeStruct
    return pl.pallas_call(
        back_kernel,
        grid=(PAIRS,),
        in_specs=[WHERE] * 11
        + [
            block(QROWS), block(KEYS), block(KEYS), block(QROWS), block(QROWS),
            pl.BlockSpec((None, 2, QROWS), lambda pair: (pair, 0, 0)),
            pl.BlockSpec((CLEN, OWN), lambda pair: (0, 0)),
        ],
        out_specs=[WHERE] * 8
        + [
            pl.BlockSpec((2, MEM, width), lambda pair: (0, 0, 0)),
            pl.BlockSpec((VECTORS, width), lambda pair: (0, 0)),
        ],
        out_shape=[
            shape((width, width), low),
            shape((part, 4 * width), low),
            shape((part, width), low),
            shape((3, 2, part, width // 2), low),
            shape((OWN // 2, width), low),
            shape((HALF, width), low),
            shape((OWN // 2, width), low),
            shape((OWN // 2, width), low),
            shape((2, MEM, width), wide),
            shape((VECTORS, width), wide),
        ],
        scratch_shapes=buffers(WIDE, width)
        + buffers(NARROW, width // 2)
        + [
            pltpu.VMEM((4, QROWS, width), low),
            pltpu.VMEM((KEYS, width), low),
            pltpu.VMEM((QROWS, width), low),
            pltpu.VMEM((KEYS, width), low),
            pltpu.VMEM((KEYS, width), low),
            pltpu.VMEM((KEYS, 2 * HEAD), wide),
            pltpu.VMEM((KEYS, 2 * HEAD), wide),
            pltpu.VMEM((2 * HEAD, QROWS), wide),
            pltpu.VMEM((2 * HEAD, KEYS), low),
            pltpu.VMEM((2 * HEAD, QROWS), wide),
            pltpu.VMEM((HALF, width), low),
            pltpu.VMEM((2, 256, width), wide),
            pltpu.VMEM((2, 256, width), low),
            pltpu.VMEM((6, 2 * VECTORS, width), wide),
            pltpu.VMEM((5, 2 * VECTORS, width), wide),
            dma((WIDE + NARROW, SEND + 1)),
            dma((WIDE + NARROW, SEND + 1)),
            dma((5,)),
            dma((5,)),
            dma((6,)),
            dma((6,)),
            dma((10,)),
            dma((WIDE + NARROW,)),
        ],
        compiler_params=pltpu.CompilerParams(
            vmem_limit_bytes=67043328, collective_id=1, has_side_effects=True
        ),
        name="back",
    )(
        act, gdown, first, ginner, mixed, gbranch, ghidden, rows, qkv, out_taken, sums,
        query, key, value, grads, mixed, log, bias,
    )


def cont_ranks(owner_ref, shard):
    prompt_of = shard // 2
    conts = OWN // CLEN
    place = []
    before = jnp.int32(0)
    for cont in range(conts):
        owned = (owner_ref[0, shard * conts + cont] == prompt_of).astype(jnp.int32)
        place.append(jnp.where(owned == 1, before, 2 + cont - before))
        before = before + owned
    order = []
    for position in range(conts):
        found = jnp.int32(0)
        for cont in range(conts):
            found = found + jnp.where(place[cont] == position, cont, 0)
        order.append(found)
    return place, order


def block_of(index):
    return pl.ds(pl.multiple_of(index * CLEN, CLEN), CLEN)


def prepare_kernel(
    owner_ref, length_ref, follow_ref, cotan_ref, memory_ref, query_ref, key_ref, value_ref,
    out_ref, up_ref, *refs,
):
    vectors = refs[:9]
    (
        qkv, wide, vec, kept, sent, memory, kept_cot, sent_cot, bias,
    ) = refs[9:]
    shard = lax.axis_index("shard")
    across = shard ^ 2
    conts = OWN // CLEN
    width = query_ref.shape[1]
    _, order = cont_ranks(owner_ref, shard)
    _, order_across = cont_ranks(owner_ref, across)
    for index in range(2):
        span = slice(index * CLEN, (index + 1) * CLEN)
        kept[span] = follow_ref[0, block_of(order[index])]
        sent[span] = follow_ref[0, block_of(order[2 + index])]
        kept_cot[span] = cotan_ref[0, block_of(order[index])]
        sent_cot[span] = cotan_ref[0, block_of(order[2 + index])]
    position = lax.broadcasted_iota(jnp.int32, (CLEN, CLEN), 0)
    for index in range(conts):
        if index < 2:
            length = length_ref[0, shard * conts + order[index]]
        else:
            length = length_ref[0, across * conts + order_across[index]]
        valid = (position < length) | (position >= CLEN - WRITE)
        bias[:, index * CLEN : (index + 1) * CLEN] = jnp.where(valid, 0.0, NEGATIVE)
    memory[...] = jnp.zeros_like(memory)
    memory[:READ] = memory_ref[0, shard // 2]
    qkv[:, :width] = query_ref[...]
    qkv[:, width : 2 * width] = key_ref[...]
    qkv[:, 2 * width :] = value_ref[...]
    wide[:, :width] = out_ref[...]
    wide[:, width:] = up_ref[...]
    vec[...] = jnp.zeros_like(vec)
    for index, vector in enumerate(vectors):
        vec[index : index + 1, : vector.shape[1]] = vector[...]


def prepare(owner, length, follow, cotan, memory, query, key, value, out, up, vectors):
    low = jnp.bfloat16
    width = query.shape[1]
    share = query.shape[0]
    shape = jax.ShapeDtypeStruct
    half = shape((OWN // 2, width), low)
    inside = pl.BlockSpec(memory_space=pltpu.VMEM)
    scalars = pl.BlockSpec(memory_space=pltpu.SMEM)
    return pl.pallas_call(
        prepare_kernel,
        in_specs=[scalars] * 2 + [inside] * 17,
        out_specs=[inside] * 9,
        out_shape=[
            shape((share, 3 * width), low), shape((share, 5 * width), low),
            shape((VECTORS, 2 * HEAD), low), half, half, shape((MEM, width), low), half, half,
            shape((CLEN, OWN), jnp.float32),
        ],
        name="prepare",
    )(
        owner, length, follow, cotan, memory, query, key, value, out, up,
        *(vector[None] for vector in vectors),
    )


def finish_kernel(
    owner_ref, output_ref, returned_ref, kept_grad, back_grad, down_ref, up_ref, out_ref, qkv_ref,
    memory_ref, vec_ref,
    prompt_out, follow_out, follow_grad, memory_grad, query_sum, key_sum, value_sum, out_sum,
    up_sum, down_sum, *vectors,
):
    shard = lax.axis_index("shard")
    wide = jnp.float32
    width = down_ref.shape[1]
    part = width // 4
    place, _ = cont_ranks(owner_ref, shard)
    prompt_out[0] = output_ref[:HALF]
    for cont, position in enumerate(place):
        span = slice(cont * CLEN, (cont + 1) * CLEN)
        here = block_of(jnp.where(position < 2, position, 0))
        there = block_of(jnp.where(position < 2, 0, position - 2))
        kept = position < 2

        @pl.when(kept)
        def _():
            follow_out[0, span] = output_ref[pl.ds(HALF + here.start, CLEN)]
            follow_grad[0, span] = kept_grad[here]

        @pl.when(jnp.logical_not(kept))
        def _():
            follow_out[0, span] = returned_ref[there]
            follow_grad[0, span] = back_grad[there]

    memory_grad[0] = memory_ref[:, :READ].astype(jnp.bfloat16)
    down_sum[...] = down_ref[...].astype(wide)
    up_sum[...] = up_ref[...].astype(wide)
    out_sum[...] = out_ref[...].astype(wide)
    for index in range(3):
        for side in range(2):
            lanes = slice((2 * index + side) * 2 * HEAD, (2 * index + side + 1) * 2 * HEAD)
            for number, target in enumerate((query_sum, key_sum, value_sum)):
                source = slice(number * 2 * HEAD, (number + 1) * 2 * HEAD)
                target[:, lanes] = qkv_ref[index, side, :, source].astype(wide)
    for index in range(8):
        row = vec_ref[index : index + 1]
        total = jnp.zeros((1, part), wide)
        for quarter in range(4):
            total += jnp.where(shard == quarter, row[:, quarter * part : (quarter + 1) * part], 0.0)
        vectors[index][...] = total.reshape(part)
    total = jnp.zeros((1, width), wide)
    for quarter in range(4):
        total += jnp.where(shard == quarter, vec_ref[8 + quarter : 9 + quarter], 0.0)
    vectors[8][...] = total.reshape(width)


def finish(owner, output, returned, kept, back_grad, down, up, out, qkv, memory, vec):
    low = jnp.bfloat16
    wide = jnp.float32
    shape = jax.ShapeDtypeStruct
    width = down.shape[1]
    part = width // 4
    inside = pl.BlockSpec(memory_space=pltpu.VMEM)
    square = shape((part, width), wide)

    def whole(array):
        return pl.BlockSpec(array.shape, lambda step: (0,) * array.ndim)

    return pl.pallas_call(
        finish_kernel,
        grid=(1,),
        in_specs=[pl.BlockSpec(memory_space=pltpu.SMEM)]
        + [
            whole(array)
            for array in (output, returned, kept, back_grad, down, up, out, qkv, memory, vec)
        ],
        out_specs=[inside] * 19,
        out_shape=[
            shape((1, HALF, width), low), shape((1, OWN, width), low), shape((1, OWN, width), low),
            shape((1, 2, READ, width), low), square, square, square, square,
            shape((part, 4 * width), wide), shape((width, width), wide),
        ]
        + [shape((part,), wide)] * 8
        + [shape((width,), wide)],
        compiler_params=pltpu.CompilerParams(vmem_limit_bytes=67043328),
        name="finish",
    )(owner, output, returned, kept, back_grad, down, up, out, qkv, memory, vec)


def body_pairs(
    prompt_rows, follow_rows, memory_rows, follow_owner, follow_length,
    query_weight, key_weight, value_weight, out_weight, query_bias, value_bias, out_bias,
    first_gain, first_shift, up_weight, up_bias, down_weight, down_bias,
    second_gain, second_shift, prompt_cotan, follow_cotan,
):
    qkv, wide, vec, kept, sent, memory, kept_cot, sent_cot, bias = prepare(
        follow_owner, follow_length, follow_rows, follow_cotan, memory_rows,
        query_weight, key_weight, value_weight, out_weight, up_weight,
        (
            query_bias, value_bias, out_bias, first_gain, first_shift, down_bias,
            second_gain, second_shift, up_bias,
        ),
    )
    (
        qkv_mat, _, _, _, key_rows,
        output, activated, first_low, grad_down, grad_inner, grad_branch, grad_mixed, grad_hidden,
        mixed, log, query_low, key_low, value_low, sums,
    ) = front(
        qkv, wide, down_weight, vec, prompt_rows[0], kept, sent, memory, prompt_cotan[0],
        kept_cot, sent_cot, bias,
    )
    (
        down_sum, up_sum, out_sum, qkv_sum, returned_out, grad_prompt, grad_kept, returned_grad,
        memory_sum, sums,
    ) = back(
        activated, grad_down, first_low, grad_inner, mixed, grad_branch, grad_hidden, key_rows,
        qkv_mat, output, sums,
        query_low, key_low, value_low, grad_mixed, log, bias,
    )
    (
        prompt_out, follow_out, follow_grad, grad_memory, query_sum, key_sum, value_sum, out_sum,
        up_sum, down_sum, *vectors,
    ) = finish(
        follow_owner, output, returned_out, grad_kept, returned_grad, down_sum, up_sum, out_sum,
        qkv_sum, memory_sum, sums,
    )
    return (
        prompt_out, follow_out, grad_prompt[None], follow_grad, grad_memory,
        query_sum, key_sum, value_sum, out_sum, vectors[0], vectors[1], vectors[2], vectors[3],
        vectors[4], up_sum, vectors[8], down_sum, vectors[5], vectors[6], vectors[7],
    )


def solution(mesh):
    return jax.shard_map(
        body_pairs if pairs_fit(mesh) else body_any,
        mesh=mesh,
        in_specs=(
            P("grp", "shard", None),
            P("grp", "shard", None),
            P("grp", None, None, None),
            P("grp", None),
            P("grp", None),
            P(("grp", "shard"), None),
            P(("grp", "shard"), None),
            P(("grp", "shard"), None),
            P(("grp", "shard"), None),
            P(("grp", "shard")),
            P(("grp", "shard")),
            P(("grp", "shard")),
            P(("grp", "shard")),
            P(("grp", "shard")),
            P(("grp", "shard"), None),
            P(("grp", "shard")),
            P(("grp", "shard"), None),
            P(("grp", "shard")),
            P(("grp", "shard")),
            P(("grp", "shard")),
            P("grp", "shard", None),
            P("grp", "shard", None),
        ),
        out_specs=(
            P("grp", "shard", None),
            P("grp", "shard", None),
            P("grp", "shard", None),
            P("grp", "shard", None),
            P("grp", None, None, None),
            P("shard", None),
            P("shard", None),
            P("shard", None),
            P("shard", None),
            P("shard"),
            P("shard"),
            P("shard"),
            P("shard"),
            P("shard"),
            P("shard", None),
            P("shard"),
            P("shard", None),
            P("shard"),
            P("shard"),
            P("shard"),
        ),
        check_vma=False,
    )
```

```python
import jax
import jax.numpy as jnp
from jax import lax
from jax.experimental import pallas as pl
from jax.experimental.pallas import tpu as pltpu
from jax.sharding import PartitionSpec as P

HEADS = 12
HEAD = 64
READ = 10
WRITE = 10
PLEN = 1024
CLEN = 128
CONTS_PER = 8


EPSILON = 1e-12
SCALE = 0.125
NEGATIVE = -1e30
ROOT_HALF = 0.7071067811865476
ROOT_GAUSS = 0.3989422804014327


def product(left, right):
    return jnp.dot(left, right, preferred_element_type=jnp.float32)


def times_back(left, right):
    return lax.dot_general(
        left, right, (((1,), (1,)), ((), ())), preferred_element_type=jnp.float32
    )


def outer_sum(left, right):
    return lax.dot_general(
        left, right, (((0,), (0,)), ((), ())), preferred_element_type=jnp.float32
    )


def column_sum(values):
    return jnp.sum(values.astype(jnp.float32), axis=0)


def layer_norm(hidden, gain, shift):
    center = hidden - jnp.mean(hidden, axis=-1, keepdims=True)
    inverse = lax.rsqrt(jnp.mean(center * center, axis=-1, keepdims=True) + EPSILON)
    normed = center * inverse
    return (normed * gain.astype(jnp.float32) + shift.astype(jnp.float32), normed, inverse)


def norm_back(grad_normed, normed, inverse):
    centered = grad_normed - jnp.mean(grad_normed, axis=-1, keepdims=True)
    return inverse * (centered - normed * jnp.mean(grad_normed * normed, axis=-1, keepdims=True))


def gelu_exact(hidden):
    return 0.5 * hidden * (1.0 + lax.erf(hidden * ROOT_HALF))


def gelu_slope(hidden):
    return (
        0.5 * (1.0 + lax.erf(hidden * ROOT_HALF))
        + hidden * jnp.exp(-0.5 * hidden * hidden) * ROOT_GAUSS
    )


def split_heads(values):
    return values.reshape(values.shape[0], values.shape[1], HEADS, HEAD)


def block_scores(queries, keys, valid):
    scores = (
        jnp.einsum(
            "nqhd,nkhd->nhqk",
            split_heads(queries),
            split_heads(keys),
            preferred_element_type=jnp.float32,
        )
        * SCALE
    )
    return jnp.where(valid[:, None, None, :], scores, NEGATIVE)


def attend_forward(queries, keys, values, valid):
    scores = block_scores(queries, keys, valid)
    maximum = jnp.max(scores, axis=-1, keepdims=True)
    powers = jnp.exp(scores - maximum)
    totals = jnp.sum(powers, axis=-1, keepdims=True)
    chances = (powers / totals).astype(jnp.bfloat16)
    result = jnp.einsum(
        "nhqk,nkhd->nqhd", chances, split_heads(values), preferred_element_type=jnp.float32
    )
    return (result.reshape(-1, queries.shape[2]), maximum + jnp.log(totals))


def attend_backward(queries, keys, values, valid, logsum, grad_out):
    width = queries.shape[2]
    scores = block_scores(queries, keys, valid)
    chances = jnp.exp(scores - logsum)
    grad_heads = split_heads(grad_out)
    grad_chance = jnp.einsum(
        "nqhd,nkhd->nhqk", grad_heads, split_heads(values), preferred_element_type=jnp.float32
    )
    inner = jnp.sum(chances * grad_chance, axis=-1, keepdims=True)
    grad_score = (chances * (grad_chance - inner)).astype(jnp.bfloat16)
    grad_query = (
        jnp.einsum(
            "nhqk,nkhd->nqhd", grad_score, split_heads(keys), preferred_element_type=jnp.float32
        )
        * SCALE
    )
    grad_key = (
        jnp.einsum(
            "nhqk,nqhd->nkhd", grad_score, split_heads(queries), preferred_element_type=jnp.float32
        )
        * SCALE
    )
    grad_value = jnp.einsum(
        "nhqk,nqhd->nkhd",
        chances.astype(jnp.bfloat16),
        grad_heads,
        preferred_element_type=jnp.float32,
    )
    span = keys.shape[1]
    return (
        grad_query.reshape(-1, width),
        grad_key.reshape(keys.shape[0], span, width),
        grad_value.reshape(keys.shape[0], span, width),
    )


def body_any(
    prompt_rows,
    follow_rows,
    memory_rows,
    follow_owner,
    follow_length,
    query_weight,
    key_weight,
    value_weight,
    out_weight,
    query_bias,
    value_bias,
    out_bias,
    first_gain,
    first_shift,
    up_weight,
    up_bias,
    down_weight,
    down_bias,
    second_gain,
    second_shift,
    prompt_cotan,
    follow_cotan,
):
    (
        query_mat,
        key_mat,
        value_mat,
        out_mat,
        query_add,
        value_add,
        out_add,
        gain_one,
        shift_one,
        up_mat,
        up_add,
        down_mat,
        down_add,
        gain_two,
        shift_two,
    ) = (
        lax.all_gather(query_weight, ("grp", "shard"), axis=0, tiled=True),
        lax.all_gather(key_weight, ("grp", "shard"), axis=0, tiled=True),
        lax.all_gather(value_weight, ("grp", "shard"), axis=0, tiled=True),
        lax.all_gather(out_weight, ("grp", "shard"), axis=0, tiled=True),
        lax.all_gather(query_bias, ("grp", "shard"), axis=0, tiled=True),
        lax.all_gather(value_bias, ("grp", "shard"), axis=0, tiled=True),
        lax.all_gather(out_bias, ("grp", "shard"), axis=0, tiled=True),
        lax.all_gather(first_gain, ("grp", "shard"), axis=0, tiled=True),
        lax.all_gather(first_shift, ("grp", "shard"), axis=0, tiled=True),
        lax.all_gather(up_weight, ("grp", "shard"), axis=0, tiled=True),
        lax.all_gather(up_bias, ("grp", "shard"), axis=0, tiled=True),
        lax.all_gather(down_weight, ("grp", "shard"), axis=0, tiled=True),
        lax.all_gather(down_bias, ("grp", "shard"), axis=0, tiled=True),
        lax.all_gather(second_gain, ("grp", "shard"), axis=0, tiled=True),
        lax.all_gather(second_shift, ("grp", "shard"), axis=0, tiled=True),
    )
    shard_index = lax.axis_index("shard")
    prompt = prompt_rows[0]
    follow = follow_rows[0]
    p_count = prompt.shape[0]
    f_count = follow.shape[0]
    width = prompt.shape[1]
    families = memory_rows.shape[1]
    all_rows = jnp.concatenate([prompt, follow], axis=0)
    memory_flat = memory_rows[0].reshape(families * READ, width)
    query_low = (product(all_rows, query_mat) + query_add.astype(jnp.float32)).astype(jnp.bfloat16)
    key_low = product(all_rows, key_mat).astype(jnp.bfloat16)
    value_low = (product(all_rows, value_mat) + value_add.astype(jnp.float32)).astype(jnp.bfloat16)
    mem_key = product(memory_flat, key_mat).astype(jnp.bfloat16).reshape(families, READ, width)
    mem_value = (
        (product(memory_flat, value_mat) + value_add.astype(jnp.float32))
        .astype(jnp.bfloat16)
        .reshape(families, READ, width)
    )
    half_prompt = PLEN // 2
    per_block = CONTS_PER // 2
    prompt_blocks = p_count // half_prompt
    conts_here = f_count // CLEN
    positions = jnp.arange(CLEN)
    open_span = jnp.ones((per_block, READ + PLEN), dtype=bool)
    owner_row = follow_owner[0]
    length_row = follow_length[0]
    prompt_keys, prompt_values = (
        lax.all_gather(key_low[:p_count], "shard", axis=0, tiled=True),
        lax.all_gather(value_low[:p_count], "shard", axis=0, tiled=True),
    )
    key_table = prompt_keys.reshape(families, PLEN, width)
    value_table = prompt_values.reshape(families, PLEN, width)

    def prompt_inputs(block):
        start = block * half_prompt
        family = (shard_index * p_count + start) // PLEN
        keys = jnp.concatenate([mem_key[family], key_table[family]], axis=0)[None]
        values = jnp.concatenate([mem_value[family], value_table[family]], axis=0)[None]
        valid = jnp.ones((1, READ + PLEN), dtype=bool)
        return (query_low[start : start + half_prompt][None], keys, values, valid, family)

    def follow_inputs(block):
        first_row = p_count + block * per_block * CLEN
        chosen = shard_index * conts_here + block * per_block + jnp.arange(per_block)
        owners = owner_row[chosen]
        lengths = length_row[chosen]
        own_keys = key_low[first_row : first_row + per_block * CLEN].reshape(per_block, CLEN, width)
        own_values = value_low[first_row : first_row + per_block * CLEN].reshape(
            per_block, CLEN, width
        )
        keys = jnp.concatenate([mem_key[owners], key_table[owners], own_keys], axis=1)
        values = jnp.concatenate([mem_value[owners], value_table[owners], own_values], axis=1)
        own_valid = (positions[None, :] < lengths[:, None]) | (positions[None, :] >= CLEN - WRITE)
        valid = jnp.concatenate([open_span, own_valid], axis=1)
        queries = query_low[first_row : first_row + per_block * CLEN].reshape(
            per_block, CLEN, width
        )
        return (queries, keys, values, valid, owners)

    attended = []
    saved = []
    block = 0
    queries, keys, values, valid, family = prompt_inputs(block)
    result, logsum = attend_forward(queries, keys, values, valid)
    attended.append(result)
    saved.append(logsum)
    block = 0
    queries, keys, values, valid, owners = follow_inputs(block)
    result, logsum = attend_forward(queries, keys, values, valid)
    attended.append(result)
    saved.append(logsum)
    mixed = jnp.concatenate(attended, axis=0).astype(jnp.bfloat16)
    branch = product(mixed, out_mat) + out_add.astype(jnp.float32)
    first, normed_one, inverse_one = layer_norm(
        all_rows.astype(jnp.float32) + branch, gain_one, shift_one
    )
    first_low = first.astype(jnp.bfloat16)
    inner = product(first_low, up_mat) + up_add.astype(jnp.float32)
    activated = gelu_exact(inner).astype(jnp.bfloat16)
    second = product(activated, down_mat) + down_add.astype(jnp.float32)
    output, normed_two, inverse_two = layer_norm(first + second, gain_two, shift_two)
    output = output.astype(jnp.bfloat16)
    (
        query_mat,
        key_mat,
        value_mat,
        out_mat,
        query_add,
        value_add,
        out_add,
        gain_one,
        shift_one,
        up_mat,
        up_add,
        down_mat,
        down_add,
        gain_two,
        shift_two,
    ) = (
        lax.all_gather(query_weight, ("grp", "shard"), axis=0, tiled=True),
        lax.all_gather(key_weight, ("grp", "shard"), axis=0, tiled=True),
        lax.all_gather(value_weight, ("grp", "shard"), axis=0, tiled=True),
        lax.all_gather(out_weight, ("grp", "shard"), axis=0, tiled=True),
        lax.all_gather(query_bias, ("grp", "shard"), axis=0, tiled=True),
        lax.all_gather(value_bias, ("grp", "shard"), axis=0, tiled=True),
        lax.all_gather(out_bias, ("grp", "shard"), axis=0, tiled=True),
        lax.all_gather(first_gain, ("grp", "shard"), axis=0, tiled=True),
        lax.all_gather(first_shift, ("grp", "shard"), axis=0, tiled=True),
        lax.all_gather(up_weight, ("grp", "shard"), axis=0, tiled=True),
        lax.all_gather(up_bias, ("grp", "shard"), axis=0, tiled=True),
        lax.all_gather(down_weight, ("grp", "shard"), axis=0, tiled=True),
        lax.all_gather(down_bias, ("grp", "shard"), axis=0, tiled=True),
        lax.all_gather(second_gain, ("grp", "shard"), axis=0, tiled=True),
        lax.all_gather(second_shift, ("grp", "shard"), axis=0, tiled=True),
    )
    cotangent = jnp.concatenate([prompt_cotan[0], follow_cotan[0]], axis=0).astype(jnp.float32)
    grad_gain_two = jnp.sum(cotangent * normed_two, axis=0)
    grad_shift_two = jnp.sum(cotangent, axis=0)
    grad_mid = norm_back(cotangent * gain_two.astype(jnp.float32), normed_two, inverse_two)
    grad_down = grad_mid.astype(jnp.bfloat16)
    grad_down_mat = outer_sum(activated, grad_down)
    grad_down_add = column_sum(grad_down)
    grad_inner = (times_back(grad_down, down_mat) * gelu_slope(inner)).astype(jnp.bfloat16)
    grad_up_mat = outer_sum(first_low, grad_inner)
    grad_up_add = column_sum(grad_inner)
    grad_first = grad_mid + times_back(grad_inner, up_mat)
    grad_gain_one = jnp.sum(grad_first * normed_one, axis=0)
    grad_shift_one = jnp.sum(grad_first, axis=0)
    grad_hidden = norm_back(grad_first * gain_one.astype(jnp.float32), normed_one, inverse_one)
    grad_branch = grad_hidden.astype(jnp.bfloat16)
    grad_out_mat = outer_sum(mixed, grad_branch)
    grad_out_add = column_sum(grad_branch)
    grad_mixed = times_back(grad_branch, out_mat).astype(jnp.bfloat16)
    mem_key_acc = jnp.zeros((families, READ, width), jnp.float32)
    mem_value_acc = jnp.zeros((families, READ, width), jnp.float32)
    prompt_key_acc = jnp.zeros((families, PLEN, width), jnp.float32)
    prompt_value_acc = jnp.zeros((families, PLEN, width), jnp.float32)
    block = 0
    queries, keys, values, valid, family = prompt_inputs(block)
    start = block * half_prompt
    grad_query, grad_key, grad_value = attend_backward(
        queries, keys, values, valid, saved[block], grad_mixed[start : start + half_prompt][None]
    )
    query_parts = grad_query
    mem_key_acc = mem_key_acc.at[family].add(grad_key[0, :READ])
    mem_value_acc = mem_value_acc.at[family].add(grad_value[0, :READ])
    prompt_key_acc = prompt_key_acc.at[family].add(grad_key[0, READ:])
    prompt_value_acc = prompt_value_acc.at[family].add(grad_value[0, READ:])
    prompt_query_low = query_parts.astype(jnp.bfloat16)
    block = 0
    queries, keys, values, valid, owners = follow_inputs(block)
    first_row = p_count + block * per_block * CLEN
    grad_slice = grad_mixed[first_row : first_row + per_block * CLEN].reshape(
        per_block, CLEN, width
    )
    grad_query, grad_key, grad_value = attend_backward(
        queries, keys, values, valid, saved[prompt_blocks + block], grad_slice
    )
    mem_key_acc = mem_key_acc.at[owners].add(grad_key[:, :READ])
    mem_value_acc = mem_value_acc.at[owners].add(grad_value[:, :READ])
    prompt_key_acc = prompt_key_acc.at[owners].add(grad_key[:, READ : READ + PLEN])
    prompt_value_acc = prompt_value_acc.at[owners].add(grad_value[:, READ : READ + PLEN])
    own_key_parts = grad_key[:, READ + PLEN :].reshape(-1, width)
    own_value_parts = grad_value[:, READ + PLEN :].reshape(-1, width)
    prompt_key_grad, prompt_value_grad = (
        lax.psum_scatter(
            prompt_key_acc.reshape(families * PLEN, width).astype(jnp.bfloat16),
            "shard",
            scatter_dimension=0,
            tiled=True,
        ).astype(jnp.float32),
        lax.psum_scatter(
            prompt_value_acc.reshape(families * PLEN, width).astype(jnp.bfloat16),
            "shard",
            scatter_dimension=0,
            tiled=True,
        ).astype(jnp.float32),
    )
    follow_query_low = grad_query.astype(jnp.bfloat16)
    follow_key_low = own_key_parts.astype(jnp.bfloat16)
    follow_value_low = own_value_parts.astype(jnp.bfloat16)
    mem_key_sum, mem_value_sum = (
        lax.psum(mem_key_acc.astype(jnp.bfloat16), "shard").astype(jnp.float32),
        lax.psum(mem_value_acc.astype(jnp.bfloat16), "shard").astype(jnp.float32),
    )
    grad_query_low = jnp.concatenate([prompt_query_low, follow_query_low], axis=0)
    grad_key_low = jnp.concatenate([prompt_key_grad.astype(jnp.bfloat16), follow_key_low], axis=0)
    grad_value_low = jnp.concatenate(
        [prompt_value_grad.astype(jnp.bfloat16), follow_value_low], axis=0
    )
    mem_key_low = mem_key_sum.astype(jnp.bfloat16).reshape(families * READ, width)
    mem_value_low = mem_value_sum.astype(jnp.bfloat16).reshape(families * READ, width)
    grad_rows_all = (
        grad_hidden
        + times_back(grad_query_low, query_mat)
        + times_back(grad_key_low, key_mat)
        + times_back(grad_value_low, value_mat)
    ).astype(jnp.bfloat16)
    grad_memory = (
        (times_back(mem_key_low, key_mat) + times_back(mem_value_low, value_mat))
        .astype(jnp.bfloat16)
        .reshape(1, families, READ, width)
    )
    leader = (shard_index == 0).astype(jnp.float32)
    grad_query_mat = outer_sum(all_rows, grad_query_low)
    grad_query_add = column_sum(grad_query_low)
    grad_key_mat = outer_sum(all_rows, grad_key_low) + leader * outer_sum(memory_flat, mem_key_low)
    grad_value_mat = outer_sum(all_rows, grad_value_low) + leader * outer_sum(
        memory_flat, mem_value_low
    )
    grad_value_add = column_sum(grad_value_low) + leader * column_sum(mem_value_low)
    pieces = (
        lax.psum_scatter(
            grad_query_mat.astype(jnp.bfloat16), "shard", scatter_dimension=0, tiled=True
        ).astype(jnp.float32),
        lax.psum_scatter(
            grad_key_mat.astype(jnp.bfloat16), "shard", scatter_dimension=0, tiled=True
        ).astype(jnp.float32),
        lax.psum_scatter(
            grad_value_mat.astype(jnp.bfloat16), "shard", scatter_dimension=0, tiled=True
        ).astype(jnp.float32),
        lax.psum_scatter(
            grad_out_mat.astype(jnp.bfloat16), "shard", scatter_dimension=0, tiled=True
        ).astype(jnp.float32),
        lax.psum_scatter(
            grad_query_add.astype(jnp.bfloat16), "shard", scatter_dimension=0, tiled=True
        ).astype(jnp.float32),
        lax.psum_scatter(
            grad_value_add.astype(jnp.bfloat16), "shard", scatter_dimension=0, tiled=True
        ).astype(jnp.float32),
        lax.psum_scatter(
            grad_out_add.astype(jnp.bfloat16), "shard", scatter_dimension=0, tiled=True
        ).astype(jnp.float32),
        lax.psum_scatter(
            grad_gain_one.astype(jnp.bfloat16), "shard", scatter_dimension=0, tiled=True
        ).astype(jnp.float32),
        lax.psum_scatter(
            grad_shift_one.astype(jnp.bfloat16), "shard", scatter_dimension=0, tiled=True
        ).astype(jnp.float32),
        lax.psum_scatter(
            grad_up_mat.astype(jnp.bfloat16), "shard", scatter_dimension=0, tiled=True
        ).astype(jnp.float32),
        lax.psum_scatter(
            grad_up_add.astype(jnp.bfloat16), "shard", scatter_dimension=0, tiled=True
        ).astype(jnp.float32),
        lax.psum_scatter(
            grad_down_mat.astype(jnp.bfloat16), "shard", scatter_dimension=0, tiled=True
        ).astype(jnp.float32),
        lax.psum_scatter(
            grad_down_add.astype(jnp.bfloat16), "shard", scatter_dimension=0, tiled=True
        ).astype(jnp.float32),
        lax.psum_scatter(
            grad_gain_two.astype(jnp.bfloat16), "shard", scatter_dimension=0, tiled=True
        ).astype(jnp.float32),
        lax.psum_scatter(
            grad_shift_two.astype(jnp.bfloat16), "shard", scatter_dimension=0, tiled=True
        ).astype(jnp.float32),
    )
    summed = (
        lax.psum(pieces[0].astype(jnp.bfloat16), "grp").astype(jnp.float32),
        lax.psum(pieces[1].astype(jnp.bfloat16), "grp").astype(jnp.float32),
        lax.psum(pieces[2].astype(jnp.bfloat16), "grp").astype(jnp.float32),
        lax.psum(pieces[3].astype(jnp.bfloat16), "grp").astype(jnp.float32),
        lax.psum(pieces[4].astype(jnp.bfloat16), "grp").astype(jnp.float32),
        lax.psum(pieces[5].astype(jnp.bfloat16), "grp").astype(jnp.float32),
        lax.psum(pieces[6].astype(jnp.bfloat16), "grp").astype(jnp.float32),
        lax.psum(pieces[7].astype(jnp.bfloat16), "grp").astype(jnp.float32),
        lax.psum(pieces[8].astype(jnp.bfloat16), "grp").astype(jnp.float32),
        lax.psum(pieces[9].astype(jnp.bfloat16), "grp").astype(jnp.float32),
        lax.psum(pieces[10].astype(jnp.bfloat16), "grp").astype(jnp.float32),
        lax.psum(pieces[11].astype(jnp.bfloat16), "grp").astype(jnp.float32),
        lax.psum(pieces[12].astype(jnp.bfloat16), "grp").astype(jnp.float32),
        lax.psum(pieces[13].astype(jnp.bfloat16), "grp").astype(jnp.float32),
        lax.psum(pieces[14].astype(jnp.bfloat16), "grp").astype(jnp.float32),
    )
    return (
        output[:p_count][None],
        output[p_count:][None],
        grad_rows_all[:p_count][None],
        grad_rows_all[p_count:][None],
        grad_memory,
        summed[0],
        summed[1],
        summed[2],
        summed[3],
        summed[4],
        summed[5],
        summed[6],
        summed[7],
        summed[8],
        summed[9],
        summed[10],
        summed[11],
        summed[12],
        summed[13],
        summed[14],
    )


MEM = 16
HALF = PLEN // 2
OWN = 512
CONT = HALF + HALF + MEM
KEYS = CONT + OWN
QROWS = HALF + OWN
PAIRS = HEADS // 2
NAMES = ("grp", "shard")


def pairs_fit(mesh):
    return mesh.shape["shard"] == 4 and mesh.shape["grp"] == 8


def head_mask(head):
    lane = lax.broadcasted_iota(jnp.int32, (1, 2 * HEAD), 1)
    return lane // HEAD == head


def pick(mask, values):
    return jnp.where(mask, values.astype(jnp.float32), 0.0).astype(jnp.bfloat16)


def flip(values):
    return values.astype(jnp.float32).T.astype(jnp.bfloat16)


def own_scores(keys, queries):
    parts = []
    for cont in range(OWN // CLEN):
        part = slice(cont * CLEN, (cont + 1) * CLEN)
        parts.append(times_back(keys[part], queries[part]))
    return jnp.concatenate(parts, axis=1)


def attend_pair(query_ref, key_ref, value_ref, bias_ref, out_ref, log_ref):
    mem_valid = lax.broadcasted_iota(jnp.int32, (MEM, 1), 0) < READ
    value_flip = flip(value_ref[...])
    results = []
    for head in range(2):
        mask = head_mask(head)
        queries = pick(mask, query_ref[...])
        main = times_back(key_ref[: 2 * HALF], queries)
        memory = jnp.where(mem_valid, times_back(key_ref[2 * HALF : CONT], queries), NEGATIVE)
        own = own_scores(key_ref[CONT:], queries[HALF:]) + bias_ref[...]
        top = jnp.maximum(
            jnp.max(main, axis=0, keepdims=True), jnp.max(memory, axis=0, keepdims=True)
        )
        top_own = jnp.maximum(top[:, HALF:], jnp.max(own, axis=0, keepdims=True))
        top = jnp.concatenate([top[:, :HALF], top_own], axis=1)
        main = jnp.exp(main - top)
        memory = jnp.exp(memory - top)
        own = jnp.exp(own - top_own)
        total = jnp.sum(main, axis=0, keepdims=True) + jnp.sum(memory, axis=0, keepdims=True)
        total = jnp.concatenate(
            [total[:, :HALF], total[:, HALF:] + jnp.sum(own, axis=0, keepdims=True)], axis=1
        )
        flipped = value_flip[head * HEAD : (head + 1) * HEAD]
        result = product(flipped[:, : 2 * HALF], main.astype(jnp.bfloat16))
        result += product(flipped[:, 2 * HALF : CONT], memory.astype(jnp.bfloat16))
        own = own.astype(jnp.bfloat16)
        own_parts = []
        for cont in range(OWN // CLEN):
            own_parts.append(
                product(
                    flipped[:, CONT + cont * CLEN : CONT + (cont + 1) * CLEN],
                    own[:, cont * CLEN : (cont + 1) * CLEN],
                )
            )
        result = jnp.concatenate(
            [result[:, :HALF], result[:, HALF:] + jnp.concatenate(own_parts, axis=1)], axis=1
        )
        results.append(result / total)
        log_ref[head : head + 1] = top + jnp.log(total)
    out_ref[...] = jnp.concatenate(results, axis=0).T.astype(jnp.bfloat16)


MESH = pl.DeviceIdType.MESH
WHERE = pl.BlockSpec(memory_space=pl.ANY)
INSIDE = pl.BlockSpec(memory_space=pltpu.VMEM)
VECTORS = 16


def seat():
    grp = lax.axis_index("grp")
    return (grp // 2, grp % 2, lax.axis_index("shard"))


def unit_of(z, core, shard):
    return (z * 2 + core) * 4 + shard


def device_of(z, core, shard):
    return (z * 2 + core, shard)


def greet():
    z, core, shard = seat()
    barrier = pltpu.get_barrier_semaphore()
    others = [device_of((z + step) % 4, core, shard) for step in (1, 2, 3)]
    others += [
        device_of(z, core, shard ^ 1),
        device_of(z, core, shard ^ 2),
        device_of(z, 1 - core, shard),
    ]
    for other in others:
        pl.semaphore_signal(barrier, inc=1, device_id=other, device_id_type=MESH)
    pl.semaphore_wait(barrier, len(others))


class Gather:
    def __init__(self, mine, full, send, recv, by_y=(0, 2)):
        self.mine, self.full, self.send, self.recv = mine, full, send, recv
        self.share = mine.shape[0]
        self.by_y = by_y
        self.z, self.core, self.shard = seat()
        self.sent = 0

    def rows(self, unit):
        return self.full.at[pl.ds(pl.multiple_of(unit * self.share, 8), self.share)]

    def link(self, index, unit, z, core, shard, source=None):
        return pltpu.make_async_remote_copy(
            src_ref=self.rows(unit) if source is None else source,
            dst_ref=self.rows(unit),
            send_sem=self.send.at[index],
            recv_sem=self.recv.at[unit],
            device_id=device_of(z, core, shard),
            device_id_type=MESH,
        )

    def push(self, unit, z, core, shard, source=None):
        self.link(self.sent, unit, z, core, shard, source).start()
        self.sent += 1

    def arrive(self, unit):
        self.link(0, unit, self.z, 1 - self.core, self.shard).wait_recv()

    def start_line(self):
        me = unit_of(self.z, self.core, self.shard)
        for step in (1, 2, 3):
            self.push(me, (self.z + step) % 4, self.core, self.shard, self.mine)

    def start_plane(self):
        z, core, shard = self.z, self.core, self.shard
        me = unit_of(z, core, shard)
        self.push(me, z, core, shard ^ 1, self.mine)
        self.push(me, z, core, shard ^ 2, self.mine)
        self.push(me, z, 1 - core, shard, self.mine)

    def own(self, semaphore):
        return pltpu.make_async_copy(
            self.mine, self.rows(unit_of(self.z, self.core, self.shard)), semaphore
        )

    def column(self, step):
        z, core, shard = self.z, self.core, self.shard
        unit = unit_of((z + step) % 4, core, shard)
        self.arrive(unit)
        self.push(unit, z, core, shard ^ 1)
        self.push(unit, z, core, shard ^ 2)
        self.push(unit, z, 1 - core, shard)

    def side(self, step):
        z, core, shard = self.z, self.core, self.shard
        for hop in (1, 2):
            unit = unit_of((z + step) % 4, core, shard ^ hop)
            self.arrive(unit)
            if (step in self.by_y) == (hop == 1):
                self.push(unit, z, core, shard ^ (3 - hop))
            self.push(unit, z, 1 - core, shard)

    def corner(self, step):
        z, core, shard = self.z, self.core, self.shard
        unit = unit_of((z + step) % 4, core, shard ^ 3)
        self.arrive(unit)
        self.push(unit, z, 1 - core, shard)

    def sibling(self):
        def wait(index, carry):
            unit = (index // 4) * 8 + (1 - self.core) * 4 + index % 4
            self.arrive(unit)
            return carry

        lax.fori_loop(0, 16, wait, 0)

    def finish(self):
        def wait(index, carry):
            pltpu.make_async_remote_copy(
                src_ref=self.mine,
                dst_ref=self.mine,
                send_sem=self.send.at[index],
                recv_sem=self.recv.at[0],
                device_id=device_of(self.z, 1 - self.core, self.shard),
                device_id_type=MESH,
            ).wait_send()
            return carry

        lax.fori_loop(0, self.sent, wait, 0)


class PlaneGather(Gather):
    def start_plane(self):
        z, core, shard = self.z, self.core, self.shard
        me = unit_of(z, core, shard)
        self.link(96, me, z, core, shard ^ 1, self.mine).start()
        self.link(97, me, z, core, shard ^ 2, self.mine).start()
        self.link(me, me, z, 1 - core, shard, self.mine).start()

    def along(self, unit, z_of, source=None):
        z, core, shard = self.z, self.core, self.shard

        @pl.when((z_of <= z) & (z < 3))
        def _():
            self.link(32 + unit, unit, z + 1, core, shard, source).start()

        @pl.when((z_of >= z) & (z > 0))
        def _():
            self.link(64 + unit, unit, z - 1, core, shard, source).start()

    def start_line(self):
        me = unit_of(self.z, self.core, self.shard)
        self.along(me, self.z, self.mine)

    def plane(self):
        z, core, shard = self.z, self.core, self.shard
        over_x = unit_of(z, core, shard ^ 1)
        over_y = unit_of(z, core, shard ^ 2)
        self.arrive(over_x)

        @pl.when(core == 0)
        def _():
            self.link(98, over_x, z, core, shard ^ 2).start()

        self.link(over_x, over_x, z, 1 - core, shard).start()
        self.along(over_x, z)
        self.arrive(over_y)

        @pl.when(core == 1)
        def _():
            self.link(98, over_y, z, core, shard ^ 1).start()

        self.link(over_y, over_y, z, 1 - core, shard).start()
        self.along(over_y, z)

    def corners(self):
        z, core, shard = self.z, self.core, self.shard
        unit = unit_of(z, core, shard ^ 3)
        self.arrive(unit)
        self.link(unit, unit, z, 1 - core, shard).start()
        self.along(unit, z)

    def far(self, distance, other):
        z, core, shard = self.z, self.core, self.shard
        for sign in (-1, 1):
            plane = z + sign * distance

            @pl.when((plane >= 0) & (plane < 4))
            def _():
                unit = unit_of(plane, core, shard ^ other)
                self.arrive(unit)
                self.link(unit, unit, z, 1 - core, shard).start()
                self.along(unit, plane)

    def finish(self):
        z, core, shard = self.z, self.core, self.shard

        def done(index, unit):
            self.link(index, unit, z, 1 - core, shard, self.mine).wait_send()

        for index in (96, 97, 98):
            done(index, 0)

        def wait(index, carry):
            plane = index // 4
            unit = plane * 8 + core * 4 + index % 4
            done(unit, unit)

            @pl.when((plane <= z) & (z < 3))
            def _():
                done(32 + unit, unit)

            @pl.when((plane >= z) & (z > 0))
            def _():
                done(64 + unit, unit)

            return carry

        lax.fori_loop(0, 16, wait, 0)


class Swap:
    def __init__(self, source, target, send, recv, z, core, shard):
        self.copy = pltpu.make_async_remote_copy(
            src_ref=source, dst_ref=target, send_sem=send, recv_sem=recv,
            device_id=device_of(z, core, shard), device_id_type=MESH,
        )

    def start(self):
        self.copy.start()

    def arrive(self):
        self.copy.wait_recv()

    def finish(self):
        self.copy.wait_send()


def spread_vector(vectors, index, width):
    narrow, broad = width // 32, 4 * width // 32
    row = lax.broadcasted_iota(jnp.int32, (32 * VECTORS, width), 0)
    lane = lax.broadcasted_iota(jnp.int32, (32 * VECTORS, width), 1)
    small = index < 8
    start = jnp.where(small, index, 8 + VECTORS * 8 * (index - 8))
    block = jnp.where(small, lane // narrow, lane // broad)
    select = jnp.where(row == VECTORS * block + start, 1.0, 0.0).astype(jnp.bfloat16)
    table = outer_sum(vectors, select)
    piece = lax.broadcasted_iota(jnp.int32, table.shape, 0)
    lane = lax.broadcasted_iota(jnp.int32, table.shape, 1)
    offset = jnp.where(small, lane % narrow, lane % broad)
    return jnp.sum(jnp.where(piece == offset, table, 0.0), axis=0, keepdims=True)


TILE = 512
PARTNERS = 4


def front_kernel(
    qkv_ref, wide_ref, down_ref, vec_ref, prompt_ref, kept_ref, sent_ref, mem_ref,
    prompt_cot, kept_cot, sent_cot, bias_ref,
    qkv_full, wide_full, down_full, vec_full, rows_out,
    out_ref, act_ref, first_ref, gdown_ref, ginner_ref, gbranch_ref, gmixed_ref, ghidden_ref,
    mixed_ref, log_ref, query_out, key_out, value_out, sums_ref,
    rows, weights, vectors, table, query, key, value, mixed, cotan, wide, down,
    act, slope, normed, first, total, hidden, small_low,
    send_a, recv_a, send_b, recv_b, send_c, recv_c, send_d, recv_d, swap_send, swap_recv, local,
    store,
):
    pair = pl.program_id(0)
    width = prompt_ref.shape[1]
    low = jnp.bfloat16
    one = Gather(qkv_ref, qkv_full, send_a, recv_a, (0, 1))
    small = Gather(vec_ref, vec_full, send_d, recv_d)
    two = Gather(wide_ref, wide_full, send_b, recv_b, (0, 1))
    three = PlaneGather(down_ref, down_full, send_c, recv_c)
    z, core, shard = seat()
    step_rows = HALF // PARTNERS
    partner = [
        Swap(
            prompt_ref.at[pl.ds(index * step_rows, step_rows)],
            rows.at[pl.ds(HALF + index * step_rows, step_rows)],
            swap_send.at[index], swap_recv.at[index], z, core, shard ^ 1,
        )
        for index in range(PARTNERS)
    ]
    taken = [
        Swap(
            sent_ref.at[pl.ds(index * step_rows, step_rows)],
            rows.at[pl.ds(CONT + OWN // 2 + index * step_rows, step_rows)],
            swap_send.at[PARTNERS + index], swap_recv.at[PARTNERS + index], z, core, shard ^ 2,
        )
        for index in range(2)
    ]
    taken_cot = Swap(
        sent_cot, cotan.at[pl.ds(HALF + OWN // 2, OWN // 2)],
        swap_send.at[PARTNERS + 2], swap_recv.at[PARTNERS + 2], z, core, shard ^ 2,
    )
    swaps = partner + taken + [taken_cot]
    own = [gather.own(local.at[index]) for index, gather in enumerate((one, small, two, three))]
    own += [
        pltpu.make_async_copy(prompt_ref, rows.at[pl.ds(0, HALF)], local.at[4]),
        pltpu.make_async_copy(mem_ref, rows.at[pl.ds(2 * HALF, MEM)], local.at[5]),
        pltpu.make_async_copy(kept_ref, rows.at[pl.ds(CONT, OWN // 2)], local.at[6]),
        pltpu.make_async_copy(prompt_cot, cotan.at[pl.ds(0, HALF)], local.at[7]),
        pltpu.make_async_copy(kept_cot, cotan.at[pl.ds(HALF, OWN // 2)], local.at[8]),
    ]
    load_weights = pltpu.make_async_copy(qkv_full, weights, local.at[9])
    load_vectors = pltpu.make_async_copy(vec_full, vectors, local.at[10])
    store_rows = pltpu.make_async_copy(rows, rows_out, local.at[11])
    load_wide = pltpu.make_async_copy(wide_full, wide, local.at[12])
    load_down = pltpu.make_async_copy(down_full, down, local.at[13])

    def project(start, query_start, count, queries):
        span = pl.ds(start, count)
        block = rows[span]
        if queries:
            result = (product(block, weights[:, :width]) + table[0:1]).astype(low)
            result = (result.astype(jnp.float32) * SCALE).astype(low)
            query[pl.ds(query_start, count)] = result
        key[span] = product(block, weights[:, width : 2 * width]).astype(low)
        value[span] = (product(block, weights[:, 2 * width :]) + table[1:2]).astype(low)

    @pl.when(pair == 0)
    def _():
        for copy in own[4:]:
            copy.start()
        greet()
        small.start_line()
        one.start_line()
        small.start_plane()
        one.start_plane()
        partner[0].start()
        three.start_line()
        taken[0].start()
        three.start_plane()
        for copy in own[:4]:
            copy.start()
        for step in (1, 2, 3):
            small.column(step)
            one.column(step)
        two.start_line()
        for step in range(4):
            small.side(step)
            one.side(step)
        partner[1].start()
        taken[1].start()
        partner[2].start()
        partner[3].start()
        two.start_plane()
        for step in range(4):
            small.corner(step)
            one.corner(step)
        small.sibling()
        own[1].wait()
        load_vectors.start()
        one.sibling()
        own[0].wait()
        load_weights.start()
        three.plane()
        for step in (1, 2, 3):
            two.column(step)
        load_vectors.wait()

        def spread(index, carry):
            table[pl.ds(index, 1)] = spread_vector(vectors[...], index, width)
            return carry

        lax.fori_loop(0, 12, spread, 0)
        for index in (2, 3, 4, 5, 6):
            own[index].wait()
        load_weights.wait()
        project(0, 0, HALF, True)
        three.corners()
        three.far(1, 0)
        for swap in taken:
            swap.arrive()
        project(CONT, HALF, OWN, True)
        three.far(1, 1)
        for swap in partner:
            swap.arrive()
        project(HALF, 0, HALF + MEM, False)
        store_rows.start()

    def later(when, *actions):
        @pl.when(pair == when)
        def _():
            for action in actions:
                action[0](*action[1:])

    later(0, (two.side, 0), (three.far, 1, 2))
    later(1, (two.side, 1), (three.far, 1, 3))
    later(2, (two.side, 2), (three.far, 2, 0), (three.far, 2, 1))
    later(3, (two.side, 3), (three.far, 2, 2))
    later(4, (two.corner, 0), (two.corner, 1), (three.far, 2, 3), (three.far, 3, 0))
    later(5, (two.corner, 2), (three.far, 3, 1))

    lanes = pl.ds(pl.multiple_of(pair * (2 * HEAD), 2 * HEAD), 2 * HEAD)
    query_out[...] = query[:, lanes]
    key_out[...] = key[:, lanes]
    value_out[...] = value[:, lanes]
    attend_pair(query_out, key_out, value_out, bias_ref, mixed_ref, log_ref)
    mixed[:, lanes] = mixed_ref[...]

    def fine(index):
        return table[index : index + 1]

    def save(tile, index):
        span = pl.ds(pl.multiple_of(tile * TILE, TILE), TILE)
        source, target = (
            (act, act_ref), (slope, ginner_ref), (hidden, ghidden_ref),
            (small_low.at[0], out_ref), (small_low.at[1], first_ref), (small_low.at[2], gdown_ref),
            (small_low.at[3], gbranch_ref), (small_low.at[4], gmixed_ref),
        )[index]
        return pltpu.make_async_copy(source, target.at[span], store.at[index])

    def up_chunk(step):
        return pl.ds(pl.multiple_of(step * width, 128), width)

    def up_columns(step):
        return pl.ds(pl.multiple_of((step + 1) * width, 128), width)

    def add_sum(index, values):
        sums_ref[pl.ds(index, 1)] += jnp.sum(values, axis=0, keepdims=True)

    def start_tile(tile):
        span = pl.ds(pl.multiple_of(tile * TILE, TILE), TILE)
        held = rows[pl.ds(pl.multiple_of(tile * CONT, MEM), TILE)].astype(jnp.float32)
        held = held + (product(mixed[span], wide[:, :width]) + fine(2))
        result, value_n, value_r = layer_norm(held, fine(3), fine(4))

        @pl.when(tile == 1)
        def _():
            for index in range(1, 8):
                save(0, index).wait()

        normed[...] = value_n
        first[...] = result
        small_low[1] = result.astype(low)
        return value_r

    def forward_chunk(step, carry):
        chunk = up_chunk(step)
        inner = product(small_low[1], wide[:, up_columns(step)]) + table[pl.ds(8 + step, 1)]
        half = 0.5 * (1.0 + lax.erf(inner * ROOT_HALF))
        active = (inner * half).astype(low)
        act[:, chunk] = active
        slope[:, chunk] = (half + inner * jnp.exp(-0.5 * inner * inner) * ROOT_GAUSS).astype(low)
        total[...] += product(active, down[chunk])
        return carry

    def backward_chunk(step, carry):
        chunk = up_chunk(step)
        grad = times_back(small_low[2], down[chunk]) * slope[:, chunk].astype(jnp.float32)
        grad = grad.astype(low)
        slope[:, chunk] = grad
        add_sum(8 + step, grad.astype(jnp.float32))
        total[...] += times_back(grad, wide[:, up_columns(step)])
        return carry

    def tile_body(tile, carry):
        span = pl.ds(pl.multiple_of(tile * TILE, TILE), TILE)
        inverse_one = start_tile(tile)
        total[...] = jnp.zeros_like(total)

        @pl.when(tile == 0)
        def _():
            three.far(3, 2)
            three.far(3, 3)
            three.sibling()
            load_down.start()
            load_down.wait()

        @pl.when(tile == 1)
        def _():
            save(0, 0).wait()
            taken_cot.arrive()

        lax.fori_loop(0, 4, forward_chunk, 0)
        save(tile, 0).start()
        result, value_n, inverse_two = layer_norm(
            first[...] + (total[...] + fine(5)), fine(6), fine(7)
        )
        small_low[0] = result.astype(low)
        save(tile, 3).start()
        save(tile, 4).start()
        cot = cotan[span].astype(jnp.float32)
        add_sum(6, cot * value_n)
        add_sum(7, cot)
        grad_mid = norm_back(cot * fine(6), value_n, inverse_two)
        grad_low = grad_mid.astype(low)
        small_low[2] = grad_low
        save(tile, 5).start()
        add_sum(5, grad_low.astype(jnp.float32))
        total[...] = grad_mid
        lax.fori_loop(0, 4, backward_chunk, 0)
        save(tile, 1).start()
        grad_first = total[...]
        add_sum(3, grad_first * normed[...])
        add_sum(4, grad_first)
        grad_hidden = norm_back(grad_first * fine(3), normed[...], inverse_one)
        hidden[...] = grad_hidden
        save(tile, 2).start()
        grad_low = grad_hidden.astype(low)
        small_low[3] = grad_low
        save(tile, 6).start()
        add_sum(2, grad_low.astype(jnp.float32))
        small_low[4] = times_back(grad_low, wide[:, :width]).astype(low)
        save(tile, 7).start()
        return carry

    @pl.when(pair == PAIRS - 1)
    def _():
        taken_cot.start()
        two.corner(3)
        two.sibling()
        load_wide.start()
        own[7].wait()
        own[8].wait()
        sums_ref[...] = jnp.zeros_like(sums_ref)
        load_wide.wait()
        lax.fori_loop(0, 2, tile_body, 0)
        store_rows.wait()
        for index in range(8):
            save(1, index).wait()
        for sender in (one, small, two, three, *swaps):
            sender.finish()


def front(
    qkv, wide_share, down_share, vec, prompt, kept, sent, memory, prompt_cot, kept_cot, sent_cot,
    bias,
):
    width = prompt.shape[1]
    low = jnp.bfloat16
    wide = jnp.float32
    shape = jax.ShapeDtypeStruct

    def block(rows):
        return pl.BlockSpec((rows, 2 * HEAD), lambda pair: (0, pair))

    def full(share):
        return shape((32 * share.shape[0], share.shape[1]), low)

    dma = pltpu.SemaphoreType.DMA
    memory_space = pltpu.VMEM
    return pl.pallas_call(
        front_kernel,
        grid=(PAIRS,),
        in_specs=[INSIDE] * 4
        + [WHERE] * 7
        + [pl.BlockSpec((CLEN, OWN), lambda pair: (0, 0))],
        out_specs=[WHERE] * 13
        + [
            block(QROWS), pl.BlockSpec((None, 2, QROWS), lambda pair: (pair, 0, 0)),
            block(QROWS), block(KEYS), block(KEYS),
            pl.BlockSpec((VECTORS, width), lambda pair: (0, 0)),
        ],
        out_shape=[
            full(qkv), full(wide_share), full(down_share), full(vec),
            shape((KEYS, width), low),
            shape((QROWS, width), low),
            shape((QROWS, 4 * width), low),
            shape((QROWS, width), low),
            shape((QROWS, width), low),
            shape((QROWS, 4 * width), low),
            shape((QROWS, width), low),
            shape((QROWS, width), low),
            shape((QROWS, width), wide),
            shape((QROWS, width), low),
            shape((PAIRS, 2, QROWS), wide),
            shape((QROWS, width), low),
            shape((KEYS, width), low),
            shape((KEYS, width), low),
            shape((VECTORS, width), wide),
        ],
        scratch_shapes=[
            memory_space((KEYS, width), low),
            memory_space((width, 3 * width), low),
            memory_space((32 * VECTORS, 2 * HEAD), low),
            memory_space((VECTORS, width), wide),
            memory_space((QROWS, width), low),
            memory_space((KEYS, width), low),
            memory_space((KEYS, width), low),
            memory_space((QROWS, width), low),
            memory_space((QROWS, width), low),
            memory_space((width, 5 * width), low),
            memory_space((4 * width, width), low),
            memory_space((TILE, 4 * width), low),
            memory_space((TILE, 4 * width), low),
            memory_space((TILE, width), wide),
            memory_space((TILE, width), wide),
            memory_space((TILE, width), wide),
            memory_space((TILE, width), wide),
            memory_space((5, TILE, width), low),
        ]
        + [dma((32,))] * 4
        + [dma((100,)), dma((32,)), dma((32,)), dma((32,))]
        + [dma((PARTNERS + 3,)), dma((PARTNERS + 3,)), dma((14,)), dma((8,))],
        compiler_params=pltpu.CompilerParams(
            vmem_limit_bytes=67043328, collective_id=0, has_side_effects=True
        ),
        name="front",
    )(
        qkv, wide_share, down_share, vec, prompt, kept, sent, memory, prompt_cot, kept_cot,
        sent_cot, bias,
    )


SEND = 13
CHIP, PLANE, LINE, MIDDLE, SPREAD, SHARE, SMALL, PARTNER = range(8)
SLOTS = {
    0: ((PLANE, 0), (CHIP, 2), (PLANE, 1), (CHIP, 3), (CHIP, 4),),
    1: ((LINE, 0),),
    3: ((MIDDLE, 0), (LINE, 1), (PLANE, 2),),
    4: ((PLANE, 3), (CHIP, 5),),
    5: ((SPREAD, 0), (MIDDLE, 1), (PLANE, 4),),
    6: ((LINE, 2),),
    7: ((SHARE, 0), (SPREAD, 1), (LINE, 3), (LINE, 4), (PLANE, 5),),
    8: ((MIDDLE, 2), (LINE, 5), (CHIP, 6),),
    9: ((SHARE, 1), (MIDDLE, 3), (PLANE, 6),),
    10: ((SPREAD, 2), (MIDDLE, 4), (LINE, 6), (CHIP, 7), (MIDDLE, 5),),
    11: ((SPREAD, 3), (MIDDLE, 6), (PLANE, 7),),
}
TAIL = {
    0: ((SHARE, 2), (SPREAD, 4), (LINE, 7),),
    1: ((PLANE, 8), (PARTNER, 1), (PARTNER, 2), (PARTNER, 3), (SPREAD, 5), (SMALL, 0),),
    2: ((MIDDLE, 7), (SMALL, 1),),
    3: ((SHARE, 3), (SPREAD, 6), (SMALL, 2), (LINE, 8), (SPREAD, 7), (SHARE, 4), (MIDDLE, 8), (SHARE, 5), (SPREAD, 8), (SHARE, 6),),
    4: ((SHARE, 7), (SMALL, 3),),
    5: ((SHARE, 8),),
}
LAST = ((SMALL, 4),)
WIDE = 4
NARROW = 3
TINY = 2
ITEMS = WIDE + NARROW + TINY


class Reduce:
    def __init__(self, mine, theirs, got, from_x, from_y, last_x, last_y, outer, total, send, recv):
        self.mine, self.theirs, self.got = mine, theirs, got
        self.from_x, self.from_y, self.last_x, self.last_y = from_x, from_y, last_x, last_y
        self.outer, self.total, self.send, self.recv = outer, total, send, recv
        self.half = mine.shape[1] // 2
        self.z, self.core, self.shard = seat()
        self.inner = (self.z == 1) | (self.z == 2)

    def copy(self, source, target, index, z, core, shard):
        return pltpu.make_async_remote_copy(
            src_ref=source, dst_ref=target, send_sem=self.send.at[index],
            recv_sem=self.recv.at[index], device_id=device_of(z, core, shard), device_id_type=MESH,
        )

    def upper(self, part):
        return self.mine.at[part, pl.ds(0, self.half)]

    def lower(self, part):
        return self.mine.at[part, pl.ds(self.half, self.half)]

    def link(self, index):
        z, core, shard = self.z, self.core, self.shard
        near = jnp.where(z < 2, 1 - z, 5 - z)
        if index < 4:
            ends = (self.theirs.at[index], self.got.at[index], z, 1 - core, shard)
        elif index < 6:
            source = self.upper(shard ^ (1 if index == 4 else 3))
            ends = (source, self.from_x.at[index - 4], z, core, shard ^ 1)
        elif index < 8:
            source = self.lower(shard ^ (2 if index == 6 else 3))
            ends = (source, self.from_y.at[index - 6], z, core, shard ^ 2)
        elif index == 8:
            ends = (self.upper(shard ^ 2), self.last_y, z, core, shard ^ 2)
        elif index == 9:
            ends = (self.lower(shard ^ 1), self.last_x, z, core, shard ^ 1)
        elif index == 10:
            ends = (self.mine.at[shard], self.outer, near, core, shard)
        elif index == 11:
            ends = (self.mine.at[shard], self.total, 3 - z, core, shard)
        else:
            ends = (self.total, self.total, near, core, shard)
        return self.copy(ends[0], ends[1], index, *ends[2:])

    def give(self, part):
        self.copy(
            self.theirs.at[part], self.got.at[part], part, self.z, 1 - self.core, self.shard
        ).start()

    def given(self):
        for part in range(4):
            self.link(part).wait_send()

    def add(self, part, start, count, other):
        def step(index, carry):
            rows = pl.ds(pl.multiple_of(index * 48, 16), 48)
            span = pl.ds(pl.multiple_of(start + index * 48, 16), 48)
            self.mine[part, span] = self.mine[part, span] + other[rows]
            return carry

        lax.fori_loop(0, count // 48, step, 0)

    def chip(self):
        for part in range(4):
            self.link(part).wait_recv()

        def add_part(part, carry):
            self.add(part, 0, 2 * self.half, self.got.at[part])
            return carry

        lax.fori_loop(0, 4, add_part, 0)
        for index in (4, 5, 6, 7):
            self.link(index).start()

    def plane(self):
        shard = self.shard
        self.link(4).wait_recv()
        self.link(5).wait_recv()
        self.add(shard ^ 2, 0, self.half, self.from_x.at[1])
        self.link(8).start()
        self.link(6).wait_recv()
        self.link(7).wait_recv()
        self.add(shard ^ 1, self.half, self.half, self.from_y.at[1])
        self.link(9).start()
        self.add(shard, 0, self.half, self.from_x.at[0])
        self.add(shard, self.half, self.half, self.from_y.at[0])

    def line(self):
        self.link(8).wait_recv()
        self.add(self.shard, 0, self.half, self.last_y)
        self.link(9).wait_recv()
        self.add(self.shard, self.half, self.half, self.last_x)

        @pl.when(jnp.logical_not(self.inner))
        def _():
            self.link(10).start()

    def middle(self):
        @pl.when(self.inner)
        def _():
            self.link(10).wait_recv()
            self.add(self.shard, 0, 2 * self.half, self.outer)
            self.link(11).start()

    def spread(self):
        @pl.when(self.inner)
        def _():
            self.link(11).wait_recv()

            def step(index, carry):
                rows = pl.ds(pl.multiple_of(index * 48, 16), 48)
                self.total[rows] = self.total[rows] + self.mine[self.shard, rows]
                return carry

            lax.fori_loop(0, 2 * self.half // 48, step, 0)
            self.link(12).start()

    def share(self, place, semaphore):
        @pl.when(jnp.logical_not(self.inner))
        def _():
            self.link(12).wait_recv()

        pltpu.make_async_copy(self.total, place, semaphore).start()
        pltpu.make_async_remote_copy(
            src_ref=self.total, dst_ref=place, send_sem=self.send.at[13],
            recv_sem=self.recv.at[13],
            device_id=device_of(self.z, 1 - self.core, self.shard), device_id_type=MESH,
        ).start()

    def finish(self, place, semaphore):
        pltpu.make_async_copy(self.total, place, semaphore).wait()
        last = pltpu.make_async_remote_copy(
            src_ref=self.total, dst_ref=place, send_sem=self.send.at[13],
            recv_sem=self.recv.at[13],
            device_id=device_of(self.z, 1 - self.core, self.shard), device_id_type=MESH,
        )
        last.wait_send()
        last.wait_recv()
        for index in range(4, 10):
            self.link(index).wait_send()

        @pl.when(jnp.logical_not(self.inner))
        def _():
            self.link(10).wait_send()

        @pl.when(self.inner)
        def _():
            self.link(11).wait_send()
            self.link(12).wait_send()


class Butterfly:
    def __init__(self, held, got, send, recv):
        self.held, self.got, self.send, self.recv = held, got, send, recv
        self.z, self.core, self.shard = seat()

    def copy(self, step):
        z, core, shard = self.z, self.core, self.shard
        where = ((z, core, shard ^ 1), (z, core, shard ^ 2), (z ^ 1, core, shard),
                 (z ^ 2, core, shard), (z, 1 - core, shard))[step]
        rows = pl.ds(0, 2 * VECTORS if step < 2 else VECTORS)
        return pltpu.make_async_remote_copy(
            src_ref=self.held.at[step, rows], dst_ref=self.got.at[step, rows],
            send_sem=self.send.at[step], recv_sem=self.recv.at[step],
            device_id=device_of(*where), device_id_type=MESH,
        )

    def start(self):
        self.copy(0).start()

    def step(self, step):
        self.copy(step).wait_recv()
        rows = slice(0, 2 * VECTORS if step < 2 else VECTORS)
        self.held[step + 1, rows] = self.held[step, rows] + self.got[step, rows]
        if step < 4:
            self.copy(step + 1).start()

    def finish(self):
        for step in range(5):
            self.copy(step).wait_send()


def back_piece(
    head, half, query_ref, key_ref, value_ref, bias_ref, log_ref, grad_ref,
    overlap, key_acc, value_acc, query_flip,
):
    mem_valid = lax.broadcasted_iota(jnp.int32, (MEM, 1), 0) < READ
    mask = head_mask(head)
    span = pl.ds(pl.multiple_of(head * HEAD, HEAD), HEAD)

    mine = lax.broadcasted_iota(jnp.int32, (2 * HEAD, 1), 0) // HEAD == head

    def keep(lanes, values):
        query_flip[:, lanes] = jnp.where(mine, values, query_flip[:, lanes])

    def block_back(keys, values, bias, valid, queries, grads, log, delta, rows):
        scores = times_back(keys, queries)
        if bias is not None:
            scores = scores + bias
        chances = jnp.exp(scores - log)
        if valid is not None:
            chances = jnp.where(valid, chances, 0.0)
        slopes = (chances * (times_back(values, grads) - delta)).astype(jnp.bfloat16)
        value_acc[rows] += product(chances.astype(jnp.bfloat16), grads)
        key_acc[rows] += product(slopes, queries)
        return outer_sum(keys, slopes)

    part = slice(half * HALF, (half + 1) * HALF)
    queries = pick(mask, query_ref[part])
    grads = pick(mask, grad_ref[part])
    delta = jnp.sum(overlap[span, part], axis=0, keepdims=True)
    log = log_ref[pl.ds(head, 1), part]
    main_rows = slice(0, 2 * HALF)
    mem_rows = slice(2 * HALF, CONT)
    piece = block_back(
        key_ref[main_rows], value_ref[main_rows], None, None,
        queries, grads, log, delta, main_rows,
    )
    piece += block_back(
        key_ref[mem_rows], value_ref[mem_rows], None, mem_valid,
        queries, grads, log, delta, mem_rows,
    )
    if half == 0:
        keep(part, piece)
        return
    own_parts = []
    for cont in range(OWN // CLEN):
        rows = slice(CONT + cont * CLEN, CONT + (cont + 1) * CLEN)
        part = slice(cont * CLEN, (cont + 1) * CLEN)
        own_parts.append(
            block_back(
                key_ref[rows], value_ref[rows], bias_ref[:, part], None,
                queries[part], grads[part], log[:, part], delta[:, part], rows,
            )
        )
    keep(slice(HALF, QROWS), piece + jnp.concatenate(own_parts, axis=1))


def back_kernel(
    act_ref, gdown_ref, first_ref, ginner_ref, mixed_all, gbranch_ref, ghidden_ref, rows_ref,
    qkv_ref, out_ref, sums_ref,
    query_ref, key_ref, value_ref, grad_ref, mixed_ref, log_ref, bias_ref,
    down_out, up_out, out_out, qkv_out, last_out, returned_out, grad_prompt, grad_kept, grad_back,
    memory_out, vec_out,
    wide_mine, wide_theirs, wide_got, wide_x, wide_y, wide_lx, wide_ly, wide_outer, wide_total,
    thin_mine, thin_theirs, thin_got, thin_x, thin_y, thin_lx, thin_ly, thin_outer, thin_total,
    tiny_mine, tiny_theirs, tiny_got, tiny_x, tiny_y, tiny_lx, tiny_ly, tiny_outer, tiny_total,
    pool, rows, dquery, dkey, dvalue, key_acc, value_acc, overlap, query_flip,
    partner, ghidden, staged, held, got,
    send, recv, small_send, small_recv, swap_send, swap_recv, local, out_sem,
):
    pair = pl.program_id(0)
    z, core, shard = seat()
    other = 1 - core
    width = rows_ref.shape[1]
    part_rows = width // 4
    low = jnp.bfloat16

    def item(index):
        if isinstance(index, int) and index >= WIDE:
            return thin(index - WIDE) if index < WIDE + NARROW else tiny(index - WIDE - NARROW)
        return Reduce(
            wide_mine.at[index], wide_theirs.at[index % 2], wide_got.at[index],
            wide_x.at[index], wide_y.at[index], wide_lx.at[index], wide_ly.at[index],
            wide_outer.at[index], wide_total.at[index], send.at[index], recv.at[index],
        )

    def thin(index):
        return Reduce(
            thin_mine.at[index], thin_theirs.at[index % 2], thin_got.at[index],
            thin_x.at[index], thin_y.at[index], thin_lx.at[index], thin_ly.at[index],
            thin_outer.at[index], thin_total.at[index], send.at[WIDE + index],
            recv.at[WIDE + index],
        )

    def tiny(index):
        number = WIDE + NARROW + index
        return Reduce(
            tiny_mine.at[index], tiny_theirs.at[index % 2], tiny_got.at[index],
            tiny_x.at[index], tiny_y.at[index], tiny_lx.at[index], tiny_ly.at[index],
            tiny_outer.at[index], tiny_total.at[index], send.at[number], recv.at[number],
        )

    small = Butterfly(held, got, small_send, small_recv)
    half_hidden = width // 2

    def place(index):
        if index < 2:
            start = core * half_hidden + index * part_rows
            return down_out.at[pl.ds(pl.multiple_of(start, 64), part_rows)]
        if index < 4:
            start = core * (2 * width) + (index - 2) * width
            return up_out.at[:, pl.ds(pl.multiple_of(start, 128), width)]
        if index == 4:
            return out_out.at[:, pl.ds(pl.multiple_of(core * half_hidden, 128), half_hidden)]
        if index < WIDE + NARROW:
            return qkv_out.at[index - 5, core]
        start = pl.multiple_of(core * (part_rows // 2), 16)
        return last_out.at[index - WIDE - NARROW, pl.ds(start, part_rows // 2)]

    def stage(name, index):
        if name == SHARE:
            item(index).share(place(index), out_sem.at[index])
        else:
            held = item(index)
            (held.chip, held.plane, held.line, held.middle, held.spread)[name]()

    returned = Swap(
        out_ref.at[pl.ds(HALF + OWN // 2, OWN // 2)], returned_out, swap_send.at[0], swap_recv.at[0], z, core, shard ^ 2
    )
    def to_partner(index):
        span = pl.ds(pl.multiple_of(128 * index, 128), 128)
        return Swap(
            pool.at[3, span], partner.at[span], swap_send.at[index + 1], swap_recv.at[index + 1],
            z, core, shard ^ 1,
        )

    cont_back = Swap(
        pool.at[3, pl.ds(2 * 256, 256)], grad_back, swap_send.at[5], swap_recv.at[5],
        z, core, shard ^ 2,
    )

    def load(source, slot, semaphore):
        return pltpu.make_async_copy(source, pool.at[slot], local.at[semaphore])

    def act_chunk(part):
        return load(act_ref.at[:, pl.ds(part * width, width)], part % 2, part % 2)

    def inner_chunk(step):
        half = other if step < 2 else core
        start = pl.multiple_of(half * (2 * width) + (step % 2) * width, 128)
        return load(ginner_ref.at[:, pl.ds(start, width)], step % 2, step % 2)

    def parts_of(target, values):
        for part in range(4):
            target[part] = values[part * part_rows : (part + 1) * part_rows].astype(low)

    load_rows = pltpu.make_async_copy(rows_ref, rows, local.at[4])

    def inner_load(step):
        half = jnp.where(step < 2, other, core)
        start = pl.multiple_of(half * (2 * width) + (step % 2) * width, 128)
        return load(ginner_ref.at[:, pl.ds(start, width)], step % 2, step % 2)

    def act_load(part):
        lanes = pl.ds(pl.multiple_of(part * width, 128), width)
        return load(act_ref.at[:, lanes], part % 2, part % 2)

    def weight_load(index):
        return pltpu.make_async_copy(
            qkv_ref.at[:, pl.ds(index * width, width)],
            pool.at[index, pl.ds(0, width)], local.at[index],
        )

    def down_part(part, carry):
        act_load(part).wait()

        def down_half(side, carry):
            half = jnp.where(side == 0, other, core)
            lanes = pl.ds(pl.multiple_of(half * half_hidden, 128), half_hidden)
            result = outer_sum(pool[part % 2, :, lanes], pool[2]).astype(low)
            for index in range(2):
                piece = result[index * part_rows : (index + 1) * part_rows]

                @pl.when(side == 0)
                def _():
                    wide_theirs[index, part] = piece
                    item(index).give(part)

                @pl.when(side == 1)
                def _():
                    wide_mine[index, part] = piece

            return carry

        lax.fori_loop(0, 2, down_half, 0)

        @pl.when(part < 2)
        def _():
            act_load(part + 2).start()

        @pl.when(part >= 2)
        def _():
            inner_load(part - 2).start()

        return carry

    def up_part(step, carry):
        inner_load(step).wait()
        result = outer_sum(pool[3], pool[step % 2])

        @pl.when(step < 2)
        def _():
            item(step).given()
            parts_of(wide_theirs.at[step], result)
            for part in range(4):
                item(step + 2).give(part)
            inner_load(step + 2).start()

        @pl.when(step >= 2)
        def _():
            parts_of(wide_mine.at[step], result)

        @pl.when((step == 1) | (step == 2))
        def _():
            item(step - 1).chip()

        return carry

    def out_half(side, carry):
        half = jnp.where(side == 0, other, core)
        lanes = pl.ds(pl.multiple_of(half * half_hidden, 128), half_hidden)
        result = outer_sum(pool[2], pool[3, :, lanes])

        @pl.when(side == 0)
        def _():
            parts_of(thin_theirs.at[0], result)
            for part in range(4):
                thin(0).give(part)

        @pl.when(side == 1)
        def _():
            parts_of(thin_mine.at[0], result)

        return carry

    def qkv_part(index):
        def one_half(side, carry):
            half = jnp.where(side == 0, other, core)
            lanes = pl.ds(pl.multiple_of((2 * index + half) * (2 * HEAD), 2 * HEAD), 2 * HEAD)
            query_side = outer_sum(rows[:HALF], dquery[:HALF, lanes])
            query_side += outer_sum(rows[CONT:], dquery[HALF:, lanes])
            both = jnp.concatenate([dkey[:, lanes], dvalue[:, lanes]], axis=1)
            result = jnp.concatenate([query_side, outer_sum(rows[...], both)], axis=1)

            @pl.when(side == 0)
            def _():
                @pl.when(index > 0)
                def _():
                    thin(0).given()

                parts_of(thin_theirs.at[(1 + index) % 2], result)
                for part in range(4):
                    thin(1 + index).give(part)

            @pl.when(side == 1)
            def _():
                parts_of(thin_mine.at[1 + index], result)

            return carry

        lax.fori_loop(0, 2, one_half, 0)

    def last_part(index):
        lanes = pl.ds(pl.multiple_of((4 + index) * (2 * HEAD), 2 * HEAD), 2 * HEAD)
        query_side = outer_sum(rows[:HALF], dquery[:HALF, lanes])
        query_side += outer_sum(rows[CONT:], dquery[HALF:, lanes])
        both = jnp.concatenate([dkey[:, lanes], dvalue[:, lanes]], axis=1)
        result = jnp.concatenate([query_side, outer_sum(rows[...], both)], axis=1).astype(low)
        half = part_rows // 2
        for side in range(2):

            @pl.when(core == side)
            def _():
                for part in range(4):
                    start = part * part_rows
                    tiny_theirs[index % 2, part] = result[
                        start + (1 - side) * half : start + (2 - side) * half
                    ]
                    tiny_mine[index, part] = result[start + side * half : start + (side + 1) * half]

        for part in range(4):
            tiny(index).give(part)

    @pl.when(pair == 0)
    def _():
        act_load(0).start()
        load(gdown_ref, 2, 2).start()
        act_load(1).start()
        load(first_ref, 3, 3).start()
        load_rows.start()
        greet()
        returned.start()
        load(gdown_ref, 2, 2).wait()
        lax.fori_loop(0, 4, down_part, 0)
        load(mixed_all, 2, 2).start()
        load(first_ref, 3, 3).wait()
        lax.fori_loop(0, 4, up_part, 0)
        load(gbranch_ref, 3, 3).start()
        load(mixed_all, 2, 2).wait()
        load(gbranch_ref, 3, 3).wait()
        lax.fori_loop(0, 2, out_half, 0)
        for index in range(3):
            weight_load(index).start()
        load_rows.wait()

    lanes = pl.ds(pl.multiple_of(pair * (2 * HEAD), 2 * HEAD), 2 * HEAD)
    overlap[...] = (mixed_ref[...].astype(jnp.float32) * grad_ref[...].astype(jnp.float32)).T
    key_acc[...] = jnp.zeros_like(key_acc)
    value_acc[...] = jnp.zeros_like(value_acc)

    def piece_body(piece, carry):
        for half in range(2):
            back_piece(
                piece, half, query_ref, key_ref, value_ref, bias_ref, log_ref, grad_ref,
                overlap, key_acc, value_acc, query_flip,
            )

        @pl.when(piece == 1)
        def _():
            dquery[:, lanes] = (query_flip[...].T * SCALE).astype(low)
            dkey[:, lanes] = key_acc[...].astype(low)
            dvalue[:, lanes] = value_acc[...].astype(low)

        @pl.when((piece == 1) & (pair % 2 == 1) & (pair < 4))
        def _():
            qkv_part(pair // 2)

        @pl.when((piece == 1) & (pair >= 4))
        def _():
            last_part(pair - 4)

        for number, stages in SLOTS.items():

            @pl.when(pair * 2 + piece == number)
            def _():
                for name, index in stages:
                    stage(name, index)

        return carry

    lax.fori_loop(0, 2, piece_body, 0)

    def hidden_load(step):
        start = pl.multiple_of((5 - step) * 256, 256)
        return pltpu.make_async_copy(
            ghidden_ref.at[pl.ds(start, 256)], ghidden.at[step % 2], local.at[5 + step % 2]
        )

    def staged_store(step):
        slot = step % 2
        return staged.at[slot], local.at[8 + slot]

    def chunk_body(step, carry):
        start = jnp.where(step < 2, HALF + 256 * step, jnp.where(step < 4, CONT, HALF))
        start = jnp.where(step >= 2, start + jnp.where(step % 2 == 0, 256, 0), start)
        start = jnp.where(step >= 4, start - HALF, start)
        span = pl.ds(pl.multiple_of(start, MEM), 256)
        result = times_back(dkey[span], pool[1, :width]) + times_back(dvalue[span], pool[2, :width])

        @pl.when(step < 2)
        def _():
            pool[3, pl.ds(pl.multiple_of(256 * step, 256), 256)] = result.astype(low)

        @pl.when(step == 0)
        def _():
            to_partner(0).start()

        @pl.when(step >= 2)
        def _():
            hidden_load(step).wait()
            mine = pl.ds(pl.multiple_of((5 - step) * 256, 256), 256)
            full = result + (
                ghidden[step % 2] + times_back(dquery[mine], pool[0, :width])
            )

            @pl.when(step == 2)
            def _():
                pool[3, 512:768] = full.astype(low)
                cont_back.start()

            @pl.when(step == 3)
            def _():
                staged[1] = full.astype(low)
                pltpu.make_async_copy(staged.at[1], grad_kept, local.at[9]).start()

            @pl.when(step >= 4)
            def _():
                to_partner(2 * (5 - step)).arrive()
                to_partner(2 * (5 - step) + 1).arrive()

                @pl.when(step == 5)
                def _():
                    pltpu.make_async_copy(staged.at[1], grad_kept, local.at[9]).wait()

                mine = pl.ds(pl.multiple_of((5 - step) * 256, 256), 256)
                staged[step % 2] = (full + partner[mine].astype(jnp.float32)).astype(low)
                pltpu.make_async_copy(
                    staged.at[step % 2], grad_prompt.at[mine], local.at[8 + step % 2]
                ).start()

            @pl.when(step < 4)
            def _():
                hidden_load(step + 2).start()

        for number, stages in TAIL.items():

            @pl.when(step == number)
            def _():
                for name, index in stages:
                    if name == SMALL:
                        small.step(index)
                    elif name == PARTNER:
                        to_partner(index).start()
                    else:
                        stage(name, index)

        return carry

    @pl.when(pair == PAIRS - 1)
    def _():
        hidden_load(2).start()
        hidden_load(3).start()
        sums = pltpu.make_async_copy(sums_ref, held.at[0, pl.ds(0, VECTORS)], local.at[7])
        sums.start()
        for index in range(3):
            weight_load(index).wait()
        sums.wait()
        held[0, 0:1] = jnp.sum(dquery[...].astype(jnp.float32), axis=0, keepdims=True)
        held[0, 1:2] = jnp.sum(dvalue[...].astype(jnp.float32), axis=0, keepdims=True)
        mem_span = slice(2 * HALF, CONT)
        held[0, VECTORS:] = times_back(dkey[mem_span], pool[1, :width]) + times_back(
            dvalue[mem_span], pool[2, :width]
        )
        stage(CHIP, 8)
        small.start()
        lax.fori_loop(0, 6, chunk_body, 0)
        for name, index in LAST:
            if name == SMALL:
                small.step(index)
            else:
                stage(name, index)
        family = shard // 2
        memory_out[family] = held[1, VECTORS:]
        memory_out[1 - family] = got[1, VECTORS:]
        vec_out[...] = held[5, :VECTORS]
        returned.arrive()
        cont_back.arrive()
        for step in (4, 5):
            mine = pl.ds((5 - step) * 256, 256)
            pltpu.make_async_copy(
                staged.at[step % 2], grad_prompt.at[mine], local.at[8 + step % 2]
            ).wait()
        for index in (2, 3, 4, 5, 6, 7, 8):
            if index != 4:
                item(index).given()
        for index in range(ITEMS):
            item(index).finish(place(index), out_sem.at[index])
        small.finish()
        for swap in (returned, cont_back, *(to_partner(index) for index in range(4))):
            swap.finish()


def back(
    act, gdown, first, ginner, mixed, gbranch, ghidden, rows, qkv, out_taken, sums,
    query, key, value, grads, log, bias,
):
    width = rows.shape[1]
    low = jnp.bfloat16
    wide = jnp.float32

    def block(count):
        return pl.BlockSpec((count, 2 * HEAD), lambda pair: (0, pair))

    dma = pltpu.SemaphoreType.DMA
    part = width // 4

    def buffers(count, columns, part=part):
        return [
            pltpu.VMEM((count, 4, part, columns), low),
            pltpu.VMEM((2, 4, part, columns), low),
            pltpu.VMEM((count, 4, part, columns), low),
            pltpu.VMEM((count, 2, part // 2, columns), low),
            pltpu.VMEM((count, 2, part // 2, columns), low),
            pltpu.VMEM((count, part // 2, columns), low),
            pltpu.VMEM((count, part // 2, columns), low),
            pltpu.VMEM((count, part, columns), low),
            pltpu.VMEM((count, part, columns), low),
        ]

    shape = jax.ShapeDtypeStruct
    return pl.pallas_call(
        back_kernel,
        grid=(PAIRS,),
        in_specs=[WHERE] * 11
        + [
            block(QROWS), block(KEYS), block(KEYS), block(QROWS), block(QROWS),
            pl.BlockSpec((None, 2, QROWS), lambda pair: (pair, 0, 0)),
            pl.BlockSpec((CLEN, OWN), lambda pair: (0, 0)),
        ],
        out_specs=[WHERE] * 9
        + [
            pl.BlockSpec((2, MEM, width), lambda pair: (0, 0, 0)),
            pl.BlockSpec((VECTORS, width), lambda pair: (0, 0)),
        ],
        out_shape=[
            shape((width, width), low),
            shape((part, 4 * width), low),
            shape((part, width), low),
            shape((2, 2, part, width // 2), low),
            shape((TINY, part, width // 2), low),
            shape((OWN // 2, width), low),
            shape((HALF, width), low),
            shape((OWN // 2, width), low),
            shape((OWN // 2, width), low),
            shape((2, MEM, width), wide),
            shape((VECTORS, width), wide),
        ],
        scratch_shapes=buffers(WIDE, width)
        + buffers(NARROW, width // 2)
        + buffers(TINY, width // 2, part // 2)
        + [
            pltpu.VMEM((4, QROWS, width), low),
            pltpu.VMEM((KEYS, width), low),
            pltpu.VMEM((QROWS, width), low),
            pltpu.VMEM((KEYS, width), low),
            pltpu.VMEM((KEYS, width), low),
            pltpu.VMEM((KEYS, 2 * HEAD), wide),
            pltpu.VMEM((KEYS, 2 * HEAD), wide),
            pltpu.VMEM((2 * HEAD, QROWS), wide),
            pltpu.VMEM((2 * HEAD, QROWS), wide),
            pltpu.VMEM((HALF, width), low),
            pltpu.VMEM((2, 256, width), wide),
            pltpu.VMEM((2, 256, width), low),
            pltpu.VMEM((6, 2 * VECTORS, width), wide),
            pltpu.VMEM((5, 2 * VECTORS, width), wide),
            dma((ITEMS, SEND + 1)),
            dma((ITEMS, SEND + 1)),
            dma((5,)),
            dma((5,)),
            dma((6,)),
            dma((6,)),
            dma((10,)),
            dma((ITEMS,)),
        ],
        compiler_params=pltpu.CompilerParams(
            vmem_limit_bytes=67043328, collective_id=1, has_side_effects=True
        ),
        name="back",
    )(
        act, gdown, first, ginner, mixed, gbranch, ghidden, rows, qkv, out_taken, sums,
        query, key, value, grads, mixed, log, bias,
    )


def cont_ranks(owner_ref, shard):
    prompt_of = shard // 2
    conts = OWN // CLEN
    place = []
    before = jnp.int32(0)
    for cont in range(conts):
        owned = (owner_ref[0, shard * conts + cont] == prompt_of).astype(jnp.int32)
        place.append(jnp.where(owned == 1, before, 2 + cont - before))
        before = before + owned
    order = []
    for position in range(conts):
        found = jnp.int32(0)
        for cont in range(conts):
            found = found + jnp.where(place[cont] == position, cont, 0)
        order.append(found)
    return place, order


def block_of(index):
    return pl.ds(pl.multiple_of(index * CLEN, CLEN), CLEN)


def prepare_kernel(
    owner_ref, length_ref, follow_ref, cotan_ref, memory_ref, query_ref, key_ref, value_ref,
    out_ref, up_ref, *refs,
):
    vectors = refs[:9]
    (
        qkv, wide, vec, kept, sent, memory, kept_cot, sent_cot, bias,
    ) = refs[9:]
    shard = lax.axis_index("shard")
    across = shard ^ 2
    conts = OWN // CLEN
    width = query_ref.shape[1]
    _, order = cont_ranks(owner_ref, shard)
    _, order_across = cont_ranks(owner_ref, across)
    for index in range(2):
        span = slice(index * CLEN, (index + 1) * CLEN)
        kept[span] = follow_ref[0, block_of(order[index])]
        sent[span] = follow_ref[0, block_of(order[2 + index])]
        kept_cot[span] = cotan_ref[0, block_of(order[index])]
        sent_cot[span] = cotan_ref[0, block_of(order[2 + index])]
    position = lax.broadcasted_iota(jnp.int32, (CLEN, CLEN), 0)
    for index in range(conts):
        if index < 2:
            length = length_ref[0, shard * conts + order[index]]
        else:
            length = length_ref[0, across * conts + order_across[index]]
        valid = (position < length) | (position >= CLEN - WRITE)
        bias[:, index * CLEN : (index + 1) * CLEN] = jnp.where(valid, 0.0, NEGATIVE)
    memory[...] = jnp.zeros_like(memory)
    memory[:READ] = memory_ref[0, shard // 2]
    qkv[:, :width] = query_ref[...]
    qkv[:, width : 2 * width] = key_ref[...]
    qkv[:, 2 * width :] = value_ref[...]
    wide[:, :width] = out_ref[...]
    wide[:, width:] = up_ref[...]
    vec[...] = jnp.zeros_like(vec)
    for index, vector in enumerate(vectors):
        vec[index : index + 1, : vector.shape[1]] = vector[...]


def prepare(owner, length, follow, cotan, memory, query, key, value, out, up, vectors):
    low = jnp.bfloat16
    width = query.shape[1]
    share = query.shape[0]
    shape = jax.ShapeDtypeStruct
    half = shape((OWN // 2, width), low)
    inside = pl.BlockSpec(memory_space=pltpu.VMEM)
    scalars = pl.BlockSpec(memory_space=pltpu.SMEM)
    return pl.pallas_call(
        prepare_kernel,
        in_specs=[scalars] * 2 + [inside] * 17,
        out_specs=[inside] * 9,
        out_shape=[
            shape((share, 3 * width), low), shape((share, 5 * width), low),
            shape((VECTORS, 2 * HEAD), low), half, half, shape((MEM, width), low), half, half,
            shape((CLEN, OWN), jnp.float32),
        ],
        name="prepare",
    )(
        owner, length, follow, cotan, memory, query, key, value, out, up,
        *(vector[None] for vector in vectors),
    )


def finish_kernel(
    owner_ref, output_ref, returned_ref, kept_grad, back_grad, down_ref, up_ref, out_ref, qkv_ref,
    last_ref, memory_ref, vec_ref,
    prompt_out, follow_out, follow_grad, memory_grad, query_sum, key_sum, value_sum, out_sum,
    up_sum, down_sum, *vectors,
):
    shard = lax.axis_index("shard")
    wide = jnp.float32
    width = down_ref.shape[1]
    part = width // 4
    place, _ = cont_ranks(owner_ref, shard)
    prompt_out[0] = output_ref[:HALF]
    for cont, position in enumerate(place):
        span = slice(cont * CLEN, (cont + 1) * CLEN)
        here = block_of(jnp.where(position < 2, position, 0))
        there = block_of(jnp.where(position < 2, 0, position - 2))
        kept = position < 2

        @pl.when(kept)
        def _():
            follow_out[0, span] = output_ref[pl.ds(HALF + here.start, CLEN)]
            follow_grad[0, span] = kept_grad[here]

        @pl.when(jnp.logical_not(kept))
        def _():
            follow_out[0, span] = returned_ref[there]
            follow_grad[0, span] = back_grad[there]

    memory_grad[0] = memory_ref[:, :READ].astype(jnp.bfloat16)
    down_sum[...] = down_ref[...].astype(wide)
    up_sum[...] = up_ref[...].astype(wide)
    out_sum[...] = out_ref[...].astype(wide)
    for number, target in enumerate((query_sum, key_sum, value_sum)):
        source = slice(number * 2 * HEAD, (number + 1) * 2 * HEAD)
        for index in range(TINY):
            lanes = slice((4 + index) * 2 * HEAD, (5 + index) * 2 * HEAD)
            target[:, lanes] = last_ref[index, :, source].astype(wide)
    for index in range(2):
        for side in range(2):
            lanes = slice((2 * index + side) * 2 * HEAD, (2 * index + side + 1) * 2 * HEAD)
            for number, target in enumerate((query_sum, key_sum, value_sum)):
                source = slice(number * 2 * HEAD, (number + 1) * 2 * HEAD)
                target[:, lanes] = qkv_ref[index, side, :, source].astype(wide)
    for index in range(8):
        row = vec_ref[index : index + 1]
        total = jnp.zeros((1, part), wide)
        for quarter in range(4):
            total += jnp.where(shard == quarter, row[:, quarter * part : (quarter + 1) * part], 0.0)
        vectors[index][...] = total.reshape(part)
    total = jnp.zeros((1, width), wide)
    for quarter in range(4):
        total += jnp.where(shard == quarter, vec_ref[8 + quarter : 9 + quarter], 0.0)
    vectors[8][...] = total.reshape(width)


def finish(owner, output, returned, kept, back_grad, down, up, out, qkv, last, memory, vec):
    low = jnp.bfloat16
    wide = jnp.float32
    shape = jax.ShapeDtypeStruct
    width = down.shape[1]
    part = width // 4
    inside = pl.BlockSpec(memory_space=pltpu.VMEM)
    square = shape((part, width), wide)

    def whole(array):
        return pl.BlockSpec(array.shape, lambda step: (0,) * array.ndim)

    return pl.pallas_call(
        finish_kernel,
        grid=(1,),
        in_specs=[pl.BlockSpec(memory_space=pltpu.SMEM)]
        + [
            whole(array)
            for array in (
                output, returned, kept, back_grad, down, up, out, qkv, last, memory, vec
            )
        ],
        out_specs=[inside] * 19,
        out_shape=[
            shape((1, HALF, width), low), shape((1, OWN, width), low), shape((1, OWN, width), low),
            shape((1, 2, READ, width), low), square, square, square, square,
            shape((part, 4 * width), wide), shape((width, width), wide),
        ]
        + [shape((part,), wide)] * 8
        + [shape((width,), wide)],
        compiler_params=pltpu.CompilerParams(vmem_limit_bytes=67043328),
        name="finish",
    )(owner, output, returned, kept, back_grad, down, up, out, qkv, last, memory, vec)


def body_pairs(
    prompt_rows, follow_rows, memory_rows, follow_owner, follow_length,
    query_weight, key_weight, value_weight, out_weight, query_bias, value_bias, out_bias,
    first_gain, first_shift, up_weight, up_bias, down_weight, down_bias,
    second_gain, second_shift, prompt_cotan, follow_cotan,
):
    qkv, wide, vec, kept, sent, memory, kept_cot, sent_cot, bias = prepare(
        follow_owner, follow_length, follow_rows, follow_cotan, memory_rows,
        query_weight, key_weight, value_weight, out_weight, up_weight,
        (
            query_bias, value_bias, out_bias, first_gain, first_shift, down_bias,
            second_gain, second_shift, up_bias,
        ),
    )
    (
        qkv_mat, _, _, _, key_rows,
        output, activated, first_low, grad_down, grad_inner, grad_branch, grad_mixed, grad_hidden,
        mixed, log, query_low, key_low, value_low, sums,
    ) = front(
        qkv, wide, down_weight, vec, prompt_rows[0], kept, sent, memory, prompt_cotan[0],
        kept_cot, sent_cot, bias,
    )
    (
        down_sum, up_sum, out_sum, qkv_sum, last_sum, returned_out, grad_prompt, grad_kept, returned_grad,
        memory_sum, sums,
    ) = back(
        activated, grad_down, first_low, grad_inner, mixed, grad_branch, grad_hidden, key_rows,
        qkv_mat, output, sums,
        query_low, key_low, value_low, grad_mixed, log, bias,
    )
    (
        prompt_out, follow_out, follow_grad, grad_memory, query_sum, key_sum, value_sum, out_sum,
        up_sum, down_sum, *vectors,
    ) = finish(
        follow_owner, output, returned_out, grad_kept, returned_grad, down_sum, up_sum, out_sum,
        qkv_sum, last_sum, memory_sum, sums,
    )
    return (
        prompt_out, follow_out, grad_prompt[None], follow_grad, grad_memory,
        query_sum, key_sum, value_sum, out_sum, vectors[0], vectors[1], vectors[2], vectors[3],
        vectors[4], up_sum, vectors[8], down_sum, vectors[5], vectors[6], vectors[7],
    )


def solution(mesh):
    return jax.shard_map(
        body_pairs if pairs_fit(mesh) else body_any,
        mesh=mesh,
        in_specs=(
            P("grp", "shard", None),
            P("grp", "shard", None),
            P("grp", None, None, None),
            P("grp", None),
            P("grp", None),
            P(("grp", "shard"), None),
            P(("grp", "shard"), None),
            P(("grp", "shard"), None),
            P(("grp", "shard"), None),
            P(("grp", "shard")),
            P(("grp", "shard")),
            P(("grp", "shard")),
            P(("grp", "shard")),
            P(("grp", "shard")),
            P(("grp", "shard"), None),
            P(("grp", "shard")),
            P(("grp", "shard"), None),
            P(("grp", "shard")),
            P(("grp", "shard")),
            P(("grp", "shard")),
            P("grp", "shard", None),
            P("grp", "shard", None),
        ),
        out_specs=(
            P("grp", "shard", None),
            P("grp", "shard", None),
            P("grp", "shard", None),
            P("grp", "shard", None),
            P("grp", None, None, None),
            P("shard", None),
            P("shard", None),
            P("shard", None),
            P("shard", None),
            P("shard"),
            P("shard"),
            P("shard"),
            P("shard"),
            P("shard"),
            P("shard", None),
            P("shard"),
            P("shard", None),
            P("shard"),
            P("shard"),
            P("shard"),
        ),
        check_vma=False,
    )
```

```python
import jax
import jax.numpy as jnp
from jax import lax
from jax.experimental import pallas as pl
from jax.experimental.pallas import tpu as pltpu
from jax.sharding import PartitionSpec as P

HEADS = 12
HEAD = 64
READ = 10
WRITE = 10
PLEN = 1024
CLEN = 128
CONTS_PER = 8


EPSILON = 1e-12
SCALE = 0.125
NEGATIVE = -1e30
ROOT_HALF = 0.7071067811865476
ROOT_GAUSS = 0.3989422804014327


def product(left, right):
    return jnp.dot(left, right, preferred_element_type=jnp.float32)


def times_back(left, right):
    return lax.dot_general(
        left, right, (((1,), (1,)), ((), ())), preferred_element_type=jnp.float32
    )


def outer_sum(left, right):
    return lax.dot_general(
        left, right, (((0,), (0,)), ((), ())), preferred_element_type=jnp.float32
    )


def column_sum(values):
    return jnp.sum(values.astype(jnp.float32), axis=0)


def layer_norm(hidden, gain, shift):
    center = hidden - jnp.mean(hidden, axis=-1, keepdims=True)
    inverse = lax.rsqrt(jnp.mean(center * center, axis=-1, keepdims=True) + EPSILON)
    normed = center * inverse
    return (normed * gain.astype(jnp.float32) + shift.astype(jnp.float32), normed, inverse)


def norm_back(grad_normed, normed, inverse):
    centered = grad_normed - jnp.mean(grad_normed, axis=-1, keepdims=True)
    return inverse * (centered - normed * jnp.mean(grad_normed * normed, axis=-1, keepdims=True))


def gelu_exact(hidden):
    return 0.5 * hidden * (1.0 + lax.erf(hidden * ROOT_HALF))


def gelu_slope(hidden):
    return (
        0.5 * (1.0 + lax.erf(hidden * ROOT_HALF))
        + hidden * jnp.exp(-0.5 * hidden * hidden) * ROOT_GAUSS
    )


def split_heads(values):
    return values.reshape(values.shape[0], values.shape[1], HEADS, HEAD)


def block_scores(queries, keys, valid):
    scores = (
        jnp.einsum(
            "nqhd,nkhd->nhqk",
            split_heads(queries),
            split_heads(keys),
            preferred_element_type=jnp.float32,
        )
        * SCALE
    )
    return jnp.where(valid[:, None, None, :], scores, NEGATIVE)


def attend_forward(queries, keys, values, valid):
    scores = block_scores(queries, keys, valid)
    maximum = jnp.max(scores, axis=-1, keepdims=True)
    powers = jnp.exp(scores - maximum)
    totals = jnp.sum(powers, axis=-1, keepdims=True)
    chances = (powers / totals).astype(jnp.bfloat16)
    result = jnp.einsum(
        "nhqk,nkhd->nqhd", chances, split_heads(values), preferred_element_type=jnp.float32
    )
    return (result.reshape(-1, queries.shape[2]), maximum + jnp.log(totals))


def attend_backward(queries, keys, values, valid, logsum, grad_out):
    width = queries.shape[2]
    scores = block_scores(queries, keys, valid)
    chances = jnp.exp(scores - logsum)
    grad_heads = split_heads(grad_out)
    grad_chance = jnp.einsum(
        "nqhd,nkhd->nhqk", grad_heads, split_heads(values), preferred_element_type=jnp.float32
    )
    inner = jnp.sum(chances * grad_chance, axis=-1, keepdims=True)
    grad_score = (chances * (grad_chance - inner)).astype(jnp.bfloat16)
    grad_query = (
        jnp.einsum(
            "nhqk,nkhd->nqhd", grad_score, split_heads(keys), preferred_element_type=jnp.float32
        )
        * SCALE
    )
    grad_key = (
        jnp.einsum(
            "nhqk,nqhd->nkhd", grad_score, split_heads(queries), preferred_element_type=jnp.float32
        )
        * SCALE
    )
    grad_value = jnp.einsum(
        "nhqk,nqhd->nkhd",
        chances.astype(jnp.bfloat16),
        grad_heads,
        preferred_element_type=jnp.float32,
    )
    span = keys.shape[1]
    return (
        grad_query.reshape(-1, width),
        grad_key.reshape(keys.shape[0], span, width),
        grad_value.reshape(keys.shape[0], span, width),
    )


def body_any(
    prompt_rows,
    follow_rows,
    memory_rows,
    follow_owner,
    follow_length,
    query_weight,
    key_weight,
    value_weight,
    out_weight,
    query_bias,
    value_bias,
    out_bias,
    first_gain,
    first_shift,
    up_weight,
    up_bias,
    down_weight,
    down_bias,
    second_gain,
    second_shift,
    prompt_cotan,
    follow_cotan,
):
    (
        query_mat,
        key_mat,
        value_mat,
        out_mat,
        query_add,
        value_add,
        out_add,
        gain_one,
        shift_one,
        up_mat,
        up_add,
        down_mat,
        down_add,
        gain_two,
        shift_two,
    ) = (
        lax.all_gather(query_weight, ("grp", "shard"), axis=0, tiled=True),
        lax.all_gather(key_weight, ("grp", "shard"), axis=0, tiled=True),
        lax.all_gather(value_weight, ("grp", "shard"), axis=0, tiled=True),
        lax.all_gather(out_weight, ("grp", "shard"), axis=0, tiled=True),
        lax.all_gather(query_bias, ("grp", "shard"), axis=0, tiled=True),
        lax.all_gather(value_bias, ("grp", "shard"), axis=0, tiled=True),
        lax.all_gather(out_bias, ("grp", "shard"), axis=0, tiled=True),
        lax.all_gather(first_gain, ("grp", "shard"), axis=0, tiled=True),
        lax.all_gather(first_shift, ("grp", "shard"), axis=0, tiled=True),
        lax.all_gather(up_weight, ("grp", "shard"), axis=0, tiled=True),
        lax.all_gather(up_bias, ("grp", "shard"), axis=0, tiled=True),
        lax.all_gather(down_weight, ("grp", "shard"), axis=0, tiled=True),
        lax.all_gather(down_bias, ("grp", "shard"), axis=0, tiled=True),
        lax.all_gather(second_gain, ("grp", "shard"), axis=0, tiled=True),
        lax.all_gather(second_shift, ("grp", "shard"), axis=0, tiled=True),
    )
    shard_index = lax.axis_index("shard")
    prompt = prompt_rows[0]
    follow = follow_rows[0]
    p_count = prompt.shape[0]
    f_count = follow.shape[0]
    width = prompt.shape[1]
    families = memory_rows.shape[1]
    all_rows = jnp.concatenate([prompt, follow], axis=0)
    memory_flat = memory_rows[0].reshape(families * READ, width)
    query_low = (product(all_rows, query_mat) + query_add.astype(jnp.float32)).astype(jnp.bfloat16)
    key_low = product(all_rows, key_mat).astype(jnp.bfloat16)
    value_low = (product(all_rows, value_mat) + value_add.astype(jnp.float32)).astype(jnp.bfloat16)
    mem_key = product(memory_flat, key_mat).astype(jnp.bfloat16).reshape(families, READ, width)
    mem_value = (
        (product(memory_flat, value_mat) + value_add.astype(jnp.float32))
        .astype(jnp.bfloat16)
        .reshape(families, READ, width)
    )
    half_prompt = PLEN // 2
    per_block = CONTS_PER // 2
    prompt_blocks = p_count // half_prompt
    conts_here = f_count // CLEN
    positions = jnp.arange(CLEN)
    open_span = jnp.ones((per_block, READ + PLEN), dtype=bool)
    owner_row = follow_owner[0]
    length_row = follow_length[0]
    prompt_keys, prompt_values = (
        lax.all_gather(key_low[:p_count], "shard", axis=0, tiled=True),
        lax.all_gather(value_low[:p_count], "shard", axis=0, tiled=True),
    )
    key_table = prompt_keys.reshape(families, PLEN, width)
    value_table = prompt_values.reshape(families, PLEN, width)

    def prompt_inputs(block):
        start = block * half_prompt
        family = (shard_index * p_count + start) // PLEN
        keys = jnp.concatenate([mem_key[family], key_table[family]], axis=0)[None]
        values = jnp.concatenate([mem_value[family], value_table[family]], axis=0)[None]
        valid = jnp.ones((1, READ + PLEN), dtype=bool)
        return (query_low[start : start + half_prompt][None], keys, values, valid, family)

    def follow_inputs(block):
        first_row = p_count + block * per_block * CLEN
        chosen = shard_index * conts_here + block * per_block + jnp.arange(per_block)
        owners = owner_row[chosen]
        lengths = length_row[chosen]
        own_keys = key_low[first_row : first_row + per_block * CLEN].reshape(per_block, CLEN, width)
        own_values = value_low[first_row : first_row + per_block * CLEN].reshape(
            per_block, CLEN, width
        )
        keys = jnp.concatenate([mem_key[owners], key_table[owners], own_keys], axis=1)
        values = jnp.concatenate([mem_value[owners], value_table[owners], own_values], axis=1)
        own_valid = (positions[None, :] < lengths[:, None]) | (positions[None, :] >= CLEN - WRITE)
        valid = jnp.concatenate([open_span, own_valid], axis=1)
        queries = query_low[first_row : first_row + per_block * CLEN].reshape(
            per_block, CLEN, width
        )
        return (queries, keys, values, valid, owners)

    attended = []
    saved = []
    block = 0
    queries, keys, values, valid, family = prompt_inputs(block)
    result, logsum = attend_forward(queries, keys, values, valid)
    attended.append(result)
    saved.append(logsum)
    block = 0
    queries, keys, values, valid, owners = follow_inputs(block)
    result, logsum = attend_forward(queries, keys, values, valid)
    attended.append(result)
    saved.append(logsum)
    mixed = jnp.concatenate(attended, axis=0).astype(jnp.bfloat16)
    branch = product(mixed, out_mat) + out_add.astype(jnp.float32)
    first, normed_one, inverse_one = layer_norm(
        all_rows.astype(jnp.float32) + branch, gain_one, shift_one
    )
    first_low = first.astype(jnp.bfloat16)
    inner = product(first_low, up_mat) + up_add.astype(jnp.float32)
    activated = gelu_exact(inner).astype(jnp.bfloat16)
    second = product(activated, down_mat) + down_add.astype(jnp.float32)
    output, normed_two, inverse_two = layer_norm(first + second, gain_two, shift_two)
    output = output.astype(jnp.bfloat16)
    (
        query_mat,
        key_mat,
        value_mat,
        out_mat,
        query_add,
        value_add,
        out_add,
        gain_one,
        shift_one,
        up_mat,
        up_add,
        down_mat,
        down_add,
        gain_two,
        shift_two,
    ) = (
        lax.all_gather(query_weight, ("grp", "shard"), axis=0, tiled=True),
        lax.all_gather(key_weight, ("grp", "shard"), axis=0, tiled=True),
        lax.all_gather(value_weight, ("grp", "shard"), axis=0, tiled=True),
        lax.all_gather(out_weight, ("grp", "shard"), axis=0, tiled=True),
        lax.all_gather(query_bias, ("grp", "shard"), axis=0, tiled=True),
        lax.all_gather(value_bias, ("grp", "shard"), axis=0, tiled=True),
        lax.all_gather(out_bias, ("grp", "shard"), axis=0, tiled=True),
        lax.all_gather(first_gain, ("grp", "shard"), axis=0, tiled=True),
        lax.all_gather(first_shift, ("grp", "shard"), axis=0, tiled=True),
        lax.all_gather(up_weight, ("grp", "shard"), axis=0, tiled=True),
        lax.all_gather(up_bias, ("grp", "shard"), axis=0, tiled=True),
        lax.all_gather(down_weight, ("grp", "shard"), axis=0, tiled=True),
        lax.all_gather(down_bias, ("grp", "shard"), axis=0, tiled=True),
        lax.all_gather(second_gain, ("grp", "shard"), axis=0, tiled=True),
        lax.all_gather(second_shift, ("grp", "shard"), axis=0, tiled=True),
    )
    cotangent = jnp.concatenate([prompt_cotan[0], follow_cotan[0]], axis=0).astype(jnp.float32)
    grad_gain_two = jnp.sum(cotangent * normed_two, axis=0)
    grad_shift_two = jnp.sum(cotangent, axis=0)
    grad_mid = norm_back(cotangent * gain_two.astype(jnp.float32), normed_two, inverse_two)
    grad_down = grad_mid.astype(jnp.bfloat16)
    grad_down_mat = outer_sum(activated, grad_down)
    grad_down_add = column_sum(grad_down)
    grad_inner = (times_back(grad_down, down_mat) * gelu_slope(inner)).astype(jnp.bfloat16)
    grad_up_mat = outer_sum(first_low, grad_inner)
    grad_up_add = column_sum(grad_inner)
    grad_first = grad_mid + times_back(grad_inner, up_mat)
    grad_gain_one = jnp.sum(grad_first * normed_one, axis=0)
    grad_shift_one = jnp.sum(grad_first, axis=0)
    grad_hidden = norm_back(grad_first * gain_one.astype(jnp.float32), normed_one, inverse_one)
    grad_branch = grad_hidden.astype(jnp.bfloat16)
    grad_out_mat = outer_sum(mixed, grad_branch)
    grad_out_add = column_sum(grad_branch)
    grad_mixed = times_back(grad_branch, out_mat).astype(jnp.bfloat16)
    mem_key_acc = jnp.zeros((families, READ, width), jnp.float32)
    mem_value_acc = jnp.zeros((families, READ, width), jnp.float32)
    prompt_key_acc = jnp.zeros((families, PLEN, width), jnp.float32)
    prompt_value_acc = jnp.zeros((families, PLEN, width), jnp.float32)
    block = 0
    queries, keys, values, valid, family = prompt_inputs(block)
    start = block * half_prompt
    grad_query, grad_key, grad_value = attend_backward(
        queries, keys, values, valid, saved[block], grad_mixed[start : start + half_prompt][None]
    )
    query_parts = grad_query
    mem_key_acc = mem_key_acc.at[family].add(grad_key[0, :READ])
    mem_value_acc = mem_value_acc.at[family].add(grad_value[0, :READ])
    prompt_key_acc = prompt_key_acc.at[family].add(grad_key[0, READ:])
    prompt_value_acc = prompt_value_acc.at[family].add(grad_value[0, READ:])
    prompt_query_low = query_parts.astype(jnp.bfloat16)
    block = 0
    queries, keys, values, valid, owners = follow_inputs(block)
    first_row = p_count + block * per_block * CLEN
    grad_slice = grad_mixed[first_row : first_row + per_block * CLEN].reshape(
        per_block, CLEN, width
    )
    grad_query, grad_key, grad_value = attend_backward(
        queries, keys, values, valid, saved[prompt_blocks + block], grad_slice
    )
    mem_key_acc = mem_key_acc.at[owners].add(grad_key[:, :READ])
    mem_value_acc = mem_value_acc.at[owners].add(grad_value[:, :READ])
    prompt_key_acc = prompt_key_acc.at[owners].add(grad_key[:, READ : READ + PLEN])
    prompt_value_acc = prompt_value_acc.at[owners].add(grad_value[:, READ : READ + PLEN])
    own_key_parts = grad_key[:, READ + PLEN :].reshape(-1, width)
    own_value_parts = grad_value[:, READ + PLEN :].reshape(-1, width)
    prompt_key_grad, prompt_value_grad = (
        lax.psum_scatter(
            prompt_key_acc.reshape(families * PLEN, width).astype(jnp.bfloat16),
            "shard",
            scatter_dimension=0,
            tiled=True,
        ).astype(jnp.float32),
        lax.psum_scatter(
            prompt_value_acc.reshape(families * PLEN, width).astype(jnp.bfloat16),
            "shard",
            scatter_dimension=0,
            tiled=True,
        ).astype(jnp.float32),
    )
    follow_query_low = grad_query.astype(jnp.bfloat16)
    follow_key_low = own_key_parts.astype(jnp.bfloat16)
    follow_value_low = own_value_parts.astype(jnp.bfloat16)
    mem_key_sum, mem_value_sum = (
        lax.psum(mem_key_acc.astype(jnp.bfloat16), "shard").astype(jnp.float32),
        lax.psum(mem_value_acc.astype(jnp.bfloat16), "shard").astype(jnp.float32),
    )
    grad_query_low = jnp.concatenate([prompt_query_low, follow_query_low], axis=0)
    grad_key_low = jnp.concatenate([prompt_key_grad.astype(jnp.bfloat16), follow_key_low], axis=0)
    grad_value_low = jnp.concatenate(
        [prompt_value_grad.astype(jnp.bfloat16), follow_value_low], axis=0
    )
    mem_key_low = mem_key_sum.astype(jnp.bfloat16).reshape(families * READ, width)
    mem_value_low = mem_value_sum.astype(jnp.bfloat16).reshape(families * READ, width)
    grad_rows_all = (
        grad_hidden
        + times_back(grad_query_low, query_mat)
        + times_back(grad_key_low, key_mat)
        + times_back(grad_value_low, value_mat)
    ).astype(jnp.bfloat16)
    grad_memory = (
        (times_back(mem_key_low, key_mat) + times_back(mem_value_low, value_mat))
        .astype(jnp.bfloat16)
        .reshape(1, families, READ, width)
    )
    leader = (shard_index == 0).astype(jnp.float32)
    grad_query_mat = outer_sum(all_rows, grad_query_low)
    grad_query_add = column_sum(grad_query_low)
    grad_key_mat = outer_sum(all_rows, grad_key_low) + leader * outer_sum(memory_flat, mem_key_low)
    grad_value_mat = outer_sum(all_rows, grad_value_low) + leader * outer_sum(
        memory_flat, mem_value_low
    )
    grad_value_add = column_sum(grad_value_low) + leader * column_sum(mem_value_low)
    pieces = (
        lax.psum_scatter(
            grad_query_mat.astype(jnp.bfloat16), "shard", scatter_dimension=0, tiled=True
        ).astype(jnp.float32),
        lax.psum_scatter(
            grad_key_mat.astype(jnp.bfloat16), "shard", scatter_dimension=0, tiled=True
        ).astype(jnp.float32),
        lax.psum_scatter(
            grad_value_mat.astype(jnp.bfloat16), "shard", scatter_dimension=0, tiled=True
        ).astype(jnp.float32),
        lax.psum_scatter(
            grad_out_mat.astype(jnp.bfloat16), "shard", scatter_dimension=0, tiled=True
        ).astype(jnp.float32),
        lax.psum_scatter(
            grad_query_add.astype(jnp.bfloat16), "shard", scatter_dimension=0, tiled=True
        ).astype(jnp.float32),
        lax.psum_scatter(
            grad_value_add.astype(jnp.bfloat16), "shard", scatter_dimension=0, tiled=True
        ).astype(jnp.float32),
        lax.psum_scatter(
            grad_out_add.astype(jnp.bfloat16), "shard", scatter_dimension=0, tiled=True
        ).astype(jnp.float32),
        lax.psum_scatter(
            grad_gain_one.astype(jnp.bfloat16), "shard", scatter_dimension=0, tiled=True
        ).astype(jnp.float32),
        lax.psum_scatter(
            grad_shift_one.astype(jnp.bfloat16), "shard", scatter_dimension=0, tiled=True
        ).astype(jnp.float32),
        lax.psum_scatter(
            grad_up_mat.astype(jnp.bfloat16), "shard", scatter_dimension=0, tiled=True
        ).astype(jnp.float32),
        lax.psum_scatter(
            grad_up_add.astype(jnp.bfloat16), "shard", scatter_dimension=0, tiled=True
        ).astype(jnp.float32),
        lax.psum_scatter(
            grad_down_mat.astype(jnp.bfloat16), "shard", scatter_dimension=0, tiled=True
        ).astype(jnp.float32),
        lax.psum_scatter(
            grad_down_add.astype(jnp.bfloat16), "shard", scatter_dimension=0, tiled=True
        ).astype(jnp.float32),
        lax.psum_scatter(
            grad_gain_two.astype(jnp.bfloat16), "shard", scatter_dimension=0, tiled=True
        ).astype(jnp.float32),
        lax.psum_scatter(
            grad_shift_two.astype(jnp.bfloat16), "shard", scatter_dimension=0, tiled=True
        ).astype(jnp.float32),
    )
    summed = (
        lax.psum(pieces[0].astype(jnp.bfloat16), "grp").astype(jnp.float32),
        lax.psum(pieces[1].astype(jnp.bfloat16), "grp").astype(jnp.float32),
        lax.psum(pieces[2].astype(jnp.bfloat16), "grp").astype(jnp.float32),
        lax.psum(pieces[3].astype(jnp.bfloat16), "grp").astype(jnp.float32),
        lax.psum(pieces[4].astype(jnp.bfloat16), "grp").astype(jnp.float32),
        lax.psum(pieces[5].astype(jnp.bfloat16), "grp").astype(jnp.float32),
        lax.psum(pieces[6].astype(jnp.bfloat16), "grp").astype(jnp.float32),
        lax.psum(pieces[7].astype(jnp.bfloat16), "grp").astype(jnp.float32),
        lax.psum(pieces[8].astype(jnp.bfloat16), "grp").astype(jnp.float32),
        lax.psum(pieces[9].astype(jnp.bfloat16), "grp").astype(jnp.float32),
        lax.psum(pieces[10].astype(jnp.bfloat16), "grp").astype(jnp.float32),
        lax.psum(pieces[11].astype(jnp.bfloat16), "grp").astype(jnp.float32),
        lax.psum(pieces[12].astype(jnp.bfloat16), "grp").astype(jnp.float32),
        lax.psum(pieces[13].astype(jnp.bfloat16), "grp").astype(jnp.float32),
        lax.psum(pieces[14].astype(jnp.bfloat16), "grp").astype(jnp.float32),
    )
    return (
        output[:p_count][None],
        output[p_count:][None],
        grad_rows_all[:p_count][None],
        grad_rows_all[p_count:][None],
        grad_memory,
        summed[0],
        summed[1],
        summed[2],
        summed[3],
        summed[4],
        summed[5],
        summed[6],
        summed[7],
        summed[8],
        summed[9],
        summed[10],
        summed[11],
        summed[12],
        summed[13],
        summed[14],
    )


MEM = 16
HALF = PLEN // 2
OWN = 512
CONT = HALF + HALF + MEM
KEYS = CONT + OWN
QROWS = HALF + OWN
PAIRS = HEADS // 2
NAMES = ("grp", "shard")


def pairs_fit(mesh):
    return mesh.shape["shard"] == 4 and mesh.shape["grp"] == 8


def head_mask(head):
    lane = lax.broadcasted_iota(jnp.int32, (1, 2 * HEAD), 1)
    return lane // HEAD == head


def pick(mask, values):
    return jnp.where(mask, values.astype(jnp.float32), 0.0).astype(jnp.bfloat16)


def flip(values):
    return values.astype(jnp.float32).T.astype(jnp.bfloat16)


def own_scores(keys, queries):
    parts = []
    for cont in range(OWN // CLEN):
        part = slice(cont * CLEN, (cont + 1) * CLEN)
        parts.append(times_back(keys[part], queries[part]))
    return jnp.concatenate(parts, axis=1)


def attend_pair(query_ref, key_ref, value_ref, bias_ref, out_ref, log_ref):
    mem_valid = lax.broadcasted_iota(jnp.int32, (MEM, 1), 0) < READ
    value_flip = flip(value_ref[...])
    results = []
    for head in range(2):
        mask = head_mask(head)
        queries = pick(mask, query_ref[...])
        main = times_back(key_ref[: 2 * HALF], queries)
        memory = jnp.where(mem_valid, times_back(key_ref[2 * HALF : CONT], queries), NEGATIVE)
        own = own_scores(key_ref[CONT:], queries[HALF:]) + bias_ref[...]
        top = jnp.maximum(
            jnp.max(main, axis=0, keepdims=True), jnp.max(memory, axis=0, keepdims=True)
        )
        top_own = jnp.maximum(top[:, HALF:], jnp.max(own, axis=0, keepdims=True))
        top = jnp.concatenate([top[:, :HALF], top_own], axis=1)
        main = jnp.exp(main - top)
        memory = jnp.exp(memory - top)
        own = jnp.exp(own - top_own)
        total = jnp.sum(main, axis=0, keepdims=True) + jnp.sum(memory, axis=0, keepdims=True)
        total = jnp.concatenate(
            [total[:, :HALF], total[:, HALF:] + jnp.sum(own, axis=0, keepdims=True)], axis=1
        )
        flipped = value_flip[head * HEAD : (head + 1) * HEAD]
        result = product(flipped[:, : 2 * HALF], main.astype(jnp.bfloat16))
        result += product(flipped[:, 2 * HALF : CONT], memory.astype(jnp.bfloat16))
        own = own.astype(jnp.bfloat16)
        own_parts = []
        for cont in range(OWN // CLEN):
            own_parts.append(
                product(
                    flipped[:, CONT + cont * CLEN : CONT + (cont + 1) * CLEN],
                    own[:, cont * CLEN : (cont + 1) * CLEN],
                )
            )
        result = jnp.concatenate(
            [result[:, :HALF], result[:, HALF:] + jnp.concatenate(own_parts, axis=1)], axis=1
        )
        results.append(result / total)
        log_ref[head : head + 1] = top + jnp.log(total)
    out_ref[...] = jnp.concatenate(results, axis=0).T.astype(jnp.bfloat16)


MESH = pl.DeviceIdType.MESH
WHERE = pl.BlockSpec(memory_space=pl.ANY)
INSIDE = pl.BlockSpec(memory_space=pltpu.VMEM)
VECTORS = 16


def seat():
    grp = lax.axis_index("grp")
    return (grp // 2, grp % 2, lax.axis_index("shard"))


def unit_of(z, core, shard):
    return (z * 2 + core) * 4 + shard


def device_of(z, core, shard):
    return (z * 2 + core, shard)


def greet():
    z, core, shard = seat()
    barrier = pltpu.get_barrier_semaphore()
    others = [device_of((z + step) % 4, core, shard) for step in (1, 2, 3)]
    others += [
        device_of(z, core, shard ^ 1),
        device_of(z, core, shard ^ 2),
        device_of(z, 1 - core, shard),
    ]
    for other in others:
        pl.semaphore_signal(barrier, inc=1, device_id=other, device_id_type=MESH)
    pl.semaphore_wait(barrier, len(others))


class Gather:
    def __init__(self, mine, full, send, recv, by_y=(0, 2)):
        self.mine, self.full, self.send, self.recv = mine, full, send, recv
        self.share = mine.shape[0]
        self.by_y = by_y
        self.z, self.core, self.shard = seat()
        self.sent = 0

    def rows(self, unit):
        return self.full.at[pl.ds(pl.multiple_of(unit * self.share, 8), self.share)]

    def link(self, index, unit, z, core, shard, source=None):
        return pltpu.make_async_remote_copy(
            src_ref=self.rows(unit) if source is None else source,
            dst_ref=self.rows(unit),
            send_sem=self.send.at[index],
            recv_sem=self.recv.at[unit],
            device_id=device_of(z, core, shard),
            device_id_type=MESH,
        )

    def push(self, unit, z, core, shard, source=None):
        self.link(self.sent, unit, z, core, shard, source).start()
        self.sent += 1

    def arrive(self, unit):
        self.link(0, unit, self.z, 1 - self.core, self.shard).wait_recv()

    def start_line(self):
        me = unit_of(self.z, self.core, self.shard)
        for step in (1, 2, 3):
            self.push(me, (self.z + step) % 4, self.core, self.shard, self.mine)

    def start_plane(self):
        z, core, shard = self.z, self.core, self.shard
        me = unit_of(z, core, shard)
        self.push(me, z, core, shard ^ 1, self.mine)
        self.push(me, z, core, shard ^ 2, self.mine)
        self.push(me, z, 1 - core, shard, self.mine)

    def own(self, semaphore):
        return pltpu.make_async_copy(
            self.mine, self.rows(unit_of(self.z, self.core, self.shard)), semaphore
        )

    def column(self, step):
        z, core, shard = self.z, self.core, self.shard
        unit = unit_of((z + step) % 4, core, shard)
        self.arrive(unit)
        self.push(unit, z, core, shard ^ 1)
        self.push(unit, z, core, shard ^ 2)
        self.push(unit, z, 1 - core, shard)

    def side(self, step):
        z, core, shard = self.z, self.core, self.shard
        for hop in (1, 2):
            unit = unit_of((z + step) % 4, core, shard ^ hop)
            self.arrive(unit)
            if (step in self.by_y) == (hop == 1):
                self.push(unit, z, core, shard ^ (3 - hop))
            self.push(unit, z, 1 - core, shard)

    def corner(self, step):
        z, core, shard = self.z, self.core, self.shard
        unit = unit_of((z + step) % 4, core, shard ^ 3)
        self.arrive(unit)
        self.push(unit, z, 1 - core, shard)

    def sibling(self):
        def wait(index, carry):
            unit = (index // 4) * 8 + (1 - self.core) * 4 + index % 4
            self.arrive(unit)
            return carry

        lax.fori_loop(0, 16, wait, 0)

    def finish(self):
        def wait(index, carry):
            pltpu.make_async_remote_copy(
                src_ref=self.mine,
                dst_ref=self.mine,
                send_sem=self.send.at[index],
                recv_sem=self.recv.at[0],
                device_id=device_of(self.z, 1 - self.core, self.shard),
                device_id_type=MESH,
            ).wait_send()
            return carry

        lax.fori_loop(0, self.sent, wait, 0)


class PlaneGather(Gather):
    def start_plane(self):
        z, core, shard = self.z, self.core, self.shard
        me = unit_of(z, core, shard)
        self.link(96, me, z, core, shard ^ 1, self.mine).start()
        self.link(97, me, z, core, shard ^ 2, self.mine).start()
        self.link(me, me, z, 1 - core, shard, self.mine).start()

    def along(self, unit, z_of, source=None):
        z, core, shard = self.z, self.core, self.shard

        @pl.when((z_of <= z) & (z < 3))
        def _():
            self.link(32 + unit, unit, z + 1, core, shard, source).start()

        @pl.when((z_of >= z) & (z > 0))
        def _():
            self.link(64 + unit, unit, z - 1, core, shard, source).start()

    def start_line(self):
        me = unit_of(self.z, self.core, self.shard)
        self.along(me, self.z, self.mine)

    def plane(self):
        z, core, shard = self.z, self.core, self.shard
        over_x = unit_of(z, core, shard ^ 1)
        over_y = unit_of(z, core, shard ^ 2)
        self.arrive(over_x)

        @pl.when(core == 0)
        def _():
            self.link(98, over_x, z, core, shard ^ 2).start()

        self.link(over_x, over_x, z, 1 - core, shard).start()
        self.along(over_x, z)
        self.arrive(over_y)

        @pl.when(core == 1)
        def _():
            self.link(98, over_y, z, core, shard ^ 1).start()

        self.link(over_y, over_y, z, 1 - core, shard).start()
        self.along(over_y, z)

    def corners(self):
        z, core, shard = self.z, self.core, self.shard
        unit = unit_of(z, core, shard ^ 3)
        self.arrive(unit)
        self.link(unit, unit, z, 1 - core, shard).start()
        self.along(unit, z)

    def far(self, distance, other):
        z, core, shard = self.z, self.core, self.shard
        for sign in (-1, 1):
            plane = z + sign * distance

            @pl.when((plane >= 0) & (plane < 4))
            def _():
                unit = unit_of(plane, core, shard ^ other)
                self.arrive(unit)
                self.link(unit, unit, z, 1 - core, shard).start()
                self.along(unit, plane)

    def finish(self):
        z, core, shard = self.z, self.core, self.shard

        def done(index, unit):
            self.link(index, unit, z, 1 - core, shard, self.mine).wait_send()

        for index in (96, 97, 98):
            done(index, 0)

        def wait(index, carry):
            plane = index // 4
            unit = plane * 8 + core * 4 + index % 4
            done(unit, unit)

            @pl.when((plane <= z) & (z < 3))
            def _():
                done(32 + unit, unit)

            @pl.when((plane >= z) & (z > 0))
            def _():
                done(64 + unit, unit)

            return carry

        lax.fori_loop(0, 16, wait, 0)


class Swap:
    def __init__(self, source, target, send, recv, z, core, shard):
        self.copy = pltpu.make_async_remote_copy(
            src_ref=source, dst_ref=target, send_sem=send, recv_sem=recv,
            device_id=device_of(z, core, shard), device_id_type=MESH,
        )

    def start(self):
        self.copy.start()

    def arrive(self):
        self.copy.wait_recv()

    def finish(self):
        self.copy.wait_send()


def spread_vector(vectors, index, width):
    narrow, broad = width // 32, 4 * width // 32
    row = lax.broadcasted_iota(jnp.int32, (32 * VECTORS, width), 0)
    lane = lax.broadcasted_iota(jnp.int32, (32 * VECTORS, width), 1)
    small = index < 8
    start = jnp.where(small, index, 8 + VECTORS * 8 * (index - 8))
    block = jnp.where(small, lane // narrow, lane // broad)
    select = jnp.where(row == VECTORS * block + start, 1.0, 0.0).astype(jnp.bfloat16)
    table = outer_sum(vectors, select)
    piece = lax.broadcasted_iota(jnp.int32, table.shape, 0)
    lane = lax.broadcasted_iota(jnp.int32, table.shape, 1)
    offset = jnp.where(small, lane % narrow, lane % broad)
    return jnp.sum(jnp.where(piece == offset, table, 0.0), axis=0, keepdims=True)


TILE = 512
PARTNERS = 4


def front_kernel(
    qkv_ref, wide_ref, down_ref, vec_ref, prompt_ref, kept_ref, sent_ref, mem_ref,
    prompt_cot, kept_cot, sent_cot, bias_ref,
    qkv_full, wide_full, down_full, vec_full, rows_out,
    out_ref, act_ref, first_ref, gdown_ref, ginner_ref, gbranch_ref, gmixed_ref, ghidden_ref,
    mixed_ref, log_ref, query_out, key_out, value_out, sums_ref,
    rows, weights, vectors, table, query, key, value, mixed, cotan, wide, down,
    act, slope, normed, first, total, hidden, small_low,
    send_a, recv_a, send_b, recv_b, send_c, recv_c, send_d, recv_d, swap_send, swap_recv, local,
    store,
):
    pair = pl.program_id(0)
    width = prompt_ref.shape[1]
    low = jnp.bfloat16
    one = Gather(qkv_ref, qkv_full, send_a, recv_a, (0, 1))
    small = Gather(vec_ref, vec_full, send_d, recv_d)
    two = Gather(wide_ref, wide_full, send_b, recv_b, (0, 1))
    three = PlaneGather(down_ref, down_full, send_c, recv_c)
    z, core, shard = seat()
    step_rows = HALF // PARTNERS
    partner = [
        Swap(
            prompt_ref.at[pl.ds(index * step_rows, step_rows)],
            rows.at[pl.ds(HALF + index * step_rows, step_rows)],
            swap_send.at[index], swap_recv.at[index], z, core, shard ^ 1,
        )
        for index in range(PARTNERS)
    ]
    taken = [
        Swap(
            sent_ref.at[pl.ds(index * step_rows, step_rows)],
            rows.at[pl.ds(CONT + OWN // 2 + index * step_rows, step_rows)],
            swap_send.at[PARTNERS + index], swap_recv.at[PARTNERS + index], z, core, shard ^ 2,
        )
        for index in range(2)
    ]
    taken_cot = Swap(
        sent_cot, cotan.at[pl.ds(HALF + OWN // 2, OWN // 2)],
        swap_send.at[PARTNERS + 2], swap_recv.at[PARTNERS + 2], z, core, shard ^ 2,
    )
    swaps = partner + taken + [taken_cot]
    own = [gather.own(local.at[index]) for index, gather in enumerate((one, small, two, three))]
    own += [
        pltpu.make_async_copy(prompt_ref, rows.at[pl.ds(0, HALF)], local.at[4]),
        pltpu.make_async_copy(mem_ref, rows.at[pl.ds(2 * HALF, MEM)], local.at[5]),
        pltpu.make_async_copy(kept_ref, rows.at[pl.ds(CONT, OWN // 2)], local.at[6]),
        pltpu.make_async_copy(prompt_cot, cotan.at[pl.ds(0, HALF)], local.at[7]),
        pltpu.make_async_copy(kept_cot, cotan.at[pl.ds(HALF, OWN // 2)], local.at[8]),
    ]
    load_weights = pltpu.make_async_copy(qkv_full, weights, local.at[9])
    load_vectors = pltpu.make_async_copy(vec_full, vectors, local.at[10])
    store_rows = pltpu.make_async_copy(rows, rows_out, local.at[11])
    load_wide = pltpu.make_async_copy(wide_full, wide, local.at[12])
    load_down = pltpu.make_async_copy(down_full, down, local.at[13])

    def project(start, query_start, count, queries):
        span = pl.ds(start, count)
        block = rows[span]
        if queries:
            result = (product(block, weights[:, :width]) + table[0:1]).astype(low)
            result = (result.astype(jnp.float32) * SCALE).astype(low)
            query[pl.ds(query_start, count)] = result
        key[span] = product(block, weights[:, width : 2 * width]).astype(low)
        value[span] = (product(block, weights[:, 2 * width :]) + table[1:2]).astype(low)

    @pl.when(pair == 0)
    def _():
        for copy in own[4:]:
            copy.start()
        greet()
        small.start_line()
        one.start_line()
        small.start_plane()
        one.start_plane()
        partner[0].start()
        three.start_line()
        taken[0].start()
        three.start_plane()
        for copy in own[:4]:
            copy.start()
        for step in (1, 2, 3):
            small.column(step)
            one.column(step)
        two.start_line()
        for step in range(4):
            small.side(step)
            one.side(step)
        partner[1].start()
        taken[1].start()
        partner[2].start()
        partner[3].start()
        two.start_plane()
        for step in range(4):
            small.corner(step)
            one.corner(step)
        small.sibling()
        own[1].wait()
        load_vectors.start()
        one.sibling()
        own[0].wait()
        load_weights.start()
        three.plane()
        for step in (1, 2, 3):
            two.column(step)
        load_vectors.wait()

        def spread(index, carry):
            table[pl.ds(index, 1)] = spread_vector(vectors[...], index, width)
            return carry

        lax.fori_loop(0, 12, spread, 0)
        for index in (2, 3, 4, 5, 6):
            own[index].wait()
        load_weights.wait()
        project(0, 0, HALF, True)
        three.corners()
        three.far(1, 0)
        for swap in taken:
            swap.arrive()
        project(CONT, HALF, OWN, True)
        three.far(1, 1)
        for swap in partner:
            swap.arrive()
        project(HALF, 0, HALF + MEM, False)
        store_rows.start()

    def later(when, *actions):
        @pl.when(pair == when)
        def _():
            for action in actions:
                action[0](*action[1:])

    later(0, (two.side, 0), (three.far, 1, 2))
    later(1, (two.side, 1), (three.far, 1, 3))
    later(2, (two.side, 2), (three.far, 2, 0), (three.far, 2, 1))
    later(3, (two.side, 3), (three.far, 2, 2))
    later(4, (two.corner, 0), (two.corner, 1), (three.far, 2, 3), (three.far, 3, 0))
    later(5, (two.corner, 2), (three.far, 3, 1))

    lanes = pl.ds(pl.multiple_of(pair * (2 * HEAD), 2 * HEAD), 2 * HEAD)
    query_out[...] = query[:, lanes]
    key_out[...] = key[:, lanes]
    value_out[...] = value[:, lanes]
    attend_pair(query_out, key_out, value_out, bias_ref, mixed_ref, log_ref)
    mixed[:, lanes] = mixed_ref[...]

    def fine(index):
        return table[index : index + 1]

    def save(tile, index):
        span = pl.ds(pl.multiple_of(tile * TILE, TILE), TILE)
        source, target = (
            (act, act_ref), (slope, ginner_ref), (hidden, ghidden_ref),
            (small_low.at[0], out_ref), (small_low.at[1], first_ref), (small_low.at[2], gdown_ref),
            (small_low.at[3], gbranch_ref), (small_low.at[4], gmixed_ref),
        )[index]
        return pltpu.make_async_copy(source, target.at[span], store.at[index])

    def up_chunk(step):
        return pl.ds(pl.multiple_of(step * width, 128), width)

    def up_columns(step):
        return pl.ds(pl.multiple_of((step + 1) * width, 128), width)

    def add_sum(index, values):
        sums_ref[pl.ds(index, 1)] += jnp.sum(values, axis=0, keepdims=True)

    def start_tile(tile):
        span = pl.ds(pl.multiple_of(tile * TILE, TILE), TILE)
        held = rows[pl.ds(pl.multiple_of(tile * CONT, MEM), TILE)].astype(jnp.float32)
        held = held + (product(mixed[span], wide[:, :width]) + fine(2))
        result, value_n, value_r = layer_norm(held, fine(3), fine(4))

        @pl.when(tile == 1)
        def _():
            for index in range(1, 8):
                save(0, index).wait()

        normed[...] = value_n
        first[...] = result
        small_low[1] = result.astype(low)
        return value_r

    def forward_chunk(step, carry):
        chunk = up_chunk(step)
        inner = product(small_low[1], wide[:, up_columns(step)]) + table[pl.ds(8 + step, 1)]
        half = 0.5 * (1.0 + lax.erf(inner * ROOT_HALF))
        active = (inner * half).astype(low)
        act[:, chunk] = active
        slope[:, chunk] = (half + inner * jnp.exp(-0.5 * inner * inner) * ROOT_GAUSS).astype(low)
        total[...] += product(active, down[chunk])
        return carry

    def backward_chunk(step, carry):
        chunk = up_chunk(step)
        grad = times_back(small_low[2], down[chunk]) * slope[:, chunk].astype(jnp.float32)
        grad = grad.astype(low)
        slope[:, chunk] = grad
        add_sum(8 + step, grad.astype(jnp.float32))
        total[...] += times_back(grad, wide[:, up_columns(step)])
        return carry

    def tile_body(tile, carry):
        span = pl.ds(pl.multiple_of(tile * TILE, TILE), TILE)
        inverse_one = start_tile(tile)
        total[...] = jnp.zeros_like(total)

        @pl.when(tile == 0)
        def _():
            three.far(3, 2)
            three.far(3, 3)
            three.sibling()
            load_down.start()
            load_down.wait()

        @pl.when(tile == 1)
        def _():
            save(0, 0).wait()
            taken_cot.arrive()

        lax.fori_loop(0, 4, forward_chunk, 0, unroll=2)
        save(tile, 0).start()
        result, value_n, inverse_two = layer_norm(
            first[...] + (total[...] + fine(5)), fine(6), fine(7)
        )
        small_low[0] = result.astype(low)
        save(tile, 3).start()
        save(tile, 4).start()
        cot = cotan[span].astype(jnp.float32)
        add_sum(6, cot * value_n)
        add_sum(7, cot)
        grad_mid = norm_back(cot * fine(6), value_n, inverse_two)
        grad_low = grad_mid.astype(low)
        small_low[2] = grad_low
        save(tile, 5).start()
        add_sum(5, grad_low.astype(jnp.float32))
        total[...] = grad_mid
        lax.fori_loop(0, 4, backward_chunk, 0, unroll=2)
        save(tile, 1).start()
        grad_first = total[...]
        add_sum(3, grad_first * normed[...])
        add_sum(4, grad_first)
        grad_hidden = norm_back(grad_first * fine(3), normed[...], inverse_one)
        hidden[...] = grad_hidden
        save(tile, 2).start()
        grad_low = grad_hidden.astype(low)
        small_low[3] = grad_low
        save(tile, 6).start()
        add_sum(2, grad_low.astype(jnp.float32))
        small_low[4] = times_back(grad_low, wide[:, :width]).astype(low)
        save(tile, 7).start()
        return carry

    @pl.when(pair == PAIRS - 1)
    def _():
        taken_cot.start()
        two.corner(3)
        two.sibling()
        load_wide.start()
        own[7].wait()
        own[8].wait()
        sums_ref[...] = jnp.zeros_like(sums_ref)
        load_wide.wait()
        lax.fori_loop(0, 2, tile_body, 0)
        store_rows.wait()
        for index in range(8):
            save(1, index).wait()
        for sender in (one, small, two, three, *swaps):
            sender.finish()


def front(
    qkv, wide_share, down_share, vec, prompt, kept, sent, memory, prompt_cot, kept_cot, sent_cot,
    bias,
):
    width = prompt.shape[1]
    low = jnp.bfloat16
    wide = jnp.float32
    shape = jax.ShapeDtypeStruct

    def block(rows):
        return pl.BlockSpec((rows, 2 * HEAD), lambda pair: (0, pair))

    def full(share):
        return shape((32 * share.shape[0], share.shape[1]), low)

    dma = pltpu.SemaphoreType.DMA
    memory_space = pltpu.VMEM
    return pl.pallas_call(
        front_kernel,
        grid=(PAIRS,),
        in_specs=[INSIDE] * 4
        + [WHERE] * 7
        + [pl.BlockSpec((CLEN, OWN), lambda pair: (0, 0))],
        out_specs=[WHERE] * 13
        + [
            block(QROWS), pl.BlockSpec((None, 2, QROWS), lambda pair: (pair, 0, 0)),
            block(QROWS), block(KEYS), block(KEYS),
            pl.BlockSpec((VECTORS, width), lambda pair: (0, 0)),
        ],
        out_shape=[
            full(qkv), full(wide_share), full(down_share), full(vec),
            shape((KEYS, width), low),
            shape((QROWS, width), low),
            shape((QROWS, 4 * width), low),
            shape((QROWS, width), low),
            shape((QROWS, width), low),
            shape((QROWS, 4 * width), low),
            shape((QROWS, width), low),
            shape((QROWS, width), low),
            shape((QROWS, width), wide),
            shape((QROWS, width), low),
            shape((PAIRS, 2, QROWS), wide),
            shape((QROWS, width), low),
            shape((KEYS, width), low),
            shape((KEYS, width), low),
            shape((VECTORS, width), wide),
        ],
        scratch_shapes=[
            memory_space((KEYS, width), low),
            memory_space((width, 3 * width), low),
            memory_space((32 * VECTORS, 2 * HEAD), low),
            memory_space((VECTORS, width), wide),
            memory_space((QROWS, width), low),
            memory_space((KEYS, width), low),
            memory_space((KEYS, width), low),
            memory_space((QROWS, width), low),
            memory_space((QROWS, width), low),
            memory_space((width, 5 * width), low),
            memory_space((4 * width, width), low),
            memory_space((TILE, 4 * width), low),
            memory_space((TILE, 4 * width), low),
            memory_space((TILE, width), wide),
            memory_space((TILE, width), wide),
            memory_space((TILE, width), wide),
            memory_space((TILE, width), wide),
            memory_space((5, TILE, width), low),
        ]
        + [dma((32,))] * 4
        + [dma((100,)), dma((32,)), dma((32,)), dma((32,))]
        + [dma((PARTNERS + 3,)), dma((PARTNERS + 3,)), dma((14,)), dma((8,))],
        compiler_params=pltpu.CompilerParams(
            vmem_limit_bytes=67043328, collective_id=0, has_side_effects=True
        ),
        name="front",
    )(
        qkv, wide_share, down_share, vec, prompt, kept, sent, memory, prompt_cot, kept_cot,
        sent_cot, bias,
    )


SEND = 13
CHIP, PLANE, LINE, MIDDLE, SPREAD, SHARE, SMALL, PARTNER = range(8)
SLOTS = {
    0: ((PLANE, 0), (CHIP, 2), (PLANE, 1), (CHIP, 3), (CHIP, 4),),
    1: ((LINE, 0),),
    3: ((MIDDLE, 0), (LINE, 1), (PLANE, 2),),
    4: ((PLANE, 3), (CHIP, 5),),
    5: ((SPREAD, 0), (MIDDLE, 1), (PLANE, 4),),
    6: ((LINE, 2),),
    7: ((SHARE, 0), (SPREAD, 1), (LINE, 3), (LINE, 4), (PLANE, 5),),
    8: ((MIDDLE, 2), (LINE, 5), (CHIP, 6),),
    9: ((SHARE, 1), (MIDDLE, 3), (PLANE, 6),),
    10: ((SPREAD, 2), (MIDDLE, 4), (LINE, 6), (CHIP, 7), (MIDDLE, 5),),
    11: ((SPREAD, 3), (MIDDLE, 6), (PLANE, 7),),
}
TAIL = {
    0: ((SHARE, 2), (SPREAD, 4), (LINE, 7),),
    1: ((PLANE, 8), (PARTNER, 1), (PARTNER, 2), (PARTNER, 3), (SPREAD, 5), (SMALL, 0),),
    2: ((MIDDLE, 7), (SMALL, 1),),
    3: ((SHARE, 3), (SPREAD, 6), (SMALL, 2), (LINE, 8), (SPREAD, 7), (SHARE, 4), (MIDDLE, 8), (SHARE, 5), (SPREAD, 8), (SHARE, 6),),
    4: ((SHARE, 7), (SMALL, 3),),
    5: ((SHARE, 8),),
}
LAST = ((SMALL, 4),)
WIDE = 4
NARROW = 3
TINY = 2
ITEMS = WIDE + NARROW + TINY


class Reduce:
    def __init__(self, mine, theirs, got, from_x, from_y, last_x, last_y, outer, total, send, recv):
        self.mine, self.theirs, self.got = mine, theirs, got
        self.from_x, self.from_y, self.last_x, self.last_y = from_x, from_y, last_x, last_y
        self.outer, self.total, self.send, self.recv = outer, total, send, recv
        self.half = mine.shape[1] // 2
        self.z, self.core, self.shard = seat()
        self.inner = (self.z == 1) | (self.z == 2)

    def copy(self, source, target, index, z, core, shard):
        return pltpu.make_async_remote_copy(
            src_ref=source, dst_ref=target, send_sem=self.send.at[index],
            recv_sem=self.recv.at[index], device_id=device_of(z, core, shard), device_id_type=MESH,
        )

    def upper(self, part):
        return self.mine.at[part, pl.ds(0, self.half)]

    def lower(self, part):
        return self.mine.at[part, pl.ds(self.half, self.half)]

    def link(self, index):
        z, core, shard = self.z, self.core, self.shard
        near = jnp.where(z < 2, 1 - z, 5 - z)
        if index < 4:
            ends = (self.theirs.at[index], self.got.at[index], z, 1 - core, shard)
        elif index < 6:
            source = self.upper(shard ^ (1 if index == 4 else 3))
            ends = (source, self.from_x.at[index - 4], z, core, shard ^ 1)
        elif index < 8:
            source = self.lower(shard ^ (2 if index == 6 else 3))
            ends = (source, self.from_y.at[index - 6], z, core, shard ^ 2)
        elif index == 8:
            ends = (self.upper(shard ^ 2), self.last_y, z, core, shard ^ 2)
        elif index == 9:
            ends = (self.lower(shard ^ 1), self.last_x, z, core, shard ^ 1)
        elif index == 10:
            ends = (self.mine.at[shard], self.outer, near, core, shard)
        elif index == 11:
            ends = (self.mine.at[shard], self.total, 3 - z, core, shard)
        else:
            ends = (self.total, self.total, near, core, shard)
        return self.copy(ends[0], ends[1], index, *ends[2:])

    def give(self, part):
        self.copy(
            self.theirs.at[part], self.got.at[part], part, self.z, 1 - self.core, self.shard
        ).start()

    def given(self):
        for part in range(4):
            self.link(part).wait_send()

    def add(self, part, start, count, other):
        def step(index, carry):
            rows = pl.ds(pl.multiple_of(index * 48, 16), 48)
            span = pl.ds(pl.multiple_of(start + index * 48, 16), 48)
            self.mine[part, span] = self.mine[part, span] + other[rows]
            return carry

        lax.fori_loop(0, count // 48, step, 0)

    def chip(self):
        for part in range(4):
            self.link(part).wait_recv()

        def add_part(part, carry):
            self.add(part, 0, 2 * self.half, self.got.at[part])
            return carry

        lax.fori_loop(0, 4, add_part, 0)
        for index in (4, 5, 6, 7):
            self.link(index).start()

    def plane(self):
        shard = self.shard
        self.link(4).wait_recv()
        self.link(5).wait_recv()
        self.add(shard ^ 2, 0, self.half, self.from_x.at[1])
        self.link(8).start()
        self.link(6).wait_recv()
        self.link(7).wait_recv()
        self.add(shard ^ 1, self.half, self.half, self.from_y.at[1])
        self.link(9).start()
        self.add(shard, 0, self.half, self.from_x.at[0])
        self.add(shard, self.half, self.half, self.from_y.at[0])

    def line(self):
        self.link(8).wait_recv()
        self.add(self.shard, 0, self.half, self.last_y)
        self.link(9).wait_recv()
        self.add(self.shard, self.half, self.half, self.last_x)

        @pl.when(jnp.logical_not(self.inner))
        def _():
            self.link(10).start()

    def middle(self):
        @pl.when(self.inner)
        def _():
            self.link(10).wait_recv()
            self.add(self.shard, 0, 2 * self.half, self.outer)
            self.link(11).start()

    def spread(self):
        @pl.when(self.inner)
        def _():
            self.link(11).wait_recv()

            def step(index, carry):
                rows = pl.ds(pl.multiple_of(index * 48, 16), 48)
                self.total[rows] = self.total[rows] + self.mine[self.shard, rows]
                return carry

            lax.fori_loop(0, 2 * self.half // 48, step, 0)
            self.link(12).start()

    def share(self, place, semaphore):
        @pl.when(jnp.logical_not(self.inner))
        def _():
            self.link(12).wait_recv()

        pltpu.make_async_copy(self.total, place, semaphore).start()
        pltpu.make_async_remote_copy(
            src_ref=self.total, dst_ref=place, send_sem=self.send.at[13],
            recv_sem=self.recv.at[13],
            device_id=device_of(self.z, 1 - self.core, self.shard), device_id_type=MESH,
        ).start()

    def finish(self, place, semaphore):
        pltpu.make_async_copy(self.total, place, semaphore).wait()
        last = pltpu.make_async_remote_copy(
            src_ref=self.total, dst_ref=place, send_sem=self.send.at[13],
            recv_sem=self.recv.at[13],
            device_id=device_of(self.z, 1 - self.core, self.shard), device_id_type=MESH,
        )
        last.wait_send()
        last.wait_recv()
        for index in range(4, 10):
            self.link(index).wait_send()

        @pl.when(jnp.logical_not(self.inner))
        def _():
            self.link(10).wait_send()

        @pl.when(self.inner)
        def _():
            self.link(11).wait_send()
            self.link(12).wait_send()


class Butterfly:
    def __init__(self, held, got, send, recv):
        self.held, self.got, self.send, self.recv = held, got, send, recv
        self.z, self.core, self.shard = seat()

    def copy(self, step):
        z, core, shard = self.z, self.core, self.shard
        where = ((z, core, shard ^ 1), (z, core, shard ^ 2), (z ^ 1, core, shard),
                 (z ^ 2, core, shard), (z, 1 - core, shard))[step]
        rows = pl.ds(0, 2 * VECTORS if step < 2 else VECTORS)
        return pltpu.make_async_remote_copy(
            src_ref=self.held.at[step, rows], dst_ref=self.got.at[step, rows],
            send_sem=self.send.at[step], recv_sem=self.recv.at[step],
            device_id=device_of(*where), device_id_type=MESH,
        )

    def start(self):
        self.copy(0).start()

    def step(self, step):
        self.copy(step).wait_recv()
        rows = slice(0, 2 * VECTORS if step < 2 else VECTORS)
        self.held[step + 1, rows] = self.held[step, rows] + self.got[step, rows]
        if step < 4:
            self.copy(step + 1).start()

    def finish(self):
        for step in range(5):
            self.copy(step).wait_send()


def back_piece(
    head, half, query_ref, key_ref, value_ref, bias_ref, log_ref, grad_ref,
    overlap, key_acc, value_acc, query_flip,
):
    mem_valid = lax.broadcasted_iota(jnp.int32, (MEM, 1), 0) < READ
    mask = head_mask(head)
    span = pl.ds(pl.multiple_of(head * HEAD, HEAD), HEAD)

    mine = lax.broadcasted_iota(jnp.int32, (2 * HEAD, 1), 0) // HEAD == head

    def keep(lanes, values):
        query_flip[:, lanes] = jnp.where(mine, values, query_flip[:, lanes])

    def block_back(keys, values, bias, valid, queries, grads, log, delta, rows):
        scores = times_back(keys, queries)
        if bias is not None:
            scores = scores + bias
        chances = jnp.exp(scores - log)
        if valid is not None:
            chances = jnp.where(valid, chances, 0.0)
        slopes = (chances * (times_back(values, grads) - delta)).astype(jnp.bfloat16)
        value_acc[rows] += product(chances.astype(jnp.bfloat16), grads)
        key_acc[rows] += product(slopes, queries)
        return outer_sum(keys, slopes)

    part = slice(half * HALF, (half + 1) * HALF)
    queries = pick(mask, query_ref[part])
    grads = pick(mask, grad_ref[part])
    delta = jnp.sum(overlap[span, part], axis=0, keepdims=True)
    log = log_ref[pl.ds(head, 1), part]
    main_rows = slice(0, 2 * HALF)
    mem_rows = slice(2 * HALF, CONT)
    piece = block_back(
        key_ref[main_rows], value_ref[main_rows], None, None,
        queries, grads, log, delta, main_rows,
    )
    piece += block_back(
        key_ref[mem_rows], value_ref[mem_rows], None, mem_valid,
        queries, grads, log, delta, mem_rows,
    )
    if half == 0:
        keep(part, piece)
        return
    own_parts = []
    for cont in range(OWN // CLEN):
        rows = slice(CONT + cont * CLEN, CONT + (cont + 1) * CLEN)
        part = slice(cont * CLEN, (cont + 1) * CLEN)
        own_parts.append(
            block_back(
                key_ref[rows], value_ref[rows], bias_ref[:, part], None,
                queries[part], grads[part], log[:, part], delta[:, part], rows,
            )
        )
    keep(slice(HALF, QROWS), piece + jnp.concatenate(own_parts, axis=1))


def back_kernel(
    act_ref, gdown_ref, first_ref, ginner_ref, mixed_all, gbranch_ref, ghidden_ref, rows_ref,
    qkv_ref, out_ref, sums_ref,
    query_ref, key_ref, value_ref, grad_ref, mixed_ref, log_ref, bias_ref,
    down_out, up_out, out_out, qkv_out, last_out, returned_out, grad_prompt, grad_kept, grad_back,
    memory_out, vec_out,
    wide_mine, wide_theirs, wide_got, wide_x, wide_y, wide_lx, wide_ly, wide_outer, wide_total,
    thin_mine, thin_theirs, thin_got, thin_x, thin_y, thin_lx, thin_ly, thin_outer, thin_total,
    tiny_mine, tiny_theirs, tiny_got, tiny_x, tiny_y, tiny_lx, tiny_ly, tiny_outer, tiny_total,
    pool, rows, dquery, dkey, dvalue, key_acc, value_acc, overlap, query_flip,
    partner, ghidden, staged, held, got,
    send, recv, small_send, small_recv, swap_send, swap_recv, local, out_sem,
):
    pair = pl.program_id(0)
    z, core, shard = seat()
    other = 1 - core
    width = rows_ref.shape[1]
    part_rows = width // 4
    low = jnp.bfloat16

    def item(index):
        if isinstance(index, int) and index >= WIDE:
            return thin(index - WIDE) if index < WIDE + NARROW else tiny(index - WIDE - NARROW)
        return Reduce(
            wide_mine.at[index], wide_theirs.at[index % 2], wide_got.at[index],
            wide_x.at[index], wide_y.at[index], wide_lx.at[index], wide_ly.at[index],
            wide_outer.at[index], wide_total.at[index], send.at[index], recv.at[index],
        )

    def thin(index):
        return Reduce(
            thin_mine.at[index], thin_theirs.at[index % 2], thin_got.at[index],
            thin_x.at[index], thin_y.at[index], thin_lx.at[index], thin_ly.at[index],
            thin_outer.at[index], thin_total.at[index], send.at[WIDE + index],
            recv.at[WIDE + index],
        )

    def tiny(index):
        number = WIDE + NARROW + index
        return Reduce(
            tiny_mine.at[index], tiny_theirs.at[index % 2], tiny_got.at[index],
            tiny_x.at[index], tiny_y.at[index], tiny_lx.at[index], tiny_ly.at[index],
            tiny_outer.at[index], tiny_total.at[index], send.at[number], recv.at[number],
        )

    small = Butterfly(held, got, small_send, small_recv)
    half_hidden = width // 2

    def place(index):
        if index < 2:
            start = core * half_hidden + index * part_rows
            return down_out.at[pl.ds(pl.multiple_of(start, 64), part_rows)]
        if index < 4:
            start = core * (2 * width) + (index - 2) * width
            return up_out.at[:, pl.ds(pl.multiple_of(start, 128), width)]
        if index == 4:
            return out_out.at[:, pl.ds(pl.multiple_of(core * half_hidden, 128), half_hidden)]
        if index < WIDE + NARROW:
            return qkv_out.at[index - 5, core]
        start = pl.multiple_of(core * (part_rows // 2), 16)
        return last_out.at[index - WIDE - NARROW, pl.ds(start, part_rows // 2)]

    def stage(name, index):
        if name == SHARE:
            item(index).share(place(index), out_sem.at[index])
        else:
            held = item(index)
            (held.chip, held.plane, held.line, held.middle, held.spread)[name]()

    returned = Swap(
        out_ref.at[pl.ds(HALF + OWN // 2, OWN // 2)], returned_out, swap_send.at[0], swap_recv.at[0], z, core, shard ^ 2
    )
    def to_partner(index):
        span = pl.ds(pl.multiple_of(128 * index, 128), 128)
        return Swap(
            pool.at[3, span], partner.at[span], swap_send.at[index + 1], swap_recv.at[index + 1],
            z, core, shard ^ 1,
        )

    cont_back = Swap(
        pool.at[3, pl.ds(2 * 256, 256)], grad_back, swap_send.at[5], swap_recv.at[5],
        z, core, shard ^ 2,
    )

    def load(source, slot, semaphore):
        return pltpu.make_async_copy(source, pool.at[slot], local.at[semaphore])

    def act_chunk(part):
        return load(act_ref.at[:, pl.ds(part * width, width)], part % 2, part % 2)

    def inner_chunk(step):
        half = other if step < 2 else core
        start = pl.multiple_of(half * (2 * width) + (step % 2) * width, 128)
        return load(ginner_ref.at[:, pl.ds(start, width)], step % 2, step % 2)

    def parts_of(target, values):
        for part in range(4):
            target[part] = values[part * part_rows : (part + 1) * part_rows].astype(low)

    load_rows = pltpu.make_async_copy(rows_ref, rows, local.at[4])

    def inner_load(step):
        half = jnp.where(step < 2, other, core)
        start = pl.multiple_of(half * (2 * width) + (step % 2) * width, 128)
        return load(ginner_ref.at[:, pl.ds(start, width)], step % 2, step % 2)

    def act_load(part):
        lanes = pl.ds(pl.multiple_of(part * width, 128), width)
        return load(act_ref.at[:, lanes], part % 2, part % 2)

    def weight_load(index):
        return pltpu.make_async_copy(
            qkv_ref.at[:, pl.ds(index * width, width)],
            pool.at[index, pl.ds(0, width)], local.at[index],
        )

    def down_part(part, carry):
        act_load(part).wait()

        def down_half(side, carry):
            half = jnp.where(side == 0, other, core)
            lanes = pl.ds(pl.multiple_of(half * half_hidden, 128), half_hidden)
            result = outer_sum(pool[part % 2, :, lanes], pool[2]).astype(low)
            for index in range(2):
                piece = result[index * part_rows : (index + 1) * part_rows]

                @pl.when(side == 0)
                def _():
                    wide_theirs[index, part] = piece
                    item(index).give(part)

                @pl.when(side == 1)
                def _():
                    wide_mine[index, part] = piece

            return carry

        lax.fori_loop(0, 2, down_half, 0)

        @pl.when(part < 2)
        def _():
            act_load(part + 2).start()

        @pl.when(part >= 2)
        def _():
            inner_load(part - 2).start()

        return carry

    def up_part(step, carry):
        inner_load(step).wait()
        result = outer_sum(pool[3], pool[step % 2])

        @pl.when(step < 2)
        def _():
            item(step).given()
            parts_of(wide_theirs.at[step], result)
            for part in range(4):
                item(step + 2).give(part)
            inner_load(step + 2).start()

        @pl.when(step >= 2)
        def _():
            parts_of(wide_mine.at[step], result)

        @pl.when((step == 1) | (step == 2))
        def _():
            item(step - 1).chip()

        return carry

    def out_half(side, carry):
        half = jnp.where(side == 0, other, core)
        lanes = pl.ds(pl.multiple_of(half * half_hidden, 128), half_hidden)
        result = outer_sum(pool[2], pool[3, :, lanes])

        @pl.when(side == 0)
        def _():
            parts_of(thin_theirs.at[0], result)
            for part in range(4):
                thin(0).give(part)

        @pl.when(side == 1)
        def _():
            parts_of(thin_mine.at[0], result)

        return carry

    def qkv_part(index):
        def one_half(side, carry):
            half = jnp.where(side == 0, other, core)
            lanes = pl.ds(pl.multiple_of((2 * index + half) * (2 * HEAD), 2 * HEAD), 2 * HEAD)
            query_side = outer_sum(rows[:HALF], dquery[:HALF, lanes])
            query_side += outer_sum(rows[CONT:], dquery[HALF:, lanes])
            both = jnp.concatenate([dkey[:, lanes], dvalue[:, lanes]], axis=1)
            result = jnp.concatenate([query_side, outer_sum(rows[...], both)], axis=1)

            @pl.when(side == 0)
            def _():
                @pl.when(index > 0)
                def _():
                    thin(0).given()

                parts_of(thin_theirs.at[(1 + index) % 2], result)
                for part in range(4):
                    thin(1 + index).give(part)

            @pl.when(side == 1)
            def _():
                parts_of(thin_mine.at[1 + index], result)

            return carry

        lax.fori_loop(0, 2, one_half, 0)

    def last_part(index):
        lanes = pl.ds(pl.multiple_of((4 + index) * (2 * HEAD), 2 * HEAD), 2 * HEAD)
        query_side = outer_sum(rows[:HALF], dquery[:HALF, lanes])
        query_side += outer_sum(rows[CONT:], dquery[HALF:, lanes])
        both = jnp.concatenate([dkey[:, lanes], dvalue[:, lanes]], axis=1)
        result = jnp.concatenate([query_side, outer_sum(rows[...], both)], axis=1).astype(low)
        half = part_rows // 2
        for side in range(2):

            @pl.when(core == side)
            def _():
                for part in range(4):
                    start = part * part_rows
                    tiny_theirs[index % 2, part] = result[
                        start + (1 - side) * half : start + (2 - side) * half
                    ]
                    tiny_mine[index, part] = result[start + side * half : start + (side + 1) * half]

        for part in range(4):
            tiny(index).give(part)

    @pl.when(pair == 0)
    def _():
        act_load(0).start()
        load(gdown_ref, 2, 2).start()
        act_load(1).start()
        load(first_ref, 3, 3).start()
        load_rows.start()
        greet()
        returned.start()
        load(gdown_ref, 2, 2).wait()
        lax.fori_loop(0, 4, down_part, 0)
        load(mixed_all, 2, 2).start()
        load(first_ref, 3, 3).wait()
        lax.fori_loop(0, 4, up_part, 0)
        load(gbranch_ref, 3, 3).start()
        load(mixed_all, 2, 2).wait()
        load(gbranch_ref, 3, 3).wait()
        lax.fori_loop(0, 2, out_half, 0)
        for index in range(3):
            weight_load(index).start()
        load_rows.wait()

    lanes = pl.ds(pl.multiple_of(pair * (2 * HEAD), 2 * HEAD), 2 * HEAD)
    overlap[...] = (mixed_ref[...].astype(jnp.float32) * grad_ref[...].astype(jnp.float32)).T
    key_acc[...] = jnp.zeros_like(key_acc)
    value_acc[...] = jnp.zeros_like(value_acc)

    def piece_body(piece, carry):
        for half in range(2):
            back_piece(
                piece, half, query_ref, key_ref, value_ref, bias_ref, log_ref, grad_ref,
                overlap, key_acc, value_acc, query_flip,
            )

        @pl.when(piece == 1)
        def _():
            dquery[:, lanes] = (query_flip[...].T * SCALE).astype(low)
            dkey[:, lanes] = key_acc[...].astype(low)
            dvalue[:, lanes] = value_acc[...].astype(low)

        @pl.when((piece == 1) & (pair % 2 == 1) & (pair < 4))
        def _():
            qkv_part(pair // 2)

        @pl.when((piece == 1) & (pair >= 4))
        def _():
            last_part(pair - 4)

        for number, stages in SLOTS.items():

            @pl.when(pair * 2 + piece == number)
            def _():
                for name, index in stages:
                    stage(name, index)

        return carry

    lax.fori_loop(0, 2, piece_body, 0)

    def hidden_load(step):
        start = pl.multiple_of((5 - step) * 256, 256)
        return pltpu.make_async_copy(
            ghidden_ref.at[pl.ds(start, 256)], ghidden.at[step % 2], local.at[5 + step % 2]
        )

    def staged_store(step):
        slot = step % 2
        return staged.at[slot], local.at[8 + slot]

    def chunk_body(step, carry):
        start = jnp.where(step < 2, HALF + 256 * step, jnp.where(step < 4, CONT, HALF))
        start = jnp.where(step >= 2, start + jnp.where(step % 2 == 0, 256, 0), start)
        start = jnp.where(step >= 4, start - HALF, start)
        span = pl.ds(pl.multiple_of(start, MEM), 256)
        result = times_back(dkey[span], pool[1, :width]) + times_back(dvalue[span], pool[2, :width])

        @pl.when(step < 2)
        def _():
            pool[3, pl.ds(pl.multiple_of(256 * step, 256), 256)] = result.astype(low)

        @pl.when(step == 0)
        def _():
            to_partner(0).start()

        @pl.when(step >= 2)
        def _():
            hidden_load(step).wait()
            mine = pl.ds(pl.multiple_of((5 - step) * 256, 256), 256)
            full = result + (
                ghidden[step % 2] + times_back(dquery[mine], pool[0, :width])
            )

            @pl.when(step == 2)
            def _():
                pool[3, 512:768] = full.astype(low)
                cont_back.start()

            @pl.when(step == 3)
            def _():
                staged[1] = full.astype(low)
                pltpu.make_async_copy(staged.at[1], grad_kept, local.at[9]).start()

            @pl.when(step >= 4)
            def _():
                to_partner(2 * (5 - step)).arrive()
                to_partner(2 * (5 - step) + 1).arrive()

                @pl.when(step == 5)
                def _():
                    pltpu.make_async_copy(staged.at[1], grad_kept, local.at[9]).wait()

                mine = pl.ds(pl.multiple_of((5 - step) * 256, 256), 256)
                staged[step % 2] = (full + partner[mine].astype(jnp.float32)).astype(low)
                pltpu.make_async_copy(
                    staged.at[step % 2], grad_prompt.at[mine], local.at[8 + step % 2]
                ).start()

            @pl.when(step < 4)
            def _():
                hidden_load(step + 2).start()

        for number, stages in TAIL.items():

            @pl.when(step == number)
            def _():
                for name, index in stages:
                    if name == SMALL:
                        small.step(index)
                    elif name == PARTNER:
                        to_partner(index).start()
                    else:
                        stage(name, index)

        return carry

    @pl.when(pair == PAIRS - 1)
    def _():
        hidden_load(2).start()
        hidden_load(3).start()
        sums = pltpu.make_async_copy(sums_ref, held.at[0, pl.ds(0, VECTORS)], local.at[7])
        sums.start()
        for index in range(3):
            weight_load(index).wait()
        sums.wait()
        held[0, 0:1] = jnp.sum(dquery[...].astype(jnp.float32), axis=0, keepdims=True)
        held[0, 1:2] = jnp.sum(dvalue[...].astype(jnp.float32), axis=0, keepdims=True)
        mem_span = slice(2 * HALF, CONT)
        held[0, VECTORS:] = times_back(dkey[mem_span], pool[1, :width]) + times_back(
            dvalue[mem_span], pool[2, :width]
        )
        stage(CHIP, 8)
        small.start()
        lax.fori_loop(0, 6, chunk_body, 0)
        for name, index in LAST:
            if name == SMALL:
                small.step(index)
            else:
                stage(name, index)
        family = shard // 2
        memory_out[family] = held[1, VECTORS:]
        memory_out[1 - family] = got[1, VECTORS:]
        vec_out[...] = held[5, :VECTORS]
        returned.arrive()
        cont_back.arrive()
        for step in (4, 5):
            mine = pl.ds((5 - step) * 256, 256)
            pltpu.make_async_copy(
                staged.at[step % 2], grad_prompt.at[mine], local.at[8 + step % 2]
            ).wait()
        for index in (2, 3, 4, 5, 6, 7, 8):
            if index != 4:
                item(index).given()
        for index in range(ITEMS):
            item(index).finish(place(index), out_sem.at[index])
        small.finish()
        for swap in (returned, cont_back, *(to_partner(index) for index in range(4))):
            swap.finish()


def back(
    act, gdown, first, ginner, mixed, gbranch, ghidden, rows, qkv, out_taken, sums,
    query, key, value, grads, log, bias,
):
    width = rows.shape[1]
    low = jnp.bfloat16
    wide = jnp.float32

    def block(count):
        return pl.BlockSpec((count, 2 * HEAD), lambda pair: (0, pair))

    dma = pltpu.SemaphoreType.DMA
    part = width // 4

    def buffers(count, columns, part=part):
        return [
            pltpu.VMEM((count, 4, part, columns), low),
            pltpu.VMEM((2, 4, part, columns), low),
            pltpu.VMEM((count, 4, part, columns), low),
            pltpu.VMEM((count, 2, part // 2, columns), low),
            pltpu.VMEM((count, 2, part // 2, columns), low),
            pltpu.VMEM((count, part // 2, columns), low),
            pltpu.VMEM((count, part // 2, columns), low),
            pltpu.VMEM((count, part, columns), low),
            pltpu.VMEM((count, part, columns), low),
        ]

    shape = jax.ShapeDtypeStruct
    return pl.pallas_call(
        back_kernel,
        grid=(PAIRS,),
        in_specs=[WHERE] * 11
        + [
            block(QROWS), block(KEYS), block(KEYS), block(QROWS), block(QROWS),
            pl.BlockSpec((None, 2, QROWS), lambda pair: (pair, 0, 0)),
            pl.BlockSpec((CLEN, OWN), lambda pair: (0, 0)),
        ],
        out_specs=[WHERE] * 9
        + [
            pl.BlockSpec((2, MEM, width), lambda pair: (0, 0, 0)),
            pl.BlockSpec((VECTORS, width), lambda pair: (0, 0)),
        ],
        out_shape=[
            shape((width, width), low),
            shape((part, 4 * width), low),
            shape((part, width), low),
            shape((2, 2, part, width // 2), low),
            shape((TINY, part, width // 2), low),
            shape((OWN // 2, width), low),
            shape((HALF, width), low),
            shape((OWN // 2, width), low),
            shape((OWN // 2, width), low),
            shape((2, MEM, width), wide),
            shape((VECTORS, width), wide),
        ],
        scratch_shapes=buffers(WIDE, width)
        + buffers(NARROW, width // 2)
        + buffers(TINY, width // 2, part // 2)
        + [
            pltpu.VMEM((4, QROWS, width), low),
            pltpu.VMEM((KEYS, width), low),
            pltpu.VMEM((QROWS, width), low),
            pltpu.VMEM((KEYS, width), low),
            pltpu.VMEM((KEYS, width), low),
            pltpu.VMEM((KEYS, 2 * HEAD), wide),
            pltpu.VMEM((KEYS, 2 * HEAD), wide),
            pltpu.VMEM((2 * HEAD, QROWS), wide),
            pltpu.VMEM((2 * HEAD, QROWS), wide),
            pltpu.VMEM((HALF, width), low),
            pltpu.VMEM((2, 256, width), wide),
            pltpu.VMEM((2, 256, width), low),
            pltpu.VMEM((6, 2 * VECTORS, width), wide),
            pltpu.VMEM((5, 2 * VECTORS, width), wide),
            dma((ITEMS, SEND + 1)),
            dma((ITEMS, SEND + 1)),
            dma((5,)),
            dma((5,)),
            dma((6,)),
            dma((6,)),
            dma((10,)),
            dma((ITEMS,)),
        ],
        compiler_params=pltpu.CompilerParams(
            vmem_limit_bytes=67043328, collective_id=1, has_side_effects=True
        ),
        name="back",
    )(
        act, gdown, first, ginner, mixed, gbranch, ghidden, rows, qkv, out_taken, sums,
        query, key, value, grads, mixed, log, bias,
    )


def cont_ranks(owner_ref, shard):
    prompt_of = shard // 2
    conts = OWN // CLEN
    place = []
    before = jnp.int32(0)
    for cont in range(conts):
        owned = (owner_ref[0, shard * conts + cont] == prompt_of).astype(jnp.int32)
        place.append(jnp.where(owned == 1, before, 2 + cont - before))
        before = before + owned
    order = []
    for position in range(conts):
        found = jnp.int32(0)
        for cont in range(conts):
            found = found + jnp.where(place[cont] == position, cont, 0)
        order.append(found)
    return place, order


def block_of(index):
    return pl.ds(pl.multiple_of(index * CLEN, CLEN), CLEN)


def prepare_kernel(
    owner_ref, length_ref, follow_ref, cotan_ref, memory_ref, query_ref, key_ref, value_ref,
    out_ref, up_ref, *refs,
):
    vectors = refs[:9]
    (
        qkv, wide, vec, kept, sent, memory, kept_cot, sent_cot, bias,
    ) = refs[9:]
    shard = lax.axis_index("shard")
    across = shard ^ 2
    conts = OWN // CLEN
    width = query_ref.shape[1]
    _, order = cont_ranks(owner_ref, shard)
    _, order_across = cont_ranks(owner_ref, across)
    for index in range(2):
        span = slice(index * CLEN, (index + 1) * CLEN)
        kept[span] = follow_ref[0, block_of(order[index])]
        sent[span] = follow_ref[0, block_of(order[2 + index])]
        kept_cot[span] = cotan_ref[0, block_of(order[index])]
        sent_cot[span] = cotan_ref[0, block_of(order[2 + index])]
    position = lax.broadcasted_iota(jnp.int32, (CLEN, CLEN), 0)
    for index in range(conts):
        if index < 2:
            length = length_ref[0, shard * conts + order[index]]
        else:
            length = length_ref[0, across * conts + order_across[index]]
        valid = (position < length) | (position >= CLEN - WRITE)
        bias[:, index * CLEN : (index + 1) * CLEN] = jnp.where(valid, 0.0, NEGATIVE)
    memory[...] = jnp.zeros_like(memory)
    memory[:READ] = memory_ref[0, shard // 2]
    qkv[:, :width] = query_ref[...]
    qkv[:, width : 2 * width] = key_ref[...]
    qkv[:, 2 * width :] = value_ref[...]
    wide[:, :width] = out_ref[...]
    wide[:, width:] = up_ref[...]
    vec[...] = jnp.zeros_like(vec)
    for index, vector in enumerate(vectors):
        vec[index : index + 1, : vector.shape[1]] = vector[...]


def prepare(owner, length, follow, cotan, memory, query, key, value, out, up, vectors):
    low = jnp.bfloat16
    width = query.shape[1]
    share = query.shape[0]
    shape = jax.ShapeDtypeStruct
    half = shape((OWN // 2, width), low)
    inside = pl.BlockSpec(memory_space=pltpu.VMEM)
    scalars = pl.BlockSpec(memory_space=pltpu.SMEM)
    return pl.pallas_call(
        prepare_kernel,
        in_specs=[scalars] * 2 + [inside] * 17,
        out_specs=[inside] * 9,
        out_shape=[
            shape((share, 3 * width), low), shape((share, 5 * width), low),
            shape((VECTORS, 2 * HEAD), low), half, half, shape((MEM, width), low), half, half,
            shape((CLEN, OWN), jnp.float32),
        ],
        name="prepare",
    )(
        owner, length, follow, cotan, memory, query, key, value, out, up,
        *(vector[None] for vector in vectors),
    )


def finish_kernel(
    owner_ref, output_ref, returned_ref, kept_grad, back_grad, down_ref, up_ref, out_ref, qkv_ref,
    last_ref, memory_ref, vec_ref,
    prompt_out, follow_out, follow_grad, memory_grad, query_sum, key_sum, value_sum, out_sum,
    up_sum, down_sum, *vectors,
):
    shard = lax.axis_index("shard")
    wide = jnp.float32
    width = down_ref.shape[1]
    part = width // 4
    place, _ = cont_ranks(owner_ref, shard)
    prompt_out[0] = output_ref[:HALF]
    for cont, position in enumerate(place):
        span = slice(cont * CLEN, (cont + 1) * CLEN)
        here = block_of(jnp.where(position < 2, position, 0))
        there = block_of(jnp.where(position < 2, 0, position - 2))
        kept = position < 2

        @pl.when(kept)
        def _():
            follow_out[0, span] = output_ref[pl.ds(HALF + here.start, CLEN)]
            follow_grad[0, span] = kept_grad[here]

        @pl.when(jnp.logical_not(kept))
        def _():
            follow_out[0, span] = returned_ref[there]
            follow_grad[0, span] = back_grad[there]

    memory_grad[0] = memory_ref[:, :READ].astype(jnp.bfloat16)
    down_sum[...] = down_ref[...].astype(wide)
    up_sum[...] = up_ref[...].astype(wide)
    out_sum[...] = out_ref[...].astype(wide)
    for number, target in enumerate((query_sum, key_sum, value_sum)):
        source = slice(number * 2 * HEAD, (number + 1) * 2 * HEAD)
        for index in range(TINY):
            lanes = slice((4 + index) * 2 * HEAD, (5 + index) * 2 * HEAD)
            target[:, lanes] = last_ref[index, :, source].astype(wide)
    for index in range(2):
        for side in range(2):
            lanes = slice((2 * index + side) * 2 * HEAD, (2 * index + side + 1) * 2 * HEAD)
            for number, target in enumerate((query_sum, key_sum, value_sum)):
                source = slice(number * 2 * HEAD, (number + 1) * 2 * HEAD)
                target[:, lanes] = qkv_ref[index, side, :, source].astype(wide)
    for index in range(8):
        row = vec_ref[index : index + 1]
        total = jnp.zeros((1, part), wide)
        for quarter in range(4):
            total += jnp.where(shard == quarter, row[:, quarter * part : (quarter + 1) * part], 0.0)
        vectors[index][...] = total.reshape(part)
    total = jnp.zeros((1, width), wide)
    for quarter in range(4):
        total += jnp.where(shard == quarter, vec_ref[8 + quarter : 9 + quarter], 0.0)
    vectors[8][...] = total.reshape(width)


def finish(owner, output, returned, kept, back_grad, down, up, out, qkv, last, memory, vec):
    low = jnp.bfloat16
    wide = jnp.float32
    shape = jax.ShapeDtypeStruct
    width = down.shape[1]
    part = width // 4
    inside = pl.BlockSpec(memory_space=pltpu.VMEM)
    square = shape((part, width), wide)

    def whole(array):
        return pl.BlockSpec(array.shape, lambda step: (0,) * array.ndim)

    return pl.pallas_call(
        finish_kernel,
        grid=(1,),
        in_specs=[pl.BlockSpec(memory_space=pltpu.SMEM)]
        + [
            whole(array)
            for array in (
                output, returned, kept, back_grad, down, up, out, qkv, last, memory, vec
            )
        ],
        out_specs=[inside] * 19,
        out_shape=[
            shape((1, HALF, width), low), shape((1, OWN, width), low), shape((1, OWN, width), low),
            shape((1, 2, READ, width), low), square, square, square, square,
            shape((part, 4 * width), wide), shape((width, width), wide),
        ]
        + [shape((part,), wide)] * 8
        + [shape((width,), wide)],
        compiler_params=pltpu.CompilerParams(vmem_limit_bytes=67043328),
        name="finish",
    )(owner, output, returned, kept, back_grad, down, up, out, qkv, last, memory, vec)


def body_pairs(
    prompt_rows, follow_rows, memory_rows, follow_owner, follow_length,
    query_weight, key_weight, value_weight, out_weight, query_bias, value_bias, out_bias,
    first_gain, first_shift, up_weight, up_bias, down_weight, down_bias,
    second_gain, second_shift, prompt_cotan, follow_cotan,
):
    qkv, wide, vec, kept, sent, memory, kept_cot, sent_cot, bias = prepare(
        follow_owner, follow_length, follow_rows, follow_cotan, memory_rows,
        query_weight, key_weight, value_weight, out_weight, up_weight,
        (
            query_bias, value_bias, out_bias, first_gain, first_shift, down_bias,
            second_gain, second_shift, up_bias,
        ),
    )
    (
        qkv_mat, _, _, _, key_rows,
        output, activated, first_low, grad_down, grad_inner, grad_branch, grad_mixed, grad_hidden,
        mixed, log, query_low, key_low, value_low, sums,
    ) = front(
        qkv, wide, down_weight, vec, prompt_rows[0], kept, sent, memory, prompt_cotan[0],
        kept_cot, sent_cot, bias,
    )
    (
        down_sum, up_sum, out_sum, qkv_sum, last_sum, returned_out, grad_prompt, grad_kept, returned_grad,
        memory_sum, sums,
    ) = back(
        activated, grad_down, first_low, grad_inner, mixed, grad_branch, grad_hidden, key_rows,
        qkv_mat, output, sums,
        query_low, key_low, value_low, grad_mixed, log, bias,
    )
    (
        prompt_out, follow_out, follow_grad, grad_memory, query_sum, key_sum, value_sum, out_sum,
        up_sum, down_sum, *vectors,
    ) = finish(
        follow_owner, output, returned_out, grad_kept, returned_grad, down_sum, up_sum, out_sum,
        qkv_sum, last_sum, memory_sum, sums,
    )
    return (
        prompt_out, follow_out, grad_prompt[None], follow_grad, grad_memory,
        query_sum, key_sum, value_sum, out_sum, vectors[0], vectors[1], vectors[2], vectors[3],
        vectors[4], up_sum, vectors[8], down_sum, vectors[5], vectors[6], vectors[7],
    )


def solution(mesh):
    return jax.shard_map(
        body_pairs if pairs_fit(mesh) else body_any,
        mesh=mesh,
        in_specs=(
            P("grp", "shard", None),
            P("grp", "shard", None),
            P("grp", None, None, None),
            P("grp", None),
            P("grp", None),
            P(("grp", "shard"), None),
            P(("grp", "shard"), None),
            P(("grp", "shard"), None),
            P(("grp", "shard"), None),
            P(("grp", "shard")),
            P(("grp", "shard")),
            P(("grp", "shard")),
            P(("grp", "shard")),
            P(("grp", "shard")),
            P(("grp", "shard"), None),
            P(("grp", "shard")),
            P(("grp", "shard"), None),
            P(("grp", "shard")),
            P(("grp", "shard")),
            P(("grp", "shard")),
            P("grp", "shard", None),
            P("grp", "shard", None),
        ),
        out_specs=(
            P("grp", "shard", None),
            P("grp", "shard", None),
            P("grp", "shard", None),
            P("grp", "shard", None),
            P("grp", None, None, None),
            P("shard", None),
            P("shard", None),
            P("shard", None),
            P("shard", None),
            P("shard"),
            P("shard"),
            P("shard"),
            P("shard"),
            P("shard"),
            P("shard", None),
            P("shard"),
            P("shard", None),
            P("shard"),
            P("shard"),
            P("shard"),
        ),
        check_vma=False,
    )
```

```python
import jax
import jax.numpy as jnp
from jax import lax
from jax.experimental import pallas as pl
from jax.experimental.pallas import tpu as pltpu
from jax.sharding import PartitionSpec as P

HEADS = 12
HEAD = 64
READ = 10
WRITE = 10
PLEN = 1024
CLEN = 128
CONTS_PER = 8


EPSILON = 1e-12
SCALE = 0.125
NEGATIVE = -1e30
ROOT_HALF = 0.7071067811865476
ROOT_GAUSS = 0.3989422804014327


def product(left, right):
    return jnp.dot(left, right, preferred_element_type=jnp.float32)


def times_back(left, right):
    return lax.dot_general(
        left, right, (((1,), (1,)), ((), ())), preferred_element_type=jnp.float32
    )


def outer_sum(left, right):
    return lax.dot_general(
        left, right, (((0,), (0,)), ((), ())), preferred_element_type=jnp.float32
    )


def column_sum(values):
    return jnp.sum(values.astype(jnp.float32), axis=0)


def layer_norm(hidden, gain, shift):
    center = hidden - jnp.mean(hidden, axis=-1, keepdims=True)
    inverse = lax.rsqrt(jnp.mean(center * center, axis=-1, keepdims=True) + EPSILON)
    normed = center * inverse
    return (normed * gain.astype(jnp.float32) + shift.astype(jnp.float32), normed, inverse)


def norm_back(grad_normed, normed, inverse):
    centered = grad_normed - jnp.mean(grad_normed, axis=-1, keepdims=True)
    return inverse * (centered - normed * jnp.mean(grad_normed * normed, axis=-1, keepdims=True))


def gelu_exact(hidden):
    return 0.5 * hidden * (1.0 + lax.erf(hidden * ROOT_HALF))


def gelu_slope(hidden):
    return (
        0.5 * (1.0 + lax.erf(hidden * ROOT_HALF))
        + hidden * jnp.exp(-0.5 * hidden * hidden) * ROOT_GAUSS
    )


def split_heads(values):
    return values.reshape(values.shape[0], values.shape[1], HEADS, HEAD)


def block_scores(queries, keys, valid):
    scores = (
        jnp.einsum(
            "nqhd,nkhd->nhqk",
            split_heads(queries),
            split_heads(keys),
            preferred_element_type=jnp.float32,
        )
        * SCALE
    )
    return jnp.where(valid[:, None, None, :], scores, NEGATIVE)


def attend_forward(queries, keys, values, valid):
    scores = block_scores(queries, keys, valid)
    maximum = jnp.max(scores, axis=-1, keepdims=True)
    powers = jnp.exp(scores - maximum)
    totals = jnp.sum(powers, axis=-1, keepdims=True)
    chances = (powers / totals).astype(jnp.bfloat16)
    result = jnp.einsum(
        "nhqk,nkhd->nqhd", chances, split_heads(values), preferred_element_type=jnp.float32
    )
    return (result.reshape(-1, queries.shape[2]), maximum + jnp.log(totals))


def attend_backward(queries, keys, values, valid, logsum, grad_out):
    width = queries.shape[2]
    scores = block_scores(queries, keys, valid)
    chances = jnp.exp(scores - logsum)
    grad_heads = split_heads(grad_out)
    grad_chance = jnp.einsum(
        "nqhd,nkhd->nhqk", grad_heads, split_heads(values), preferred_element_type=jnp.float32
    )
    inner = jnp.sum(chances * grad_chance, axis=-1, keepdims=True)
    grad_score = (chances * (grad_chance - inner)).astype(jnp.bfloat16)
    grad_query = (
        jnp.einsum(
            "nhqk,nkhd->nqhd", grad_score, split_heads(keys), preferred_element_type=jnp.float32
        )
        * SCALE
    )
    grad_key = (
        jnp.einsum(
            "nhqk,nqhd->nkhd", grad_score, split_heads(queries), preferred_element_type=jnp.float32
        )
        * SCALE
    )
    grad_value = jnp.einsum(
        "nhqk,nqhd->nkhd",
        chances.astype(jnp.bfloat16),
        grad_heads,
        preferred_element_type=jnp.float32,
    )
    span = keys.shape[1]
    return (
        grad_query.reshape(-1, width),
        grad_key.reshape(keys.shape[0], span, width),
        grad_value.reshape(keys.shape[0], span, width),
    )


def body_any(
    prompt_rows,
    follow_rows,
    memory_rows,
    follow_owner,
    follow_length,
    query_weight,
    key_weight,
    value_weight,
    out_weight,
    query_bias,
    value_bias,
    out_bias,
    first_gain,
    first_shift,
    up_weight,
    up_bias,
    down_weight,
    down_bias,
    second_gain,
    second_shift,
    prompt_cotan,
    follow_cotan,
):
    (
        query_mat,
        key_mat,
        value_mat,
        out_mat,
        query_add,
        value_add,
        out_add,
        gain_one,
        shift_one,
        up_mat,
        up_add,
        down_mat,
        down_add,
        gain_two,
        shift_two,
    ) = (
        lax.all_gather(query_weight, ("grp", "shard"), axis=0, tiled=True),
        lax.all_gather(key_weight, ("grp", "shard"), axis=0, tiled=True),
        lax.all_gather(value_weight, ("grp", "shard"), axis=0, tiled=True),
        lax.all_gather(out_weight, ("grp", "shard"), axis=0, tiled=True),
        lax.all_gather(query_bias, ("grp", "shard"), axis=0, tiled=True),
        lax.all_gather(value_bias, ("grp", "shard"), axis=0, tiled=True),
        lax.all_gather(out_bias, ("grp", "shard"), axis=0, tiled=True),
        lax.all_gather(first_gain, ("grp", "shard"), axis=0, tiled=True),
        lax.all_gather(first_shift, ("grp", "shard"), axis=0, tiled=True),
        lax.all_gather(up_weight, ("grp", "shard"), axis=0, tiled=True),
        lax.all_gather(up_bias, ("grp", "shard"), axis=0, tiled=True),
        lax.all_gather(down_weight, ("grp", "shard"), axis=0, tiled=True),
        lax.all_gather(down_bias, ("grp", "shard"), axis=0, tiled=True),
        lax.all_gather(second_gain, ("grp", "shard"), axis=0, tiled=True),
        lax.all_gather(second_shift, ("grp", "shard"), axis=0, tiled=True),
    )
    shard_index = lax.axis_index("shard")
    prompt = prompt_rows[0]
    follow = follow_rows[0]
    p_count = prompt.shape[0]
    f_count = follow.shape[0]
    width = prompt.shape[1]
    families = memory_rows.shape[1]
    all_rows = jnp.concatenate([prompt, follow], axis=0)
    memory_flat = memory_rows[0].reshape(families * READ, width)
    query_low = (product(all_rows, query_mat) + query_add.astype(jnp.float32)).astype(jnp.bfloat16)
    key_low = product(all_rows, key_mat).astype(jnp.bfloat16)
    value_low = (product(all_rows, value_mat) + value_add.astype(jnp.float32)).astype(jnp.bfloat16)
    mem_key = product(memory_flat, key_mat).astype(jnp.bfloat16).reshape(families, READ, width)
    mem_value = (
        (product(memory_flat, value_mat) + value_add.astype(jnp.float32))
        .astype(jnp.bfloat16)
        .reshape(families, READ, width)
    )
    half_prompt = PLEN // 2
    per_block = CONTS_PER // 2
    prompt_blocks = p_count // half_prompt
    conts_here = f_count // CLEN
    positions = jnp.arange(CLEN)
    open_span = jnp.ones((per_block, READ + PLEN), dtype=bool)
    owner_row = follow_owner[0]
    length_row = follow_length[0]
    prompt_keys, prompt_values = (
        lax.all_gather(key_low[:p_count], "shard", axis=0, tiled=True),
        lax.all_gather(value_low[:p_count], "shard", axis=0, tiled=True),
    )
    key_table = prompt_keys.reshape(families, PLEN, width)
    value_table = prompt_values.reshape(families, PLEN, width)

    def prompt_inputs(block):
        start = block * half_prompt
        family = (shard_index * p_count + start) // PLEN
        keys = jnp.concatenate([mem_key[family], key_table[family]], axis=0)[None]
        values = jnp.concatenate([mem_value[family], value_table[family]], axis=0)[None]
        valid = jnp.ones((1, READ + PLEN), dtype=bool)
        return (query_low[start : start + half_prompt][None], keys, values, valid, family)

    def follow_inputs(block):
        first_row = p_count + block * per_block * CLEN
        chosen = shard_index * conts_here + block * per_block + jnp.arange(per_block)
        owners = owner_row[chosen]
        lengths = length_row[chosen]
        own_keys = key_low[first_row : first_row + per_block * CLEN].reshape(per_block, CLEN, width)
        own_values = value_low[first_row : first_row + per_block * CLEN].reshape(
            per_block, CLEN, width
        )
        keys = jnp.concatenate([mem_key[owners], key_table[owners], own_keys], axis=1)
        values = jnp.concatenate([mem_value[owners], value_table[owners], own_values], axis=1)
        own_valid = (positions[None, :] < lengths[:, None]) | (positions[None, :] >= CLEN - WRITE)
        valid = jnp.concatenate([open_span, own_valid], axis=1)
        queries = query_low[first_row : first_row + per_block * CLEN].reshape(
            per_block, CLEN, width
        )
        return (queries, keys, values, valid, owners)

    attended = []
    saved = []
    block = 0
    queries, keys, values, valid, family = prompt_inputs(block)
    result, logsum = attend_forward(queries, keys, values, valid)
    attended.append(result)
    saved.append(logsum)
    block = 0
    queries, keys, values, valid, owners = follow_inputs(block)
    result, logsum = attend_forward(queries, keys, values, valid)
    attended.append(result)
    saved.append(logsum)
    mixed = jnp.concatenate(attended, axis=0).astype(jnp.bfloat16)
    branch = product(mixed, out_mat) + out_add.astype(jnp.float32)
    first, normed_one, inverse_one = layer_norm(
        all_rows.astype(jnp.float32) + branch, gain_one, shift_one
    )
    first_low = first.astype(jnp.bfloat16)
    inner = product(first_low, up_mat) + up_add.astype(jnp.float32)
    activated = gelu_exact(inner).astype(jnp.bfloat16)
    second = product(activated, down_mat) + down_add.astype(jnp.float32)
    output, normed_two, inverse_two = layer_norm(first + second, gain_two, shift_two)
    output = output.astype(jnp.bfloat16)
    (
        query_mat,
        key_mat,
        value_mat,
        out_mat,
        query_add,
        value_add,
        out_add,
        gain_one,
        shift_one,
        up_mat,
        up_add,
        down_mat,
        down_add,
        gain_two,
        shift_two,
    ) = (
        lax.all_gather(query_weight, ("grp", "shard"), axis=0, tiled=True),
        lax.all_gather(key_weight, ("grp", "shard"), axis=0, tiled=True),
        lax.all_gather(value_weight, ("grp", "shard"), axis=0, tiled=True),
        lax.all_gather(out_weight, ("grp", "shard"), axis=0, tiled=True),
        lax.all_gather(query_bias, ("grp", "shard"), axis=0, tiled=True),
        lax.all_gather(value_bias, ("grp", "shard"), axis=0, tiled=True),
        lax.all_gather(out_bias, ("grp", "shard"), axis=0, tiled=True),
        lax.all_gather(first_gain, ("grp", "shard"), axis=0, tiled=True),
        lax.all_gather(first_shift, ("grp", "shard"), axis=0, tiled=True),
        lax.all_gather(up_weight, ("grp", "shard"), axis=0, tiled=True),
        lax.all_gather(up_bias, ("grp", "shard"), axis=0, tiled=True),
        lax.all_gather(down_weight, ("grp", "shard"), axis=0, tiled=True),
        lax.all_gather(down_bias, ("grp", "shard"), axis=0, tiled=True),
        lax.all_gather(second_gain, ("grp", "shard"), axis=0, tiled=True),
        lax.all_gather(second_shift, ("grp", "shard"), axis=0, tiled=True),
    )
    cotangent = jnp.concatenate([prompt_cotan[0], follow_cotan[0]], axis=0).astype(jnp.float32)
    grad_gain_two = jnp.sum(cotangent * normed_two, axis=0)
    grad_shift_two = jnp.sum(cotangent, axis=0)
    grad_mid = norm_back(cotangent * gain_two.astype(jnp.float32), normed_two, inverse_two)
    grad_down = grad_mid.astype(jnp.bfloat16)
    grad_down_mat = outer_sum(activated, grad_down)
    grad_down_add = column_sum(grad_down)
    grad_inner = (times_back(grad_down, down_mat) * gelu_slope(inner)).astype(jnp.bfloat16)
    grad_up_mat = outer_sum(first_low, grad_inner)
    grad_up_add = column_sum(grad_inner)
    grad_first = grad_mid + times_back(grad_inner, up_mat)
    grad_gain_one = jnp.sum(grad_first * normed_one, axis=0)
    grad_shift_one = jnp.sum(grad_first, axis=0)
    grad_hidden = norm_back(grad_first * gain_one.astype(jnp.float32), normed_one, inverse_one)
    grad_branch = grad_hidden.astype(jnp.bfloat16)
    grad_out_mat = outer_sum(mixed, grad_branch)
    grad_out_add = column_sum(grad_branch)
    grad_mixed = times_back(grad_branch, out_mat).astype(jnp.bfloat16)
    mem_key_acc = jnp.zeros((families, READ, width), jnp.float32)
    mem_value_acc = jnp.zeros((families, READ, width), jnp.float32)
    prompt_key_acc = jnp.zeros((families, PLEN, width), jnp.float32)
    prompt_value_acc = jnp.zeros((families, PLEN, width), jnp.float32)
    block = 0
    queries, keys, values, valid, family = prompt_inputs(block)
    start = block * half_prompt
    grad_query, grad_key, grad_value = attend_backward(
        queries, keys, values, valid, saved[block], grad_mixed[start : start + half_prompt][None]
    )
    query_parts = grad_query
    mem_key_acc = mem_key_acc.at[family].add(grad_key[0, :READ])
    mem_value_acc = mem_value_acc.at[family].add(grad_value[0, :READ])
    prompt_key_acc = prompt_key_acc.at[family].add(grad_key[0, READ:])
    prompt_value_acc = prompt_value_acc.at[family].add(grad_value[0, READ:])
    prompt_query_low = query_parts.astype(jnp.bfloat16)
    block = 0
    queries, keys, values, valid, owners = follow_inputs(block)
    first_row = p_count + block * per_block * CLEN
    grad_slice = grad_mixed[first_row : first_row + per_block * CLEN].reshape(
        per_block, CLEN, width
    )
    grad_query, grad_key, grad_value = attend_backward(
        queries, keys, values, valid, saved[prompt_blocks + block], grad_slice
    )
    mem_key_acc = mem_key_acc.at[owners].add(grad_key[:, :READ])
    mem_value_acc = mem_value_acc.at[owners].add(grad_value[:, :READ])
    prompt_key_acc = prompt_key_acc.at[owners].add(grad_key[:, READ : READ + PLEN])
    prompt_value_acc = prompt_value_acc.at[owners].add(grad_value[:, READ : READ + PLEN])
    own_key_parts = grad_key[:, READ + PLEN :].reshape(-1, width)
    own_value_parts = grad_value[:, READ + PLEN :].reshape(-1, width)
    prompt_key_grad, prompt_value_grad = (
        lax.psum_scatter(
            prompt_key_acc.reshape(families * PLEN, width).astype(jnp.bfloat16),
            "shard",
            scatter_dimension=0,
            tiled=True,
        ).astype(jnp.float32),
        lax.psum_scatter(
            prompt_value_acc.reshape(families * PLEN, width).astype(jnp.bfloat16),
            "shard",
            scatter_dimension=0,
            tiled=True,
        ).astype(jnp.float32),
    )
    follow_query_low = grad_query.astype(jnp.bfloat16)
    follow_key_low = own_key_parts.astype(jnp.bfloat16)
    follow_value_low = own_value_parts.astype(jnp.bfloat16)
    mem_key_sum, mem_value_sum = (
        lax.psum(mem_key_acc.astype(jnp.bfloat16), "shard").astype(jnp.float32),
        lax.psum(mem_value_acc.astype(jnp.bfloat16), "shard").astype(jnp.float32),
    )
    grad_query_low = jnp.concatenate([prompt_query_low, follow_query_low], axis=0)
    grad_key_low = jnp.concatenate([prompt_key_grad.astype(jnp.bfloat16), follow_key_low], axis=0)
    grad_value_low = jnp.concatenate(
        [prompt_value_grad.astype(jnp.bfloat16), follow_value_low], axis=0
    )
    mem_key_low = mem_key_sum.astype(jnp.bfloat16).reshape(families * READ, width)
    mem_value_low = mem_value_sum.astype(jnp.bfloat16).reshape(families * READ, width)
    grad_rows_all = (
        grad_hidden
        + times_back(grad_query_low, query_mat)
        + times_back(grad_key_low, key_mat)
        + times_back(grad_value_low, value_mat)
    ).astype(jnp.bfloat16)
    grad_memory = (
        (times_back(mem_key_low, key_mat) + times_back(mem_value_low, value_mat))
        .astype(jnp.bfloat16)
        .reshape(1, families, READ, width)
    )
    leader = (shard_index == 0).astype(jnp.float32)
    grad_query_mat = outer_sum(all_rows, grad_query_low)
    grad_query_add = column_sum(grad_query_low)
    grad_key_mat = outer_sum(all_rows, grad_key_low) + leader * outer_sum(memory_flat, mem_key_low)
    grad_value_mat = outer_sum(all_rows, grad_value_low) + leader * outer_sum(
        memory_flat, mem_value_low
    )
    grad_value_add = column_sum(grad_value_low) + leader * column_sum(mem_value_low)
    pieces = (
        lax.psum_scatter(
            grad_query_mat.astype(jnp.bfloat16), "shard", scatter_dimension=0, tiled=True
        ).astype(jnp.float32),
        lax.psum_scatter(
            grad_key_mat.astype(jnp.bfloat16), "shard", scatter_dimension=0, tiled=True
        ).astype(jnp.float32),
        lax.psum_scatter(
            grad_value_mat.astype(jnp.bfloat16), "shard", scatter_dimension=0, tiled=True
        ).astype(jnp.float32),
        lax.psum_scatter(
            grad_out_mat.astype(jnp.bfloat16), "shard", scatter_dimension=0, tiled=True
        ).astype(jnp.float32),
        lax.psum_scatter(
            grad_query_add.astype(jnp.bfloat16), "shard", scatter_dimension=0, tiled=True
        ).astype(jnp.float32),
        lax.psum_scatter(
            grad_value_add.astype(jnp.bfloat16), "shard", scatter_dimension=0, tiled=True
        ).astype(jnp.float32),
        lax.psum_scatter(
            grad_out_add.astype(jnp.bfloat16), "shard", scatter_dimension=0, tiled=True
        ).astype(jnp.float32),
        lax.psum_scatter(
            grad_gain_one.astype(jnp.bfloat16), "shard", scatter_dimension=0, tiled=True
        ).astype(jnp.float32),
        lax.psum_scatter(
            grad_shift_one.astype(jnp.bfloat16), "shard", scatter_dimension=0, tiled=True
        ).astype(jnp.float32),
        lax.psum_scatter(
            grad_up_mat.astype(jnp.bfloat16), "shard", scatter_dimension=0, tiled=True
        ).astype(jnp.float32),
        lax.psum_scatter(
            grad_up_add.astype(jnp.bfloat16), "shard", scatter_dimension=0, tiled=True
        ).astype(jnp.float32),
        lax.psum_scatter(
            grad_down_mat.astype(jnp.bfloat16), "shard", scatter_dimension=0, tiled=True
        ).astype(jnp.float32),
        lax.psum_scatter(
            grad_down_add.astype(jnp.bfloat16), "shard", scatter_dimension=0, tiled=True
        ).astype(jnp.float32),
        lax.psum_scatter(
            grad_gain_two.astype(jnp.bfloat16), "shard", scatter_dimension=0, tiled=True
        ).astype(jnp.float32),
        lax.psum_scatter(
            grad_shift_two.astype(jnp.bfloat16), "shard", scatter_dimension=0, tiled=True
        ).astype(jnp.float32),
    )
    summed = (
        lax.psum(pieces[0].astype(jnp.bfloat16), "grp").astype(jnp.float32),
        lax.psum(pieces[1].astype(jnp.bfloat16), "grp").astype(jnp.float32),
        lax.psum(pieces[2].astype(jnp.bfloat16), "grp").astype(jnp.float32),
        lax.psum(pieces[3].astype(jnp.bfloat16), "grp").astype(jnp.float32),
        lax.psum(pieces[4].astype(jnp.bfloat16), "grp").astype(jnp.float32),
        lax.psum(pieces[5].astype(jnp.bfloat16), "grp").astype(jnp.float32),
        lax.psum(pieces[6].astype(jnp.bfloat16), "grp").astype(jnp.float32),
        lax.psum(pieces[7].astype(jnp.bfloat16), "grp").astype(jnp.float32),
        lax.psum(pieces[8].astype(jnp.bfloat16), "grp").astype(jnp.float32),
        lax.psum(pieces[9].astype(jnp.bfloat16), "grp").astype(jnp.float32),
        lax.psum(pieces[10].astype(jnp.bfloat16), "grp").astype(jnp.float32),
        lax.psum(pieces[11].astype(jnp.bfloat16), "grp").astype(jnp.float32),
        lax.psum(pieces[12].astype(jnp.bfloat16), "grp").astype(jnp.float32),
        lax.psum(pieces[13].astype(jnp.bfloat16), "grp").astype(jnp.float32),
        lax.psum(pieces[14].astype(jnp.bfloat16), "grp").astype(jnp.float32),
    )
    return (
        output[:p_count][None],
        output[p_count:][None],
        grad_rows_all[:p_count][None],
        grad_rows_all[p_count:][None],
        grad_memory,
        summed[0],
        summed[1],
        summed[2],
        summed[3],
        summed[4],
        summed[5],
        summed[6],
        summed[7],
        summed[8],
        summed[9],
        summed[10],
        summed[11],
        summed[12],
        summed[13],
        summed[14],
    )


MEM = 16
HALF = PLEN // 2
OWN = 512
CONT = HALF + HALF + MEM
KEYS = CONT + OWN
QROWS = HALF + OWN
PAIRS = HEADS // 2
NAMES = ("grp", "shard")


def pairs_fit(mesh):
    return mesh.shape["shard"] == 4 and mesh.shape["grp"] == 8


def head_mask(head):
    lane = lax.broadcasted_iota(jnp.int32, (1, 2 * HEAD), 1)
    return lane // HEAD == head


def pick(mask, values):
    return jnp.where(mask, values.astype(jnp.float32), 0.0).astype(jnp.bfloat16)


def flip(values):
    return values.astype(jnp.float32).T.astype(jnp.bfloat16)


def own_scores(keys, queries):
    parts = []
    for cont in range(OWN // CLEN):
        part = slice(cont * CLEN, (cont + 1) * CLEN)
        parts.append(times_back(keys[part], queries[part]))
    return jnp.concatenate(parts, axis=1)


def attend_pair(query_ref, key_ref, value_ref, bias_ref, out_ref, log_ref):
    mem_valid = lax.broadcasted_iota(jnp.int32, (MEM, 1), 0) < READ
    value_flip = flip(value_ref[...])
    results = []
    for head in range(2):
        mask = head_mask(head)
        queries = pick(mask, query_ref[...])
        main = times_back(key_ref[: 2 * HALF], queries)
        memory = jnp.where(mem_valid, times_back(key_ref[2 * HALF : CONT], queries), NEGATIVE)
        own = own_scores(key_ref[CONT:], queries[HALF:]) + bias_ref[...]
        top = jnp.maximum(
            jnp.max(main, axis=0, keepdims=True), jnp.max(memory, axis=0, keepdims=True)
        )
        top_own = jnp.maximum(top[:, HALF:], jnp.max(own, axis=0, keepdims=True))
        top = jnp.concatenate([top[:, :HALF], top_own], axis=1)
        main = jnp.exp(main - top)
        memory = jnp.exp(memory - top)
        own = jnp.exp(own - top_own)
        total = jnp.sum(main, axis=0, keepdims=True) + jnp.sum(memory, axis=0, keepdims=True)
        total = jnp.concatenate(
            [total[:, :HALF], total[:, HALF:] + jnp.sum(own, axis=0, keepdims=True)], axis=1
        )
        flipped = value_flip[head * HEAD : (head + 1) * HEAD]
        result = product(flipped[:, : 2 * HALF], main.astype(jnp.bfloat16))
        result += product(flipped[:, 2 * HALF : CONT], memory.astype(jnp.bfloat16))
        own = own.astype(jnp.bfloat16)
        own_parts = []
        for cont in range(OWN // CLEN):
            own_parts.append(
                product(
                    flipped[:, CONT + cont * CLEN : CONT + (cont + 1) * CLEN],
                    own[:, cont * CLEN : (cont + 1) * CLEN],
                )
            )
        result = jnp.concatenate(
            [result[:, :HALF], result[:, HALF:] + jnp.concatenate(own_parts, axis=1)], axis=1
        )
        results.append(result / total)
        log_ref[head : head + 1] = top + jnp.log(total)
    out_ref[...] = jnp.concatenate(results, axis=0).T.astype(jnp.bfloat16)


MESH = pl.DeviceIdType.MESH
WHERE = pl.BlockSpec(memory_space=pl.ANY)
INSIDE = pl.BlockSpec(memory_space=pltpu.VMEM)
VECTORS = 16


def seat():
    grp = lax.axis_index("grp")
    return (grp // 2, grp % 2, lax.axis_index("shard"))


def unit_of(z, core, shard):
    return (z * 2 + core) * 4 + shard


def device_of(z, core, shard):
    return (z * 2 + core, shard)


def greet():
    z, core, shard = seat()
    barrier = pltpu.get_barrier_semaphore()
    others = [device_of((z + step) % 4, core, shard) for step in (1, 2, 3)]
    others += [
        device_of(z, core, shard ^ 1),
        device_of(z, core, shard ^ 2),
        device_of(z, 1 - core, shard),
    ]
    for other in others:
        pl.semaphore_signal(barrier, inc=1, device_id=other, device_id_type=MESH)
    pl.semaphore_wait(barrier, len(others))


class Gather:
    def __init__(self, mine, full, send, recv, by_y=(0, 2)):
        self.mine, self.full, self.send, self.recv = mine, full, send, recv
        self.share = mine.shape[0]
        self.by_y = by_y
        self.z, self.core, self.shard = seat()
        self.sent = 0

    def rows(self, unit):
        return self.full.at[pl.ds(pl.multiple_of(unit * self.share, 8), self.share)]

    def link(self, index, unit, z, core, shard, source=None):
        return pltpu.make_async_remote_copy(
            src_ref=self.rows(unit) if source is None else source,
            dst_ref=self.rows(unit),
            send_sem=self.send.at[index],
            recv_sem=self.recv.at[unit],
            device_id=device_of(z, core, shard),
            device_id_type=MESH,
        )

    def push(self, unit, z, core, shard, source=None):
        self.link(self.sent, unit, z, core, shard, source).start()
        self.sent += 1

    def arrive(self, unit):
        self.link(0, unit, self.z, 1 - self.core, self.shard).wait_recv()

    def start_line(self):
        me = unit_of(self.z, self.core, self.shard)
        for step in (1, 2, 3):
            self.push(me, (self.z + step) % 4, self.core, self.shard, self.mine)

    def start_plane(self):
        z, core, shard = self.z, self.core, self.shard
        me = unit_of(z, core, shard)
        self.push(me, z, core, shard ^ 1, self.mine)
        self.push(me, z, core, shard ^ 2, self.mine)
        self.push(me, z, 1 - core, shard, self.mine)

    def own(self, semaphore):
        return pltpu.make_async_copy(
            self.mine, self.rows(unit_of(self.z, self.core, self.shard)), semaphore
        )

    def column(self, step):
        z, core, shard = self.z, self.core, self.shard
        unit = unit_of((z + step) % 4, core, shard)
        self.arrive(unit)
        self.push(unit, z, core, shard ^ 1)
        self.push(unit, z, core, shard ^ 2)
        self.push(unit, z, 1 - core, shard)

    def side(self, step):
        z, core, shard = self.z, self.core, self.shard
        for hop in (1, 2):
            unit = unit_of((z + step) % 4, core, shard ^ hop)
            self.arrive(unit)
            if (step in self.by_y) == (hop == 1):
                self.push(unit, z, core, shard ^ (3 - hop))
            self.push(unit, z, 1 - core, shard)

    def corner(self, step):
        z, core, shard = self.z, self.core, self.shard
        unit = unit_of((z + step) % 4, core, shard ^ 3)
        self.arrive(unit)
        self.push(unit, z, 1 - core, shard)

    def sibling(self):
        def wait(index, carry):
            unit = (index // 4) * 8 + (1 - self.core) * 4 + index % 4
            self.arrive(unit)
            return carry

        lax.fori_loop(0, 16, wait, 0)

    def finish(self):
        def wait(index, carry):
            pltpu.make_async_remote_copy(
                src_ref=self.mine,
                dst_ref=self.mine,
                send_sem=self.send.at[index],
                recv_sem=self.recv.at[0],
                device_id=device_of(self.z, 1 - self.core, self.shard),
                device_id_type=MESH,
            ).wait_send()
            return carry

        lax.fori_loop(0, self.sent, wait, 0)


class PlaneGather(Gather):
    def start_plane(self):
        z, core, shard = self.z, self.core, self.shard
        me = unit_of(z, core, shard)
        self.link(96, me, z, core, shard ^ 1, self.mine).start()
        self.link(97, me, z, core, shard ^ 2, self.mine).start()
        self.link(me, me, z, 1 - core, shard, self.mine).start()

    def along(self, unit, z_of, source=None):
        z, core, shard = self.z, self.core, self.shard

        @pl.when((z_of <= z) & (z < 3))
        def _():
            self.link(32 + unit, unit, z + 1, core, shard, source).start()

        @pl.when((z_of >= z) & (z > 0))
        def _():
            self.link(64 + unit, unit, z - 1, core, shard, source).start()

    def start_line(self):
        me = unit_of(self.z, self.core, self.shard)
        self.along(me, self.z, self.mine)

    def plane(self):
        z, core, shard = self.z, self.core, self.shard
        over_x = unit_of(z, core, shard ^ 1)
        over_y = unit_of(z, core, shard ^ 2)
        self.arrive(over_x)

        @pl.when(core == 0)
        def _():
            self.link(98, over_x, z, core, shard ^ 2).start()

        self.link(over_x, over_x, z, 1 - core, shard).start()
        self.along(over_x, z)
        self.arrive(over_y)

        @pl.when(core == 1)
        def _():
            self.link(98, over_y, z, core, shard ^ 1).start()

        self.link(over_y, over_y, z, 1 - core, shard).start()
        self.along(over_y, z)

    def corners(self):
        z, core, shard = self.z, self.core, self.shard
        unit = unit_of(z, core, shard ^ 3)
        self.arrive(unit)
        self.link(unit, unit, z, 1 - core, shard).start()
        self.along(unit, z)

    def far(self, distance, other):
        z, core, shard = self.z, self.core, self.shard
        for sign in (-1, 1):
            plane = z + sign * distance

            @pl.when((plane >= 0) & (plane < 4))
            def _():
                unit = unit_of(plane, core, shard ^ other)
                self.arrive(unit)
                self.link(unit, unit, z, 1 - core, shard).start()
                self.along(unit, plane)

    def finish(self):
        z, core, shard = self.z, self.core, self.shard

        def done(index, unit):
            self.link(index, unit, z, 1 - core, shard, self.mine).wait_send()

        for index in (96, 97, 98):
            done(index, 0)

        def wait(index, carry):
            plane = index // 4
            unit = plane * 8 + core * 4 + index % 4
            done(unit, unit)

            @pl.when((plane <= z) & (z < 3))
            def _():
                done(32 + unit, unit)

            @pl.when((plane >= z) & (z > 0))
            def _():
                done(64 + unit, unit)

            return carry

        lax.fori_loop(0, 16, wait, 0)


class Swap:
    def __init__(self, source, target, send, recv, z, core, shard):
        self.copy = pltpu.make_async_remote_copy(
            src_ref=source, dst_ref=target, send_sem=send, recv_sem=recv,
            device_id=device_of(z, core, shard), device_id_type=MESH,
        )

    def start(self):
        self.copy.start()

    def arrive(self):
        self.copy.wait_recv()

    def finish(self):
        self.copy.wait_send()


def spread_vector(vectors, index, width):
    narrow, broad = width // 32, 4 * width // 32
    row = lax.broadcasted_iota(jnp.int32, (32 * VECTORS, width), 0)
    lane = lax.broadcasted_iota(jnp.int32, (32 * VECTORS, width), 1)
    small = index < 8
    start = jnp.where(small, index, 8 + VECTORS * 8 * (index - 8))
    block = jnp.where(small, lane // narrow, lane // broad)
    select = jnp.where(row == VECTORS * block + start, 1.0, 0.0).astype(jnp.bfloat16)
    table = outer_sum(vectors, select)
    piece = lax.broadcasted_iota(jnp.int32, table.shape, 0)
    lane = lax.broadcasted_iota(jnp.int32, table.shape, 1)
    offset = jnp.where(small, lane % narrow, lane % broad)
    return jnp.sum(jnp.where(piece == offset, table, 0.0), axis=0, keepdims=True)


TILE = 512
PARTNERS = 4


def front_kernel(
    qkv_ref, wide_ref, down_ref, vec_ref, prompt_ref, kept_ref, sent_ref, mem_ref,
    prompt_cot, kept_cot, sent_cot, bias_ref,
    qkv_full, wide_full, down_full, vec_full, rows_out,
    out_ref, act_ref, first_ref, gdown_ref, ginner_ref, gbranch_ref, gmixed_ref, ghidden_ref,
    mixed_ref, log_ref, query_out, key_out, value_out, sums_ref,
    rows, weights, vectors, table, query, key, value, mixed, cotan, wide, down,
    act, slope, normed, first, total, hidden, small_low,
    send_a, recv_a, send_b, recv_b, send_c, recv_c, send_d, recv_d, swap_send, swap_recv, local,
    store,
):
    pair = pl.program_id(0)
    width = prompt_ref.shape[1]
    low = jnp.bfloat16
    one = Gather(qkv_ref, qkv_full, send_a, recv_a, (0, 1))
    small = Gather(vec_ref, vec_full, send_d, recv_d)
    two = Gather(wide_ref, wide_full, send_b, recv_b, (0, 1))
    three = PlaneGather(down_ref, down_full, send_c, recv_c)
    z, core, shard = seat()
    step_rows = HALF // PARTNERS
    partner = [
        Swap(
            prompt_ref.at[pl.ds(index * step_rows, step_rows)],
            rows.at[pl.ds(HALF + index * step_rows, step_rows)],
            swap_send.at[index], swap_recv.at[index], z, core, shard ^ 1,
        )
        for index in range(PARTNERS)
    ]
    taken = [
        Swap(
            sent_ref.at[pl.ds(index * step_rows, step_rows)],
            rows.at[pl.ds(CONT + OWN // 2 + index * step_rows, step_rows)],
            swap_send.at[PARTNERS + index], swap_recv.at[PARTNERS + index], z, core, shard ^ 2,
        )
        for index in range(2)
    ]
    taken_cot = Swap(
        sent_cot, cotan.at[pl.ds(HALF + OWN // 2, OWN // 2)],
        swap_send.at[PARTNERS + 2], swap_recv.at[PARTNERS + 2], z, core, shard ^ 2,
    )
    swaps = partner + taken + [taken_cot]
    own = [gather.own(local.at[index]) for index, gather in enumerate((one, small, two, three))]
    own += [
        pltpu.make_async_copy(prompt_ref, rows.at[pl.ds(0, HALF)], local.at[4]),
        pltpu.make_async_copy(mem_ref, rows.at[pl.ds(2 * HALF, MEM)], local.at[5]),
        pltpu.make_async_copy(kept_ref, rows.at[pl.ds(CONT, OWN // 2)], local.at[6]),
        pltpu.make_async_copy(prompt_cot, cotan.at[pl.ds(0, HALF)], local.at[7]),
        pltpu.make_async_copy(kept_cot, cotan.at[pl.ds(HALF, OWN // 2)], local.at[8]),
    ]
    load_weights = pltpu.make_async_copy(qkv_full, weights, local.at[9])
    load_vectors = pltpu.make_async_copy(vec_full, vectors, local.at[10])
    store_rows = pltpu.make_async_copy(rows, rows_out, local.at[11])
    load_wide = pltpu.make_async_copy(wide_full, wide, local.at[12])
    load_down = pltpu.make_async_copy(down_full, down, local.at[13])

    def project(start, query_start, count, queries):
        span = pl.ds(start, count)
        block = rows[span]
        if queries:
            result = (product(block, weights[:, :width]) + table[0:1]).astype(low)
            result = (result.astype(jnp.float32) * SCALE).astype(low)
            query[pl.ds(query_start, count)] = result
        key[span] = product(block, weights[:, width : 2 * width]).astype(low)
        value[span] = (product(block, weights[:, 2 * width :]) + table[1:2]).astype(low)

    @pl.when(pair == 0)
    def _():
        for copy in own[4:]:
            copy.start()
        greet()
        small.start_line()
        one.start_line()
        small.start_plane()
        one.start_plane()
        partner[0].start()
        three.start_line()
        taken[0].start()
        three.start_plane()
        for copy in own[:4]:
            copy.start()
        for step in (1, 2, 3):
            small.column(step)
            one.column(step)
        two.start_line()
        for step in range(4):
            small.side(step)
            one.side(step)
        partner[1].start()
        taken[1].start()
        partner[2].start()
        partner[3].start()
        two.start_plane()
        for step in range(4):
            small.corner(step)
            one.corner(step)
        small.sibling()
        own[1].wait()
        load_vectors.start()
        one.sibling()
        own[0].wait()
        load_weights.start()
        three.plane()
        for step in (1, 2, 3):
            two.column(step)
        load_vectors.wait()

        def spread(index, carry):
            table[pl.ds(index, 1)] = spread_vector(vectors[...], index, width)
            return carry

        lax.fori_loop(0, 12, spread, 0)
        for index in (2, 3, 4, 5, 6):
            own[index].wait()
        load_weights.wait()
        project(0, 0, HALF, True)
        three.corners()
        three.far(1, 0)
        for swap in taken:
            swap.arrive()
        project(CONT, HALF, OWN, True)
        three.far(1, 1)
        for swap in partner:
            swap.arrive()
        project(HALF, 0, HALF + MEM, False)
        store_rows.start()

    def later(when, *actions):
        @pl.when(pair == when)
        def _():
            for action in actions:
                action[0](*action[1:])

    later(0, (two.side, 0), (three.far, 1, 2))
    later(1, (two.side, 1), (three.far, 1, 3))
    later(2, (two.side, 2), (three.far, 2, 0), (three.far, 2, 1))
    later(3, (two.side, 3), (three.far, 2, 2))
    later(4, (two.corner, 0), (two.corner, 1), (three.far, 2, 3), (three.far, 3, 0))
    later(5, (two.corner, 2), (three.far, 3, 1))

    lanes = pl.ds(pl.multiple_of(pair * (2 * HEAD), 2 * HEAD), 2 * HEAD)
    query_out[...] = query[:, lanes]
    key_out[...] = key[:, lanes]
    value_out[...] = value[:, lanes]
    attend_pair(query_out, key_out, value_out, bias_ref, mixed_ref, log_ref)
    mixed[:, lanes] = mixed_ref[...]

    def fine(index):
        return table[index : index + 1]

    def save(tile, index):
        span = pl.ds(pl.multiple_of(tile * TILE, TILE), TILE)
        source, target = (
            (act, act_ref), (slope, ginner_ref), (hidden, ghidden_ref),
            (small_low.at[0], out_ref), (small_low.at[1], first_ref), (small_low.at[2], gdown_ref),
            (small_low.at[3], gbranch_ref), (small_low.at[4], gmixed_ref),
        )[index]
        return pltpu.make_async_copy(source, target.at[span], store.at[index])

    def up_chunk(step):
        return pl.ds(pl.multiple_of(step * width, 128), width)

    def up_columns(step):
        return pl.ds(pl.multiple_of((step + 1) * width, 128), width)

    def add_sum(index, values):
        sums_ref[pl.ds(index, 1)] += jnp.sum(values, axis=0, keepdims=True)

    def start_tile(tile):
        span = pl.ds(pl.multiple_of(tile * TILE, TILE), TILE)
        held = rows[pl.ds(pl.multiple_of(tile * CONT, MEM), TILE)].astype(jnp.float32)
        held = held + (product(mixed[span], wide[:, :width]) + fine(2))
        result, value_n, value_r = layer_norm(held, fine(3), fine(4))

        @pl.when(tile == 1)
        def _():
            for index in range(1, 8):
                save(0, index).wait()

        normed[...] = value_n
        first[...] = result
        small_low[1] = result.astype(low)
        return value_r

    def forward_chunk(step, carry):
        chunk = up_chunk(step)
        inner = product(small_low[1], wide[:, up_columns(step)]) + table[pl.ds(8 + step, 1)]
        half = 0.5 * (1.0 + lax.erf(inner * ROOT_HALF))
        active = (inner * half).astype(low)
        act[:, chunk] = active
        slope[:, chunk] = (half + inner * jnp.exp(-0.5 * inner * inner) * ROOT_GAUSS).astype(low)
        total[...] += product(active, down[chunk])
        return carry

    def backward_chunk(step, carry):
        chunk = up_chunk(step)
        grad = times_back(small_low[2], down[chunk]) * slope[:, chunk].astype(jnp.float32)
        grad = grad.astype(low)
        slope[:, chunk] = grad
        add_sum(8 + step, grad.astype(jnp.float32))
        total[...] += times_back(grad, wide[:, up_columns(step)])
        return carry

    def tile_body(tile, carry):
        span = pl.ds(pl.multiple_of(tile * TILE, TILE), TILE)
        inverse_one = start_tile(tile)
        total[...] = jnp.zeros_like(total)

        @pl.when(tile == 0)
        def _():
            three.far(3, 2)
            three.far(3, 3)
            three.sibling()
            load_down.start()
            load_down.wait()

        @pl.when(tile == 1)
        def _():
            save(0, 0).wait()
            taken_cot.arrive()

        lax.fori_loop(0, 4, forward_chunk, 0, unroll=2)
        save(tile, 0).start()
        result, value_n, inverse_two = layer_norm(
            first[...] + (total[...] + fine(5)), fine(6), fine(7)
        )
        small_low[0] = result.astype(low)
        save(tile, 3).start()
        save(tile, 4).start()
        cot = cotan[span].astype(jnp.float32)
        add_sum(6, cot * value_n)
        add_sum(7, cot)
        grad_mid = norm_back(cot * fine(6), value_n, inverse_two)
        grad_low = grad_mid.astype(low)
        small_low[2] = grad_low
        save(tile, 5).start()
        add_sum(5, grad_low.astype(jnp.float32))
        total[...] = grad_mid
        lax.fori_loop(0, 4, backward_chunk, 0, unroll=2)
        save(tile, 1).start()
        grad_first = total[...]
        add_sum(3, grad_first * normed[...])
        add_sum(4, grad_first)
        grad_hidden = norm_back(grad_first * fine(3), normed[...], inverse_one)
        hidden[...] = grad_hidden
        save(tile, 2).start()
        grad_low = grad_hidden.astype(low)
        small_low[3] = grad_low
        save(tile, 6).start()
        add_sum(2, grad_low.astype(jnp.float32))
        small_low[4] = times_back(grad_low, wide[:, :width]).astype(low)
        save(tile, 7).start()
        return carry

    @pl.when(pair == PAIRS - 1)
    def _():
        taken_cot.start()
        two.corner(3)
        two.sibling()
        load_wide.start()
        own[7].wait()
        own[8].wait()
        sums_ref[...] = jnp.zeros_like(sums_ref)
        load_wide.wait()
        lax.fori_loop(0, 2, tile_body, 0)
        store_rows.wait()
        for index in range(8):
            save(1, index).wait()
        for sender in (one, small, two, three, *swaps):
            sender.finish()


def front(
    qkv, wide_share, down_share, vec, prompt, kept, sent, memory, prompt_cot, kept_cot, sent_cot,
    bias,
):
    width = prompt.shape[1]
    low = jnp.bfloat16
    wide = jnp.float32
    shape = jax.ShapeDtypeStruct

    def block(rows):
        return pl.BlockSpec((rows, 2 * HEAD), lambda pair: (0, pair))

    def full(share):
        return shape((32 * share.shape[0], share.shape[1]), low)

    dma = pltpu.SemaphoreType.DMA
    memory_space = pltpu.VMEM
    return pl.pallas_call(
        front_kernel,
        grid=(PAIRS,),
        in_specs=[INSIDE] * 4
        + [WHERE] * 7
        + [pl.BlockSpec((CLEN, OWN), lambda pair: (0, 0))],
        out_specs=[WHERE] * 13
        + [
            block(QROWS), pl.BlockSpec((None, 2, QROWS), lambda pair: (pair, 0, 0)),
            block(QROWS), block(KEYS), block(KEYS),
            pl.BlockSpec((VECTORS, width), lambda pair: (0, 0)),
        ],
        out_shape=[
            full(qkv), full(wide_share), full(down_share), full(vec),
            shape((KEYS, width), low),
            shape((QROWS, width), low),
            shape((QROWS, 4 * width), low),
            shape((QROWS, width), low),
            shape((QROWS, width), low),
            shape((QROWS, 4 * width), low),
            shape((QROWS, width), low),
            shape((QROWS, width), low),
            shape((QROWS, width), wide),
            shape((QROWS, width), low),
            shape((PAIRS, 2, QROWS), wide),
            shape((QROWS, width), low),
            shape((KEYS, width), low),
            shape((KEYS, width), low),
            shape((VECTORS, width), wide),
        ],
        scratch_shapes=[
            memory_space((KEYS, width), low),
            memory_space((width, 3 * width), low),
            memory_space((32 * VECTORS, 2 * HEAD), low),
            memory_space((VECTORS, width), wide),
            memory_space((QROWS, width), low),
            memory_space((KEYS, width), low),
            memory_space((KEYS, width), low),
            memory_space((QROWS, width), low),
            memory_space((QROWS, width), low),
            memory_space((width, 5 * width), low),
            memory_space((4 * width, width), low),
            memory_space((TILE, 4 * width), low),
            memory_space((TILE, 4 * width), low),
            memory_space((TILE, width), wide),
            memory_space((TILE, width), wide),
            memory_space((TILE, width), wide),
            memory_space((TILE, width), wide),
            memory_space((5, TILE, width), low),
        ]
        + [dma((32,))] * 4
        + [dma((100,)), dma((32,)), dma((32,)), dma((32,))]
        + [dma((PARTNERS + 3,)), dma((PARTNERS + 3,)), dma((14,)), dma((8,))],
        compiler_params=pltpu.CompilerParams(
            vmem_limit_bytes=67043328, collective_id=0, has_side_effects=True
        ),
        name="front",
    )(
        qkv, wide_share, down_share, vec, prompt, kept, sent, memory, prompt_cot, kept_cot,
        sent_cot, bias,
    )


SEND = 13
CHIP, PLANE, LINE, MIDDLE, SPREAD, SHARE, SMALL, PARTNER = range(8)
SLOTS = {
    0: ((PLANE, 0), (CHIP, 2), (PLANE, 1), (CHIP, 3), (CHIP, 4),),
    1: ((LINE, 0),),
    3: ((MIDDLE, 0), (LINE, 1), (PLANE, 2),),
    4: ((PLANE, 3), (CHIP, 5),),
    5: ((SPREAD, 0), (MIDDLE, 1), (PLANE, 4),),
    6: ((LINE, 2),),
    7: ((SHARE, 0), (SPREAD, 1), (LINE, 3), (LINE, 4), (PLANE, 5),),
    8: ((MIDDLE, 2), (LINE, 5), (CHIP, 6),),
    9: ((SHARE, 1), (MIDDLE, 3), (PLANE, 6),),
    10: ((SPREAD, 2), (MIDDLE, 4), (LINE, 6), (CHIP, 7), (MIDDLE, 5),),
    11: ((SPREAD, 3), (MIDDLE, 6), (PLANE, 7),),
}
TAIL = {
    0: ((SHARE, 2), (SPREAD, 4), (LINE, 7),),
    1: ((PLANE, 8), (PARTNER, 1), (PARTNER, 2), (PARTNER, 3), (SPREAD, 5), (SMALL, 0),),
    2: ((MIDDLE, 7), (SMALL, 1),),
    3: ((SHARE, 3), (SPREAD, 6), (SMALL, 2), (LINE, 8), (SPREAD, 7), (SHARE, 4), (MIDDLE, 8), (SHARE, 5), (SPREAD, 8), (SHARE, 6),),
    4: ((SHARE, 7), (SMALL, 3),),
    5: ((SHARE, 8),),
}
LAST = ((SMALL, 4),)
WIDE = 4
NARROW = 3
TINY = 2
ITEMS = WIDE + NARROW + TINY


class Reduce:
    def __init__(self, mine, theirs, got, from_x, from_y, last_x, last_y, outer, total, send, recv):
        self.mine, self.theirs, self.got = mine, theirs, got
        self.from_x, self.from_y, self.last_x, self.last_y = from_x, from_y, last_x, last_y
        self.outer, self.total, self.send, self.recv = outer, total, send, recv
        self.half = mine.shape[1] // 2
        self.z, self.core, self.shard = seat()
        self.inner = (self.z == 1) | (self.z == 2)

    def copy(self, source, target, index, z, core, shard):
        return pltpu.make_async_remote_copy(
            src_ref=source, dst_ref=target, send_sem=self.send.at[index],
            recv_sem=self.recv.at[index], device_id=device_of(z, core, shard), device_id_type=MESH,
        )

    def upper(self, part):
        return self.mine.at[part, pl.ds(0, self.half)]

    def lower(self, part):
        return self.mine.at[part, pl.ds(self.half, self.half)]

    def link(self, index):
        z, core, shard = self.z, self.core, self.shard
        near = jnp.where(z < 2, 1 - z, 5 - z)
        if index < 4:
            ends = (self.theirs.at[index], self.got.at[index], z, 1 - core, shard)
        elif index < 6:
            source = self.upper(shard ^ (1 if index == 4 else 3))
            ends = (source, self.from_x.at[index - 4], z, core, shard ^ 1)
        elif index < 8:
            source = self.lower(shard ^ (2 if index == 6 else 3))
            ends = (source, self.from_y.at[index - 6], z, core, shard ^ 2)
        elif index == 8:
            ends = (self.upper(shard ^ 2), self.last_y, z, core, shard ^ 2)
        elif index == 9:
            ends = (self.lower(shard ^ 1), self.last_x, z, core, shard ^ 1)
        elif index == 10:
            ends = (self.mine.at[shard], self.outer, near, core, shard)
        elif index == 11:
            ends = (self.mine.at[shard], self.total, 3 - z, core, shard)
        else:
            ends = (self.total, self.total, near, core, shard)
        return self.copy(ends[0], ends[1], index, *ends[2:])

    def give(self, part):
        self.copy(
            self.theirs.at[part], self.got.at[part], part, self.z, 1 - self.core, self.shard
        ).start()

    def given(self):
        for part in range(4):
            self.link(part).wait_send()

    def add(self, part, start, count, other):
        def step(index, carry):
            rows = pl.ds(pl.multiple_of(index * 48, 16), 48)
            span = pl.ds(pl.multiple_of(start + index * 48, 16), 48)
            self.mine[part, span] = self.mine[part, span] + other[rows]
            return carry

        lax.fori_loop(0, count // 48, step, 0)

    def chip(self):
        for part in range(4):
            self.link(part).wait_recv()

        def add_part(part, carry):
            self.add(part, 0, 2 * self.half, self.got.at[part])
            return carry

        lax.fori_loop(0, 4, add_part, 0)
        for index in (4, 5, 6, 7):
            self.link(index).start()

    def plane(self):
        shard = self.shard
        self.link(4).wait_recv()
        self.link(5).wait_recv()
        self.add(shard ^ 2, 0, self.half, self.from_x.at[1])
        self.link(8).start()
        self.link(6).wait_recv()
        self.link(7).wait_recv()
        self.add(shard ^ 1, self.half, self.half, self.from_y.at[1])
        self.link(9).start()
        self.add(shard, 0, self.half, self.from_x.at[0])
        self.add(shard, self.half, self.half, self.from_y.at[0])

    def line(self):
        self.link(8).wait_recv()
        self.add(self.shard, 0, self.half, self.last_y)
        self.link(9).wait_recv()
        self.add(self.shard, self.half, self.half, self.last_x)

        @pl.when(jnp.logical_not(self.inner))
        def _():
            self.link(10).start()

    def middle(self):
        @pl.when(self.inner)
        def _():
            self.link(10).wait_recv()
            self.add(self.shard, 0, 2 * self.half, self.outer)
            self.link(11).start()

    def spread(self):
        @pl.when(self.inner)
        def _():
            self.link(11).wait_recv()

            def step(index, carry):
                rows = pl.ds(pl.multiple_of(index * 48, 16), 48)
                self.total[rows] = self.total[rows] + self.mine[self.shard, rows]
                return carry

            lax.fori_loop(0, 2 * self.half // 48, step, 0)
            self.link(12).start()

    def share(self, place, semaphore):
        @pl.when(jnp.logical_not(self.inner))
        def _():
            self.link(12).wait_recv()

        pltpu.make_async_copy(self.total, place, semaphore).start()
        pltpu.make_async_remote_copy(
            src_ref=self.total, dst_ref=place, send_sem=self.send.at[13],
            recv_sem=self.recv.at[13],
            device_id=device_of(self.z, 1 - self.core, self.shard), device_id_type=MESH,
        ).start()

    def finish(self, place, semaphore):
        pltpu.make_async_copy(self.total, place, semaphore).wait()
        last = pltpu.make_async_remote_copy(
            src_ref=self.total, dst_ref=place, send_sem=self.send.at[13],
            recv_sem=self.recv.at[13],
            device_id=device_of(self.z, 1 - self.core, self.shard), device_id_type=MESH,
        )
        last.wait_send()
        last.wait_recv()
        for index in range(4, 10):
            self.link(index).wait_send()

        @pl.when(jnp.logical_not(self.inner))
        def _():
            self.link(10).wait_send()

        @pl.when(self.inner)
        def _():
            self.link(11).wait_send()
            self.link(12).wait_send()


class Butterfly:
    def __init__(self, held, got, send, recv):
        self.held, self.got, self.send, self.recv = held, got, send, recv
        self.z, self.core, self.shard = seat()

    def copy(self, step):
        z, core, shard = self.z, self.core, self.shard
        where = ((z, core, shard ^ 1), (z, core, shard ^ 2), (z ^ 1, core, shard),
                 (z ^ 2, core, shard), (z, 1 - core, shard))[step]
        rows = pl.ds(0, 2 * VECTORS if step < 2 else VECTORS)
        return pltpu.make_async_remote_copy(
            src_ref=self.held.at[step, rows], dst_ref=self.got.at[step, rows],
            send_sem=self.send.at[step], recv_sem=self.recv.at[step],
            device_id=device_of(*where), device_id_type=MESH,
        )

    def start(self):
        self.copy(0).start()

    def step(self, step):
        self.copy(step).wait_recv()
        rows = slice(0, 2 * VECTORS if step < 2 else VECTORS)
        self.held[step + 1, rows] = self.held[step, rows] + self.got[step, rows]
        if step < 4:
            self.copy(step + 1).start()

    def finish(self):
        for step in range(5):
            self.copy(step).wait_send()


def back_piece(
    head, half, query_ref, key_ref, value_ref, bias_ref, log_ref, grad_ref,
    overlap, key_acc, value_acc, query_flip,
):
    mem_valid = lax.broadcasted_iota(jnp.int32, (MEM, 1), 0) < READ
    mask = head_mask(head)
    span = pl.ds(pl.multiple_of(head * HEAD, HEAD), HEAD)

    mine = lax.broadcasted_iota(jnp.int32, (2 * HEAD, 1), 0) // HEAD == head

    def keep(lanes, values):
        query_flip[:, lanes] = jnp.where(mine, values, query_flip[:, lanes])

    def block_back(keys, values, bias, valid, queries, grads, log, delta, rows):
        scores = times_back(keys, queries)
        if bias is not None:
            scores = scores + bias
        chances = jnp.exp(scores - log)
        if valid is not None:
            chances = jnp.where(valid, chances, 0.0)
        slopes = (chances * (times_back(values, grads) - delta)).astype(jnp.bfloat16)
        value_acc[rows] += product(chances.astype(jnp.bfloat16), grads)
        key_acc[rows] += product(slopes, queries)
        return outer_sum(keys, slopes)

    part = slice(half * HALF, (half + 1) * HALF)
    queries = pick(mask, query_ref[part])
    grads = pick(mask, grad_ref[part])
    delta = jnp.sum(overlap[span, part], axis=0, keepdims=True)
    log = log_ref[pl.ds(head, 1), part]
    main_rows = slice(0, 2 * HALF)
    mem_rows = slice(2 * HALF, CONT)
    piece = block_back(
        key_ref[main_rows], value_ref[main_rows], None, None,
        queries, grads, log, delta, main_rows,
    )
    piece += block_back(
        key_ref[mem_rows], value_ref[mem_rows], None, mem_valid,
        queries, grads, log, delta, mem_rows,
    )
    if half == 0:
        keep(part, piece)
        return
    own_parts = []
    for cont in range(OWN // CLEN):
        rows = slice(CONT + cont * CLEN, CONT + (cont + 1) * CLEN)
        part = slice(cont * CLEN, (cont + 1) * CLEN)
        own_parts.append(
            block_back(
                key_ref[rows], value_ref[rows], bias_ref[:, part], None,
                queries[part], grads[part], log[:, part], delta[:, part], rows,
            )
        )
    keep(slice(HALF, QROWS), piece + jnp.concatenate(own_parts, axis=1))


def back_kernel(
    act_ref, gdown_ref, first_ref, ginner_ref, mixed_all, gbranch_ref, ghidden_ref, rows_ref,
    qkv_ref, out_ref, sums_ref,
    query_ref, key_ref, value_ref, grad_ref, mixed_ref, log_ref, bias_ref,
    down_out, up_out, out_out, qkv_out, last_out, returned_out, grad_prompt, grad_kept, grad_back,
    memory_out, vec_out,
    wide_mine, wide_theirs, wide_got, wide_x, wide_y, wide_lx, wide_ly, wide_outer, wide_total,
    thin_mine, thin_theirs, thin_got, thin_x, thin_y, thin_lx, thin_ly, thin_outer, thin_total,
    tiny_mine, tiny_theirs, tiny_got, tiny_x, tiny_y, tiny_lx, tiny_ly, tiny_outer, tiny_total,
    pool, rows, dquery, dkey, dvalue, key_acc, value_acc, overlap, query_flip,
    partner, ghidden, staged, held, got,
    send, recv, small_send, small_recv, swap_send, swap_recv, local, out_sem,
):
    pair = pl.program_id(0)
    z, core, shard = seat()
    other = 1 - core
    width = rows_ref.shape[1]
    part_rows = width // 4
    low = jnp.bfloat16

    def item(index):
        if isinstance(index, int) and index >= WIDE:
            return thin(index - WIDE) if index < WIDE + NARROW else tiny(index - WIDE - NARROW)
        return Reduce(
            wide_mine.at[index], wide_theirs.at[index % 2], wide_got.at[index],
            wide_x.at[index], wide_y.at[index], wide_lx.at[index], wide_ly.at[index],
            wide_outer.at[index], wide_total.at[index], send.at[index], recv.at[index],
        )

    def thin(index):
        return Reduce(
            thin_mine.at[index], thin_theirs.at[index % 2], thin_got.at[index],
            thin_x.at[index], thin_y.at[index], thin_lx.at[index], thin_ly.at[index],
            thin_outer.at[index], thin_total.at[index], send.at[WIDE + index],
            recv.at[WIDE + index],
        )

    def tiny(index):
        number = WIDE + NARROW + index
        return Reduce(
            tiny_mine.at[index], tiny_theirs.at[index % 2], tiny_got.at[index],
            tiny_x.at[index], tiny_y.at[index], tiny_lx.at[index], tiny_ly.at[index],
            tiny_outer.at[index], tiny_total.at[index], send.at[number], recv.at[number],
        )

    small = Butterfly(held, got, small_send, small_recv)
    half_hidden = width // 2

    def place(index):
        if index < 2:
            start = core * half_hidden + index * part_rows
            return down_out.at[pl.ds(pl.multiple_of(start, 64), part_rows)]
        if index < 4:
            start = core * (2 * width) + (index - 2) * width
            return up_out.at[:, pl.ds(pl.multiple_of(start, 128), width)]
        if index == 4:
            return out_out.at[:, pl.ds(pl.multiple_of(core * half_hidden, 128), half_hidden)]
        if index < WIDE + NARROW:
            return qkv_out.at[index - 5, core]
        start = pl.multiple_of(core * (part_rows // 2), 16)
        return last_out.at[index - WIDE - NARROW, pl.ds(start, part_rows // 2)]

    def stage(name, index):
        if name == SHARE:
            item(index).share(place(index), out_sem.at[index])
        else:
            held = item(index)
            (held.chip, held.plane, held.line, held.middle, held.spread)[name]()

    returned = Swap(
        out_ref.at[pl.ds(HALF + OWN // 2, OWN // 2)], returned_out, swap_send.at[0], swap_recv.at[0], z, core, shard ^ 2
    )
    def to_partner(index):
        span = pl.ds(pl.multiple_of(128 * index, 128), 128)
        return Swap(
            pool.at[3, span], partner.at[span], swap_send.at[index + 1], swap_recv.at[index + 1],
            z, core, shard ^ 1,
        )

    cont_back = Swap(
        pool.at[3, pl.ds(2 * 256, 256)], grad_back, swap_send.at[5], swap_recv.at[5],
        z, core, shard ^ 2,
    )

    def load(source, slot, semaphore):
        return pltpu.make_async_copy(source, pool.at[slot], local.at[semaphore])

    def act_chunk(part):
        return load(act_ref.at[:, pl.ds(part * width, width)], part % 2, part % 2)

    def inner_chunk(step):
        half = other if step < 2 else core
        start = pl.multiple_of(half * (2 * width) + (step % 2) * width, 128)
        return load(ginner_ref.at[:, pl.ds(start, width)], step % 2, step % 2)

    def parts_of(target, values):
        for part in range(4):
            target[part] = values[part * part_rows : (part + 1) * part_rows].astype(low)

    load_rows = pltpu.make_async_copy(rows_ref, rows, local.at[4])

    def inner_load(step):
        half = jnp.where(step < 2, other, core)
        start = pl.multiple_of(half * (2 * width) + (step % 2) * width, 128)
        return load(ginner_ref.at[:, pl.ds(start, width)], step % 2, step % 2)

    def act_load(part):
        lanes = pl.ds(pl.multiple_of(part * width, 128), width)
        return load(act_ref.at[:, lanes], part % 2, part % 2)

    def weight_load(index):
        return pltpu.make_async_copy(
            qkv_ref.at[:, pl.ds(index * width, width)],
            pool.at[index, pl.ds(0, width)], local.at[index],
        )

    def down_part(part, carry):
        act_load(part).wait()

        def down_half(side, carry):
            half = jnp.where(side == 0, other, core)
            lanes = pl.ds(pl.multiple_of(half * half_hidden, 128), half_hidden)
            result = outer_sum(pool[part % 2, :, lanes], pool[2]).astype(low)
            for index in range(2):
                piece = result[index * part_rows : (index + 1) * part_rows]

                @pl.when(side == 0)
                def _():
                    wide_theirs[index, part] = piece
                    item(index).give(part)

                @pl.when(side == 1)
                def _():
                    wide_mine[index, part] = piece

            return carry

        lax.fori_loop(0, 2, down_half, 0)

        @pl.when(part < 2)
        def _():
            act_load(part + 2).start()

        @pl.when(part >= 2)
        def _():
            inner_load(part - 2).start()

        return carry

    def up_part(step, carry):
        inner_load(step).wait()
        result = outer_sum(pool[3], pool[step % 2])

        @pl.when(step < 2)
        def _():
            item(step).given()
            parts_of(wide_theirs.at[step], result)
            for part in range(4):
                item(step + 2).give(part)
            inner_load(step + 2).start()

        @pl.when(step >= 2)
        def _():
            parts_of(wide_mine.at[step], result)

        @pl.when((step == 1) | (step == 2))
        def _():
            item(step - 1).chip()

        return carry

    def out_half(side, carry):
        half = jnp.where(side == 0, other, core)
        lanes = pl.ds(pl.multiple_of(half * half_hidden, 128), half_hidden)
        result = outer_sum(pool[2], pool[3, :, lanes])

        @pl.when(side == 0)
        def _():
            parts_of(thin_theirs.at[0], result)
            for part in range(4):
                thin(0).give(part)

        @pl.when(side == 1)
        def _():
            parts_of(thin_mine.at[0], result)

        return carry

    def qkv_part(index):
        def one_half(side, carry):
            half = jnp.where(side == 0, other, core)
            lanes = pl.ds(pl.multiple_of((2 * index + half) * (2 * HEAD), 2 * HEAD), 2 * HEAD)
            query_side = outer_sum(rows[:HALF], dquery[:HALF, lanes])
            query_side += outer_sum(rows[CONT:], dquery[HALF:, lanes])
            both = jnp.concatenate([dkey[:, lanes], dvalue[:, lanes]], axis=1)
            result = jnp.concatenate([query_side, outer_sum(rows[...], both)], axis=1)

            @pl.when(side == 0)
            def _():
                @pl.when(index > 0)
                def _():
                    thin(0).given()

                parts_of(thin_theirs.at[(1 + index) % 2], result)
                for part in range(4):
                    thin(1 + index).give(part)

            @pl.when(side == 1)
            def _():
                parts_of(thin_mine.at[1 + index], result)

            return carry

        lax.fori_loop(0, 2, one_half, 0)

    def last_part(index):
        lanes = pl.ds(pl.multiple_of((4 + index) * (2 * HEAD), 2 * HEAD), 2 * HEAD)
        query_side = outer_sum(rows[:HALF], dquery[:HALF, lanes])
        query_side += outer_sum(rows[CONT:], dquery[HALF:, lanes])
        both = jnp.concatenate([dkey[:, lanes], dvalue[:, lanes]], axis=1)
        result = jnp.concatenate([query_side, outer_sum(rows[...], both)], axis=1).astype(low)
        half = part_rows // 2
        for side in range(2):

            @pl.when(core == side)
            def _():
                for part in range(4):
                    start = part * part_rows
                    tiny_theirs[index % 2, part] = result[
                        start + (1 - side) * half : start + (2 - side) * half
                    ]
                    tiny_mine[index, part] = result[start + side * half : start + (side + 1) * half]

        for part in range(4):
            tiny(index).give(part)

    @pl.when(pair == 0)
    def _():
        act_load(0).start()
        load(gdown_ref, 2, 2).start()
        act_load(1).start()
        load(first_ref, 3, 3).start()
        load_rows.start()
        greet()
        returned.start()
        load(gdown_ref, 2, 2).wait()
        lax.fori_loop(0, 4, down_part, 0)
        load(mixed_all, 2, 2).start()
        load(first_ref, 3, 3).wait()
        lax.fori_loop(0, 4, up_part, 0)
        load(gbranch_ref, 3, 3).start()
        load(mixed_all, 2, 2).wait()
        load(gbranch_ref, 3, 3).wait()
        lax.fori_loop(0, 2, out_half, 0)
        for index in range(3):
            weight_load(index).start()
        load_rows.wait()

    lanes = pl.ds(pl.multiple_of(pair * (2 * HEAD), 2 * HEAD), 2 * HEAD)
    overlap[...] = (mixed_ref[...].astype(jnp.float32) * grad_ref[...].astype(jnp.float32)).T
    key_acc[...] = jnp.zeros_like(key_acc)
    value_acc[...] = jnp.zeros_like(value_acc)

    def piece_body(piece, carry):
        for half in range(2):
            back_piece(
                piece, half, query_ref, key_ref, value_ref, bias_ref, log_ref, grad_ref,
                overlap, key_acc, value_acc, query_flip,
            )

        @pl.when(piece == 1)
        def _():
            dquery[:, lanes] = (query_flip[...].T * SCALE).astype(low)
            dkey[:, lanes] = key_acc[...].astype(low)
            dvalue[:, lanes] = value_acc[...].astype(low)

        @pl.when((piece == 1) & (pair % 2 == 1) & (pair < 4))
        def _():
            qkv_part(pair // 2)

        @pl.when((piece == 1) & (pair >= 4))
        def _():
            last_part(pair - 4)

        for number, stages in SLOTS.items():

            @pl.when(pair * 2 + piece == number)
            def _():
                for name, index in stages:
                    stage(name, index)

        return carry

    lax.fori_loop(0, 2, piece_body, 0)

    def hidden_load(step):
        start = pl.multiple_of((5 - step) * 256, 256)
        return pltpu.make_async_copy(
            ghidden_ref.at[pl.ds(start, 256)], ghidden.at[step % 2], local.at[5 + step % 2]
        )

    def staged_store(step):
        slot = step % 2
        return staged.at[slot], local.at[8 + slot]

    def chunk_body(step, carry):
        start = jnp.where(step < 2, HALF + 256 * step, jnp.where(step < 4, CONT, HALF))
        start = jnp.where(step >= 2, start + jnp.where(step % 2 == 0, 256, 0), start)
        start = jnp.where(step >= 4, start - HALF, start)
        span = pl.ds(pl.multiple_of(start, MEM), 256)
        result = times_back(dkey[span], pool[1, :width]) + times_back(dvalue[span], pool[2, :width])

        @pl.when(step < 2)
        def _():
            pool[3, pl.ds(pl.multiple_of(256 * step, 256), 256)] = result.astype(low)

        @pl.when(step == 0)
        def _():
            to_partner(0).start()

        @pl.when(step >= 2)
        def _():
            hidden_load(step).wait()
            mine = pl.ds(pl.multiple_of((5 - step) * 256, 256), 256)
            full = result + (
                ghidden[step % 2] + times_back(dquery[mine], pool[0, :width])
            )

            @pl.when(step == 2)
            def _():
                pool[3, 512:768] = full.astype(low)
                cont_back.start()

            @pl.when(step == 3)
            def _():
                staged[1] = full.astype(low)
                pltpu.make_async_copy(staged.at[1], grad_kept, local.at[9]).start()

            @pl.when(step >= 4)
            def _():
                to_partner(2 * (5 - step)).arrive()
                to_partner(2 * (5 - step) + 1).arrive()

                @pl.when(step == 5)
                def _():
                    pltpu.make_async_copy(staged.at[1], grad_kept, local.at[9]).wait()

                mine = pl.ds(pl.multiple_of((5 - step) * 256, 256), 256)
                staged[step % 2] = (full + partner[mine].astype(jnp.float32)).astype(low)
                pltpu.make_async_copy(
                    staged.at[step % 2], grad_prompt.at[mine], local.at[8 + step % 2]
                ).start()

            @pl.when(step < 4)
            def _():
                hidden_load(step + 2).start()

        for number, stages in TAIL.items():

            @pl.when(step == number)
            def _():
                for name, index in stages:
                    if name == SMALL:
                        small.step(index)
                    elif name == PARTNER:
                        to_partner(index).start()
                    else:
                        stage(name, index)

        return carry

    @pl.when(pair == PAIRS - 1)
    def _():
        hidden_load(2).start()
        hidden_load(3).start()
        sums = pltpu.make_async_copy(sums_ref, held.at[0, pl.ds(0, VECTORS)], local.at[7])
        sums.start()
        for index in range(3):
            weight_load(index).wait()
        sums.wait()
        held[0, 0:1] = jnp.sum(dquery[...].astype(jnp.float32), axis=0, keepdims=True)
        held[0, 1:2] = jnp.sum(dvalue[...].astype(jnp.float32), axis=0, keepdims=True)
        mem_span = slice(2 * HALF, CONT)
        held[0, VECTORS:] = times_back(dkey[mem_span], pool[1, :width]) + times_back(
            dvalue[mem_span], pool[2, :width]
        )
        stage(CHIP, 8)
        small.start()
        lax.fori_loop(0, 6, chunk_body, 0)
        for name, index in LAST:
            if name == SMALL:
                small.step(index)
            else:
                stage(name, index)
        family = shard // 2
        memory_out[family] = held[1, VECTORS:]
        memory_out[1 - family] = got[1, VECTORS:]
        vec_out[...] = held[5, :VECTORS]
        returned.arrive()
        cont_back.arrive()
        for step in (4, 5):
            mine = pl.ds((5 - step) * 256, 256)
            pltpu.make_async_copy(
                staged.at[step % 2], grad_prompt.at[mine], local.at[8 + step % 2]
            ).wait()
        for index in (2, 3, 4, 5, 6, 7, 8):
            if index != 4:
                item(index).given()
        for index in range(ITEMS):
            item(index).finish(place(index), out_sem.at[index])
        small.finish()
        for swap in (returned, cont_back, *(to_partner(index) for index in range(4))):
            swap.finish()


def back(
    act, gdown, first, ginner, mixed, gbranch, ghidden, rows, qkv, out_taken, sums,
    query, key, value, grads, log, bias,
):
    width = rows.shape[1]
    low = jnp.bfloat16
    wide = jnp.float32

    def block(count):
        return pl.BlockSpec((count, 2 * HEAD), lambda pair: (0, pair))

    dma = pltpu.SemaphoreType.DMA
    part = width // 4

    def buffers(count, columns, part=part):
        return [
            pltpu.VMEM((count, 4, part, columns), low),
            pltpu.VMEM((2, 4, part, columns), low),
            pltpu.VMEM((count, 4, part, columns), low),
            pltpu.VMEM((count, 2, part // 2, columns), low),
            pltpu.VMEM((count, 2, part // 2, columns), low),
            pltpu.VMEM((count, part // 2, columns), low),
            pltpu.VMEM((count, part // 2, columns), low),
            pltpu.VMEM((count, part, columns), low),
            pltpu.VMEM((count, part, columns), low),
        ]

    shape = jax.ShapeDtypeStruct
    return pl.pallas_call(
        back_kernel,
        grid=(PAIRS,),
        in_specs=[WHERE] * 11
        + [
            block(QROWS), block(KEYS), block(KEYS), block(QROWS), block(QROWS),
            pl.BlockSpec((None, 2, QROWS), lambda pair: (pair, 0, 0)),
            pl.BlockSpec((CLEN, OWN), lambda pair: (0, 0)),
        ],
        out_specs=[WHERE] * 9
        + [
            pl.BlockSpec((2, MEM, width), lambda pair: (0, 0, 0)),
            pl.BlockSpec((VECTORS, width), lambda pair: (0, 0)),
        ],
        out_shape=[
            shape((width, width), low),
            shape((part, 4 * width), low),
            shape((part, width), low),
            shape((2, 2, part, width // 2), low),
            shape((TINY, part, width // 2), low),
            shape((OWN // 2, width), low),
            shape((HALF, width), low),
            shape((OWN // 2, width), low),
            shape((OWN // 2, width), low),
            shape((2, MEM, width), wide),
            shape((VECTORS, width), wide),
        ],
        scratch_shapes=buffers(WIDE, width)
        + buffers(NARROW, width // 2)
        + buffers(TINY, width // 2, part // 2)
        + [
            pltpu.VMEM((4, QROWS, width), low),
            pltpu.VMEM((KEYS, width), low),
            pltpu.VMEM((QROWS, width), low),
            pltpu.VMEM((KEYS, width), low),
            pltpu.VMEM((KEYS, width), low),
            pltpu.VMEM((KEYS, 2 * HEAD), wide),
            pltpu.VMEM((KEYS, 2 * HEAD), wide),
            pltpu.VMEM((2 * HEAD, QROWS), wide),
            pltpu.VMEM((2 * HEAD, QROWS), wide),
            pltpu.VMEM((HALF, width), low),
            pltpu.VMEM((2, 256, width), wide),
            pltpu.VMEM((2, 256, width), low),
            pltpu.VMEM((6, 2 * VECTORS, width), wide),
            pltpu.VMEM((5, 2 * VECTORS, width), wide),
            dma((ITEMS, SEND + 1)),
            dma((ITEMS, SEND + 1)),
            dma((5,)),
            dma((5,)),
            dma((6,)),
            dma((6,)),
            dma((10,)),
            dma((ITEMS,)),
        ],
        compiler_params=pltpu.CompilerParams(
            vmem_limit_bytes=67043328, collective_id=1, has_side_effects=True
        ),
        name="back",
    )(
        act, gdown, first, ginner, mixed, gbranch, ghidden, rows, qkv, out_taken, sums,
        query, key, value, grads, mixed, log, bias,
    )


def cont_ranks(owner_ref, shard):
    prompt_of = shard // 2
    conts = OWN // CLEN
    place = []
    before = jnp.int32(0)
    for cont in range(conts):
        owned = (owner_ref[0, shard * conts + cont] == prompt_of).astype(jnp.int32)
        place.append(jnp.where(owned == 1, before, 2 + cont - before))
        before = before + owned
    order = []
    for position in range(conts):
        found = jnp.int32(0)
        for cont in range(conts):
            found = found + jnp.where(place[cont] == position, cont, 0)
        order.append(found)
    return place, order


def block_of(index):
    return pl.ds(pl.multiple_of(index * CLEN, CLEN), CLEN)


def prepare_kernel(
    owner_ref, length_ref, follow_ref, cotan_ref, memory_ref, query_ref, key_ref, value_ref,
    out_ref, up_ref, *refs,
):
    vectors = refs[:9]
    (
        qkv, wide, vec, kept, sent, memory, kept_cot, sent_cot, bias,
    ) = refs[9:]
    shard = lax.axis_index("shard")
    across = shard ^ 2
    conts = OWN // CLEN
    width = query_ref.shape[1]
    _, order = cont_ranks(owner_ref, shard)
    _, order_across = cont_ranks(owner_ref, across)
    for index in range(2):
        span = slice(index * CLEN, (index + 1) * CLEN)
        kept[span] = follow_ref[0, block_of(order[index])]
        sent[span] = follow_ref[0, block_of(order[2 + index])]
        kept_cot[span] = cotan_ref[0, block_of(order[index])]
        sent_cot[span] = cotan_ref[0, block_of(order[2 + index])]
    position = lax.broadcasted_iota(jnp.int32, (CLEN, CLEN), 0)
    for index in range(conts):
        if index < 2:
            length = length_ref[0, shard * conts + order[index]]
        else:
            length = length_ref[0, across * conts + order_across[index]]
        valid = (position < length) | (position >= CLEN - WRITE)
        bias[:, index * CLEN : (index + 1) * CLEN] = jnp.where(valid, 0.0, NEGATIVE)
    memory[...] = jnp.zeros_like(memory)
    memory[:READ] = memory_ref[0, shard // 2]
    qkv[:, :width] = query_ref[...]
    qkv[:, width : 2 * width] = key_ref[...]
    qkv[:, 2 * width :] = value_ref[...]
    wide[:, :width] = out_ref[...]
    wide[:, width:] = up_ref[...]
    vec[...] = jnp.zeros_like(vec)
    for index, vector in enumerate(vectors):
        vec[index : index + 1, : vector.shape[1]] = vector[...]


def prepare(owner, length, follow, cotan, memory, query, key, value, out, up, vectors):
    low = jnp.bfloat16
    width = query.shape[1]
    share = query.shape[0]
    shape = jax.ShapeDtypeStruct
    half = shape((OWN // 2, width), low)
    inside = pl.BlockSpec(memory_space=pltpu.VMEM)
    scalars = pl.BlockSpec(memory_space=pltpu.SMEM)
    return pl.pallas_call(
        prepare_kernel,
        in_specs=[scalars] * 2 + [inside] * 17,
        out_specs=[inside] * 9,
        out_shape=[
            shape((share, 3 * width), low), shape((share, 5 * width), low),
            shape((VECTORS, 2 * HEAD), low), half, half, shape((MEM, width), low), half, half,
            shape((CLEN, OWN), jnp.float32),
        ],
        name="prepare",
    )(
        owner, length, follow, cotan, memory, query, key, value, out, up,
        *(vector[None] for vector in vectors),
    )


def finish_kernel(
    owner_ref, output_ref, returned_ref, prompt_ref, kept_grad, back_grad, down_ref, up_ref, out_ref, qkv_ref,
    last_ref, memory_ref, vec_ref,
    prompt_out, follow_out, prompt_grad, follow_grad, memory_grad, query_sum, key_sum, value_sum, out_sum,
    up_sum, down_sum, *vectors,
):
    shard = lax.axis_index("shard")
    wide = jnp.float32
    width = down_ref.shape[1]
    part = width // 4
    place, _ = cont_ranks(owner_ref, shard)
    prompt_out[0] = output_ref[:HALF]
    prompt_grad[0] = prompt_ref[...]
    for cont, position in enumerate(place):
        span = slice(cont * CLEN, (cont + 1) * CLEN)
        here = block_of(jnp.where(position < 2, position, 0))
        there = block_of(jnp.where(position < 2, 0, position - 2))
        kept = position < 2

        @pl.when(kept)
        def _():
            follow_out[0, span] = output_ref[pl.ds(HALF + here.start, CLEN)]
            follow_grad[0, span] = kept_grad[here]

        @pl.when(jnp.logical_not(kept))
        def _():
            follow_out[0, span] = returned_ref[there]
            follow_grad[0, span] = back_grad[there]

    memory_grad[0] = memory_ref[:, :READ].astype(jnp.bfloat16)
    down_sum[...] = down_ref[...].astype(wide)
    up_sum[...] = up_ref[...].astype(wide)
    out_sum[...] = out_ref[...].astype(wide)
    for number, target in enumerate((query_sum, key_sum, value_sum)):
        source = slice(number * 2 * HEAD, (number + 1) * 2 * HEAD)
        for index in range(TINY):
            lanes = slice((4 + index) * 2 * HEAD, (5 + index) * 2 * HEAD)
            target[:, lanes] = last_ref[index, :, source].astype(wide)
    for index in range(2):
        for side in range(2):
            lanes = slice((2 * index + side) * 2 * HEAD, (2 * index + side + 1) * 2 * HEAD)
            for number, target in enumerate((query_sum, key_sum, value_sum)):
                source = slice(number * 2 * HEAD, (number + 1) * 2 * HEAD)
                target[:, lanes] = qkv_ref[index, side, :, source].astype(wide)
    for index in range(8):
        row = vec_ref[index : index + 1]
        total = jnp.zeros((1, part), wide)
        for quarter in range(4):
            total += jnp.where(shard == quarter, row[:, quarter * part : (quarter + 1) * part], 0.0)
        vectors[index][...] = total.reshape(part)
    total = jnp.zeros((1, width), wide)
    for quarter in range(4):
        total += jnp.where(shard == quarter, vec_ref[8 + quarter : 9 + quarter], 0.0)
    vectors[8][...] = total.reshape(width)


def finish(owner, output, returned, prompt, kept, back_grad, down, up, out, qkv, last, memory, vec):
    low = jnp.bfloat16
    wide = jnp.float32
    shape = jax.ShapeDtypeStruct
    width = down.shape[1]
    part = width // 4
    inside = pl.BlockSpec(memory_space=pltpu.VMEM)
    square = shape((part, width), wide)

    def whole(array):
        return pl.BlockSpec(array.shape, lambda step: (0,) * array.ndim)

    return pl.pallas_call(
        finish_kernel,
        grid=(1,),
        in_specs=[pl.BlockSpec(memory_space=pltpu.SMEM)]
        + [
            whole(array)
            for array in (
                output, returned, prompt, kept, back_grad, down, up, out, qkv, last, memory, vec
            )
        ],
        out_specs=[inside] * 20,
        out_shape=[
            shape((1, HALF, width), low), shape((1, OWN, width), low),
            shape((1, HALF, width), low), shape((1, OWN, width), low),
            shape((1, 2, READ, width), low), square, square, square, square,
            shape((part, 4 * width), wide), shape((width, width), wide),
        ]
        + [shape((part,), wide)] * 8
        + [shape((width,), wide)],
        compiler_params=pltpu.CompilerParams(vmem_limit_bytes=67043328),
        name="finish",
    )(owner, output, returned, prompt, kept, back_grad, down, up, out, qkv, last, memory, vec)


def body_pairs(
    prompt_rows, follow_rows, memory_rows, follow_owner, follow_length,
    query_weight, key_weight, value_weight, out_weight, query_bias, value_bias, out_bias,
    first_gain, first_shift, up_weight, up_bias, down_weight, down_bias,
    second_gain, second_shift, prompt_cotan, follow_cotan,
):
    qkv, wide, vec, kept, sent, memory, kept_cot, sent_cot, bias = prepare(
        follow_owner, follow_length, follow_rows, follow_cotan, memory_rows,
        query_weight, key_weight, value_weight, out_weight, up_weight,
        (
            query_bias, value_bias, out_bias, first_gain, first_shift, down_bias,
            second_gain, second_shift, up_bias,
        ),
    )
    (
        qkv_mat, _, _, _, key_rows,
        output, activated, first_low, grad_down, grad_inner, grad_branch, grad_mixed, grad_hidden,
        mixed, log, query_low, key_low, value_low, sums,
    ) = front(
        qkv, wide, down_weight, vec, prompt_rows[0], kept, sent, memory, prompt_cotan[0],
        kept_cot, sent_cot, bias,
    )
    (
        down_sum, up_sum, out_sum, qkv_sum, last_sum, returned_out, grad_prompt, grad_kept, returned_grad,
        memory_sum, sums,
    ) = back(
        activated, grad_down, first_low, grad_inner, mixed, grad_branch, grad_hidden, key_rows,
        qkv_mat, output, sums,
        query_low, key_low, value_low, grad_mixed, log, bias,
    )
    (
        prompt_out, follow_out, prompt_grad, follow_grad, grad_memory, query_sum, key_sum, value_sum, out_sum,
        up_sum, down_sum, *vectors,
    ) = finish(
        follow_owner, output, returned_out, grad_prompt, grad_kept, returned_grad, down_sum, up_sum, out_sum,
        qkv_sum, last_sum, memory_sum, sums,
    )
    return (
        prompt_out, follow_out, prompt_grad, follow_grad, grad_memory,
        query_sum, key_sum, value_sum, out_sum, vectors[0], vectors[1], vectors[2], vectors[3],
        vectors[4], up_sum, vectors[8], down_sum, vectors[5], vectors[6], vectors[7],
    )


def solution(mesh):
    return jax.shard_map(
        body_pairs if pairs_fit(mesh) else body_any,
        mesh=mesh,
        in_specs=(
            P("grp", "shard", None),
            P("grp", "shard", None),
            P("grp", None, None, None),
            P("grp", None),
            P("grp", None),
            P(("grp", "shard"), None),
            P(("grp", "shard"), None),
            P(("grp", "shard"), None),
            P(("grp", "shard"), None),
            P(("grp", "shard")),
            P(("grp", "shard")),
            P(("grp", "shard")),
            P(("grp", "shard")),
            P(("grp", "shard")),
            P(("grp", "shard"), None),
            P(("grp", "shard")),
            P(("grp", "shard"), None),
            P(("grp", "shard")),
            P(("grp", "shard")),
            P(("grp", "shard")),
            P("grp", "shard", None),
            P("grp", "shard", None),
        ),
        out_specs=(
            P("grp", "shard", None),
            P("grp", "shard", None),
            P("grp", "shard", None),
            P("grp", "shard", None),
            P("grp", None, None, None),
            P("shard", None),
            P("shard", None),
            P("shard", None),
            P("shard", None),
            P("shard"),
            P("shard"),
            P("shard"),
            P("shard"),
            P("shard"),
            P("shard", None),
            P("shard"),
            P("shard", None),
            P("shard"),
            P("shard"),
            P("shard"),
        ),
        check_vma=False,
    )
```
